32 devices in a mesh: dp: 16 (over z, y, x), seq: 2 (over core).
Axes of the slice: x: 2, y: 2, z: 4, core: 2. Of those that a mesh axis runs over, the one named last changes fastest.
Arguments:
- tokens: bfloat16 [16, 1024, 768], P('dp', 'seq'), may hold values from -6 to 6
- cotangent: bfloat16 [16, 1024, 768], P('dp', 'seq'), may hold values from -6 to 6
- page_boxes: int32 [4, 16, 1024], P(None, 'dp', 'seq'), may hold values from 0 to 1000
- page_lengths: int32 [16, 4], P('dp'), may hold values from 1 to 512, 1024 in all within a row
- padding: int32 [16, 1024], P('dp', 'seq'), may hold values 0 or 1
- buckets: int32 [16, 1024, 1024], P('dp', 'seq'), may hold values from 0 to 31
- master: float32 [7186560], P(('dp', 'seq')), may hold values from -4 to 4
- first_moment: float32 [7186560], P(('dp', 'seq')), may hold values from -1.5 to 1.5
- second_moment: float32 [7186560], P(('dp', 'seq')), may hold values from 0.005 to 0.1
Outputs:
- activations: bfloat16 [16, 1024, 768], P('dp', 'seq')
- input_grad: float32 [16, 1024, 768], P('dp', 'seq')
- param_step: float32 [7186560], P(('dp', 'seq'))
- new_first: float32 [7186560], P(('dp', 'seq'))
- new_second: float32 [7186560], P(('dp', 'seq'))
The draws below stay inside these ranges and needn't reach their ends.
Inputs may be any that keep to these rules, and one draw needn't show every extreme that they name: `page_lengths`: each block's 4 page lengths sum to 1024; the longest page of each block has 512 tokens.
All inputs are finite; a program needn't handle non-finite values. No bound on the sum of `padding` on one device may be relied on, other than what follows from the above.
Results may differ from the reference program's by a relative error of at most 0.015.
The reference program's roundings to bfloat16 on the way count: a program that leaves them out, or rounds other values in their place, can miss the bound.
Values may be sent and summed in bfloat16 or wider, within the bound.
A program may use at most 192 MiB of HBM per device.

```python
import math
import jax
import jax.numpy as jnp
import numpy as np
from jax import lax

D = 768
H = 12
HD = 64
FF = 3072
BUCKETS = 32
FREQ = 16
LF = 128
LAYERS = 1
BLOCK = 1024
PAGES = 4
STEP = 10
BLOCKS = 16
ENTRY = 99456
LAYER_PARAMS = 7087104
RAW = 7186560
P_SIZE = 7186560


def draw_master(key, part):
    root_d = 1.0 / math.sqrt(D)
    segments = [(LF * D, 1.0 / math.sqrt(LF), 0.0), (D, 0.5, 0.0), (BUCKETS * H, 1.0, 0.0)]
    per_layer = [(D * D, root_d, 0.0), (D, 0.5, 0.0), (D * D, root_d, 0.0), (D * D, root_d, 0.0), (D, 0.5, 0.0), (D * D, 4.0 * root_d, 0.0), (D, 0.5, 0.0), (D, 0.1, 1.0), (D, 0.3, 0.0), (D * FF, root_d, 0.0), (FF, 0.5, 0.0), (FF * D, 1.0 / math.sqrt(FF), 0.0), (D, 0.3, 0.0), (D, 0.1, 1.0), (D, 0.3, 0.0)]
    segments = segments + per_layer * LAYERS + [(P_SIZE - RAW, 0.05, 0.0)]
    deviation = jnp.concatenate([jnp.full((amount,), spread_value, jnp.float32) for amount, spread_value, center_value in segments])
    centers = jnp.concatenate([jnp.full((amount,), center_value, jnp.float32) for amount, spread_value, center_value in segments])
    noise = jnp.clip(jax.random.normal(key, (P_SIZE,), jnp.float32), -3.5, 3.5)
    return centers + deviation * noise


def place_ends(entries, stream_key, low, largest):
    extent = entries.shape
    index_at = [jax.random.randint(jax.random.fold_in(stream_key, axis), (), 0, extent[axis]) for axis in range(len(extent))]
    entries = entries.at[tuple(index_at)].set(low)
    longest = extent.index(max(extent))
    index_at[longest] = (index_at[longest] + 1) % extent[longest]
    return entries.at[tuple(index_at)].set(largest)


def levels(stream_key, dims, cuts, least, high):
    def one(position, blocks):
        heights = jax.random.uniform(jax.random.fold_in(jax.random.fold_in(stream_key, 6), position), (blocks,), jnp.float32, least / len(cuts), high / len(cuts))
        return jnp.repeat(jnp.exp(heights), dims[position] // blocks).reshape((-1,) + (1,) * (len(dims) - position - 1))

    level = one(*cuts[0])
    for cut in cuts[1:]:
        level = level * one(*cut)
    return level


def length_profile(count, total, limit, skew):
    loads = [(1 << 20) // math.isqrt(rank ** skew) + 1 for rank in range(2, count + 1)]
    spare, given = total - limit - (count - 1), [1] * (count - 1)
    while spare > 0:
        free = [i for i in range(count - 1) if given[i] < limit]
        mass, remaining = sum([loads[i] for i in free]), spare
        for i in free:
            addition = min(limit - given[i], max(1, remaining * loads[i] // mass), spare)
            given[i] = given[i] + addition
            spare = spare - addition
    return np.array([limit] + given)


def uneven_parts(rng, count, total, reach, slope):
    if count == 2:
        one = jax.random.randint(rng, (), max(1, total - reach), min(reach, total - 1) + 1)
        return jnp.stack([one, total - one])
    lengths = jnp.asarray(length_profile(count, total, reach, slope), jnp.int32)
    couples = (count - 1) // 2
    giver, receiver = lengths[1:1 + 2 * couples:2], lengths[2:2 + 2 * couples:2]
    slack = jnp.minimum(giver - 1, reach - receiver)
    passed = jax.random.randint(jax.random.fold_in(rng, 1), (couples,), 0, 1 << 20) % (slack + 1)
    lengths = lengths.at[1:1 + 2 * couples:2].set(giver - passed).at[2:2 + 2 * couples:2].set(receiver + passed)
    return lengths[jax.random.permutation(jax.random.fold_in(rng, 2), count)]


def normal_values(key, dims, width, limit, cuts=(), kind=jnp.bfloat16):
    entries = width * jax.random.normal(key, dims, jnp.float32)
    if cuts:
        entries = entries * levels(key, dims, cuts, -0.22, 0.18)
    return jnp.clip(entries, -limit, limit).astype(kind)


def setup_inputs(seed: int = 0) -> dict:
    key_of = jax.random.split(jax.random.key(seed), 10)
    return {
        "tokens": normal_values(key_of[0], (BLOCKS, BLOCK, D), 1.0, 6.0, ((0, 16), (1, 2))),
        "cotangent": normal_values(key_of[1], (BLOCKS, BLOCK, D), 1.0, 6.0, ((0, 16), (1, 2))),
        "page_boxes": place_ends(jax.random.randint(key_of[2], (4, BLOCKS, BLOCK), 0, 1001), jax.random.fold_in(key_of[2], 1), 0, 1000).astype(jnp.int32),
        "page_lengths": jax.vmap(lambda own: uneven_parts(own, PAGES, BLOCK, BLOCK // 2, 0))(jax.random.split(key_of[3], BLOCKS)).reshape((BLOCKS, PAGES)).astype(jnp.int32),
        "padding": place_ends((jax.random.randint(key_of[4], (BLOCKS, BLOCK), 0, 8) < 7).astype(jnp.int32), jax.random.fold_in(key_of[4], 1), 0, 1),
        "buckets": place_ends(jax.random.randint(key_of[5], (BLOCKS, BLOCK, BLOCK), 0, BUCKETS), jax.random.fold_in(key_of[5], 1), 0, BUCKETS - 1).astype(jnp.int32),
        "master": draw_master(jax.random.fold_in(key_of[9], 71), 0),
        "first_moment": normal_values(key_of[7], (P_SIZE,), 0.1, 1.5, ((0, 32),), jnp.float32),
        "second_moment": jnp.clip(jnp.exp(math.log(0.1) - 2.9957323 * jax.random.uniform(key_of[8], (P_SIZE,), jnp.float32) ** levels(key_of[8], (P_SIZE,), ((0, 32),), -0.2, 0.2)), 0.005, 0.1),
    }


beta_one = 0.8
beta_two = 0.98
adam_eps = 1e-06
learn_rate = 0.0006
layer_decay = 0.8
weight_decay = 0.1
norm_eps = 1e-05
masked_score = -1000000000.0

@jax.custom_vjp
def low(v):
    return lax.optimization_barrier(v.astype(jnp.bfloat16)).astype(jnp.float32)

@jax.custom_vjp
def low_back(v):
    return v

def low_keep(v):
    return (low(v), None)

def low_pass(kept, grad):
    return (grad,)

def back_keep(v):
    return (v, None)

def back_low(kept, grad):
    return (low(grad),)
low.defvjp(low_keep, low_pass)
low_back.defvjp(back_keep, back_low)

def entry_shapes():
    return [('layout_weight', (LF, D)), ('layout_bias', (D,)), ('bias_table', (BUCKETS, H))]

def layer_shapes():
    return [('query_weight', (D, D)), ('query_bias', (D,)), ('key_weight', (D, D)), ('value_weight', (D, D)), ('value_bias', (D,)), ('output_weight', (D, D)), ('output_bias', (D,)), ('first_gain', (D,)), ('first_shift', (D,)), ('up_weight', (D, FF)), ('up_bias', (FF,)), ('down_weight', (FF, D)), ('down_bias', (D,)), ('second_gain', (D,)), ('second_shift', (D,))]

def take_pieces(flat_params, listing, offset):
    pieces = {}
    for piece_name, piece_shape in listing:
        amount = 1
        for length in piece_shape:
            amount = amount * length
        pieces[piece_name] = flat_params[offset:offset + amount].reshape(piece_shape)
        offset = offset + amount
    return (pieces, offset)

def unpack(flat_params):
    entry_part, offset = take_pieces(flat_params, entry_shapes(), 0)
    layers = []
    for number in range(LAYERS):
        pieces, offset = take_pieces(flat_params, layer_shapes(), offset)
        layers.append(pieces)
    return (entry_part, layers)

def highest(left, right):
    return jnp.dot(left, right, precision=lax.Precision.HIGHEST)

def layer_norm(values, gain, shift):
    center = values - lax.optimization_barrier(jnp.mean(values, axis=-1, keepdims=True))
    spread = lax.optimization_barrier(jnp.mean(center * center, axis=-1, keepdims=True))
    return center * lax.rsqrt(spread + norm_eps) * gain + shift

def layout_features(page_boxes):
    rates_sin = jnp.power(10000.0, -jnp.arange(FREQ, dtype=jnp.float32) / FREQ)
    angles = page_boxes.astype(jnp.float32)[:, :, None] * rates_sin
    stacked = jnp.stack([jnp.sin(angles), jnp.cos(angles)], axis=1)
    return jnp.transpose(stacked, (2, 0, 1, 3)).reshape(page_boxes.shape[1], LF)

def forward(flat_params, tokens, page_boxes, page_lengths, padding, buckets):
    entry_part, layers = unpack(flat_params)
    features = low(layout_features(page_boxes))
    hidden = tokens + low_back(highest(features, entry_part['layout_weight'])) + entry_part['layout_bias']
    places = jnp.arange(BLOCK, dtype=jnp.int32)
    page_ends = jnp.cumsum(page_lengths)
    page_of = lax.optimization_barrier(jnp.sum((places[:, None] >= page_ends[None, :]).astype(jnp.int32), axis=1))
    allowed = (page_of[:, None] == page_of[None, :]) & (padding[None, :] > 0) | (places[:, None] == places[None, :])
    score_bias = jnp.transpose(entry_part['bias_table'][buckets], (2, 0, 1))
    for weights in layers:
        inputs_low = low(hidden)
        query_low = low((low_back(highest(inputs_low, weights['query_weight'])) + weights['query_bias']) * 0.125)
        key_low = low(low_back(highest(inputs_low, weights['key_weight'])))
        value_low = low(low_back(highest(inputs_low, weights['value_weight'])) + weights['value_bias'])
        query_heads = query_low.reshape(BLOCK, H, HD)
        key_heads = key_low.reshape(BLOCK, H, HD)
        value_heads = value_low.reshape(BLOCK, H, HD)
        scores = low_back(jnp.einsum('qhd,khd->hqk', query_heads, key_heads, precision=lax.Precision.HIGHEST) + score_bias)
        masked = jnp.where(allowed[None], scores, masked_score)
        soft = jax.nn.softmax(masked, axis=-1)
        context = jnp.einsum('hqk,khd->qhd', low(soft), value_heads, precision=lax.Precision.HIGHEST).reshape(BLOCK, D)
        context_low = low(low_back(context))
        attended = low_back(highest(context_low, weights['output_weight'])) + weights['output_bias']
        first_out = layer_norm(hidden + attended, weights['first_gain'], weights['first_shift'])
        up_sum = low_back(highest(low(first_out), weights['up_weight'])) + weights['up_bias']
        activated = low(jax.nn.gelu(up_sum, approximate=False))
        down_sum = low_back(highest(activated, weights['down_weight'])) + weights['down_bias']
        hidden = layer_norm(first_out + down_sum, weights['second_gain'], weights['second_shift'])
    return hidden

def adam_update(master, first_moment, second_moment, gradient, global_index):
    exponent = jnp.where(global_index < ENTRY, LAYERS, jnp.maximum(LAYERS - 1 - (global_index - ENTRY) // LAYER_PARAMS, 0))
    rate = jnp.where(global_index < RAW, learn_rate * jnp.power(layer_decay, exponent.astype(jnp.float32)), 0.0)
    moment_one = beta_one * first_moment + (1.0 - beta_one) * gradient
    moment_two = beta_two * second_moment + (1.0 - beta_two) * gradient * gradient
    fixed_one = moment_one / (1.0 - beta_one ** STEP)
    fixed_two = moment_two / (1.0 - beta_two ** STEP)
    param_step = -rate * (fixed_one / (jnp.sqrt(fixed_two) + adam_eps) + weight_decay * master)
    return (param_step, moment_one, moment_two)

def reference(tokens, cotangent, page_boxes, page_lengths, padding, buckets, master, first_moment, second_moment):
    flat_params = lax.optimization_barrier(master.astype(jnp.bfloat16)).astype(jnp.float32)
    boxes_by_block = jnp.transpose(page_boxes, (1, 0, 2))

    def one_block(running, items):
        block_tokens, block_cotangent, block_boxes, block_lengths, block_padding, block_buckets = items

        def apply_layers(params_now, inputs_now):
            return forward(params_now, inputs_now, block_boxes, block_lengths, block_padding, block_buckets)
        outcome, pullback = jax.vjp(apply_layers, flat_params, block_tokens.astype(jnp.float32))
        grad_params, grad_tokens = pullback(block_cotangent.astype(jnp.float32))
        return (running + grad_params, (outcome.astype(jnp.bfloat16), grad_tokens))
    summed, (activations, input_grad) = lax.scan(one_block, jnp.zeros_like(flat_params), (tokens, cotangent, boxes_by_block, page_lengths, padding, buckets))
    factor = jnp.minimum(1.0, lax.rsqrt(jnp.sum(summed * summed) / RAW + 1e-06))
    global_index = jnp.arange(P_SIZE, dtype=jnp.int32)
    param_step, new_first, new_second = adam_update(master, first_moment, second_moment, summed * factor, global_index)
    return (activations, input_grad, param_step, new_first, new_second)
```

```python
from types import SimpleNamespace
from typing import Any, NamedTuple

import functools
import jax
import jax.numpy as jnp
from jax import lax
from jax.experimental import pallas as pl
from jax.experimental.pallas import tpu as pltpu
from jax.sharding import PartitionSpec as P

D = 768
H = 12
HD = 64
FF = 3072
BUCKETS = 32
FREQ = 16
LF = 128
LAYERS = 1
BLOCK = 1024
STEP = 10
ENTRY = 99456
LAYER_PARAMS = 7087104
RAW = 7186560


beta_one = 0.8
beta_two = 0.98
adam_eps = 1e-06
learn_rate = 0.0006
layer_decay = 0.8
weight_decay = 0.1
norm_eps = 1e-05
masked_score = -1000000000.0


class Params(NamedTuple):
    layout_weight: Any
    layout_bias: Any
    bias_table: Any
    query_weight: Any
    query_bias: Any
    key_weight: Any
    value_weight: Any
    value_bias: Any
    output_weight: Any
    output_bias: Any
    first_gain: Any
    first_shift: Any
    up_weight: Any
    up_bias: Any
    down_weight: Any
    down_bias: Any
    second_gain: Any
    second_shift: Any


SHAPES = (
    (LF, D), (D,), (BUCKETS, H),
    (D, D), (D,), (D, D), (D, D), (D,), (D, D), (D,), (D,), (D,),
    (D, FF), (FF,), (FF, D), (D,), (D,), (D,),
)


def unpack(flat_params):
    pieces, offset = [], 0
    for shape in SHAPES:
        amount = shape[0] * (shape[1] if len(shape) > 1 else 1)
        pieces.append(flat_params[offset : offset + amount].reshape(shape))
        offset = offset + amount
    return Params(*pieces)


def as_float(piece):
    return piece.astype(jnp.float32)


def matmul_low(left, right):
    return jnp.dot(left, right, preferred_element_type=jnp.float32)


def layer_norm(values, gain, shift):
    center = values - jnp.mean(values, axis=-1, keepdims=True)
    spread = jnp.mean(center * center, axis=-1, keepdims=True)
    return center * lax.rsqrt(spread + norm_eps) * gain + shift


def gelu_exact(values):
    return jax.nn.gelu(values, approximate=False)


def layout_features(page_boxes):
    rates_sin = jnp.power(10000.0, -jnp.arange(FREQ, dtype=jnp.float32) / FREQ)
    angles = page_boxes.astype(jnp.float32)[:, :, None] * rates_sin
    stacked = jnp.stack([jnp.sin(angles), jnp.cos(angles)], axis=1)
    return jnp.transpose(stacked, (2, 0, 1, 3)).reshape(page_boxes.shape[1], LF)


def attention_scores(query_low, key_all, score_bias, allowed, blocks_here, rows):
    query_heads = query_low.reshape(blocks_here, rows, H, HD)
    key_heads = key_all.reshape(blocks_here, BLOCK, H, HD)
    products = (
        jnp.einsum("cqhd,ckhd->chqk", query_heads, key_heads, preferred_element_type=jnp.float32)
        + score_bias
    )
    return jnp.where(allowed, products, masked_score)


def adam_update(master, first_moment, second_moment, gradient, global_index):
    exponent = jnp.where(
        global_index < ENTRY,
        LAYERS,
        jnp.maximum(LAYERS - 1 - (global_index - ENTRY) // LAYER_PARAMS, 0),
    )
    rate = jnp.where(
        global_index < RAW, learn_rate * jnp.power(layer_decay, exponent.astype(jnp.float32)), 0.0
    )
    moment_one = beta_one * first_moment + (1.0 - beta_one) * gradient
    moment_two = beta_two * second_moment + (1.0 - beta_two) * gradient * gradient
    fixed_one = moment_one / (1.0 - beta_one**STEP)
    fixed_two = moment_two / (1.0 - beta_two**STEP)
    param_step = -rate * (fixed_one / (jnp.sqrt(fixed_two) + adam_eps) + weight_decay * master)
    return (param_step, moment_one, moment_two)


def running_sum(lengths):
    total, sums = lengths[:, :1], [lengths[:, :1]]
    for i in range(1, lengths.shape[1]):
        total = total + lengths[:, i : i + 1]
        sums.append(total)
    return jnp.concatenate(sums, axis=1)


MESH = pl.DeviceIdType.MESH
SHARD = 224580
ROWS = 1760
TAIL, HEAD = 160, 176
WIN = 2176
SLOTS = 37
CHIP = 74
PARTS = ((0, 19), (19, 18))


def place():
    k = lax.axis_index("dp")
    return k, lax.axis_index("seq"), k // 4, (k // 2) % 2, k % 2


def shard_start(d):
    return d * 1754 + (d * 68) // 128, (d * 68) % 128


def early_vectors(k):
    return (k == 0) | (k == 4) | (k == 5)


def vector_row(k, other):
    at = other
    for chip, row in ((0, 768), (1, 5385), (4, 14607), (5, 19221), (10, 37671), (15, 56127)):
        at = jnp.where(k == chip, row, at)
    return at


def tile_start(w):
    at = w * 48
    for first, shift in ((16, 777 - 16 * 48), (112, 5391 - 112 * 48), (208, 9999 - 208 * 48), (304, 14613 - 304 * 48), (784, 37695 - 784 * 48)):
        at = jnp.where(w >= first, w * 48 + shift, at)
    wide = (w >= 400) & (w < 784)
    v = w - 400
    at = jnp.where(wide, 19239 + (v // 4) * 192 + (v % 4) * 6, at)
    return at, wide


def neighbours(k, c, z, y, x):
    t = k >= 0
    return [
        (t, (k, 1 - c)),
        (t, (z * 4 + y * 2 + 1 - x, c)),
        (t, (z * 4 + (1 - y) * 2 + x, c)),
        (z < 3, (jnp.minimum(k + 4, 15), c)),
        (z > 0, (jnp.maximum(k - 4, 0), c)),
        ((c == 1) & (k < 15), (jnp.minimum(k + 1, 15), 0)),
        ((c == 0) & (k > 0), (jnp.maximum(k - 1, 0), 1)),
    ]


def greet(k, c, z, y, x):
    bar = pltpu.get_barrier_semaphore()
    for cond, dev in neighbours(k, c, z, y, x):
        @pl.when(cond)
        def _():
            pl.semaphore_signal(bar, inc=1, device_id=dev, device_id_type=MESH)
    peers = 3
    for cond, _ in neighbours(k, c, z, y, x)[3:]:
        peers = peers + jnp.where(cond, 1, 0)
    pl.semaphore_wait(bar, peers)


def rcopy(src, dst, ssem, rsem, dev):
    return pltpu.make_async_remote_copy(src_ref=src, dst_ref=dst, send_sem=ssem, recv_sem=rsem, device_id=dev, device_id_type=MESH)


def gather_kernel(x_ref, g_ref, xv, tail, head, win, chunk, lsem, hsend, hrecv, own,
                  zs, zr, xas, xar, xbs, xbr, yas, yar, ybs, ybr, cs, cr):
    k, c, z, y, x = place()
    d = 2 * k + c
    greet(k, c, z, y, x)
    load = pltpu.make_async_copy(x_ref, xv, lsem)
    load.start()
    prev = (jnp.where(c == 1, k, jnp.maximum(k - 1, 0)), 1 - c)
    nxt = (jnp.where(c == 0, k, jnp.minimum(k + 1, 15)), 1 - c)
    to_next = rcopy(x_ref.at[pl.ds(ROWS - TAIL, TAIL)], tail, hsend.at[0], hrecv.at[0], nxt)
    to_prev = rcopy(x_ref.at[pl.ds(0, HEAD)], head, hsend.at[1], hrecv.at[1], prev)

    @pl.when(d < 31)
    def _():
        to_next.start()

    @pl.when(d > 0)
    def _():
        to_prev.start()

    win[...] = jnp.zeros_like(win)
    lanes = lax.broadcasted_iota(jnp.int32, (80, 128), 1)
    q, sh = shard_start(d)
    load.wait()

    @pl.loop(0, ROWS // 80)
    def _(i):
        r = pl.multiple_of(i * 80, 8)
        rolled = pltpu.roll(xv[pl.ds(r, 80), :], sh, 1)
        win[pl.ds(160 + r, 80), :] += jnp.where(lanes >= sh, rolled, 0.0)
        win[pl.ds(161 + r, 80), :] += jnp.where(lanes < sh, rolled, 0.0)

    @pl.when(d > 0)
    def _():
        to_next.wait_recv()
        qp, shp = shard_start(d - 1)
        lanes = lax.broadcasted_iota(jnp.int32, (TAIL, 128), 1)
        rolled = pltpu.roll(tail[...], shp, 1)
        at = 1760 - (q - qp)
        win[pl.ds(at, TAIL), :] += jnp.where(lanes >= shp, rolled, 0.0)
        win[pl.ds(at + 1, TAIL), :] += jnp.where(lanes < shp, rolled, 0.0)

    @pl.when(d < 31)
    def _():
        to_prev.wait_recv()
        qn, shn = shard_start(d + 1)
        lanes = lax.broadcasted_iota(jnp.int32, (HEAD, 128), 1)
        rolled = pltpu.roll(head[...], shn, 1)
        at = 160 + (qn - q)
        win[pl.ds(at, HEAD), :] += jnp.where(lanes >= shn, rolled, 0.0)
        win[pl.ds(at + 1, HEAD), :] += jnp.where(lanes < shn, rolled, 0.0)

    early = early_vectors(k)
    nw0 = jnp.where(early, 36, 37)
    vecs = early == (c == 0)
    first = jnp.where(c == 0, 73 * k, 73 * k + nw0)
    base = q - 160

    @pl.loop(0, SLOTS)
    def _(t):
        at, wide = tile_start(first + t)
        is_vec = vecs & (t == 36)
        at = jnp.where(is_vec, vector_row(k, q), at) - base
        wide = wide & jnp.logical_not(is_vec)

        @pl.when(wide)
        def _():
            parts = [win[pl.ds(at + j, 8, stride=24), :] for j in range(6)]
            chunk[t] = jnp.concatenate(parts, axis=1).astype(jnp.bfloat16)

        @pl.when(jnp.logical_not(wide))
        def _():
            parts = [win[pl.ds(at + j, 8, stride=6), :] for j in range(6)]
            chunk[t] = jnp.concatenate(parts, axis=1).astype(jnp.bfloat16)

    @pl.when(d < 31)
    def _():
        to_next.wait_send()

    @pl.when(d > 0)
    def _():
        to_prev.wait_send()

    xdev, ydev, cdev = (z * 4 + y * 2 + 1 - x, c), (z * 4 + (1 - y) * 2 + x, c), (k, 1 - c)
    zdev = {1: (jnp.minimum(k + 4, 15), c), -1: (jnp.maximum(k - 4, 0), c)}

    def gsl(chip, p):
        off, n = PARTS[p]
        return g_ref.at[chip, pl.ds(37 * c + off, n)]

    def src(chip, p, mine=False):
        off, n = PARTS[p]
        return chunk.at[pl.ds(off, n)] if mine else gsl(chip, p)

    def chip_of(zo, yo, xo):
        return zo * 4 + yo * 2 + xo

    def zcopy(zo, p, way, mine=False):
        chip = chip_of(zo, y, x)
        w = (way + 1) // 2
        return rcopy(src(chip, p, mine), gsl(chip, p), zs.at[w, zo, p], zr.at[zo, p], zdev[way])

    def xcopy(zo, yo, xo, p, mine=False):
        chip = chip_of(zo, yo, xo)
        s, r = (xas, xar) if p == 0 else (xbs, xbr)
        i = zo if p == 0 else zo * 2 + yo
        return rcopy(src(chip, p, mine), gsl(chip, p), s.at[i], r.at[i], xdev)

    def ycopy(zo, yo, xo, p, mine=False):
        chip = chip_of(zo, yo, xo)
        s, r = (ybs, ybr) if p == 1 else (yas, yar)
        i = zo if p == 1 else zo * 2 + xo
        return rcopy(src(chip, p, mine), gsl(chip, p), s.at[i], r.at[i], ydev)

    def ccopy(chip, p, mine=False):
        return rcopy(src(chip, p, mine), gsl(chip, p), cs.at[chip, p], cr.at[chip, p], cdev)

    for p in (0, 1):
        for way in (1, -1):
            @pl.when((z + way >= 0) & (z + way <= 3))
            def _():
                zcopy(z, p, way, True).start()
    xcopy(z, y, x, 0, True).start()
    ycopy(z, y, x, 1, True).start()
    ycopy(z, y, x, 0, True).start()
    xcopy(z, y, x, 1, True).start()
    mine = [pltpu.make_async_copy(chunk.at[pl.ds(*PARTS[p])], gsl(k, p), own.at[p]) for p in (0, 1)]
    for p in (0, 1):
        mine[p].start()
        ccopy(k, p, True).start()

    def column(zo, way):
        for p in (0, 1):
            zcopy(zo, p, way).wait_recv()

            @pl.when((zo + way * 0 + 0 >= 0) & (z + way >= 0) & (z + way <= 3))
            def _():
                zcopy(zo, p, way).start()
            if p == 0:
                xcopy(zo, y, x, 0).start()
                ycopy(zo, y, x, 0).start()
            else:
                ycopy(zo, y, x, 1).start()
                xcopy(zo, y, x, 1).start()
            ccopy(chip_of(zo, y, x), p).start()

    def beside(zo):
        xcopy(zo, y, 1 - x, 0).wait_recv()
        ycopy(zo, y, 1 - x, 0).start()
        ccopy(chip_of(zo, y, 1 - x), 0).start()
        ycopy(zo, 1 - y, x, 1).wait_recv()
        xcopy(zo, 1 - y, x, 1).start()
        ccopy(chip_of(zo, 1 - y, x), 1).start()

    def last(zo):
        ycopy(zo, 1 - y, x, 0).wait_recv()
        ccopy(chip_of(zo, 1 - y, x), 0).start()
        xcopy(zo, y, 1 - x, 1).wait_recv()
        ccopy(chip_of(zo, y, 1 - x), 1).start()
        ycopy(zo, 1 - y, 1 - x, 0).wait_recv()
        ccopy(chip_of(zo, 1 - y, 1 - x), 0).start()
        xcopy(zo, 1 - y, 1 - x, 1).wait_recv()
        ccopy(chip_of(zo, 1 - y, 1 - x), 1).start()

    def at_distance(s, f):
        for way in (1, -1):
            @pl.when((z - s * way >= 0) & (z - s * way <= 3))
            def _():
                f(z - s * way, way)

    at_distance(1, column)
    beside(z)
    at_distance(2, column)
    at_distance(1, lambda zo, way: beside(zo))
    at_distance(3, column)
    last(z)
    at_distance(2, lambda zo, way: beside(zo))
    at_distance(1, lambda zo, way: last(zo))
    at_distance(3, lambda zo, way: beside(zo))
    at_distance(2, lambda zo, way: last(zo))
    at_distance(3, lambda zo, way: last(zo))

    for p in (0, 1):
        mine[p].wait()
        for way in (1, -1):
            for zo in range(4):
                @pl.when(((z - zo) * way >= 0) & (z + way >= 0) & (z + way <= 3))
                def _():
                    zcopy(zo, p, way).wait_send()
    for zo in range(4):
        xcopy(zo, y, x, 0).wait_send()
        ycopy(zo, y, x, 1).wait_send()
        for o in range(2):
            ycopy(zo, y, o, 0).wait_send()
            xcopy(zo, o, x, 1).wait_send()
    for chip in range(16):
        for p in (0, 1):
            ccopy(chip, p).wait_send()
            off, n = PARTS[p]
            theirs = g_ref.at[chip, pl.ds(37 * (1 - c) + off, n)]
            rcopy(theirs, theirs, cs.at[chip, p], cr.at[chip, p], cdev).wait_recv()


def gather_weights(master):
    x = jnp.pad(master, (0, ROWS * 128 - SHARD)).reshape(ROWS, 128)
    sem = pltpu.SemaphoreType.DMA
    any_ = pl.BlockSpec(memory_space=pl.ANY)
    return pl.pallas_call(
        gather_kernel,
        out_shape=jax.ShapeDtypeStruct((16, CHIP, 8, 768), jnp.bfloat16),
        in_specs=[any_],
        out_specs=any_,
        scratch_shapes=[
            pltpu.VMEM((ROWS, 128), jnp.float32),
            pltpu.VMEM((TAIL, 128), jnp.float32),
            pltpu.VMEM((HEAD, 128), jnp.float32),
            pltpu.VMEM((WIN, 128), jnp.float32),
            pltpu.VMEM((SLOTS, 8, 768), jnp.bfloat16),
            sem, sem((2,)), sem((2,)), sem((2,)),
            sem((2, 4, 2)), sem((4, 2)),
            sem((4,)), sem((4,)), sem((8,)), sem((8,)),
            sem((8,)), sem((8,)), sem((4,)), sem((4,)),
            sem((16, 2)), sem((16, 2)),
        ],
        compiler_params=pltpu.CompilerParams(collective_id=0, has_side_effects=True, vmem_limit_bytes=40 << 20),
        name="gather_weights",
    )(x)


FRONT = 344
WIN2 = 2464
EDGE = 4
ENTRY_ROWS = 777


def reduce_kernel(g_ref, m_ref, one_ref, two_ref, step_ref, new1_ref, new2_ref,
                  acc, crecv, a1, b1, a2, b2, up, dn, total, ebuf, sq, sqr, win, mv, onev, twov,
                  lsem, asem, cs, cr, a1s, a1r, b1s, b1r, a2s, a2r, b2s, b2r, us, ur, ds_, dr, es, er, qs, qr):
    k, c, z, y, x = place()
    d = 2 * k + c
    xdev, ydev, cdev = (z * 4 + y * 2 + 1 - x, c), (z * 4 + (1 - y) * 2 + x, c), (k, 1 - c)
    zdev = {1: (jnp.minimum(k + 4, 15), c), -1: (jnp.maximum(k - 4, 0), c)}
    column_devs = [((z + s) % 4 * 4 + y * 2 + x, c) for s in (1, 2, 3)]
    prev = (jnp.where(c == 1, k, jnp.maximum(k - 1, 0)), 1 - c)
    nxt = (jnp.where(c == 0, k, jnp.minimum(k + 1, 15)), 1 - c)
    bar = pltpu.get_barrier_semaphore()
    far_next, far_prev = (c == 1) & (k < 15), (c == 0) & (k > 0)
    for dev in [xdev, ydev, cdev] + column_devs:
        pl.semaphore_signal(bar, inc=1, device_id=dev, device_id_type=MESH)

    @pl.when(far_next)
    def _():
        pl.semaphore_signal(bar, inc=1, device_id=nxt, device_id_type=MESH)

    @pl.when(far_prev)
    def _():
        pl.semaphore_signal(bar, inc=1, device_id=prev, device_id_type=MESH)

    pl.semaphore_wait(bar, 6 + jnp.where(far_next | far_prev, 1, 0))

    def chip_of(zo, yo, xo):
        return zo * 4 + yo * 2 + xo

    def load(chip):
        return pltpu.make_async_copy(g_ref.at[chip, pl.ds(37 * c, 37)], acc.at[chip], asem.at[chip])

    def ccopy(chip):
        return rcopy(g_ref.at[chip, pl.ds(37 * (1 - c), 37)], crecv.at[chip], cs.at[chip], cr.at[chip], cdev)

    def at_distance(s, f):
        if s == 0:
            f(z, 0)
            return
        for way in (1, -1):
            @pl.when((z + s * way >= 0) & (z + s * way <= 3))
            def _():
                f(z + s * way, way)

    def order(f):
        for s in (3, 2, 1, 0):
            at_distance(s, f)

    corners = ((1, 1), (1, 0), (0, 1), (0, 0))

    def flip(v, o):
        return 1 - v if o else v

    for oy, ox in corners:
        def go(zo, way):
            chip = chip_of(zo, flip(y, oy), flip(x, ox))
            load(chip).start()
            ccopy(chip).start()
        order(go)
    shards = [pltpu.make_async_copy(r, v, lsem.at[i]) for i, (r, v) in enumerate(((m_ref, mv), (one_ref, onev), (two_ref, twov)))]
    for s in shards:
        s.start()

    def psl(p):
        return pl.ds(*PARTS[p])

    def gain(dst, at, p, ref):
        off, n = PARTS[p]

        @pl.loop(0, n)
        def _(i):
            acc[at, off + i] = acc[at, off + i] + ref[i]

    def pair(chip):
        load(chip).wait()
        ccopy(chip).wait_recv()

        @pl.loop(0, 37)
        def _(i):
            acc[chip, i] = acc[chip, i] + crecv[chip, i]

    def a1copy(zo, xo):
        return rcopy(acc.at[chip_of(zo, 1 - y, xo), psl(0)], a1.at[zo * 2 + xo], a1s.at[zo * 2 + xo], a1r.at[zo * 2 + xo], ydev)

    def b1copy(zo, yo):
        return rcopy(acc.at[chip_of(zo, yo, 1 - x), psl(1)], b1.at[zo * 2 + yo], b1s.at[zo * 2 + yo], b1r.at[zo * 2 + yo], xdev)

    def a2copy(zo):
        return rcopy(acc.at[chip_of(zo, y, 1 - x), psl(0)], a2.at[zo], a2s.at[zo], a2r.at[zo], xdev)

    def b2copy(zo):
        return rcopy(acc.at[chip_of(zo, 1 - y, x), psl(1)], b2.at[zo], b2s.at[zo], b2r.at[zo], ydev)

    def zcopy(zo, way):
        buf, s, r = (up, us, ur) if way == 1 else (dn, ds_, dr)
        return rcopy(acc.at[chip_of(zo, y, x)], buf.at[zo], s.at[zo], r.at[zo], zdev[way])

    def first(oy, ox):
        def go(zo, way):
            yo, xo = flip(y, oy), flip(x, ox)
            pair(chip_of(zo, yo, xo))
            if oy:
                a1copy(zo, xo).start()
            if ox:
                b1copy(zo, yo).start()
        return go

    def second(zo, way):
        a1copy(zo, 1 - x).wait_recv()
        gain(acc, chip_of(zo, y, 1 - x), 0, a1.at[zo * 2 + 1 - x])
        a2copy(zo).start()
        b1copy(zo, 1 - y).wait_recv()
        gain(acc, chip_of(zo, 1 - y, x), 1, b1.at[zo * 2 + 1 - y])
        b2copy(zo).start()

    def third(zo, way):
        chip = chip_of(zo, y, x)
        a1copy(zo, x).wait_recv()
        gain(acc, chip, 0, a1.at[zo * 2 + x])
        b1copy(zo, y).wait_recv()
        gain(acc, chip, 1, b1.at[zo * 2 + y])
        a2copy(zo).wait_recv()
        gain(acc, chip, 0, a2.at[zo])
        b2copy(zo).wait_recv()
        gain(acc, chip, 1, b2.at[zo])
        if way:
            @pl.when((z - way >= 0) & (z - way <= 3))
            def _():
                zcopy(zo, way).wait_recv()
                buf = up if way == 1 else dn

                @pl.loop(0, 37)
                def _(i):
                    acc[chip, i] = acc[chip, i] + buf[zo, i]
            zcopy(zo, way).start()

    order(first(1, 1))
    order(first(1, 0))
    order(first(0, 1))
    order(second)
    order(first(0, 0))
    order(third)

    f32 = jnp.float32

    @pl.loop(0, 37)
    def _(i):
        total[i] = acc[k, i].astype(f32)

    for way in (1, -1):
        @pl.when((z - way >= 0) & (z - way <= 3))
        def _():
            zcopy(z, way).wait_recv()
            buf = up if way == 1 else dn

            @pl.loop(0, 37)
            def _(i):
                total[i] = total[i] + buf[z, i].astype(f32)

    early = early_vectors(k)
    nw0 = jnp.where(early, 36, 37)
    vecs = early == (c == 0)
    mine = jnp.where(vecs, 36, 37)
    to_next = rcopy(total.at[pl.ds(mine - EDGE, EDGE)], ebuf.at[0], es.at[0], er.at[0], nxt)
    to_prev = rcopy(total.at[pl.ds(0, EDGE)], ebuf.at[1], es.at[1], er.at[1], prev)

    @pl.when(d < 31)
    def _():
        to_next.start()

    @pl.when(d > 0)
    def _():
        to_prev.start()

    def square(i, run):
        t = total[i]
        t = t * t
        for j in range(6):
            run = run + t[:, 128 * j:128 * j + 128]
        return run

    sq[0] = lax.fori_loop(0, 37, square, jnp.zeros((8, 128), f32))
    for i, dev in enumerate((cdev, xdev, ydev)):
        step = rcopy(sq.at[i], sqr.at[i], qs.at[i], qr.at[i], dev)
        step.start()
        step.wait_recv()
        sq[i + 1] = sq[i] + sqr[i]
    hops = [rcopy(sq.at[3], sqr.at[3 + i], qs.at[3 + i], qr.at[3 + i], column_devs[i]) for i in range(3)]
    for h in hops:
        h.start()

    q, sh = shard_start(d)
    base = q - FRONT

    def flatten(ref, i, at, wide):
        @pl.when(wide)
        def _():
            t = ref[i]
            for j in range(6):
                win[pl.ds(at + j, 8, stride=24), :] = t[:, 128 * j:128 * j + 128]

        @pl.when(jnp.logical_not(wide))
        def _():
            t = ref[i]
            for j in range(6):
                win[pl.ds(at + j, 8, stride=6), :] = t[:, 128 * j:128 * j + 128]

    own_vectors = vecs & (vector_row(k, -1) >= 0)

    @pl.when(own_vectors)
    def _():
        flatten(total, 36, vector_row(k, q) - base, k < 0)

    w0 = jnp.where(c == 0, 73 * k, 73 * k + nw0)

    @pl.loop(0, mine)
    def _(t):
        at, wide = tile_start(w0 + t)
        flatten(total, t, at - base, wide)

    @pl.when(d > 0)
    def _():
        to_next.wait_recv()

        @pl.loop(0, EDGE)
        def _(t):
            at, wide = tile_start(w0 - EDGE + t)
            flatten(ebuf.at[0], t, at - base, wide)

    @pl.when(d < 31)
    def _():
        to_prev.wait_recv()

        @pl.loop(0, EDGE)
        def _(t):
            at, wide = tile_start(w0 + mine + t)
            flatten(ebuf.at[1], t, at - base, wide)

    for i, h in enumerate(hops):
        h.wait_recv()
    parts = [sqr[3], sqr[4], sqr[5]]
    rows = [sq[3]] + parts
    whole = (rows[0] + rows[2]) + (rows[1] + rows[3])
    square_sum = jnp.sum(jnp.sum(whole, axis=1, keepdims=True), axis=0, keepdims=True)
    factor = jnp.minimum(1.0, lax.rsqrt(square_sum / RAW + 1e-06))
    for s in shards:
        s.wait()
    lanes = lax.broadcasted_iota(jnp.int32, (80, 128), 1)
    rowi = lax.broadcasted_iota(jnp.int32, (80, 128), 0)
    back = (128 - sh) % 128

    @pl.loop(0, ROWS // 80)
    def _(i):
        r = pl.multiple_of(i * 80, 8)
        here = pltpu.roll(win[pl.ds(FRONT + r, 80), :], back, 1)
        there = pltpu.roll(win[pl.ds(FRONT + 1 + r, 80), :], back, 1)
        grad = jnp.where(lanes < 128 - sh, here, there) * factor
        entry = (d == 0) & (rowi + r < ENTRY_ROWS)
        rate = jnp.where(entry, learn_rate * layer_decay, learn_rate)
        one = beta_one * onev[pl.ds(r, 80), :] + (1.0 - beta_one) * grad
        two = beta_two * twov[pl.ds(r, 80), :] + (1.0 - beta_two) * grad * grad
        fixed_one = one / (1.0 - beta_one ** STEP)
        fixed_two = two / (1.0 - beta_two ** STEP)
        step_ref[pl.ds(r, 80), :] = -rate * (fixed_one / (jnp.sqrt(fixed_two) + adam_eps) + weight_decay * mv[pl.ds(r, 80), :])
        new1_ref[pl.ds(r, 80), :] = one
        new2_ref[pl.ds(r, 80), :] = two

    for i, dev in enumerate((cdev, xdev, ydev)):
        rcopy(sq.at[i], sqr.at[i], qs.at[i], qr.at[i], dev).wait_send()
    for h in hops:
        h.wait_send()

    @pl.when(d < 31)
    def _():
        to_next.wait_send()

    @pl.when(d > 0)
    def _():
        to_prev.wait_send()

    for chip in range(16):
        ccopy(chip).wait_send()
    for zo in range(4):
        a2copy(zo).wait_send()
        b2copy(zo).wait_send()
        for o in range(2):
            a1copy(zo, o).wait_send()
            b1copy(zo, o).wait_send()
        for way in (1, -1):
            @pl.when((zo - z) * way > 0)
            def _():
                zcopy(zo, way).wait_send()


def reduce_and_step(grads, master, first_moment, second_moment):
    def rows(v):
        return jnp.pad(v, (0, ROWS * 128 - SHARD)).reshape(ROWS, 128)

    sem = pltpu.SemaphoreType.DMA
    any_ = pl.BlockSpec(memory_space=pl.ANY)
    vm = pl.BlockSpec(memory_space=pltpu.VMEM)
    bf, f32 = jnp.bfloat16, jnp.float32
    tile = (8, 768)
    outs = pl.pallas_call(
        reduce_kernel,
        out_shape=[jax.ShapeDtypeStruct((ROWS, 128), f32)] * 3,
        in_specs=[any_] * 4,
        out_specs=[vm] * 3,
        scratch_shapes=[
            pltpu.VMEM((16, 37) + tile, bf), pltpu.VMEM((16, 37) + tile, bf),
            pltpu.VMEM((8, 19) + tile, bf), pltpu.VMEM((8, 18) + tile, bf),
            pltpu.VMEM((4, 19) + tile, bf), pltpu.VMEM((4, 18) + tile, bf),
            pltpu.VMEM((4, 37) + tile, bf), pltpu.VMEM((4, 37) + tile, bf),
            pltpu.VMEM((37,) + tile, f32), pltpu.VMEM((2, EDGE) + tile, f32),
            pltpu.VMEM((4, 8, 128), f32), pltpu.VMEM((6, 8, 128), f32),
            pltpu.VMEM((WIN2, 128), f32),
            pltpu.VMEM((ROWS, 128), f32), pltpu.VMEM((ROWS, 128), f32), pltpu.VMEM((ROWS, 128), f32),
            sem((3,)), sem((16,)), sem((16,)), sem((16,)),
            sem((8,)), sem((8,)), sem((8,)), sem((8,)), sem((4,)), sem((4,)), sem((4,)), sem((4,)),
            sem((4,)), sem((4,)), sem((4,)), sem((4,)), sem((2,)), sem((2,)), sem((6,)), sem((6,)),
        ],
        compiler_params=pltpu.CompilerParams(collective_id=1, has_side_effects=True, vmem_limit_bytes=56 << 20),
        name="reduce_and_step",
    )(grads, rows(master), rows(first_moment), rows(second_moment))
    return [o.reshape(-1)[:SHARD] for o in outs]


WEIGHTS = (
    (0, 0, 16),
    (3, 16, 96),
    (5, 112, 96),
    (6, 208, 96),
    (8, 304, 96),
    (12, 400, 384),
    (14, 784, 384),
)
VECTORS = (
    (1, 0, 0),
    (2, 0, 1),
    (4, 1, 0),
    (7, 4, 0),
    (9, 5, 0),
    (10, 5, 1),
    (11, 5, 2),
    (13, 10, 0),
    (15, 15, 0),
    (16, 15, 1),
    (17, 15, 2),
)


def vector_slot(chip):
    return 36 if chip in (0, 4, 5) else 73


def slots_of(first, count):
    runs = []
    for w in range(first, first + count):
        chip, at = divmod(w, 73)
        slot = chip * CHIP + at + (1 if at >= vector_slot(chip) else 0)
        if runs and runs[-1][0] + runs[-1][1] == slot:
            runs[-1][1] += 1
        else:
            runs.append([slot, 1])
    return runs


def unpack_gathered(gathered):
    tiles = gathered.reshape(16 * CHIP, 8, D)
    pieces = {}
    for name, first, count in WEIGHTS:
        got = jnp.concatenate([tiles[s : s + n] for s, n in slots_of(first, count)])
        if name == 12:
            got = got.reshape(96, 4, 8, D).transpose(0, 2, 1, 3).reshape(D, FF)
        pieces[name] = got.reshape(-1, FF if name == 12 else D)
    for name, chip, row in VECTORS:
        block = gathered[chip, vector_slot(chip)]
        if name == 13:
            pieces[name] = block[row : row + 4].reshape(FF)
        elif name == 2:
            pieces[name] = block[row, : BUCKETS * H].reshape(BUCKETS, H)
        else:
            pieces[name] = block[row]
    return Params(*[pieces[i] for i in range(18)])


def pack_gradients(pieces):
    by_name = [p.astype(jnp.bfloat16) for p in pieces]
    weights = []
    for name, first, count in WEIGHTS:
        got = by_name[name]
        if name == 12:
            got = got.reshape(96, 8, 4, D).transpose(0, 2, 1, 3)
        weights.append(got.reshape(count, 8, D))
    cuts = []
    for chip in range(16):
        held = [(r, by_name[n]) for n, c, r in VECTORS if c == chip]
        rows = [jnp.pad(v.reshape(-1), (0, -v.size % D)).reshape(-1, D) for _, v in held]
        block = jnp.concatenate(rows + [jnp.zeros((8 - sum(r.shape[0] for r in rows), D), jnp.bfloat16)])
        cuts.append((73 * chip + vector_slot(chip), block[None]))
    parts = []
    for (name, first, count), tiles in zip(WEIGHTS, weights):
        at = first
        for w, block in [c for c in cuts if first <= c[0] < first + count]:
            if w > at:
                parts.append(tiles[at - first : w - first])
            parts.append(block)
            at = w
        parts.append(tiles[at - first :])
    parts.extend(block for w, block in cuts if w == 1168)
    return jnp.concatenate(parts).reshape(16, CHIP, 8, D)


def per_device(
    custom,
    tokens,
    cotangent,
    page_boxes,
    page_lengths,
    padding,
    buckets,
    master,
    first_moment,
    second_moment,
):
    blocks_here = tokens.shape[0]
    rows = tokens.shape[1]
    count_rows = blocks_here * rows
    if custom:
        entry_part = unpack_gathered(gather_weights(master))
    else:
        shard_low = master.astype(jnp.bfloat16)
        flat_params = lax.all_gather(shard_low, ("dp", "seq"), axis=0, tiled=True)
        entry_part = unpack(flat_params)
    layers = [entry_part]
    places = lax.axis_index("seq") * rows + jnp.arange(rows, dtype=jnp.int32)
    page_ends = running_sum(page_lengths)
    page_of = jnp.sum((places[None, :, None] >= page_ends[:, None, :]).astype(jnp.int32), axis=2)
    own_tags = jnp.where(padding > 0, page_of + 1, 0).astype(jnp.bfloat16)
    query_tags = (page_of + 1).astype(jnp.float32)
    key_places = jnp.arange(BLOCK, dtype=jnp.int32)
    bucket_ids = jnp.arange(BUCKETS, dtype=jnp.int32)
    onehot = (buckets[:, None, :, :] == bucket_ids[None, :, None, None]).astype(jnp.bfloat16)
    score_bias = jnp.einsum(
        "bh,cbqk->chqk", entry_part.bias_table, onehot, preferred_element_type=jnp.float32
    )
    features_low = layout_features(page_boxes.reshape(4, count_rows)).astype(jnp.bfloat16)
    hidden = (
        tokens.reshape(count_rows, D).astype(jnp.float32)
        + matmul_low(features_low, entry_part.layout_weight)
        + as_float(entry_part.layout_bias)
    )
    saved = []
    for weights in layers:
        inputs_low = hidden.astype(jnp.bfloat16)
        query_low = (
            (matmul_low(inputs_low, weights.query_weight) + as_float(weights.query_bias))
            * 0.125
        ).astype(jnp.bfloat16)
        key_low = matmul_low(inputs_low, weights.key_weight).astype(jnp.bfloat16)
        value_low = (
            matmul_low(inputs_low, weights.value_weight) + as_float(weights.value_bias)
        ).astype(jnp.bfloat16)
        key_all, value_all, tags_all = (
            lax.all_gather(key_low.reshape(blocks_here, rows, D), "seq", axis=1, tiled=True),
            lax.all_gather(value_low.reshape(blocks_here, rows, D), "seq", axis=1, tiled=True),
            lax.all_gather(own_tags, "seq", axis=1, tiled=True),
        )
        allowed = (tags_all[:, None, :].astype(jnp.float32) == query_tags[:, :, None]) | (
            key_places[None, None, :] == places[None, :, None]
        )
        allowed = allowed[:, None, :, :]
        scores = attention_scores(query_low, key_all, score_bias, allowed, blocks_here, rows)
        top_score = jnp.max(scores, axis=-1, keepdims=True)
        expo_score = jnp.exp(scores - top_score)
        total_exp = jnp.sum(expo_score, axis=-1, keepdims=True)
        soft = expo_score / total_exp
        log_total = top_score + jnp.log(total_exp)
        value_heads = value_all.reshape(blocks_here, BLOCK, H, HD)
        context = jnp.einsum(
            "chqk,ckhd->cqhd",
            soft.astype(jnp.bfloat16),
            value_heads,
            preferred_element_type=jnp.float32,
        )
        context_low = context.reshape(count_rows, D).astype(jnp.bfloat16)
        first_in = (
            hidden
            + matmul_low(context_low, weights.output_weight)
            + as_float(weights.output_bias)
        )
        first_out = layer_norm(
            first_in, as_float(weights.first_gain), as_float(weights.first_shift)
        )
        first_low = first_out.astype(jnp.bfloat16)
        up_sum = matmul_low(first_low, weights.up_weight) + as_float(weights.up_bias)
        activated = gelu_exact(up_sum).astype(jnp.bfloat16)
        second_in = (
            first_out
            + matmul_low(activated, weights.down_weight)
            + as_float(weights.down_bias)
        )
        stash = SimpleNamespace(
            inputs_low=inputs_low,
            query_low=query_low,
            key_low=key_low,
            value_low=value_low,
            allowed=allowed,
            log_total=log_total,
            context_low=context_low,
            first_in=first_in,
            first_low=first_low,
            up_sum=up_sum,
            activated=activated,
            second_in=second_in,
        )
        stash.key_all = key_all
        stash.value_all = value_all
        saved.append(stash)
        hidden = layer_norm(
            second_in, as_float(weights.second_gain), as_float(weights.second_shift)
        )
    grad_out = cotangent.reshape(count_rows, D).astype(jnp.float32)
    table_grad = jnp.zeros((BUCKETS, H), jnp.float32)
    layer_grads = []
    for number in reversed(range(LAYERS)):
        weights = layers[number]
        stash = saved[number]
        norm_pair = jax.vjp(
            layer_norm,
            stash.second_in,
            as_float(weights.second_gain),
            as_float(weights.second_shift),
        )
        grad_second, grad_gain_two, grad_shift_two = norm_pair[1](grad_out)
        grad_down_bias = jnp.sum(grad_second, axis=0)
        down_back = grad_second.astype(jnp.bfloat16)
        grad_down_weight = jnp.einsum(
            "nf,nd->fd", stash.activated, down_back, preferred_element_type=jnp.float32
        )
        grad_activated = jnp.einsum(
            "nd,fd->nf", down_back, weights.down_weight, preferred_element_type=jnp.float32
        )
        gelu_pair = jax.vjp(gelu_exact, stash.up_sum)
        grad_up = gelu_pair[1](grad_activated)[0]
        grad_up_bias = jnp.sum(grad_up, axis=0)
        up_back = grad_up.astype(jnp.bfloat16)
        grad_up_weight = jnp.einsum(
            "nd,nf->df", stash.first_low, up_back, preferred_element_type=jnp.float32
        )
        grad_first = grad_second + jnp.einsum(
            "nf,df->nd", up_back, weights.up_weight, preferred_element_type=jnp.float32
        )
        first_pair = jax.vjp(
            layer_norm,
            stash.first_in,
            as_float(weights.first_gain),
            as_float(weights.first_shift),
        )
        grad_first_in, grad_gain_one, grad_shift_one = first_pair[1](grad_first)
        grad_output_bias = jnp.sum(grad_first_in, axis=0)
        attend_back = grad_first_in.astype(jnp.bfloat16)
        grad_output_weight = jnp.einsum(
            "nd,ne->de", stash.context_low, attend_back, preferred_element_type=jnp.float32
        )
        grad_context = jnp.einsum(
            "ne,de->nd", attend_back, weights.output_weight, preferred_element_type=jnp.float32
        ).astype(jnp.bfloat16)
        grad_context = grad_context.reshape(blocks_here, rows, H, HD)
        key_all = stash.key_all
        value_all = stash.value_all
        scores = attention_scores(
            stash.query_low, key_all, score_bias, stash.allowed, blocks_here, rows
        )
        soft = jnp.exp(scores - stash.log_total)
        key_heads = key_all.reshape(blocks_here, BLOCK, H, HD)
        value_heads = value_all.reshape(blocks_here, BLOCK, H, HD)
        grad_soft = jnp.einsum(
            "cqhd,ckhd->chqk", grad_context, value_heads, preferred_element_type=jnp.float32
        )
        inner_sum = jnp.sum(soft * grad_soft, axis=-1, keepdims=True)
        grad_scores = (soft * (grad_soft - inner_sum)).astype(jnp.bfloat16)
        table_grad = jnp.einsum(
            "chqk,cbqk->bh", grad_scores, onehot, preferred_element_type=jnp.float32
        )
        query_heads = stash.query_low.reshape(blocks_here, rows, H, HD)
        grad_query = (
            jnp.einsum(
                "chqk,ckhd->cqhd", grad_scores, key_heads, preferred_element_type=jnp.float32
            ).reshape(count_rows, D)
            * 0.125
        )
        grad_key_all = jnp.einsum(
            "chqk,cqhd->ckhd", grad_scores, query_heads, preferred_element_type=jnp.float32
        ).reshape(blocks_here, BLOCK, D)
        grad_value_all = jnp.einsum(
            "chqk,cqhd->ckhd",
            soft.astype(jnp.bfloat16),
            grad_context,
            preferred_element_type=jnp.float32,
        ).reshape(blocks_here, BLOCK, D)
        grad_key, grad_value = (
            lax.psum_scatter(
                grad_key_all.astype(jnp.bfloat16), "seq", scatter_dimension=1, tiled=True
            ).astype(jnp.float32),
            lax.psum_scatter(
                grad_value_all.astype(jnp.bfloat16), "seq", scatter_dimension=1, tiled=True
            ).astype(jnp.float32),
        )
        grad_key = grad_key.reshape(count_rows, D)
        grad_value = grad_value.reshape(count_rows, D)
        grad_query_bias = jnp.sum(grad_query, axis=0)
        grad_value_bias = jnp.sum(grad_value, axis=0)
        query_back = grad_query.astype(jnp.bfloat16)
        key_back = grad_key.astype(jnp.bfloat16)
        value_back = grad_value.astype(jnp.bfloat16)
        grad_query_weight = jnp.einsum(
            "nd,ne->de", stash.inputs_low, query_back, preferred_element_type=jnp.float32
        )
        grad_key_weight = jnp.einsum(
            "nd,ne->de", stash.inputs_low, key_back, preferred_element_type=jnp.float32
        )
        grad_value_weight = jnp.einsum(
            "nd,ne->de", stash.inputs_low, value_back, preferred_element_type=jnp.float32
        )
        grad_out = grad_first_in + jnp.einsum(
            "ne,de->nd", query_back, weights.query_weight, preferred_element_type=jnp.float32
        )
        grad_out = grad_out + jnp.einsum(
            "ne,de->nd", key_back, weights.key_weight, preferred_element_type=jnp.float32
        )
        grad_out = grad_out + jnp.einsum(
            "ne,de->nd", value_back, weights.value_weight, preferred_element_type=jnp.float32
        )
        layer_grads.insert(
            0,
            [
                grad_query_weight,
                grad_query_bias,
                grad_key_weight,
                grad_value_weight,
                grad_value_bias,
                grad_output_weight,
                grad_output_bias,
                grad_gain_one,
                grad_shift_one,
                grad_up_weight,
                grad_up_bias,
                grad_down_weight,
                grad_down_bias,
                grad_gain_two,
                grad_shift_two,
            ],
        )
    embed_back = grad_out.astype(jnp.bfloat16)
    grad_layout_weight = jnp.einsum(
        "nf,nd->fd", features_low, embed_back, preferred_element_type=jnp.float32
    )
    grad_layout_bias = jnp.sum(grad_out, axis=0)
    all_pieces = [grad_layout_weight, grad_layout_bias, table_grad]
    layer_list = layer_grads[0]
    all_pieces = all_pieces + layer_list
    if custom:
        param_step, new_first, new_second = reduce_and_step(
            pack_gradients(all_pieces), master, first_moment, second_moment
        )
    else:
        flat_grad = jnp.concatenate([piece.reshape(-1) for piece in all_pieces])
        grad_shard = lax.psum_scatter(flat_grad, ("dp", "seq"), scatter_dimension=0, tiled=True)
        square = lax.psum(jnp.sum(grad_shard * grad_shard), ("dp", "seq"))
        factor = jnp.minimum(1.0, lax.rsqrt(square / RAW + 1e-06))
        shard_size = master.shape[0]
        global_index = lax.axis_index(("dp", "seq")) * shard_size + jnp.arange(
            shard_size, dtype=jnp.int32
        )
        param_step, new_first, new_second = adam_update(
            master, first_moment, second_moment, grad_shard * factor, global_index
        )
    activations = hidden.reshape(blocks_here, rows, D).astype(jnp.bfloat16)
    input_grad = grad_out.reshape(blocks_here, rows, D)
    return (activations, input_grad, param_step, new_first, new_second)


def solution(mesh):
    in_specs = (
        P("dp", "seq", None),
        P("dp", "seq", None),
        P(None, "dp", "seq"),
        P("dp", None),
        P("dp", "seq"),
        P("dp", "seq", None),
        P(("dp", "seq")),
        P(("dp", "seq")),
        P(("dp", "seq")),
    )
    out_specs = (
        P("dp", "seq", None),
        P("dp", "seq", None),
        P(("dp", "seq")),
        P(("dp", "seq")),
        P(("dp", "seq")),
    )
    custom = dict(mesh.shape) == {"dp": 16, "seq": 2}
    return jax.shard_map(
        functools.partial(per_device, custom), mesh=mesh, in_specs=in_specs, out_specs=out_specs, check_vma=False
    )
```

```python
from types import SimpleNamespace
from typing import Any, NamedTuple

import functools
import jax
import jax.numpy as jnp
from jax import lax
from jax.experimental import pallas as pl
from jax.experimental.pallas import tpu as pltpu
from jax.sharding import PartitionSpec as P

D = 768
H = 12
HD = 64
FF = 3072
BUCKETS = 32
FREQ = 16
LF = 128
LAYERS = 1
BLOCK = 1024
STEP = 10
ENTRY = 99456
LAYER_PARAMS = 7087104
RAW = 7186560


beta_one = 0.8
beta_two = 0.98
adam_eps = 1e-06
learn_rate = 0.0006
layer_decay = 0.8
weight_decay = 0.1
norm_eps = 1e-05
masked_score = -1000000000.0


class Params(NamedTuple):
    layout_weight: Any
    layout_bias: Any
    bias_table: Any
    query_weight: Any
    query_bias: Any
    key_weight: Any
    value_weight: Any
    value_bias: Any
    output_weight: Any
    output_bias: Any
    first_gain: Any
    first_shift: Any
    up_weight: Any
    up_bias: Any
    down_weight: Any
    down_bias: Any
    second_gain: Any
    second_shift: Any


SHAPES = (
    (LF, D), (D,), (BUCKETS, H),
    (D, D), (D,), (D, D), (D, D), (D,), (D, D), (D,), (D,), (D,),
    (D, FF), (FF,), (FF, D), (D,), (D,), (D,),
)


def unpack(flat_params):
    pieces, offset = [], 0
    for shape in SHAPES:
        amount = shape[0] * (shape[1] if len(shape) > 1 else 1)
        pieces.append(flat_params[offset : offset + amount].reshape(shape))
        offset = offset + amount
    return Params(*pieces)


def as_float(piece):
    return piece.astype(jnp.float32)


def matmul_low(left, right):
    return jnp.dot(left, right, preferred_element_type=jnp.float32)


def layer_norm(values, gain, shift):
    center = values - jnp.mean(values, axis=-1, keepdims=True)
    spread = jnp.mean(center * center, axis=-1, keepdims=True)
    return center * lax.rsqrt(spread + norm_eps) * gain + shift


def gelu_exact(values):
    return jax.nn.gelu(values, approximate=False)


def layout_features(page_boxes):
    rates_sin = jnp.power(10000.0, -jnp.arange(FREQ, dtype=jnp.float32) / FREQ)
    angles = page_boxes.astype(jnp.float32)[:, :, None] * rates_sin
    stacked = jnp.stack([jnp.sin(angles), jnp.cos(angles)], axis=1)
    return jnp.transpose(stacked, (2, 0, 1, 3)).reshape(page_boxes.shape[1], LF)


def adam_update(master, first_moment, second_moment, gradient, global_index):
    exponent = jnp.where(
        global_index < ENTRY,
        LAYERS,
        jnp.maximum(LAYERS - 1 - (global_index - ENTRY) // LAYER_PARAMS, 0),
    )
    rate = jnp.where(
        global_index < RAW, learn_rate * jnp.power(layer_decay, exponent.astype(jnp.float32)), 0.0
    )
    moment_one = beta_one * first_moment + (1.0 - beta_one) * gradient
    moment_two = beta_two * second_moment + (1.0 - beta_two) * gradient * gradient
    fixed_one = moment_one / (1.0 - beta_one**STEP)
    fixed_two = moment_two / (1.0 - beta_two**STEP)
    param_step = -rate * (fixed_one / (jnp.sqrt(fixed_two) + adam_eps) + weight_decay * master)
    return (param_step, moment_one, moment_two)


def running_sum(lengths):
    total, sums = lengths[:, :1], [lengths[:, :1]]
    for i in range(1, lengths.shape[1]):
        total = total + lengths[:, i : i + 1]
        sums.append(total)
    return jnp.concatenate(sums, axis=1)


NT = (((1,), (1,)), ((), ()))
TN = (((0,), (0,)), ((), ()))


def half(ref_value, hh):
    lanes = lax.broadcasted_iota(jnp.int32, ref_value.shape, 1)
    keep = lanes < 64 if hh == 0 else lanes >= 64
    return jnp.where(keep, ref_value, jnp.zeros_like(ref_value))


def attend_kernel(q_ref, k_ref, v_ref, code_ref, tab_ref, ctx_ref, p_ref, s_scr):
    pair = pl.program_id(0)
    keys, rows = s_scr.shape
    f32, bf = jnp.float32, jnp.bfloat16
    STEP_ROWS = keys
    out = []
    vt = v_ref[...].T
    for hh in range(2):
        qm = half(q_ref[...], hh)
        line = jnp.broadcast_to(tab_ref[pl.ds(2 * pair + hh, 1), :], (STEP_ROWS, 128))

        def score(i, top):
            at = pl.multiple_of(i * STEP_ROWS, STEP_ROWS)
            s = lax.dot_general(k_ref[pl.ds(at, STEP_ROWS), :], qm, NT, preferred_element_type=f32)
            cols = []
            for j in range(rows // 128):
                code = code_ref[pl.ds(at, STEP_ROWS), 128 * j : 128 * j + 128]
                bias = jnp.take_along_axis(line, code, axis=1, mode="promise_in_bounds")
                cols.append(jnp.where(bias < 0.5 * masked_score, masked_score, s[:, 128 * j : 128 * j + 128] + bias))
            s = jnp.concatenate(cols, axis=1)
            s_scr[pl.ds(at, STEP_ROWS), :] = s
            return jnp.maximum(top, jnp.max(s.reshape(STEP_ROWS // 8, 8, rows), axis=0))

        top = lax.fori_loop(0, keys // STEP_ROWS, score, jnp.full((8, rows), -jnp.inf, f32))
        top = jnp.max(top, axis=0, keepdims=True)

        def expo(i, total):
            at = pl.multiple_of(i * STEP_ROWS, STEP_ROWS)
            e = jnp.exp(s_scr[pl.ds(at, STEP_ROWS), :] - top)
            s_scr[pl.ds(at, STEP_ROWS), :] = e
            return total + jnp.sum(e.reshape(STEP_ROWS // 8, 8, rows), axis=0)

        total = lax.fori_loop(0, keys // STEP_ROWS, expo, jnp.zeros((8, rows), f32))
        inverse = 1.0 / jnp.sum(total, axis=0, keepdims=True)

        def scale(i, _):
            at = pl.multiple_of(i * STEP_ROWS, STEP_ROWS)
            p_ref[hh, pl.ds(at, STEP_ROWS), :] = (s_scr[pl.ds(at, STEP_ROWS), :] * inverse).astype(bf)
            return 0

        lax.fori_loop(0, keys // STEP_ROWS, scale, 0)
        out.append(jnp.dot(vt, p_ref[hh], preferred_element_type=f32))
    sub = lax.broadcasted_iota(jnp.int32, out[0].shape, 0)
    ctx_ref[...] = jnp.where(sub < 64, out[0], out[1]).T.astype(bf)


def attend(query, key_all, value_all, code, table):
    rows, keys = query.shape[0], key_all.shape[0]
    lines = jnp.full((16, 128), masked_score, jnp.float32).at[:H, :BUCKETS].set(table.astype(jnp.float32).T)
    bf = jnp.bfloat16
    return pl.pallas_call(
        attend_kernel,
        grid=(H // 2,),
        out_shape=[jax.ShapeDtypeStruct((rows, D), bf), jax.ShapeDtypeStruct((H, keys, rows), bf)],
        in_specs=[
            pl.BlockSpec((rows, 128), lambda p: (0, p)),
            pl.BlockSpec((keys, 128), lambda p: (0, p)),
            pl.BlockSpec((keys, 128), lambda p: (0, p)),
            pl.BlockSpec((keys, rows), lambda p: (0, 0)),
            pl.BlockSpec((16, 128), lambda p: (0, 0)),
        ],
        out_specs=[pl.BlockSpec((rows, 128), lambda p: (0, p)), pl.BlockSpec((2, keys, rows), lambda p: (p, 0, 0))],
        scratch_shapes=[pltpu.VMEM((keys, rows), jnp.float32)],
        compiler_params=pltpu.CompilerParams(vmem_limit_bytes=56 << 20),
        name="attend",
    )(query, key_all, value_all, code, lines)


def attend_back_kernel(q_ref, k_ref, v_ref, do_ref, p_ref, code_ref, dq_ref, dk_ref, dv_ref, tab_ref, spread, held):
    pair = pl.program_id(0)
    keys, rows = code_ref.shape
    f32, bf = jnp.float32, jnp.bfloat16
    STEP_ROWS = keys
    kt = k_ref[...].T
    dq = []
    for hh in range(2):
        qm = half(q_ref[...], hh)
        dom = half(do_ref[...], hh)

        def inner(i, total):
            at = pl.multiple_of(i * STEP_ROWS, STEP_ROWS)
            g = lax.dot_general(v_ref[pl.ds(at, STEP_ROWS), :], dom, NT, preferred_element_type=f32)
            w = g * p_ref[hh, pl.ds(at, STEP_ROWS), :].astype(f32)
            return total + jnp.sum(w.reshape(STEP_ROWS // 8, 8, rows), axis=0)

        total = lax.fori_loop(0, keys // STEP_ROWS, inner, jnp.zeros((8, rows), f32))
        total = jnp.sum(total, axis=0, keepdims=True)

        def grads(i, acc):
            at = pl.multiple_of(i * STEP_ROWS, STEP_ROWS)
            sl = pl.ds(at, STEP_ROWS)
            g = lax.dot_general(v_ref[sl, :], dom, NT, preferred_element_type=f32)
            p = p_ref[hh, sl, :]
            ds = p.astype(f32) * (g - total)
            wide = ds.reshape(STEP_ROWS // 8, 8, rows)
            if hh == 0:
                held[...] = wide
            else:
                both = jnp.concatenate([held[...], wide], axis=1).astype(bf)
                spread[:, pl.ds(pl.multiple_of(pair * 16, 16), 16), :] = both
            ds = ds.astype(bf)
            dv = jnp.dot(p, dom, preferred_element_type=f32)
            dk = jnp.dot(ds, qm, preferred_element_type=f32)
            if hh == 0:
                dv_ref[sl, :] = dv
                dk_ref[sl, :] = dk
            else:
                dv_ref[sl, :] += dv
                dk_ref[sl, :] += dk
            return acc + lax.dot_general(k_ref[sl, :], ds, TN, preferred_element_type=f32)

        dq.append(lax.fori_loop(0, keys // STEP_ROWS, grads, jnp.zeros((128, rows), f32)))
    sub = lax.broadcasted_iota(jnp.int32, dq[0].shape, 0)
    dq_ref[...] = jnp.where(sub < 64, dq[0], dq[1]).T * 0.125

    @pl.when(pair == H // 2 - 1)
    def _():
        bucket = lax.broadcasted_iota(jnp.int32, (BUCKETS, rows), 0)

        def count(i, acc):
            code = code_ref[pl.ds(pl.multiple_of(i * 8, 8), 8), :]
            hot = jnp.concatenate(
                [jnp.where(jnp.broadcast_to(code[r : r + 1], bucket.shape) == bucket, 1.0, 0.0) for r in range(8)]
            ).astype(bf)
            return acc + lax.dot_general(spread[i], hot, NT, preferred_element_type=f32)

        acc = lax.fori_loop(0, keys // 8, count, jnp.zeros((8 * H, 8 * BUCKETS), f32), unroll=8)
        a = lax.broadcasted_iota(jnp.int32, acc.shape, 0) % 8
        b = lax.broadcasted_iota(jnp.int32, acc.shape, 1) // BUCKETS
        tab_ref[...] = jnp.where(a == b, acc, 0.0)


def soft_back(query, key_all, value_all, grad_context, soft, code):
    rows, keys = query.shape[0], key_all.shape[0]
    f32 = jnp.float32
    row = pl.BlockSpec((rows, 128), lambda p: (0, p))
    key = pl.BlockSpec((keys, 128), lambda p: (0, p))
    dq, dk, dv, tab = pl.pallas_call(
        attend_back_kernel,
        grid=(H // 2,),
        out_shape=[
            jax.ShapeDtypeStruct((rows, D), f32),
            jax.ShapeDtypeStruct((keys, D), f32),
            jax.ShapeDtypeStruct((keys, D), f32),
            jax.ShapeDtypeStruct((8 * H, 8 * BUCKETS), f32),
        ],
        in_specs=[row, key, key, row, pl.BlockSpec((2, keys, rows), lambda p: (p, 0, 0)), pl.BlockSpec((keys, rows), lambda p: (0, 0))],
        out_specs=[row, key, key, pl.BlockSpec((8 * H, 8 * BUCKETS), lambda p: (0, 0))],
        scratch_shapes=[pltpu.VMEM((keys // 8, 8 * H, rows), jnp.bfloat16), pltpu.VMEM((keys // 8, 8, rows), f32)],
        compiler_params=pltpu.CompilerParams(vmem_limit_bytes=58 << 20),
        name="attend_back",
    )(query, key_all, value_all, grad_context, soft, code)
    table_grad = jnp.sum(tab.reshape(H, 8, 8, BUCKETS), axis=(1, 2)).T
    return dq, dk, dv, table_grad


MESH = pl.DeviceIdType.MESH
SHARD = 224580
ROWS = 1760
TAIL, HEAD = 160, 176
WIN = 2176
SLOTS = 37
CHIP = 74
PARTS = ((0, 19), (19, 18))


def place():
    k = lax.axis_index("dp")
    return k, lax.axis_index("seq"), k // 4, (k // 2) % 2, k % 2


def shard_start(d):
    return d * 1754 + (d * 68) // 128, (d * 68) % 128


def early_vectors(k):
    return (k == 0) | (k == 4) | (k == 5)


def vector_row(k, other):
    at = other
    for chip, row in ((0, 768), (1, 5385), (4, 14607), (5, 19221), (10, 37671), (15, 56127)):
        at = jnp.where(k == chip, row, at)
    return at


def tile_start(w):
    at = w * 48
    for first, shift in ((16, 777 - 16 * 48), (112, 5391 - 112 * 48), (208, 9999 - 208 * 48), (304, 14613 - 304 * 48), (784, 37695 - 784 * 48)):
        at = jnp.where(w >= first, w * 48 + shift, at)
    wide = (w >= 400) & (w < 784)
    v = w - 400
    at = jnp.where(wide, 19239 + (v // 4) * 192 + (v % 4) * 6, at)
    return at, wide


def neighbours(k, c, z, y, x):
    t = k >= 0
    return [
        (t, (k, 1 - c)),
        (t, (z * 4 + y * 2 + 1 - x, c)),
        (t, (z * 4 + (1 - y) * 2 + x, c)),
        (z < 3, (jnp.minimum(k + 4, 15), c)),
        (z > 0, (jnp.maximum(k - 4, 0), c)),
        ((c == 1) & (k < 15), (jnp.minimum(k + 1, 15), 0)),
        ((c == 0) & (k > 0), (jnp.maximum(k - 1, 0), 1)),
    ]


def greet(k, c, z, y, x):
    bar = pltpu.get_barrier_semaphore()
    for cond, dev in neighbours(k, c, z, y, x):
        @pl.when(cond)
        def _():
            pl.semaphore_signal(bar, inc=1, device_id=dev, device_id_type=MESH)
    peers = 3
    for cond, _ in neighbours(k, c, z, y, x)[3:]:
        peers = peers + jnp.where(cond, 1, 0)
    pl.semaphore_wait(bar, peers)


def rcopy(src, dst, ssem, rsem, dev):
    return pltpu.make_async_remote_copy(src_ref=src, dst_ref=dst, send_sem=ssem, recv_sem=rsem, device_id=dev, device_id_type=MESH)


def gather_kernel(x_ref, g_ref, xv, tail, head, win, chunk, lsem, hsend, hrecv, own,
                  zs, zr, xas, xar, xbs, xbr, yas, yar, ybs, ybr, cs, cr):
    k, c, z, y, x = place()
    d = 2 * k + c
    greet(k, c, z, y, x)
    load = pltpu.make_async_copy(x_ref, xv, lsem)
    load.start()
    prev = (jnp.where(c == 1, k, jnp.maximum(k - 1, 0)), 1 - c)
    nxt = (jnp.where(c == 0, k, jnp.minimum(k + 1, 15)), 1 - c)
    to_next = rcopy(x_ref.at[pl.ds(ROWS - TAIL, TAIL)], tail, hsend.at[0], hrecv.at[0], nxt)
    to_prev = rcopy(x_ref.at[pl.ds(0, HEAD)], head, hsend.at[1], hrecv.at[1], prev)

    @pl.when(d < 31)
    def _():
        to_next.start()

    @pl.when(d > 0)
    def _():
        to_prev.start()

    win[...] = jnp.zeros_like(win)
    lanes = lax.broadcasted_iota(jnp.int32, (80, 128), 1)
    q, sh = shard_start(d)
    load.wait()

    @pl.loop(0, ROWS // 80)
    def _(i):
        r = pl.multiple_of(i * 80, 8)
        rolled = pltpu.roll(xv[pl.ds(r, 80), :], sh, 1)
        win[pl.ds(160 + r, 80), :] += jnp.where(lanes >= sh, rolled, 0.0)
        win[pl.ds(161 + r, 80), :] += jnp.where(lanes < sh, rolled, 0.0)

    @pl.when(d > 0)
    def _():
        to_next.wait_recv()
        qp, shp = shard_start(d - 1)
        lanes = lax.broadcasted_iota(jnp.int32, (TAIL, 128), 1)
        rolled = pltpu.roll(tail[...], shp, 1)
        at = 1760 - (q - qp)
        win[pl.ds(at, TAIL), :] += jnp.where(lanes >= shp, rolled, 0.0)
        win[pl.ds(at + 1, TAIL), :] += jnp.where(lanes < shp, rolled, 0.0)

    @pl.when(d < 31)
    def _():
        to_prev.wait_recv()
        qn, shn = shard_start(d + 1)
        lanes = lax.broadcasted_iota(jnp.int32, (HEAD, 128), 1)
        rolled = pltpu.roll(head[...], shn, 1)
        at = 160 + (qn - q)
        win[pl.ds(at, HEAD), :] += jnp.where(lanes >= shn, rolled, 0.0)
        win[pl.ds(at + 1, HEAD), :] += jnp.where(lanes < shn, rolled, 0.0)

    early = early_vectors(k)
    nw0 = jnp.where(early, 36, 37)
    vecs = early == (c == 0)
    first = jnp.where(c == 0, 73 * k, 73 * k + nw0)
    base = q - 160

    @pl.loop(0, SLOTS)
    def _(t):
        at, wide = tile_start(first + t)
        is_vec = vecs & (t == 36)
        at = jnp.where(is_vec, vector_row(k, q), at) - base
        wide = wide & jnp.logical_not(is_vec)

        @pl.when(wide)
        def _():
            parts = [win[pl.ds(at + j, 8, stride=24), :] for j in range(6)]
            chunk[t] = jnp.concatenate(parts, axis=1).astype(jnp.bfloat16)

        @pl.when(jnp.logical_not(wide))
        def _():
            parts = [win[pl.ds(at + j, 8, stride=6), :] for j in range(6)]
            chunk[t] = jnp.concatenate(parts, axis=1).astype(jnp.bfloat16)

    @pl.when(d < 31)
    def _():
        to_next.wait_send()

    @pl.when(d > 0)
    def _():
        to_prev.wait_send()

    xdev, ydev, cdev = (z * 4 + y * 2 + 1 - x, c), (z * 4 + (1 - y) * 2 + x, c), (k, 1 - c)
    zdev = {1: (jnp.minimum(k + 4, 15), c), -1: (jnp.maximum(k - 4, 0), c)}

    def gsl(chip, p):
        off, n = PARTS[p]
        return g_ref.at[chip, pl.ds(37 * c + off, n)]

    def src(chip, p, mine=False):
        off, n = PARTS[p]
        return chunk.at[pl.ds(off, n)] if mine else gsl(chip, p)

    def chip_of(zo, yo, xo):
        return zo * 4 + yo * 2 + xo

    def zcopy(zo, p, way, mine=False):
        chip = chip_of(zo, y, x)
        w = (way + 1) // 2
        return rcopy(src(chip, p, mine), gsl(chip, p), zs.at[w, zo, p], zr.at[zo, p], zdev[way])

    def xcopy(zo, yo, xo, p, mine=False):
        chip = chip_of(zo, yo, xo)
        s, r = (xas, xar) if p == 0 else (xbs, xbr)
        i = zo if p == 0 else zo * 2 + yo
        return rcopy(src(chip, p, mine), gsl(chip, p), s.at[i], r.at[i], xdev)

    def ycopy(zo, yo, xo, p, mine=False):
        chip = chip_of(zo, yo, xo)
        s, r = (ybs, ybr) if p == 1 else (yas, yar)
        i = zo if p == 1 else zo * 2 + xo
        return rcopy(src(chip, p, mine), gsl(chip, p), s.at[i], r.at[i], ydev)

    def ccopy(chip, p, mine=False):
        return rcopy(src(chip, p, mine), gsl(chip, p), cs.at[chip, p], cr.at[chip, p], cdev)

    for p in (0, 1):
        for way in (1, -1):
            @pl.when((z + way >= 0) & (z + way <= 3))
            def _():
                zcopy(z, p, way, True).start()
    xcopy(z, y, x, 0, True).start()
    ycopy(z, y, x, 1, True).start()
    ycopy(z, y, x, 0, True).start()
    xcopy(z, y, x, 1, True).start()
    mine = [pltpu.make_async_copy(chunk.at[pl.ds(*PARTS[p])], gsl(k, p), own.at[p]) for p in (0, 1)]
    for p in (0, 1):
        mine[p].start()
        ccopy(k, p, True).start()

    def column(zo, way):
        for p in (0, 1):
            zcopy(zo, p, way).wait_recv()

            @pl.when((zo + way * 0 + 0 >= 0) & (z + way >= 0) & (z + way <= 3))
            def _():
                zcopy(zo, p, way).start()
            if p == 0:
                xcopy(zo, y, x, 0).start()
                ycopy(zo, y, x, 0).start()
            else:
                ycopy(zo, y, x, 1).start()
                xcopy(zo, y, x, 1).start()
            ccopy(chip_of(zo, y, x), p).start()

    def beside(zo):
        xcopy(zo, y, 1 - x, 0).wait_recv()
        ycopy(zo, y, 1 - x, 0).start()
        ccopy(chip_of(zo, y, 1 - x), 0).start()
        ycopy(zo, 1 - y, x, 1).wait_recv()
        xcopy(zo, 1 - y, x, 1).start()
        ccopy(chip_of(zo, 1 - y, x), 1).start()

    def last(zo):
        ycopy(zo, 1 - y, x, 0).wait_recv()
        ccopy(chip_of(zo, 1 - y, x), 0).start()
        xcopy(zo, y, 1 - x, 1).wait_recv()
        ccopy(chip_of(zo, y, 1 - x), 1).start()
        ycopy(zo, 1 - y, 1 - x, 0).wait_recv()
        ccopy(chip_of(zo, 1 - y, 1 - x), 0).start()
        xcopy(zo, 1 - y, 1 - x, 1).wait_recv()
        ccopy(chip_of(zo, 1 - y, 1 - x), 1).start()

    def at_distance(s, f):
        for way in (1, -1):
            @pl.when((z - s * way >= 0) & (z - s * way <= 3))
            def _():
                f(z - s * way, way)

    at_distance(1, column)
    beside(z)
    at_distance(2, column)
    at_distance(1, lambda zo, way: beside(zo))
    at_distance(3, column)
    last(z)
    at_distance(2, lambda zo, way: beside(zo))
    at_distance(1, lambda zo, way: last(zo))
    at_distance(3, lambda zo, way: beside(zo))
    at_distance(2, lambda zo, way: last(zo))
    at_distance(3, lambda zo, way: last(zo))

    for p in (0, 1):
        mine[p].wait()
        for way in (1, -1):
            for zo in range(4):
                @pl.when(((z - zo) * way >= 0) & (z + way >= 0) & (z + way <= 3))
                def _():
                    zcopy(zo, p, way).wait_send()
    for zo in range(4):
        xcopy(zo, y, x, 0).wait_send()
        ycopy(zo, y, x, 1).wait_send()
        for o in range(2):
            ycopy(zo, y, o, 0).wait_send()
            xcopy(zo, o, x, 1).wait_send()
    for chip in range(16):
        for p in (0, 1):
            ccopy(chip, p).wait_send()
            off, n = PARTS[p]
            theirs = g_ref.at[chip, pl.ds(37 * (1 - c) + off, n)]
            rcopy(theirs, theirs, cs.at[chip, p], cr.at[chip, p], cdev).wait_recv()


def gather_weights(master):
    x = jnp.pad(master, (0, ROWS * 128 - SHARD)).reshape(ROWS, 128)
    sem = pltpu.SemaphoreType.DMA
    any_ = pl.BlockSpec(memory_space=pl.ANY)
    return pl.pallas_call(
        gather_kernel,
        out_shape=jax.ShapeDtypeStruct((16, CHIP, 8, 768), jnp.bfloat16),
        in_specs=[any_],
        out_specs=any_,
        scratch_shapes=[
            pltpu.VMEM((ROWS, 128), jnp.float32),
            pltpu.VMEM((TAIL, 128), jnp.float32),
            pltpu.VMEM((HEAD, 128), jnp.float32),
            pltpu.VMEM((WIN, 128), jnp.float32),
            pltpu.VMEM((SLOTS, 8, 768), jnp.bfloat16),
            sem, sem((2,)), sem((2,)), sem((2,)),
            sem((2, 4, 2)), sem((4, 2)),
            sem((4,)), sem((4,)), sem((8,)), sem((8,)),
            sem((8,)), sem((8,)), sem((4,)), sem((4,)),
            sem((16, 2)), sem((16, 2)),
        ],
        compiler_params=pltpu.CompilerParams(collective_id=0, has_side_effects=True, vmem_limit_bytes=40 << 20),
        name="gather_weights",
    )(x)


FRONT = 344
WIN2 = 2464
EDGE = 4
ENTRY_ROWS = 777


def reduce_kernel(g_ref, m_ref, one_ref, two_ref, step_ref, new1_ref, new2_ref,
                  acc, crecv, a1, b1, a2, b2, up, dn, total, ebuf, sq, sqr, win, mv, onev, twov,
                  lsem, asem, cs, cr, a1s, a1r, b1s, b1r, a2s, a2r, b2s, b2r, us, ur, ds_, dr, es, er, qs, qr):
    k, c, z, y, x = place()
    d = 2 * k + c
    xdev, ydev, cdev = (z * 4 + y * 2 + 1 - x, c), (z * 4 + (1 - y) * 2 + x, c), (k, 1 - c)
    zdev = {1: (jnp.minimum(k + 4, 15), c), -1: (jnp.maximum(k - 4, 0), c)}
    column_devs = [((z + s) % 4 * 4 + y * 2 + x, c) for s in (1, 2, 3)]
    prev = (jnp.where(c == 1, k, jnp.maximum(k - 1, 0)), 1 - c)
    nxt = (jnp.where(c == 0, k, jnp.minimum(k + 1, 15)), 1 - c)
    bar = pltpu.get_barrier_semaphore()
    far_next, far_prev = (c == 1) & (k < 15), (c == 0) & (k > 0)
    for dev in [xdev, ydev, cdev] + column_devs:
        pl.semaphore_signal(bar, inc=1, device_id=dev, device_id_type=MESH)

    @pl.when(far_next)
    def _():
        pl.semaphore_signal(bar, inc=1, device_id=nxt, device_id_type=MESH)

    @pl.when(far_prev)
    def _():
        pl.semaphore_signal(bar, inc=1, device_id=prev, device_id_type=MESH)

    pl.semaphore_wait(bar, 6 + jnp.where(far_next | far_prev, 1, 0))

    def chip_of(zo, yo, xo):
        return zo * 4 + yo * 2 + xo

    def load(chip):
        return pltpu.make_async_copy(g_ref.at[chip, pl.ds(37 * c, 37)], acc.at[chip], asem.at[chip])

    def ccopy(chip):
        return rcopy(g_ref.at[chip, pl.ds(37 * (1 - c), 37)], crecv.at[chip], cs.at[chip], cr.at[chip], cdev)

    def at_distance(s, f):
        if s == 0:
            f(z, 0)
            return
        for way in (1, -1):
            @pl.when((z + s * way >= 0) & (z + s * way <= 3))
            def _():
                f(z + s * way, way)

    def order(f):
        for s in (3, 2, 1, 0):
            at_distance(s, f)

    corners = ((1, 1), (1, 0), (0, 1), (0, 0))

    def flip(v, o):
        return 1 - v if o else v

    for oy, ox in corners:
        def go(zo, way):
            chip = chip_of(zo, flip(y, oy), flip(x, ox))
            load(chip).start()
            ccopy(chip).start()
        order(go)
    shards = [pltpu.make_async_copy(r, v, lsem.at[i]) for i, (r, v) in enumerate(((m_ref, mv), (one_ref, onev), (two_ref, twov)))]
    for s in shards:
        s.start()

    def psl(p):
        return pl.ds(*PARTS[p])

    def gain(dst, at, p, ref):
        off, n = PARTS[p]

        @pl.loop(0, n)
        def _(i):
            acc[at, off + i] = acc[at, off + i] + ref[i]

    def pair(chip):
        load(chip).wait()
        ccopy(chip).wait_recv()

        @pl.loop(0, 37)
        def _(i):
            acc[chip, i] = acc[chip, i] + crecv[chip, i]

    def a1copy(zo, xo):
        return rcopy(acc.at[chip_of(zo, 1 - y, xo), psl(0)], a1.at[zo * 2 + xo], a1s.at[zo * 2 + xo], a1r.at[zo * 2 + xo], ydev)

    def b1copy(zo, yo):
        return rcopy(acc.at[chip_of(zo, yo, 1 - x), psl(1)], b1.at[zo * 2 + yo], b1s.at[zo * 2 + yo], b1r.at[zo * 2 + yo], xdev)

    def a2copy(zo):
        return rcopy(acc.at[chip_of(zo, y, 1 - x), psl(0)], a2.at[zo], a2s.at[zo], a2r.at[zo], xdev)

    def b2copy(zo):
        return rcopy(acc.at[chip_of(zo, 1 - y, x), psl(1)], b2.at[zo], b2s.at[zo], b2r.at[zo], ydev)

    def zcopy(zo, way):
        buf, s, r = (up, us, ur) if way == 1 else (dn, ds_, dr)
        return rcopy(acc.at[chip_of(zo, y, x)], buf.at[zo], s.at[zo], r.at[zo], zdev[way])

    def first(oy, ox):
        def go(zo, way):
            yo, xo = flip(y, oy), flip(x, ox)
            pair(chip_of(zo, yo, xo))
            if oy:
                a1copy(zo, xo).start()
            if ox:
                b1copy(zo, yo).start()
        return go

    def second(zo, way):
        a1copy(zo, 1 - x).wait_recv()
        gain(acc, chip_of(zo, y, 1 - x), 0, a1.at[zo * 2 + 1 - x])
        a2copy(zo).start()
        b1copy(zo, 1 - y).wait_recv()
        gain(acc, chip_of(zo, 1 - y, x), 1, b1.at[zo * 2 + 1 - y])
        b2copy(zo).start()

    def third(zo, way):
        chip = chip_of(zo, y, x)
        a1copy(zo, x).wait_recv()
        gain(acc, chip, 0, a1.at[zo * 2 + x])
        b1copy(zo, y).wait_recv()
        gain(acc, chip, 1, b1.at[zo * 2 + y])
        a2copy(zo).wait_recv()
        gain(acc, chip, 0, a2.at[zo])
        b2copy(zo).wait_recv()
        gain(acc, chip, 1, b2.at[zo])
        if way:
            @pl.when((z - way >= 0) & (z - way <= 3))
            def _():
                zcopy(zo, way).wait_recv()
                buf = up if way == 1 else dn

                @pl.loop(0, 37)
                def _(i):
                    acc[chip, i] = acc[chip, i] + buf[zo, i]
            zcopy(zo, way).start()

    order(first(1, 1))
    order(first(1, 0))
    order(first(0, 1))
    order(second)
    order(first(0, 0))
    order(third)

    f32 = jnp.float32

    @pl.loop(0, 37)
    def _(i):
        total[i] = acc[k, i].astype(f32)

    for way in (1, -1):
        @pl.when((z - way >= 0) & (z - way <= 3))
        def _():
            zcopy(z, way).wait_recv()
            buf = up if way == 1 else dn

            @pl.loop(0, 37)
            def _(i):
                total[i] = total[i] + buf[z, i].astype(f32)

    early = early_vectors(k)
    nw0 = jnp.where(early, 36, 37)
    vecs = early == (c == 0)
    mine = jnp.where(vecs, 36, 37)
    to_next = rcopy(total.at[pl.ds(mine - EDGE, EDGE)], ebuf.at[0], es.at[0], er.at[0], nxt)
    to_prev = rcopy(total.at[pl.ds(0, EDGE)], ebuf.at[1], es.at[1], er.at[1], prev)

    @pl.when(d < 31)
    def _():
        to_next.start()

    @pl.when(d > 0)
    def _():
        to_prev.start()

    def square(i, run):
        t = total[i]
        t = t * t
        for j in range(6):
            run = run + t[:, 128 * j:128 * j + 128]
        return run

    sq[0] = lax.fori_loop(0, 37, square, jnp.zeros((8, 128), f32))
    for i, dev in enumerate((cdev, xdev, ydev)):
        step = rcopy(sq.at[i], sqr.at[i], qs.at[i], qr.at[i], dev)
        step.start()
        step.wait_recv()
        sq[i + 1] = sq[i] + sqr[i]
    hops = [rcopy(sq.at[3], sqr.at[3 + i], qs.at[3 + i], qr.at[3 + i], column_devs[i]) for i in range(3)]
    for h in hops:
        h.start()

    q, sh = shard_start(d)
    base = q - FRONT

    def flatten(ref, i, at, wide):
        @pl.when(wide)
        def _():
            t = ref[i]
            for j in range(6):
                win[pl.ds(at + j, 8, stride=24), :] = t[:, 128 * j:128 * j + 128]

        @pl.when(jnp.logical_not(wide))
        def _():
            t = ref[i]
            for j in range(6):
                win[pl.ds(at + j, 8, stride=6), :] = t[:, 128 * j:128 * j + 128]

    own_vectors = vecs & (vector_row(k, -1) >= 0)

    @pl.when(own_vectors)
    def _():
        flatten(total, 36, vector_row(k, q) - base, k < 0)

    w0 = jnp.where(c == 0, 73 * k, 73 * k + nw0)

    @pl.loop(0, mine)
    def _(t):
        at, wide = tile_start(w0 + t)
        flatten(total, t, at - base, wide)

    @pl.when(d > 0)
    def _():
        to_next.wait_recv()

        @pl.loop(0, EDGE)
        def _(t):
            at, wide = tile_start(w0 - EDGE + t)
            flatten(ebuf.at[0], t, at - base, wide)

    @pl.when(d < 31)
    def _():
        to_prev.wait_recv()

        @pl.loop(0, EDGE)
        def _(t):
            at, wide = tile_start(w0 + mine + t)
            flatten(ebuf.at[1], t, at - base, wide)

    for i, h in enumerate(hops):
        h.wait_recv()
    parts = [sqr[3], sqr[4], sqr[5]]
    rows = [sq[3]] + parts
    whole = (rows[0] + rows[2]) + (rows[1] + rows[3])
    square_sum = jnp.sum(jnp.sum(whole, axis=1, keepdims=True), axis=0, keepdims=True)
    factor = jnp.minimum(1.0, lax.rsqrt(square_sum / RAW + 1e-06))
    for s in shards:
        s.wait()
    lanes = lax.broadcasted_iota(jnp.int32, (80, 128), 1)
    rowi = lax.broadcasted_iota(jnp.int32, (80, 128), 0)
    back = (128 - sh) % 128

    @pl.loop(0, ROWS // 80)
    def _(i):
        r = pl.multiple_of(i * 80, 8)
        here = pltpu.roll(win[pl.ds(FRONT + r, 80), :], back, 1)
        there = pltpu.roll(win[pl.ds(FRONT + 1 + r, 80), :], back, 1)
        grad = jnp.where(lanes < 128 - sh, here, there) * factor
        entry = (d == 0) & (rowi + r < ENTRY_ROWS)
        rate = jnp.where(entry, learn_rate * layer_decay, learn_rate)
        one = beta_one * onev[pl.ds(r, 80), :] + (1.0 - beta_one) * grad
        two = beta_two * twov[pl.ds(r, 80), :] + (1.0 - beta_two) * grad * grad
        fixed_one = one / (1.0 - beta_one ** STEP)
        fixed_two = two / (1.0 - beta_two ** STEP)
        step_ref[pl.ds(r, 80), :] = -rate * (fixed_one / (jnp.sqrt(fixed_two) + adam_eps) + weight_decay * mv[pl.ds(r, 80), :])
        new1_ref[pl.ds(r, 80), :] = one
        new2_ref[pl.ds(r, 80), :] = two

    for i, dev in enumerate((cdev, xdev, ydev)):
        rcopy(sq.at[i], sqr.at[i], qs.at[i], qr.at[i], dev).wait_send()
    for h in hops:
        h.wait_send()

    @pl.when(d < 31)
    def _():
        to_next.wait_send()

    @pl.when(d > 0)
    def _():
        to_prev.wait_send()

    for chip in range(16):
        ccopy(chip).wait_send()
    for zo in range(4):
        a2copy(zo).wait_send()
        b2copy(zo).wait_send()
        for o in range(2):
            a1copy(zo, o).wait_send()
            b1copy(zo, o).wait_send()
        for way in (1, -1):
            @pl.when((zo - z) * way > 0)
            def _():
                zcopy(zo, way).wait_send()


def reduce_and_step(grads, master, first_moment, second_moment):
    def rows(v):
        return jnp.pad(v, (0, ROWS * 128 - SHARD)).reshape(ROWS, 128)

    sem = pltpu.SemaphoreType.DMA
    any_ = pl.BlockSpec(memory_space=pl.ANY)
    vm = pl.BlockSpec(memory_space=pltpu.VMEM)
    bf, f32 = jnp.bfloat16, jnp.float32
    tile = (8, 768)
    outs = pl.pallas_call(
        reduce_kernel,
        out_shape=[jax.ShapeDtypeStruct((ROWS, 128), f32)] * 3,
        in_specs=[any_] * 4,
        out_specs=[vm] * 3,
        scratch_shapes=[
            pltpu.VMEM((16, 37) + tile, bf), pltpu.VMEM((16, 37) + tile, bf),
            pltpu.VMEM((8, 19) + tile, bf), pltpu.VMEM((8, 18) + tile, bf),
            pltpu.VMEM((4, 19) + tile, bf), pltpu.VMEM((4, 18) + tile, bf),
            pltpu.VMEM((4, 37) + tile, bf), pltpu.VMEM((4, 37) + tile, bf),
            pltpu.VMEM((37,) + tile, f32), pltpu.VMEM((2, EDGE) + tile, f32),
            pltpu.VMEM((4, 8, 128), f32), pltpu.VMEM((6, 8, 128), f32),
            pltpu.VMEM((WIN2, 128), f32),
            pltpu.VMEM((ROWS, 128), f32), pltpu.VMEM((ROWS, 128), f32), pltpu.VMEM((ROWS, 128), f32),
            sem((3,)), sem((16,)), sem((16,)), sem((16,)),
            sem((8,)), sem((8,)), sem((8,)), sem((8,)), sem((4,)), sem((4,)), sem((4,)), sem((4,)),
            sem((4,)), sem((4,)), sem((4,)), sem((4,)), sem((2,)), sem((2,)), sem((6,)), sem((6,)),
        ],
        compiler_params=pltpu.CompilerParams(collective_id=1, has_side_effects=True, vmem_limit_bytes=56 << 20),
        name="reduce_and_step",
    )(grads, rows(master), rows(first_moment), rows(second_moment))
    return [o.reshape(-1)[:SHARD] for o in outs]


WEIGHTS = (
    (0, 0, 16),
    (3, 16, 96),
    (5, 112, 96),
    (6, 208, 96),
    (8, 304, 96),
    (12, 400, 384),
    (14, 784, 384),
)
VECTORS = (
    (1, 0, 0),
    (2, 0, 1),
    (4, 1, 0),
    (7, 4, 0),
    (9, 5, 0),
    (10, 5, 1),
    (11, 5, 2),
    (13, 10, 0),
    (15, 15, 0),
    (16, 15, 1),
    (17, 15, 2),
)


def vector_slot(chip):
    return 36 if chip in (0, 4, 5) else 73


def slots_of(first, count):
    runs = []
    for w in range(first, first + count):
        chip, at = divmod(w, 73)
        slot = chip * CHIP + at + (1 if at >= vector_slot(chip) else 0)
        if runs and runs[-1][0] + runs[-1][1] == slot:
            runs[-1][1] += 1
        else:
            runs.append([slot, 1])
    return runs


def unpack_gathered(gathered):
    tiles = gathered.reshape(16 * CHIP, 8, D)
    pieces = {}
    for name, first, count in WEIGHTS:
        got = jnp.concatenate([tiles[s : s + n] for s, n in slots_of(first, count)])
        if name == 12:
            got = got.reshape(96, 4, 8, D).transpose(0, 2, 1, 3).reshape(D, FF)
        pieces[name] = got.reshape(-1, FF if name == 12 else D)
    for name, chip, row in VECTORS:
        block = gathered[chip, vector_slot(chip)]
        if name == 13:
            pieces[name] = block[row : row + 4].reshape(FF)
        elif name == 2:
            pieces[name] = block[row, : BUCKETS * H].reshape(BUCKETS, H)
        else:
            pieces[name] = block[row]
    return Params(*[pieces[i] for i in range(18)])


def pack_gradients(pieces):
    by_name = [p.astype(jnp.bfloat16) for p in pieces]
    weights = []
    for name, first, count in WEIGHTS:
        got = by_name[name]
        if name == 12:
            got = got.reshape(96, 8, 4, D).transpose(0, 2, 1, 3)
        weights.append(got.reshape(count, 8, D))
    cuts = []
    for chip in range(16):
        held = [(r, by_name[n]) for n, c, r in VECTORS if c == chip]
        rows = [jnp.pad(v.reshape(-1), (0, -v.size % D)).reshape(-1, D) for _, v in held]
        block = jnp.concatenate(rows + [jnp.zeros((8 - sum(r.shape[0] for r in rows), D), jnp.bfloat16)])
        cuts.append((73 * chip + vector_slot(chip), block[None]))
    parts = []
    for (name, first, count), tiles in zip(WEIGHTS, weights):
        at = first
        for w, block in [c for c in cuts if first <= c[0] < first + count]:
            if w > at:
                parts.append(tiles[at - first : w - first])
            parts.append(block)
            at = w
        parts.append(tiles[at - first :])
    parts.extend(block for w, block in cuts if w == 1168)
    return jnp.concatenate(parts).reshape(16, CHIP, 8, D)


def per_device(
    custom,
    tokens,
    cotangent,
    page_boxes,
    page_lengths,
    padding,
    buckets,
    master,
    first_moment,
    second_moment,
):
    blocks_here = tokens.shape[0]
    rows = tokens.shape[1]
    count_rows = blocks_here * rows
    if custom:
        entry_part = unpack_gathered(gather_weights(master))
    else:
        shard_low = master.astype(jnp.bfloat16)
        flat_params = lax.all_gather(shard_low, ("dp", "seq"), axis=0, tiled=True)
        entry_part = unpack(flat_params)
    layers = [entry_part]
    places = lax.axis_index("seq") * rows + jnp.arange(rows, dtype=jnp.int32)
    page_ends = running_sum(page_lengths)
    page_of = jnp.sum((places[None, :, None] >= page_ends[:, None, :]).astype(jnp.int32), axis=2)
    own_tags = jnp.where(padding > 0, page_of + 1, 0).astype(jnp.bfloat16)
    query_tags = (page_of + 1).astype(jnp.float32)
    key_places = jnp.arange(BLOCK, dtype=jnp.int32)
    features_low = layout_features(page_boxes.reshape(4, count_rows)).astype(jnp.bfloat16)
    hidden = (
        tokens.reshape(count_rows, D).astype(jnp.float32)
        + matmul_low(features_low, entry_part.layout_weight)
        + as_float(entry_part.layout_bias)
    )
    saved = []
    for weights in layers:
        inputs_low = hidden.astype(jnp.bfloat16)
        query_low = (
            (matmul_low(inputs_low, weights.query_weight) + as_float(weights.query_bias))
            * 0.125
        ).astype(jnp.bfloat16)
        key_low = matmul_low(inputs_low, weights.key_weight).astype(jnp.bfloat16)
        value_low = (
            matmul_low(inputs_low, weights.value_weight) + as_float(weights.value_bias)
        ).astype(jnp.bfloat16)
        key_all, value_all, tags_all = (
            lax.all_gather(key_low.reshape(blocks_here, rows, D), "seq", axis=1, tiled=True),
            lax.all_gather(value_low.reshape(blocks_here, rows, D), "seq", axis=1, tiled=True),
            lax.all_gather(own_tags, "seq", axis=1, tiled=True),
        )
        allowed = (tags_all[:, None, :].astype(jnp.float32) == query_tags[:, :, None]) | (
            key_places[None, None, :] == places[None, :, None]
        )
        code = jnp.where(allowed[0], buckets[0], BUCKETS).T
        context_low, soft = attend(query_low, key_all[0], value_all[0], code, entry_part.bias_table)
        first_in = (
            hidden
            + matmul_low(context_low, weights.output_weight)
            + as_float(weights.output_bias)
        )
        first_out = layer_norm(
            first_in, as_float(weights.first_gain), as_float(weights.first_shift)
        )
        first_low = first_out.astype(jnp.bfloat16)
        up_sum = matmul_low(first_low, weights.up_weight) + as_float(weights.up_bias)
        activated = gelu_exact(up_sum).astype(jnp.bfloat16)
        second_in = (
            first_out
            + matmul_low(activated, weights.down_weight)
            + as_float(weights.down_bias)
        )
        stash = SimpleNamespace(
            inputs_low=inputs_low,
            query_low=query_low,
            key_low=key_low,
            value_low=value_low,
            soft=soft,
            code=code,
            context_low=context_low,
            first_in=first_in,
            first_low=first_low,
            up_sum=up_sum,
            activated=activated,
            second_in=second_in,
        )
        stash.key_all = key_all
        stash.value_all = value_all
        saved.append(stash)
        hidden = layer_norm(
            second_in, as_float(weights.second_gain), as_float(weights.second_shift)
        )
    grad_out = cotangent.reshape(count_rows, D).astype(jnp.float32)
    table_grad = jnp.zeros((BUCKETS, H), jnp.float32)
    layer_grads = []
    for number in reversed(range(LAYERS)):
        weights = layers[number]
        stash = saved[number]
        norm_pair = jax.vjp(
            layer_norm,
            stash.second_in,
            as_float(weights.second_gain),
            as_float(weights.second_shift),
        )
        grad_second, grad_gain_two, grad_shift_two = norm_pair[1](grad_out)
        grad_down_bias = jnp.sum(grad_second, axis=0)
        down_back = grad_second.astype(jnp.bfloat16)
        grad_down_weight = jnp.einsum(
            "nf,nd->fd", stash.activated, down_back, preferred_element_type=jnp.float32
        )
        grad_activated = jnp.einsum(
            "nd,fd->nf", down_back, weights.down_weight, preferred_element_type=jnp.float32
        )
        gelu_pair = jax.vjp(gelu_exact, stash.up_sum)
        grad_up = gelu_pair[1](grad_activated)[0]
        grad_up_bias = jnp.sum(grad_up, axis=0)
        up_back = grad_up.astype(jnp.bfloat16)
        grad_up_weight = jnp.einsum(
            "nd,nf->df", stash.first_low, up_back, preferred_element_type=jnp.float32
        )
        grad_first = grad_second + jnp.einsum(
            "nf,df->nd", up_back, weights.up_weight, preferred_element_type=jnp.float32
        )
        first_pair = jax.vjp(
            layer_norm,
            stash.first_in,
            as_float(weights.first_gain),
            as_float(weights.first_shift),
        )
        grad_first_in, grad_gain_one, grad_shift_one = first_pair[1](grad_first)
        grad_output_bias = jnp.sum(grad_first_in, axis=0)
        attend_back = grad_first_in.astype(jnp.bfloat16)
        grad_output_weight = jnp.einsum(
            "nd,ne->de", stash.context_low, attend_back, preferred_element_type=jnp.float32
        )
        grad_context = jnp.einsum(
            "ne,de->nd", attend_back, weights.output_weight, preferred_element_type=jnp.float32
        ).astype(jnp.bfloat16)
        grad_query, grad_key_all, grad_value_all, table_grad = soft_back(
            stash.query_low, stash.key_all[0], stash.value_all[0], grad_context, stash.soft, stash.code
        )
        grad_key_all = grad_key_all.reshape(blocks_here, BLOCK, D)
        grad_value_all = grad_value_all.reshape(blocks_here, BLOCK, D)
        grad_key, grad_value = (
            lax.psum_scatter(
                grad_key_all.astype(jnp.bfloat16), "seq", scatter_dimension=1, tiled=True
            ).astype(jnp.float32),
            lax.psum_scatter(
                grad_value_all.astype(jnp.bfloat16), "seq", scatter_dimension=1, tiled=True
            ).astype(jnp.float32),
        )
        grad_key = grad_key.reshape(count_rows, D)
        grad_value = grad_value.reshape(count_rows, D)
        grad_query_bias = jnp.sum(grad_query, axis=0)
        grad_value_bias = jnp.sum(grad_value, axis=0)
        query_back = grad_query.astype(jnp.bfloat16)
        key_back = grad_key.astype(jnp.bfloat16)
        value_back = grad_value.astype(jnp.bfloat16)
        grad_query_weight = jnp.einsum(
            "nd,ne->de", stash.inputs_low, query_back, preferred_element_type=jnp.float32
        )
        grad_key_weight = jnp.einsum(
            "nd,ne->de", stash.inputs_low, key_back, preferred_element_type=jnp.float32
        )
        grad_value_weight = jnp.einsum(
            "nd,ne->de", stash.inputs_low, value_back, preferred_element_type=jnp.float32
        )
        grad_out = grad_first_in + jnp.einsum(
            "ne,de->nd", query_back, weights.query_weight, preferred_element_type=jnp.float32
        )
        grad_out = grad_out + jnp.einsum(
            "ne,de->nd", key_back, weights.key_weight, preferred_element_type=jnp.float32
        )
        grad_out = grad_out + jnp.einsum(
            "ne,de->nd", value_back, weights.value_weight, preferred_element_type=jnp.float32
        )
        layer_grads.insert(
            0,
            [
                grad_query_weight,
                grad_query_bias,
                grad_key_weight,
                grad_value_weight,
                grad_value_bias,
                grad_output_weight,
                grad_output_bias,
                grad_gain_one,
                grad_shift_one,
                grad_up_weight,
                grad_up_bias,
                grad_down_weight,
                grad_down_bias,
                grad_gain_two,
                grad_shift_two,
            ],
        )
    embed_back = grad_out.astype(jnp.bfloat16)
    grad_layout_weight = jnp.einsum(
        "nf,nd->fd", features_low, embed_back, preferred_element_type=jnp.float32
    )
    grad_layout_bias = jnp.sum(grad_out, axis=0)
    all_pieces = [grad_layout_weight, grad_layout_bias, table_grad]
    layer_list = layer_grads[0]
    all_pieces = all_pieces + layer_list
    if custom:
        param_step, new_first, new_second = reduce_and_step(
            pack_gradients(all_pieces), master, first_moment, second_moment
        )
    else:
        flat_grad = jnp.concatenate([piece.reshape(-1) for piece in all_pieces])
        grad_shard = lax.psum_scatter(flat_grad, ("dp", "seq"), scatter_dimension=0, tiled=True)
        square = lax.psum(jnp.sum(grad_shard * grad_shard), ("dp", "seq"))
        factor = jnp.minimum(1.0, lax.rsqrt(square / RAW + 1e-06))
        shard_size = master.shape[0]
        global_index = lax.axis_index(("dp", "seq")) * shard_size + jnp.arange(
            shard_size, dtype=jnp.int32
        )
        param_step, new_first, new_second = adam_update(
            master, first_moment, second_moment, grad_shard * factor, global_index
        )
    activations = hidden.reshape(blocks_here, rows, D).astype(jnp.bfloat16)
    input_grad = grad_out.reshape(blocks_here, rows, D)
    return (activations, input_grad, param_step, new_first, new_second)


def solution(mesh):
    in_specs = (
        P("dp", "seq", None),
        P("dp", "seq", None),
        P(None, "dp", "seq"),
        P("dp", None),
        P("dp", "seq"),
        P("dp", "seq", None),
        P(("dp", "seq")),
        P(("dp", "seq")),
        P(("dp", "seq")),
    )
    out_specs = (
        P("dp", "seq", None),
        P("dp", "seq", None),
        P(("dp", "seq")),
        P(("dp", "seq")),
        P(("dp", "seq")),
    )
    custom = dict(mesh.shape) == {"dp": 16, "seq": 2}
    return jax.shard_map(
        functools.partial(per_device, custom), mesh=mesh, in_specs=in_specs, out_specs=out_specs, check_vma=False
    )
```

```python
import functools

import jax
import jax.numpy as jnp
from jax import lax
from jax.experimental import pallas as pl
from jax.experimental.pallas import tpu as pltpu
from jax.sharding import PartitionSpec as P

D = 768
H = 12
HD = 64
FF = 3072
BUCKETS = 32
FREQ = 16
LF = 128
LAYERS = 1
BLOCK = 1024
STEP = 10
ENTRY = 99456
LAYER_PARAMS = 7087104
RAW = 7186560


beta_one = 0.8
beta_two = 0.98
adam_eps = 1e-06
learn_rate = 0.0006
layer_decay = 0.8
weight_decay = 0.1
norm_eps = 1e-05
masked_score = -1000000000.0


SHAPES = (
    (LF, D), (D,), (BUCKETS, H),
    (D, D), (D,), (D, D), (D, D), (D,), (D, D), (D,), (D,), (D,),
    (D, FF), (FF,), (FF, D), (D,), (D,), (D,),
)


def unpack(flat_params):
    pieces, offset = [], 0
    for shape in SHAPES:
        amount = shape[0] * (shape[1] if len(shape) > 1 else 1)
        pieces.append(flat_params[offset : offset + amount].reshape(shape))
        offset = offset + amount
    return pieces


def adam_update(master, first_moment, second_moment, gradient, global_index):
    exponent = jnp.where(
        global_index < ENTRY,
        LAYERS,
        jnp.maximum(LAYERS - 1 - (global_index - ENTRY) // LAYER_PARAMS, 0),
    )
    rate = jnp.where(
        global_index < RAW, learn_rate * jnp.power(layer_decay, exponent.astype(jnp.float32)), 0.0
    )
    moment_one = beta_one * first_moment + (1.0 - beta_one) * gradient
    moment_two = beta_two * second_moment + (1.0 - beta_two) * gradient * gradient
    fixed_one = moment_one / (1.0 - beta_one**STEP)
    fixed_two = moment_two / (1.0 - beta_two**STEP)
    param_step = -rate * (fixed_one / (jnp.sqrt(fixed_two) + adam_eps) + weight_decay * master)
    return (param_step, moment_one, moment_two)


def layout_features(page_boxes):
    rates_sin = jnp.power(10000.0, -jnp.arange(FREQ, dtype=jnp.float32) / FREQ)
    angles = page_boxes.astype(jnp.float32)[:, :, None] * rates_sin
    stacked = jnp.stack([jnp.sin(angles), jnp.cos(angles)], axis=1)
    return jnp.transpose(stacked, (2, 0, 1, 3)).reshape(page_boxes.shape[1], LF)


MESH = pl.DeviceIdType.MESH
SHARD = 224580
ROWS = 1760
TAIL, HEAD = 160, 176
WIN = 2176
SLOTS = 37
CHIP = 74
PARTS = ((0, 19), (19, 18))


def place():
    k = lax.axis_index("dp")
    return k, lax.axis_index("seq"), k // 4, (k // 2) % 2, k % 2


def shard_start(d):
    return d * 1754 + (d * 68) // 128, (d * 68) % 128


def early_vectors(k):
    return (k == 0) | (k == 4) | (k == 5)


def vector_row(k, other):
    at = other
    for chip, row in ((0, 768), (1, 5385), (4, 14607), (5, 19221), (10, 37671), (15, 56127)):
        at = jnp.where(k == chip, row, at)
    return at


def tile_start(w):
    at = w * 48
    for first, shift in ((16, 777 - 16 * 48), (112, 5391 - 112 * 48), (208, 9999 - 208 * 48), (304, 14613 - 304 * 48), (784, 37695 - 784 * 48)):
        at = jnp.where(w >= first, w * 48 + shift, at)
    wide = (w >= 400) & (w < 784)
    v = w - 400
    at = jnp.where(wide, 19239 + (v // 4) * 192 + (v % 4) * 6, at)
    return at, wide


def neighbours(k, c, z, y, x):
    t = k >= 0
    return [
        (t, (k, 1 - c)),
        (t, (z * 4 + y * 2 + 1 - x, c)),
        (t, (z * 4 + (1 - y) * 2 + x, c)),
        (z < 3, (jnp.minimum(k + 4, 15), c)),
        (z > 0, (jnp.maximum(k - 4, 0), c)),
        ((c == 1) & (k < 15), (jnp.minimum(k + 1, 15), 0)),
        ((c == 0) & (k > 0), (jnp.maximum(k - 1, 0), 1)),
    ]


def greet(k, c, z, y, x):
    bar = pltpu.get_barrier_semaphore()
    for cond, dev in neighbours(k, c, z, y, x):
        @pl.when(cond)
        def _():
            pl.semaphore_signal(bar, inc=1, device_id=dev, device_id_type=MESH)
    peers = 3
    for cond, _ in neighbours(k, c, z, y, x)[3:]:
        peers = peers + jnp.where(cond, 1, 0)
    pl.semaphore_wait(bar, peers)


def rcopy(src, dst, ssem, rsem, dev):
    return pltpu.make_async_remote_copy(src_ref=src, dst_ref=dst, send_sem=ssem, recv_sem=rsem, device_id=dev, device_id_type=MESH)


def gather_kernel(x_ref, g_ref, xv, tail, head, win, chunk, lsem, hsend, hrecv, own,
                  zs, zr, xas, xar, xbs, xbr, yas, yar, ybs, ybr, cs, cr):
    k, c, z, y, x = place()
    d = 2 * k + c
    greet(k, c, z, y, x)
    load = pltpu.make_async_copy(x_ref, xv, lsem)
    load.start()
    prev = (jnp.where(c == 1, k, jnp.maximum(k - 1, 0)), 1 - c)
    nxt = (jnp.where(c == 0, k, jnp.minimum(k + 1, 15)), 1 - c)
    to_next = rcopy(x_ref.at[pl.ds(ROWS - TAIL, TAIL)], tail, hsend.at[0], hrecv.at[0], nxt)
    to_prev = rcopy(x_ref.at[pl.ds(0, HEAD)], head, hsend.at[1], hrecv.at[1], prev)

    @pl.when(d < 31)
    def _():
        to_next.start()

    @pl.when(d > 0)
    def _():
        to_prev.start()

    win[...] = jnp.zeros_like(win)
    lanes = lax.broadcasted_iota(jnp.int32, (80, 128), 1)
    q, sh = shard_start(d)
    load.wait()

    @pl.loop(0, ROWS // 80)
    def _(i):
        r = pl.multiple_of(i * 80, 8)
        rolled = pltpu.roll(xv[pl.ds(r, 80), :], sh, 1)
        win[pl.ds(160 + r, 80), :] += jnp.where(lanes >= sh, rolled, 0.0)
        win[pl.ds(161 + r, 80), :] += jnp.where(lanes < sh, rolled, 0.0)

    @pl.when(d > 0)
    def _():
        to_next.wait_recv()
        qp, shp = shard_start(d - 1)
        lanes = lax.broadcasted_iota(jnp.int32, (TAIL, 128), 1)
        rolled = pltpu.roll(tail[...], shp, 1)
        at = 1760 - (q - qp)
        win[pl.ds(at, TAIL), :] += jnp.where(lanes >= shp, rolled, 0.0)
        win[pl.ds(at + 1, TAIL), :] += jnp.where(lanes < shp, rolled, 0.0)

    @pl.when(d < 31)
    def _():
        to_prev.wait_recv()
        qn, shn = shard_start(d + 1)
        lanes = lax.broadcasted_iota(jnp.int32, (HEAD, 128), 1)
        rolled = pltpu.roll(head[...], shn, 1)
        at = 160 + (qn - q)
        win[pl.ds(at, HEAD), :] += jnp.where(lanes >= shn, rolled, 0.0)
        win[pl.ds(at + 1, HEAD), :] += jnp.where(lanes < shn, rolled, 0.0)

    early = early_vectors(k)
    nw0 = jnp.where(early, 36, 37)
    vecs = early == (c == 0)
    first = jnp.where(c == 0, 73 * k, 73 * k + nw0)
    base = q - 160

    @pl.loop(0, SLOTS)
    def _(t):
        at, wide = tile_start(first + t)
        is_vec = vecs & (t == 36)
        at = jnp.where(is_vec, vector_row(k, q), at) - base
        wide = wide & jnp.logical_not(is_vec)

        @pl.when(wide)
        def _():
            parts = [win[pl.ds(at + j, 8, stride=24), :] for j in range(6)]
            chunk[t] = jnp.concatenate(parts, axis=1).astype(jnp.bfloat16)

        @pl.when(jnp.logical_not(wide))
        def _():
            parts = [win[pl.ds(at + j, 8, stride=6), :] for j in range(6)]
            chunk[t] = jnp.concatenate(parts, axis=1).astype(jnp.bfloat16)

    @pl.when(d < 31)
    def _():
        to_next.wait_send()

    @pl.when(d > 0)
    def _():
        to_prev.wait_send()

    xdev, ydev, cdev = (z * 4 + y * 2 + 1 - x, c), (z * 4 + (1 - y) * 2 + x, c), (k, 1 - c)
    zdev = {1: (jnp.minimum(k + 4, 15), c), -1: (jnp.maximum(k - 4, 0), c)}

    def gsl(chip, p):
        off, n = PARTS[p]
        return g_ref.at[chip, pl.ds(37 * c + off, n)]

    def src(chip, p, mine=False):
        off, n = PARTS[p]
        return chunk.at[pl.ds(off, n)] if mine else gsl(chip, p)

    def chip_of(zo, yo, xo):
        return zo * 4 + yo * 2 + xo

    def zcopy(zo, p, way, mine=False):
        chip = chip_of(zo, y, x)
        w = (way + 1) // 2
        return rcopy(src(chip, p, mine), gsl(chip, p), zs.at[w, zo, p], zr.at[zo, p], zdev[way])

    def xcopy(zo, yo, xo, p, mine=False):
        chip = chip_of(zo, yo, xo)
        s, r = (xas, xar) if p == 0 else (xbs, xbr)
        i = zo if p == 0 else zo * 2 + yo
        return rcopy(src(chip, p, mine), gsl(chip, p), s.at[i], r.at[i], xdev)

    def ycopy(zo, yo, xo, p, mine=False):
        chip = chip_of(zo, yo, xo)
        s, r = (ybs, ybr) if p == 1 else (yas, yar)
        i = zo if p == 1 else zo * 2 + xo
        return rcopy(src(chip, p, mine), gsl(chip, p), s.at[i], r.at[i], ydev)

    def ccopy(chip, p, mine=False):
        return rcopy(src(chip, p, mine), gsl(chip, p), cs.at[chip, p], cr.at[chip, p], cdev)

    for p in (0, 1):
        for way in (1, -1):
            @pl.when((z + way >= 0) & (z + way <= 3))
            def _():
                zcopy(z, p, way, True).start()
    xcopy(z, y, x, 0, True).start()
    ycopy(z, y, x, 1, True).start()
    ycopy(z, y, x, 0, True).start()
    xcopy(z, y, x, 1, True).start()
    mine = [pltpu.make_async_copy(chunk.at[pl.ds(*PARTS[p])], gsl(k, p), own.at[p]) for p in (0, 1)]
    for p in (0, 1):
        mine[p].start()
        ccopy(k, p, True).start()

    def column(zo, way):
        for p in (0, 1):
            zcopy(zo, p, way).wait_recv()

            @pl.when((zo + way * 0 + 0 >= 0) & (z + way >= 0) & (z + way <= 3))
            def _():
                zcopy(zo, p, way).start()
            if p == 0:
                xcopy(zo, y, x, 0).start()
                ycopy(zo, y, x, 0).start()
            else:
                ycopy(zo, y, x, 1).start()
                xcopy(zo, y, x, 1).start()
            ccopy(chip_of(zo, y, x), p).start()

    def beside(zo):
        xcopy(zo, y, 1 - x, 0).wait_recv()
        ycopy(zo, y, 1 - x, 0).start()
        ccopy(chip_of(zo, y, 1 - x), 0).start()
        ycopy(zo, 1 - y, x, 1).wait_recv()
        xcopy(zo, 1 - y, x, 1).start()
        ccopy(chip_of(zo, 1 - y, x), 1).start()

    def last(zo):
        ycopy(zo, 1 - y, x, 0).wait_recv()
        ccopy(chip_of(zo, 1 - y, x), 0).start()
        xcopy(zo, y, 1 - x, 1).wait_recv()
        ccopy(chip_of(zo, y, 1 - x), 1).start()
        ycopy(zo, 1 - y, 1 - x, 0).wait_recv()
        ccopy(chip_of(zo, 1 - y, 1 - x), 0).start()
        xcopy(zo, 1 - y, 1 - x, 1).wait_recv()
        ccopy(chip_of(zo, 1 - y, 1 - x), 1).start()

    def at_distance(s, f):
        for way in (1, -1):
            @pl.when((z - s * way >= 0) & (z - s * way <= 3))
            def _():
                f(z - s * way, way)

    at_distance(1, column)
    beside(z)
    at_distance(2, column)
    at_distance(1, lambda zo, way: beside(zo))
    at_distance(3, column)
    last(z)
    at_distance(2, lambda zo, way: beside(zo))
    at_distance(1, lambda zo, way: last(zo))
    at_distance(3, lambda zo, way: beside(zo))
    at_distance(2, lambda zo, way: last(zo))
    at_distance(3, lambda zo, way: last(zo))

    for p in (0, 1):
        mine[p].wait()
        for way in (1, -1):
            for zo in range(4):
                @pl.when(((z - zo) * way >= 0) & (z + way >= 0) & (z + way <= 3))
                def _():
                    zcopy(zo, p, way).wait_send()
    for zo in range(4):
        xcopy(zo, y, x, 0).wait_send()
        ycopy(zo, y, x, 1).wait_send()
        for o in range(2):
            ycopy(zo, y, o, 0).wait_send()
            xcopy(zo, o, x, 1).wait_send()
    for chip in range(16):
        for p in (0, 1):
            ccopy(chip, p).wait_send()
            off, n = PARTS[p]
            theirs = g_ref.at[chip, pl.ds(37 * (1 - c) + off, n)]
            rcopy(theirs, theirs, cs.at[chip, p], cr.at[chip, p], cdev).wait_recv()


def gather_weights(master):
    x = jnp.pad(master, (0, ROWS * 128 - SHARD)).reshape(ROWS, 128)
    sem = pltpu.SemaphoreType.DMA
    any_ = pl.BlockSpec(memory_space=pl.ANY)
    return pl.pallas_call(
        gather_kernel,
        out_shape=jax.ShapeDtypeStruct((16, CHIP, 8, 768), jnp.bfloat16),
        in_specs=[any_],
        out_specs=any_,
        scratch_shapes=[
            pltpu.VMEM((ROWS, 128), jnp.float32),
            pltpu.VMEM((TAIL, 128), jnp.float32),
            pltpu.VMEM((HEAD, 128), jnp.float32),
            pltpu.VMEM((WIN, 128), jnp.float32),
            pltpu.VMEM((SLOTS, 8, 768), jnp.bfloat16),
            sem, sem((2,)), sem((2,)), sem((2,)),
            sem((2, 4, 2)), sem((4, 2)),
            sem((4,)), sem((4,)), sem((8,)), sem((8,)),
            sem((8,)), sem((8,)), sem((4,)), sem((4,)),
            sem((16, 2)), sem((16, 2)),
        ],
        compiler_params=pltpu.CompilerParams(collective_id=0, has_side_effects=True, vmem_limit_bytes=40 << 20),
        name="gather_weights",
    )(x)


FRONT = 344
WIN2 = 2464
EDGE = 4
ENTRY_ROWS = 777


def reduce_kernel(g_ref, m_ref, one_ref, two_ref, step_ref, new1_ref, new2_ref,
                  acc, crecv, a1, b1, a2, b2, up, dn, total, ebuf, sq, sqr, win, mv, onev, twov,
                  lsem, asem, cs, cr, a1s, a1r, b1s, b1r, a2s, a2r, b2s, b2r, us, ur, ds_, dr, es, er, qs, qr):
    k, c, z, y, x = place()
    d = 2 * k + c
    xdev, ydev, cdev = (z * 4 + y * 2 + 1 - x, c), (z * 4 + (1 - y) * 2 + x, c), (k, 1 - c)
    zdev = {1: (jnp.minimum(k + 4, 15), c), -1: (jnp.maximum(k - 4, 0), c)}
    column_devs = [((z + s) % 4 * 4 + y * 2 + x, c) for s in (1, 2, 3)]
    prev = (jnp.where(c == 1, k, jnp.maximum(k - 1, 0)), 1 - c)
    nxt = (jnp.where(c == 0, k, jnp.minimum(k + 1, 15)), 1 - c)
    bar = pltpu.get_barrier_semaphore()
    far_next, far_prev = (c == 1) & (k < 15), (c == 0) & (k > 0)
    for dev in [xdev, ydev, cdev] + column_devs:
        pl.semaphore_signal(bar, inc=1, device_id=dev, device_id_type=MESH)

    @pl.when(far_next)
    def _():
        pl.semaphore_signal(bar, inc=1, device_id=nxt, device_id_type=MESH)

    @pl.when(far_prev)
    def _():
        pl.semaphore_signal(bar, inc=1, device_id=prev, device_id_type=MESH)

    pl.semaphore_wait(bar, 6 + jnp.where(far_next | far_prev, 1, 0))

    def chip_of(zo, yo, xo):
        return zo * 4 + yo * 2 + xo

    def load(chip):
        return pltpu.make_async_copy(g_ref.at[chip, pl.ds(37 * c, 37)], acc.at[chip], asem.at[chip])

    def ccopy(chip):
        return rcopy(g_ref.at[chip, pl.ds(37 * (1 - c), 37)], crecv.at[chip], cs.at[chip], cr.at[chip], cdev)

    def at_distance(s, f):
        if s == 0:
            f(z, 0)
            return
        for way in (1, -1):
            @pl.when((z + s * way >= 0) & (z + s * way <= 3))
            def _():
                f(z + s * way, way)

    def order(f):
        for s in (3, 2, 1, 0):
            at_distance(s, f)

    corners = ((1, 1), (1, 0), (0, 1), (0, 0))

    def flip(v, o):
        return 1 - v if o else v

    for oy, ox in corners:
        def go(zo, way):
            chip = chip_of(zo, flip(y, oy), flip(x, ox))
            load(chip).start()
            ccopy(chip).start()
        order(go)
    shards = [pltpu.make_async_copy(r, v, lsem.at[i]) for i, (r, v) in enumerate(((m_ref, mv), (one_ref, onev), (two_ref, twov)))]
    for s in shards:
        s.start()

    def psl(p):
        return pl.ds(*PARTS[p])

    def gain(dst, at, p, ref):
        off, n = PARTS[p]

        @pl.loop(0, n)
        def _(i):
            acc[at, off + i] = acc[at, off + i] + ref[i]

    def pair(chip):
        load(chip).wait()
        ccopy(chip).wait_recv()

        @pl.loop(0, 37)
        def _(i):
            acc[chip, i] = acc[chip, i] + crecv[chip, i]

    def a1copy(zo, xo):
        return rcopy(acc.at[chip_of(zo, 1 - y, xo), psl(0)], a1.at[zo * 2 + xo], a1s.at[zo * 2 + xo], a1r.at[zo * 2 + xo], ydev)

    def b1copy(zo, yo):
        return rcopy(acc.at[chip_of(zo, yo, 1 - x), psl(1)], b1.at[zo * 2 + yo], b1s.at[zo * 2 + yo], b1r.at[zo * 2 + yo], xdev)

    def a2copy(zo):
        return rcopy(acc.at[chip_of(zo, y, 1 - x), psl(0)], a2.at[zo], a2s.at[zo], a2r.at[zo], xdev)

    def b2copy(zo):
        return rcopy(acc.at[chip_of(zo, 1 - y, x), psl(1)], b2.at[zo], b2s.at[zo], b2r.at[zo], ydev)

    def zcopy(zo, way):
        buf, s, r = (up, us, ur) if way == 1 else (dn, ds_, dr)
        return rcopy(acc.at[chip_of(zo, y, x)], buf.at[zo], s.at[zo], r.at[zo], zdev[way])

    def first(oy, ox):
        def go(zo, way):
            yo, xo = flip(y, oy), flip(x, ox)
            pair(chip_of(zo, yo, xo))
            if oy:
                a1copy(zo, xo).start()
            if ox:
                b1copy(zo, yo).start()
        return go

    def second(zo, way):
        a1copy(zo, 1 - x).wait_recv()
        gain(acc, chip_of(zo, y, 1 - x), 0, a1.at[zo * 2 + 1 - x])
        a2copy(zo).start()
        b1copy(zo, 1 - y).wait_recv()
        gain(acc, chip_of(zo, 1 - y, x), 1, b1.at[zo * 2 + 1 - y])
        b2copy(zo).start()

    def third(zo, way):
        chip = chip_of(zo, y, x)
        a1copy(zo, x).wait_recv()
        gain(acc, chip, 0, a1.at[zo * 2 + x])
        b1copy(zo, y).wait_recv()
        gain(acc, chip, 1, b1.at[zo * 2 + y])
        a2copy(zo).wait_recv()
        gain(acc, chip, 0, a2.at[zo])
        b2copy(zo).wait_recv()
        gain(acc, chip, 1, b2.at[zo])
        if way:
            @pl.when((z - way >= 0) & (z - way <= 3))
            def _():
                zcopy(zo, way).wait_recv()
                buf = up if way == 1 else dn

                @pl.loop(0, 37)
                def _(i):
                    acc[chip, i] = acc[chip, i] + buf[zo, i]
            zcopy(zo, way).start()

    order(first(1, 1))
    order(first(1, 0))
    order(first(0, 1))
    order(second)
    order(first(0, 0))
    order(third)

    f32 = jnp.float32

    @pl.loop(0, 37)
    def _(i):
        total[i] = acc[k, i].astype(f32)

    for way in (1, -1):
        @pl.when((z - way >= 0) & (z - way <= 3))
        def _():
            zcopy(z, way).wait_recv()
            buf = up if way == 1 else dn

            @pl.loop(0, 37)
            def _(i):
                total[i] = total[i] + buf[z, i].astype(f32)

    early = early_vectors(k)
    nw0 = jnp.where(early, 36, 37)
    vecs = early == (c == 0)
    mine = jnp.where(vecs, 36, 37)
    to_next = rcopy(total.at[pl.ds(mine - EDGE, EDGE)], ebuf.at[0], es.at[0], er.at[0], nxt)
    to_prev = rcopy(total.at[pl.ds(0, EDGE)], ebuf.at[1], es.at[1], er.at[1], prev)

    @pl.when(d < 31)
    def _():
        to_next.start()

    @pl.when(d > 0)
    def _():
        to_prev.start()

    def square(i, run):
        t = total[i]
        t = t * t
        for j in range(6):
            run = run + t[:, 128 * j:128 * j + 128]
        return run

    sq[0] = lax.fori_loop(0, 37, square, jnp.zeros((8, 128), f32))
    for i, dev in enumerate((cdev, xdev, ydev)):
        step = rcopy(sq.at[i], sqr.at[i], qs.at[i], qr.at[i], dev)
        step.start()
        step.wait_recv()
        sq[i + 1] = sq[i] + sqr[i]
    hops = [rcopy(sq.at[3], sqr.at[3 + i], qs.at[3 + i], qr.at[3 + i], column_devs[i]) for i in range(3)]
    for h in hops:
        h.start()

    q, sh = shard_start(d)
    base = q - FRONT

    def flatten(ref, i, at, wide):
        @pl.when(wide)
        def _():
            t = ref[i]
            for j in range(6):
                win[pl.ds(at + j, 8, stride=24), :] = t[:, 128 * j:128 * j + 128]

        @pl.when(jnp.logical_not(wide))
        def _():
            t = ref[i]
            for j in range(6):
                win[pl.ds(at + j, 8, stride=6), :] = t[:, 128 * j:128 * j + 128]

    own_vectors = vecs & (vector_row(k, -1) >= 0)

    @pl.when(own_vectors)
    def _():
        flatten(total, 36, vector_row(k, q) - base, k < 0)

    w0 = jnp.where(c == 0, 73 * k, 73 * k + nw0)

    @pl.loop(0, mine)
    def _(t):
        at, wide = tile_start(w0 + t)
        flatten(total, t, at - base, wide)

    @pl.when(d > 0)
    def _():
        to_next.wait_recv()

        @pl.loop(0, EDGE)
        def _(t):
            at, wide = tile_start(w0 - EDGE + t)
            flatten(ebuf.at[0], t, at - base, wide)

    @pl.when(d < 31)
    def _():
        to_prev.wait_recv()

        @pl.loop(0, EDGE)
        def _(t):
            at, wide = tile_start(w0 + mine + t)
            flatten(ebuf.at[1], t, at - base, wide)

    for i, h in enumerate(hops):
        h.wait_recv()
    parts = [sqr[3], sqr[4], sqr[5]]
    rows = [sq[3]] + parts
    whole = (rows[0] + rows[2]) + (rows[1] + rows[3])
    square_sum = jnp.sum(jnp.sum(whole, axis=1, keepdims=True), axis=0, keepdims=True)
    factor = jnp.minimum(1.0, lax.rsqrt(square_sum / RAW + 1e-06))
    for s in shards:
        s.wait()
    lanes = lax.broadcasted_iota(jnp.int32, (80, 128), 1)
    rowi = lax.broadcasted_iota(jnp.int32, (80, 128), 0)
    back = (128 - sh) % 128

    @pl.loop(0, ROWS // 80)
    def _(i):
        r = pl.multiple_of(i * 80, 8)
        here = pltpu.roll(win[pl.ds(FRONT + r, 80), :], back, 1)
        there = pltpu.roll(win[pl.ds(FRONT + 1 + r, 80), :], back, 1)
        grad = jnp.where(lanes < 128 - sh, here, there) * factor
        entry = (d == 0) & (rowi + r < ENTRY_ROWS)
        rate = jnp.where(entry, learn_rate * layer_decay, learn_rate)
        one = beta_one * onev[pl.ds(r, 80), :] + (1.0 - beta_one) * grad
        two = beta_two * twov[pl.ds(r, 80), :] + (1.0 - beta_two) * grad * grad
        fixed_one = one / (1.0 - beta_one ** STEP)
        fixed_two = two / (1.0 - beta_two ** STEP)
        step_ref[pl.ds(r, 80), :] = -rate * (fixed_one / (jnp.sqrt(fixed_two) + adam_eps) + weight_decay * mv[pl.ds(r, 80), :])
        new1_ref[pl.ds(r, 80), :] = one
        new2_ref[pl.ds(r, 80), :] = two

    for i, dev in enumerate((cdev, xdev, ydev)):
        rcopy(sq.at[i], sqr.at[i], qs.at[i], qr.at[i], dev).wait_send()
    for h in hops:
        h.wait_send()

    @pl.when(d < 31)
    def _():
        to_next.wait_send()

    @pl.when(d > 0)
    def _():
        to_prev.wait_send()

    for chip in range(16):
        ccopy(chip).wait_send()
    for zo in range(4):
        a2copy(zo).wait_send()
        b2copy(zo).wait_send()
        for o in range(2):
            a1copy(zo, o).wait_send()
            b1copy(zo, o).wait_send()
        for way in (1, -1):
            @pl.when((zo - z) * way > 0)
            def _():
                zcopy(zo, way).wait_send()


def reduce_and_step(grads, master, first_moment, second_moment):
    def rows(v):
        return jnp.pad(v, (0, ROWS * 128 - SHARD)).reshape(ROWS, 128)

    sem = pltpu.SemaphoreType.DMA
    any_ = pl.BlockSpec(memory_space=pl.ANY)
    vm = pl.BlockSpec(memory_space=pltpu.VMEM)
    bf, f32 = jnp.bfloat16, jnp.float32
    tile = (8, 768)
    outs = pl.pallas_call(
        reduce_kernel,
        out_shape=[jax.ShapeDtypeStruct((ROWS, 128), f32)] * 3,
        in_specs=[any_] * 4,
        out_specs=[vm] * 3,
        scratch_shapes=[
            pltpu.VMEM((16, 37) + tile, bf), pltpu.VMEM((16, 37) + tile, bf),
            pltpu.VMEM((8, 19) + tile, bf), pltpu.VMEM((8, 18) + tile, bf),
            pltpu.VMEM((4, 19) + tile, bf), pltpu.VMEM((4, 18) + tile, bf),
            pltpu.VMEM((4, 37) + tile, bf), pltpu.VMEM((4, 37) + tile, bf),
            pltpu.VMEM((37,) + tile, f32), pltpu.VMEM((2, EDGE) + tile, f32),
            pltpu.VMEM((4, 8, 128), f32), pltpu.VMEM((6, 8, 128), f32),
            pltpu.VMEM((WIN2, 128), f32),
            pltpu.VMEM((ROWS, 128), f32), pltpu.VMEM((ROWS, 128), f32), pltpu.VMEM((ROWS, 128), f32),
            sem((3,)), sem((16,)), sem((16,)), sem((16,)),
            sem((8,)), sem((8,)), sem((8,)), sem((8,)), sem((4,)), sem((4,)), sem((4,)), sem((4,)),
            sem((4,)), sem((4,)), sem((4,)), sem((4,)), sem((2,)), sem((2,)), sem((6,)), sem((6,)),
        ],
        compiler_params=pltpu.CompilerParams(collective_id=1, has_side_effects=True, vmem_limit_bytes=56 << 20),
        name="reduce_and_step",
    )(grads, rows(master), rows(first_moment), rows(second_moment))
    return [o.reshape(-1)[:SHARD] for o in outs]


WEIGHTS = (
    (0, 0, 16),
    (3, 16, 96),
    (5, 112, 96),
    (6, 208, 96),
    (8, 304, 96),
    (12, 400, 384),
    (14, 784, 384),
)
VECTORS = (
    (1, 0, 0),
    (2, 0, 1),
    (4, 1, 0),
    (7, 4, 0),
    (9, 5, 0),
    (10, 5, 1),
    (11, 5, 2),
    (13, 10, 0),
    (15, 15, 0),
    (16, 15, 1),
    (17, 15, 2),
)


def slots_of(first, count):
    runs = []
    for w in range(first, first + count):
        chip, at = divmod(w, 73)
        slot = chip * CHIP + at + (1 if at >= vector_slot(chip) else 0)
        if runs and runs[-1][0] + runs[-1][2] == slot:
            runs[-1][2] += 1
        else:
            runs.append([slot, w - first, 1])
    return runs


def vector_slot(chip):
    return 36 if chip in (0, 4, 5) else 73


def vector_at(chip):
    return chip * CHIP + vector_slot(chip)


def pieces(tiles, held, first, count, sems, base, out=False):
    made = []
    for i, (slot, at, n) in enumerate(slots_of(first, count)):
        a, b = tiles.at[pl.ds(slot, n)], held.at[pl.ds(at, n)]
        a, b = (b, a) if out else (a, b)
        made.append(pltpu.make_async_copy(a, b, sems.at[base + i]))
    return made


def matrix(tile_rows):
    return tile_rows.reshape(-1, D)


def col_sum(v):
    return jnp.sum(v.reshape(-1, 8, v.shape[-1]), axis=0)


def norm_stats(v):
    mean = jnp.mean(v, axis=-1, keepdims=True)
    center = v - mean
    spread = jnp.mean(center * center, axis=-1, keepdims=True)
    inv = lax.rsqrt(spread + norm_eps)
    return center * inv, inv


def norm_back(grad, gain, hat, inv):
    g = grad * gain
    return inv * (g - jnp.mean(g, axis=-1, keepdims=True) - hat * jnp.mean(g * hat, axis=-1, keepdims=True))


ROOT_HALF = 0.7071067811865476
ROOT_TAU = 0.3989422804014327


def middle_kernel(tiles, ctx, hidden, cot, act_out, gfi_out, gctx_out, grads,
                  wo, wup, wdn, vecs, vf, act, slope, low1, hat1, inv1, hat2, inv2, a, sums, dwo, dwup, dwdn, vgrads, lsem, ssem):
    f32, bf = jnp.float32, jnp.bfloat16
    rows = ctx.shape[0]
    R = 64
    steps = rows // R
    loads_o = pieces(tiles, wo, 304, 96, lsem, 0)
    loads_u = pieces(tiles, wup, 400, 384, lsem, 4)
    loads_d = pieces(tiles, wdn, 784, 384, lsem, 12)
    loads_v = [pltpu.make_async_copy(tiles.at[vector_at(c)], vecs.at[i], lsem.at[20 + i]) for i, c in enumerate((5, 10, 15))]
    for c in loads_v + loads_o + loads_u + loads_d:
        c.start()
    up4 = wup.reshape(96, 4, 8, D)
    dup4 = dwup.reshape(96, 4, 8, D)

    def vec(i, r):
        return vf[i, pl.ds(r, 1), :]

    def each(f):
        @pl.loop(0, steps)
        def _(i):
            f(pl.ds(pl.multiple_of(i * R, R), R))

    for c in loads_v + loads_o:
        c.wait()
    vf[...] = vecs[...].astype(f32)
    a[...] = jnp.dot(ctx[...], matrix(wo[...]), preferred_element_type=f32)

    def first(sl):
        hat, inv = norm_stats(hidden[sl, :] + a[sl, :] + vec(0, 0))
        hat1[sl, :] = hat
        inv1[sl, :] = inv
        out = hat * vec(0, 1) + vec(0, 2)
        a[sl, :] = out
        low1[sl, :] = out.astype(bf)

    each(first)
    for c in loads_u + loads_d:
        c.wait()

    def up(j, _):
        for half in range(2):
            sl = pl.ds(half * (rows // 2), rows // 2)
            u = jnp.dot(low1[sl, :], matrix(up4[:, j]), preferred_element_type=f32) + vec(1, j)
            share = 0.5 * (1.0 + lax.erf(u * ROOT_HALF))
            act[j, sl, :] = (u * share).astype(bf)
            slope[j, sl, :] = share + u * jnp.exp(-0.5 * u * u) * ROOT_TAU
        return 0

    lax.fori_loop(0, 4, up, 0)

    def down(j, _):
        a[...] += jnp.dot(act[j], matrix(wdn[pl.ds(96 * j, 96)]), preferred_element_type=f32)
        return 0

    lax.fori_loop(0, 4, down, 0)
    sums[...] = jnp.zeros_like(sums)

    def second(sl):
        hat, inv = norm_stats(a[sl, :] + vec(2, 0))
        act_out[sl, :] = (hat * vec(2, 1) + vec(2, 2)).astype(bf)
        g = cot[sl, :].astype(f32)
        sums[6] += col_sum(g * hat)
        sums[7] += col_sum(g)
        back = norm_back(g, vec(2, 1), hat, inv)
        sums[5] += col_sum(back)
        a[sl, :] = back
        hat2[sl, :] = back.astype(bf)

    each(second)
    down_back = hat2

    def back(j, _):
        for half in range(2):
            sl = pl.ds(half * (rows // 2), rows // 2)
            g = lax.dot_general(down_back[sl, :], matrix(wdn[pl.ds(96 * j, 96)]), NT, preferred_element_type=f32) * slope[j, sl, :]
            sums[8 + j] += col_sum(g)
            act_back[sl, :] = g.astype(bf)
        dwdn[pl.ds(96 * j, 96)] = lax.dot_general(act[j], down_back[...], TN, preferred_element_type=f32).astype(bf).reshape(96, 8, D)
        dup4[:, j] = lax.dot_general(low1[...], act_back[...], TN, preferred_element_type=f32).astype(bf).reshape(96, 8, D)
        a[...] += lax.dot_general(act_back[...], matrix(up4[:, j]), NT, preferred_element_type=f32)
        return 0

    act_back = inv2
    lax.fori_loop(0, 4, back, 0)
    stores = pieces(grads, dwup, 400, 384, ssem, 4, True) + pieces(grads, dwdn, 784, 384, ssem, 12, True)
    for c in stores:
        c.start()

    def third(sl):
        g = a[sl, :]
        sums[3] += col_sum(g * hat1[sl, :])
        sums[4] += col_sum(g)
        back = norm_back(g, vec(0, 1), hat1[sl, :], inv1[sl, :])
        sums[2] += col_sum(back)
        gfi_out[sl, :] = back
        hat2[sl, :] = back.astype(bf)

    each(third)
    gctx_out[...] = lax.dot_general(hat2[...], matrix(wo[...]), NT, preferred_element_type=f32).astype(bf)
    dwo[...] = lax.dot_general(ctx[...], hat2[...], TN, preferred_element_type=f32).astype(bf).reshape(96, 8, D)
    for i, held in enumerate(((2, 3, 4), (8, 9, 10, 11), (5, 6, 7))):
        lines = [jnp.sum(sums[s], axis=0, keepdims=True) for s in held]
        lines.append(jnp.zeros((8 - len(held), D), f32))
        vgrads[i] = jnp.concatenate(lines).astype(bf)
    last = pieces(grads, dwo, 304, 96, ssem, 0, True)
    last += [pltpu.make_async_copy(vgrads.at[i], grads.at[vector_at(c)], ssem.at[20 + i]) for i, c in enumerate((5, 10, 15))]
    for c in last:
        c.start()
    for c in stores + last:
        c.wait()


def middle(tiles, ctx, hidden, cot):
    rows = ctx.shape[0]
    f32, bf = jnp.float32, jnp.bfloat16
    vm, any_ = pl.BlockSpec(memory_space=pltpu.VMEM), pl.BlockSpec(memory_space=pl.ANY)
    S = jax.ShapeDtypeStruct
    return pl.pallas_call(
        middle_kernel,
        out_shape=[S((rows, D), bf), S((rows, D), f32), S((rows, D), bf), S((16 * CHIP, 8, D), bf)],
        in_specs=[any_, vm, vm, vm],
        out_specs=[vm, vm, vm, any_],
        scratch_shapes=[
            pltpu.VMEM((96, 8, D), bf), pltpu.VMEM((384, 8, D), bf), pltpu.VMEM((384, 8, D), bf), pltpu.VMEM((3, 8, D), bf), pltpu.VMEM((3, 8, D), f32),
            pltpu.VMEM((4, rows, D), bf), pltpu.VMEM((4, rows, D), f32), pltpu.VMEM((rows, D), bf),
            pltpu.VMEM((rows, D), f32), pltpu.VMEM((rows, 1), f32), pltpu.VMEM((rows, D), bf), pltpu.VMEM((rows, D), bf),
            pltpu.VMEM((rows, D), f32), pltpu.VMEM((12, 8, D), f32),
            pltpu.VMEM((96, 8, D), bf), pltpu.VMEM((384, 8, D), bf), pltpu.VMEM((384, 8, D), bf), pltpu.VMEM((3, 8, D), bf),
            pltpu.SemaphoreType.DMA((24,)), pltpu.SemaphoreType.DMA((24,)),
        ],
        compiler_params=pltpu.CompilerParams(vmem_limit_bytes=58 << 20),
        name="middle",
    )(tiles, ctx, hidden, cot)


NT = (((1,), (1,)), ((), ()))
TN = (((0,), (0,)), ((), ()))


def half(ref_value, hh):
    lanes = lax.broadcasted_iota(jnp.int32, ref_value.shape, 1)
    keep = lanes < 64 if hh == 0 else lanes >= 64
    return jnp.where(keep, ref_value, jnp.zeros_like(ref_value))


def page_of(at, lengths):
    end, page = 0, jnp.zeros(at.shape, jnp.int32)
    for i in range(4):
        end = end + lengths[0, i]
        page = page + jnp.where(at >= end, 1, 0)
    return page


def attend_kernel(lengths, q_ref, k_ref, v_ref, buckets, pads, lines, ctx_ref, p_ref, code_ref, s_scr, tab_ref):
    pair = pl.program_id(0)
    keys, rows = s_scr.shape
    f32, bf = jnp.float32, jnp.bfloat16

    @pl.when(pair == 0)
    def _():
        own = lax.axis_index("seq") * rows
        tag = page_of(lax.broadcasted_iota(jnp.int32, (1, keys), 1), lengths) + 1
        tag = jnp.where(jnp.concatenate([pads[0, 0:1], pads[1, 0:1]], axis=1) > 0, tag, 0)
        for i in range(rows // 128):
            at = own + 128 * i + lax.broadcasted_iota(jnp.int32, (128, 1), 0)
            page = page_of(at, lengths) + 1
            for j in range(keys // 128):
                key_at = 128 * j + lax.broadcasted_iota(jnp.int32, (1, 128), 1)
                allowed = (page == tag[:, 128 * j : 128 * j + 128]) | (key_at == at)
                code = jnp.where(allowed, buckets[128 * i : 128 * i + 128, 128 * j : 128 * j + 128], BUCKETS)
                code_ref[128 * j : 128 * j + 128, 128 * i : 128 * i + 128] = code.T
        head = lax.broadcasted_iota(jnp.int32, (16, 128), 0)
        bucket = lax.broadcasted_iota(jnp.int32, (16, 128), 1)
        place_of = bucket * H + head
        tab = jnp.full((16, 128), masked_score, f32)
        for i in range(BUCKETS * H // 128):
            row = jnp.broadcast_to(lines[1:2, 128 * i : 128 * i + 128].astype(f32), (16, 128))
            inside = jnp.clip(place_of - 128 * i, 0, 127)
            got = jnp.take_along_axis(row, inside, axis=1, mode="promise_in_bounds")
            tab = jnp.where((place_of // 128 == i) & (bucket < BUCKETS) & (head < H), got, tab)
        tab_ref[...] = tab
    STEP_ROWS = keys
    out = []
    vt = v_ref[...].T
    for hh in range(2):
        qm = half(q_ref[...], hh)
        line = jnp.broadcast_to(tab_ref[pl.ds(2 * pair + hh, 1), :], (STEP_ROWS, 128))

        def score(i, top):
            at = pl.multiple_of(i * STEP_ROWS, STEP_ROWS)
            s = lax.dot_general(k_ref[pl.ds(at, STEP_ROWS), :], qm, NT, preferred_element_type=f32)
            cols = []
            for j in range(rows // 128):
                code = code_ref[pl.ds(at, STEP_ROWS), 128 * j : 128 * j + 128]
                bias = jnp.take_along_axis(line, code, axis=1, mode="promise_in_bounds")
                cols.append(jnp.where(bias < 0.5 * masked_score, masked_score, s[:, 128 * j : 128 * j + 128] + bias))
            s = jnp.concatenate(cols, axis=1)
            s_scr[pl.ds(at, STEP_ROWS), :] = s
            return jnp.maximum(top, jnp.max(s.reshape(STEP_ROWS // 8, 8, rows), axis=0))

        top = lax.fori_loop(0, keys // STEP_ROWS, score, jnp.full((8, rows), -jnp.inf, f32))
        top = jnp.max(top, axis=0, keepdims=True)

        def expo(i, total):
            at = pl.multiple_of(i * STEP_ROWS, STEP_ROWS)
            e = jnp.exp(s_scr[pl.ds(at, STEP_ROWS), :] - top)
            s_scr[pl.ds(at, STEP_ROWS), :] = e
            return total + jnp.sum(e.reshape(STEP_ROWS // 8, 8, rows), axis=0)

        total = lax.fori_loop(0, keys // STEP_ROWS, expo, jnp.zeros((8, rows), f32))
        inverse = 1.0 / jnp.sum(total, axis=0, keepdims=True)

        def scale(i, _):
            at = pl.multiple_of(i * STEP_ROWS, STEP_ROWS)
            p_ref[hh, pl.ds(at, STEP_ROWS), :] = (s_scr[pl.ds(at, STEP_ROWS), :] * inverse).astype(bf)
            return 0

        lax.fori_loop(0, keys // STEP_ROWS, scale, 0)
        out.append(jnp.dot(vt, p_ref[hh], preferred_element_type=f32))
    sub = lax.broadcasted_iota(jnp.int32, out[0].shape, 0)
    ctx_ref[...] = jnp.where(sub < 64, out[0], out[1]).T.astype(bf)


def attend(query, key_all, value_all, buckets, page_lengths, pads, lines):
    rows, keys = query.shape[0], key_all.shape[0]
    bf = jnp.bfloat16
    const = lambda p: (0, 0)
    return pl.pallas_call(
        attend_kernel,
        grid=(H // 2,),
        out_shape=[
            jax.ShapeDtypeStruct((rows, D), bf),
            jax.ShapeDtypeStruct((H, keys, rows), bf),
            jax.ShapeDtypeStruct((keys, rows), jnp.int32),
        ],
        in_specs=[
            pl.BlockSpec(memory_space=pltpu.SMEM),
            pl.BlockSpec((rows, 128), lambda p: (0, p)),
            pl.BlockSpec((keys, 128), lambda p: (0, p)),
            pl.BlockSpec((keys, 128), lambda p: (0, p)),
            pl.BlockSpec((rows, keys), const),
            pl.BlockSpec((2, 8, rows), lambda p: (0, 0, 0)),
            pl.BlockSpec((8, D), const),
        ],
        out_specs=[pl.BlockSpec((rows, 128), lambda p: (0, p)), pl.BlockSpec((2, keys, rows), lambda p: (p, 0, 0)), pl.BlockSpec((keys, rows), const)],
        scratch_shapes=[pltpu.VMEM((keys, rows), jnp.float32), pltpu.VMEM((16, 128), jnp.float32)],
        compiler_params=pltpu.CompilerParams(vmem_limit_bytes=56 << 20),
        name="attend",
    )(page_lengths, query, key_all, value_all, buckets, pads, lines)


def attend_back_kernel(q_ref, k_ref, v_ref, do_ref, p_ref, code_ref, dq_ref, dk_ref, dv_ref, tab_ref, spread, held):
    pair = pl.program_id(0)
    keys, rows = code_ref.shape
    f32, bf = jnp.float32, jnp.bfloat16
    STEP_ROWS = keys
    kt = k_ref[...].T
    dq = []
    for hh in range(2):
        qm = half(q_ref[...], hh)
        dom = half(do_ref[...], hh)

        def inner(i, total):
            at = pl.multiple_of(i * STEP_ROWS, STEP_ROWS)
            g = lax.dot_general(v_ref[pl.ds(at, STEP_ROWS), :], dom, NT, preferred_element_type=f32)
            w = g * p_ref[hh, pl.ds(at, STEP_ROWS), :].astype(f32)
            return total + jnp.sum(w.reshape(STEP_ROWS // 8, 8, rows), axis=0)

        total = lax.fori_loop(0, keys // STEP_ROWS, inner, jnp.zeros((8, rows), f32))
        total = jnp.sum(total, axis=0, keepdims=True)

        def grads(i, acc):
            at = pl.multiple_of(i * STEP_ROWS, STEP_ROWS)
            sl = pl.ds(at, STEP_ROWS)
            g = lax.dot_general(v_ref[sl, :], dom, NT, preferred_element_type=f32)
            p = p_ref[hh, sl, :]
            ds = p.astype(f32) * (g - total)
            wide = ds.reshape(STEP_ROWS // 8, 8, rows)
            if hh == 0:
                held[...] = wide
            else:
                both = jnp.concatenate([held[...], wide], axis=1).astype(bf)
                spread[:, pl.ds(pl.multiple_of(pair * 16, 16), 16), :] = both
            ds = ds.astype(bf)
            dv = jnp.dot(p, dom, preferred_element_type=f32)
            dk = jnp.dot(ds, qm, preferred_element_type=f32)
            if hh == 0:
                dv_ref[sl, :] = dv
                dk_ref[sl, :] = dk
            else:
                dv_ref[sl, :] += dv
                dk_ref[sl, :] += dk
            return acc + lax.dot_general(k_ref[sl, :], ds, TN, preferred_element_type=f32)

        dq.append(lax.fori_loop(0, keys // STEP_ROWS, grads, jnp.zeros((128, rows), f32)))
    sub = lax.broadcasted_iota(jnp.int32, dq[0].shape, 0)
    dq_ref[...] = jnp.where(sub < 64, dq[0], dq[1]).T * 0.125

    @pl.when(pair == H // 2 - 1)
    def _():
        bucket = lax.broadcasted_iota(jnp.int32, (BUCKETS, rows), 0)

        def count(i, acc):
            code = code_ref[pl.ds(pl.multiple_of(i * 8, 8), 8), :]
            hot = jnp.concatenate(
                [jnp.where(jnp.broadcast_to(code[r : r + 1], bucket.shape) == bucket, 1.0, 0.0) for r in range(8)]
            ).astype(bf)
            return acc + lax.dot_general(spread[i], hot, NT, preferred_element_type=f32)

        acc = lax.fori_loop(0, keys // 8, count, jnp.zeros((8 * H, 8 * BUCKETS), f32), unroll=8)
        a = lax.broadcasted_iota(jnp.int32, acc.shape, 0) % 8
        b = lax.broadcasted_iota(jnp.int32, acc.shape, 1) // BUCKETS
        acc = jnp.where(a == b, acc, 0.0)
        heads = jnp.sum(acc.reshape(H, 8, 8 * BUCKETS), axis=1)
        lane = lax.broadcasted_iota(jnp.int32, (8 * BUCKETS, D), 1) // H
        wide = jnp.where(lane == lax.broadcasted_iota(jnp.int32, lane.shape, 0) % BUCKETS, 1.0, 0.0)
        out = jnp.dot(heads, wide, precision=lax.Precision.HIGHEST, preferred_element_type=f32)
        mine = lax.broadcasted_iota(jnp.int32, out.shape, 1) % H == lax.broadcasted_iota(jnp.int32, out.shape, 0)
        out = jnp.sum(jnp.where(mine, out, 0.0), axis=0, keepdims=True)
        tab_ref[...] = jnp.broadcast_to(out, tab_ref.shape)


def soft_back(query, key_all, value_all, grad_context, soft, code):
    rows, keys = query.shape[0], key_all.shape[0]
    f32 = jnp.float32
    row = pl.BlockSpec((rows, 128), lambda p: (0, p))
    key = pl.BlockSpec((keys, 128), lambda p: (0, p))
    dq, dk, dv, tab = pl.pallas_call(
        attend_back_kernel,
        grid=(H // 2,),
        out_shape=[
            jax.ShapeDtypeStruct((rows, D), f32),
            jax.ShapeDtypeStruct((keys, D), f32),
            jax.ShapeDtypeStruct((keys, D), f32),
            jax.ShapeDtypeStruct((8, D), f32),
        ],
        in_specs=[row, key, key, row, pl.BlockSpec((2, keys, rows), lambda p: (p, 0, 0)), pl.BlockSpec((keys, rows), lambda p: (0, 0))],
        out_specs=[row, key, key, pl.BlockSpec((8, D), lambda p: (0, 0))],
        scratch_shapes=[pltpu.VMEM((keys // 8, 8 * H, rows), jnp.bfloat16), pltpu.VMEM((keys // 8, 8, rows), f32)],
        compiler_params=pltpu.CompilerParams(vmem_limit_bytes=58 << 20),
        name="attend_back",
    )(query, key_all, value_all, grad_context, soft, code)
    return dq, dk, dv, tab


def meet_partner():
    dp, c = lax.axis_index("dp"), lax.axis_index("seq")
    partner = (dp, 1 - c)
    bar = pltpu.get_barrier_semaphore()
    pl.semaphore_signal(bar, inc=1, device_id=partner, device_id_type=MESH)
    pl.semaphore_wait(bar, 1)
    return c, partner


def enter_kernel(tiles, tokens, feats, pad, hidden, low, query, keys, values, pads, wl, wq, wk, wv, vecs, vf, lsem, sends, recvs):
    f32, bf = jnp.float32, jnp.bfloat16
    rows = tokens.shape[0]
    loads = [pltpu.make_async_copy(tiles.at[vector_at(ch)], vecs.at[i], lsem.at[i]) for i, ch in enumerate((0, 1, 4))]
    loads += pieces(tiles, wl, 0, 16, lsem, 4) + pieces(tiles, wk, 112, 96, lsem, 8)
    loads += pieces(tiles, wv, 208, 96, lsem, 12) + pieces(tiles, wq, 16, 96, lsem, 16)
    for c in loads:
        c.start()
    c, partner = meet_partner()
    own = pl.ds(c * rows, rows)

    def share(ref, i):
        return rcopy(ref.at[own], ref.at[own], sends.at[i], recvs.at[i], partner)

    pads[pl.ds(c, 1)] = pad[...].reshape(1, 8, rows)
    pair_pads = rcopy(pads.at[pl.ds(c, 1)], pads.at[pl.ds(c, 1)], sends.at[2], recvs.at[2], partner)
    pair_pads.start()
    for copy in loads:
        copy.wait()
    vf[...] = vecs[...].astype(f32)
    h = tokens[...].astype(f32) + jnp.dot(feats[...], matrix(wl[...]), preferred_element_type=f32) + vf[0, 0:1, :]
    hidden[...] = h
    low[...] = h.astype(bf)
    keys[own, :] = jnp.dot(low[...], matrix(wk[...]), preferred_element_type=f32).astype(bf)
    send_keys = share(keys, 0)
    send_keys.start()
    values[own, :] = (jnp.dot(low[...], matrix(wv[...]), preferred_element_type=f32) + vf[2, 0:1, :]).astype(bf)
    send_values = share(values, 1)
    send_values.start()
    query[...] = ((jnp.dot(low[...], matrix(wq[...]), preferred_element_type=f32) + vf[1, 0:1, :]) * 0.125).astype(bf)
    for copy in (pair_pads, send_keys, send_values):
        copy.wait()


def enter(tiles, tokens, feats, pad):
    rows = tokens.shape[0]
    f32, bf = jnp.float32, jnp.bfloat16
    vm, any_ = pl.BlockSpec(memory_space=pltpu.VMEM), pl.BlockSpec(memory_space=pl.ANY)
    S, sem = jax.ShapeDtypeStruct, pltpu.SemaphoreType.DMA
    w = pltpu.VMEM((96, 8, D), bf)
    return pl.pallas_call(
        enter_kernel,
        out_shape=[S((rows, D), f32), S((rows, D), bf), S((rows, D), bf), S((2 * rows, D), bf), S((2 * rows, D), bf), S((2, 8, rows), jnp.int32)],
        in_specs=[any_, vm, vm, vm],
        out_specs=[vm] * 6,
        scratch_shapes=[pltpu.VMEM((16, 8, D), bf), w, w, w, pltpu.VMEM((3, 8, D), bf), pltpu.VMEM((3, 8, D), f32), sem((20,)), sem((3,)), sem((3,))],
        compiler_params=pltpu.CompilerParams(collective_id=2, has_side_effects=True, vmem_limit_bytes=40 << 20),
        name="enter",
    )(tiles, tokens, feats, pad)


def leave_kernel(tiles, dq, dk, dv, gfi, low, feats, table, grads_in, input_grad, grads,
                 wq, wk, wv, out, come, back, dwl, dwq, dwk, dwv, vgrads, lsem, ssem, sends, recvs):
    f32, bf = jnp.float32, jnp.bfloat16
    rows = gfi.shape[0]
    loads = pieces(tiles, wk, 112, 96, lsem, 0) + pieces(tiles, wv, 208, 96, lsem, 4) + pieces(tiles, wq, 16, 96, lsem, 8)
    for c in loads:
        c.start()
    c, partner = meet_partner()
    own, other = pl.ds(c * rows, rows), pl.ds((1 - c) * rows, rows)
    swaps = []
    for i, ref in enumerate((dk, dv)):
        out[i] = ref[other, :].astype(bf)
        swaps.append(rcopy(out.at[i], come.at[i], sends.at[i], recvs.at[i], partner))
        swaps[i].start()
    back[0] = dq[...].astype(bf)
    query_bias = jnp.sum(col_sum(dq[...]), axis=0, keepdims=True)
    for copy in loads:
        copy.wait()

    def through(i, w, dw):
        dw[...] = lax.dot_general(low[...], back[i], TN, preferred_element_type=f32).astype(bf).reshape(96, 8, D)
        return lax.dot_general(back[i], matrix(w[...]), NT, preferred_element_type=f32)

    input_grad[...] = gfi[...] + through(0, wq, dwq)
    stores = pieces(grads, dwq, 16, 96, ssem, 0, True)
    swaps[0].wait_recv()
    back[1] = (dk[own, :] + come[0].astype(f32)).astype(bf)
    input_grad[...] += through(1, wk, dwk)
    stores += pieces(grads, dwk, 112, 96, ssem, 4, True)
    swaps[1].wait_recv()
    grad_value = dv[own, :] + come[1].astype(f32)
    value_bias = jnp.sum(col_sum(grad_value), axis=0, keepdims=True)
    back[2] = grad_value.astype(bf)
    total = input_grad[...] + through(2, wv, dwv)
    stores += pieces(grads, dwv, 208, 96, ssem, 8, True)
    input_grad[...] = total
    layout_bias = jnp.sum(col_sum(total), axis=0, keepdims=True)
    dwl[...] = lax.dot_general(feats[...], total.astype(bf), TN, preferred_element_type=f32).astype(bf).reshape(16, 8, D)
    stores += pieces(grads, dwl, 0, 16, ssem, 12, True)

    def block(lines):
        return jnp.concatenate(lines + [jnp.zeros((8 - len(lines), D), f32)]).astype(bf)

    vgrads[0] = block([layout_bias, table[0:1, :]])
    vgrads[1] = block([query_bias])
    vgrads[2] = block([value_bias])
    vgrads[3] = jnp.zeros((8, D), bf)
    held = {0: 0, 1: 1, 4: 2}
    for i, chip in enumerate(ch for ch in range(16) if ch not in (5, 10, 15)):
        stores.append(pltpu.make_async_copy(vgrads.at[held.get(chip, 3)], grads.at[vector_at(chip)], ssem.at[16 + i]))
    for copy in stores:
        copy.start()
    for copy in stores:
        copy.wait()
    for swap in swaps:
        swap.wait_send()


def leave(tiles, dq, dk, dv, gfi, low, feats, table, grads):
    rows = gfi.shape[0]
    f32, bf = jnp.float32, jnp.bfloat16
    vm, any_ = pl.BlockSpec(memory_space=pltpu.VMEM), pl.BlockSpec(memory_space=pl.ANY)
    S, sem = jax.ShapeDtypeStruct, pltpu.SemaphoreType.DMA
    w = pltpu.VMEM((96, 8, D), bf)
    return pl.pallas_call(
        leave_kernel,
        out_shape=[S((rows, D), f32), S(grads.shape, bf)],
        in_specs=[any_] + [vm] * 7 + [any_],
        out_specs=[vm, any_],
        scratch_shapes=[w, w, w, pltpu.VMEM((2, rows, D), bf), pltpu.VMEM((2, rows, D), bf), pltpu.VMEM((3, rows, D), bf),
                        pltpu.VMEM((16, 8, D), bf), w, w, w, pltpu.VMEM((4, 8, D), bf), sem((12,)), sem((32,)), sem((2,)), sem((2,))],
        input_output_aliases={8: 1},
        compiler_params=pltpu.CompilerParams(collective_id=3, has_side_effects=True, vmem_limit_bytes=56 << 20),
        name="leave",
    )(tiles, dq, dk, dv, gfi, low, feats, table, grads)


def from_tiles(tiles):
    got = {}
    for name, first, count in WEIGHTS:
        block = jnp.concatenate([tiles[s : s + n] for s, _, n in slots_of(first, count)])
        if name == 12:
            block = block.reshape(96, 4, 8, D).transpose(0, 2, 1, 3)
        got[name] = block.reshape(-1, FF if name == 12 else D)
    for name, chip, row in VECTORS:
        block = tiles[vector_at(chip)]
        if name == 13:
            got[name] = block[row : row + 4].reshape(FF)
        elif name == 2:
            got[name] = block[row, : BUCKETS * H].reshape(BUCKETS, H)
        else:
            got[name] = block[row]
    return [got[i] for i in range(18)]


def to_tiles(whole):
    by_name = [p.astype(jnp.bfloat16) for p in whole]
    weights = []
    for name, first, count in WEIGHTS:
        got = by_name[name]
        if name == 12:
            got = got.reshape(96, 8, 4, D).transpose(0, 2, 1, 3)
        weights.append(got.reshape(count, 8, D))
    cuts = []
    for chip in range(16):
        held = [(r, by_name[n]) for n, c, r in VECTORS if c == chip]
        rows = [jnp.pad(v.reshape(-1), (0, -v.size % D)).reshape(-1, D) for _, v in held]
        block = jnp.concatenate(rows + [jnp.zeros((8 - sum(r.shape[0] for r in rows), D), jnp.bfloat16)])
        cuts.append((73 * chip + vector_slot(chip), block[None]))
    parts = []
    for (name, first, count), tiles in zip(WEIGHTS, weights):
        at = first
        for w, block in [c for c in cuts if first <= c[0] < first + count]:
            if w > at:
                parts.append(tiles[at - first : w - first])
            parts.append(block)
            at = w
        parts.append(tiles[at - first :])
    parts.extend(block for w, block in cuts if w == 1168)
    return jnp.concatenate(parts)


def per_device(
    custom, tokens, cotangent, page_boxes, page_lengths, padding, buckets, master, first_moment, second_moment
):
    rows = tokens.shape[1]
    if custom:
        tiles = gather_weights(master).reshape(16 * CHIP, 8, D)
    else:
        tiles = to_tiles(unpack(lax.all_gather(master.astype(jnp.bfloat16), ("dp", "seq"), axis=0, tiled=True)))
    feats = layout_features(page_boxes.reshape(4, rows)).astype(jnp.bfloat16)
    pad = jnp.broadcast_to(padding, (8, rows))
    hidden, low, query, keys, values, pads = enter(tiles, tokens[0], feats, pad)
    ctx, soft, code = attend(query, keys, values, buckets[0], page_lengths, pads, tiles[vector_at(0)])
    activations, grad_first_in, grad_context, grads = middle(tiles, ctx, hidden, cotangent[0])
    dq, dk, dv, table = soft_back(query, keys, values, grad_context, soft, code)
    input_grad, grads = leave(tiles, dq, dk, dv, grad_first_in, low, feats, table, grads)
    if custom:
        stepped = reduce_and_step(grads.reshape(16, CHIP, 8, D), master, first_moment, second_moment)
    else:
        flat = jnp.concatenate([p.astype(jnp.float32).reshape(-1) for p in from_tiles(grads)])
        grad = lax.psum_scatter(flat, ("dp", "seq"), scatter_dimension=0, tiled=True)
        square = lax.psum(jnp.sum(grad * grad), ("dp", "seq"))
        factor = jnp.minimum(1.0, lax.rsqrt(square / RAW + 1e-06))
        size = master.shape[0]
        index = lax.axis_index(("dp", "seq")) * size + jnp.arange(size, dtype=jnp.int32)
        stepped = adam_update(master, first_moment, second_moment, grad * factor, index)
    return (activations[None], input_grad[None]) + tuple(stepped)


def solution(mesh):
    in_specs = (
        P("dp", "seq", None),
        P("dp", "seq", None),
        P(None, "dp", "seq"),
        P("dp", None),
        P("dp", "seq"),
        P("dp", "seq", None),
        P(("dp", "seq")),
        P(("dp", "seq")),
        P(("dp", "seq")),
    )
    out_specs = (
        P("dp", "seq", None),
        P("dp", "seq", None),
        P(("dp", "seq")),
        P(("dp", "seq")),
        P(("dp", "seq")),
    )
    custom = dict(mesh.shape) == {"dp": 16, "seq": 2}
    return jax.shard_map(
        functools.partial(per_device, custom), mesh=mesh, in_specs=in_specs, out_specs=out_specs, check_vma=False
    )
```

```python
import functools

import jax
import jax.numpy as jnp
from jax import lax
from jax.experimental import pallas as pl
from jax.experimental.pallas import tpu as pltpu
from jax.sharding import PartitionSpec as P

D = 768
H = 12
HD = 64
FF = 3072
BUCKETS = 32
FREQ = 16
LF = 128
LAYERS = 1
BLOCK = 1024
STEP = 10
ENTRY = 99456
LAYER_PARAMS = 7087104
RAW = 7186560


beta_one = 0.8
beta_two = 0.98
adam_eps = 1e-06
learn_rate = 0.0006
layer_decay = 0.8
weight_decay = 0.1
norm_eps = 1e-05
masked_score = -1000000000.0


SHAPES = (
    (LF, D), (D,), (BUCKETS, H),
    (D, D), (D,), (D, D), (D, D), (D,), (D, D), (D,), (D,), (D,),
    (D, FF), (FF,), (FF, D), (D,), (D,), (D,),
)


def unpack(flat_params):
    pieces, offset = [], 0
    for shape in SHAPES:
        amount = shape[0] * (shape[1] if len(shape) > 1 else 1)
        pieces.append(flat_params[offset : offset + amount].reshape(shape))
        offset = offset + amount
    return pieces


def adam_update(master, first_moment, second_moment, gradient, global_index):
    exponent = jnp.where(
        global_index < ENTRY,
        LAYERS,
        jnp.maximum(LAYERS - 1 - (global_index - ENTRY) // LAYER_PARAMS, 0),
    )
    rate = jnp.where(
        global_index < RAW, learn_rate * jnp.power(layer_decay, exponent.astype(jnp.float32)), 0.0
    )
    moment_one = beta_one * first_moment + (1.0 - beta_one) * gradient
    moment_two = beta_two * second_moment + (1.0 - beta_two) * gradient * gradient
    fixed_one = moment_one / (1.0 - beta_one**STEP)
    fixed_two = moment_two / (1.0 - beta_two**STEP)
    param_step = -rate * (fixed_one / (jnp.sqrt(fixed_two) + adam_eps) + weight_decay * master)
    return (param_step, moment_one, moment_two)


def layout_features(page_boxes):
    rates_sin = jnp.power(10000.0, -jnp.arange(FREQ, dtype=jnp.float32) / FREQ)
    angles = page_boxes.astype(jnp.float32)[:, :, None] * rates_sin
    stacked = jnp.stack([jnp.sin(angles), jnp.cos(angles)], axis=1)
    return jnp.transpose(stacked, (2, 0, 1, 3)).reshape(page_boxes.shape[1], LF)


MESH = pl.DeviceIdType.MESH
SHARD = 224580
ROWS = 1760
TAIL, HEAD = 160, 176
WIN = 2176
SLOTS = 37
CHIP = 74
PARTS = ((0, 19), (19, 18))


def place():
    k = lax.axis_index("dp")
    return k, lax.axis_index("seq"), k // 4, (k // 2) % 2, k % 2


def shard_start(d):
    return d * 1754 + (d * 68) // 128, (d * 68) % 128


def early_vectors(k):
    return (k == 0) | (k == 4) | (k == 5)


def vector_row(k, other):
    at = other
    for chip, row in ((0, 768), (1, 5385), (4, 14607), (5, 19221), (10, 37671), (15, 56127)):
        at = jnp.where(k == chip, row, at)
    return at


def tile_start(w):
    at = w * 48
    for first, shift in ((16, 777 - 16 * 48), (112, 5391 - 112 * 48), (208, 9999 - 208 * 48), (304, 14613 - 304 * 48), (784, 37695 - 784 * 48)):
        at = jnp.where(w >= first, w * 48 + shift, at)
    wide = (w >= 400) & (w < 784)
    v = w - 400
    at = jnp.where(wide, 19239 + (v // 4) * 192 + (v % 4) * 6, at)
    return at, wide


def neighbours(k, c, z, y, x):
    t = k >= 0
    return [
        (t, (k, 1 - c)),
        (t, (z * 4 + y * 2 + 1 - x, c)),
        (t, (z * 4 + (1 - y) * 2 + x, c)),
        (z < 3, (jnp.minimum(k + 4, 15), c)),
        (z > 0, (jnp.maximum(k - 4, 0), c)),
        ((c == 1) & (k < 15), (jnp.minimum(k + 1, 15), 0)),
        ((c == 0) & (k > 0), (jnp.maximum(k - 1, 0), 1)),
    ]


def greet(k, c, z, y, x):
    bar = pltpu.get_barrier_semaphore()
    for cond, dev in neighbours(k, c, z, y, x):
        @pl.when(cond)
        def _():
            pl.semaphore_signal(bar, inc=1, device_id=dev, device_id_type=MESH)
    peers = 3
    for cond, _ in neighbours(k, c, z, y, x)[3:]:
        peers = peers + jnp.where(cond, 1, 0)
    pl.semaphore_wait(bar, peers)


def rcopy(src, dst, ssem, rsem, dev):
    return pltpu.make_async_remote_copy(src_ref=src, dst_ref=dst, send_sem=ssem, recv_sem=rsem, device_id=dev, device_id_type=MESH)


FRONT = 344
WIN2 = 2464
EDGE = 4
ENTRY_ROWS = 777


WEIGHTS = (
    (0, 0, 16),
    (3, 16, 96),
    (5, 112, 96),
    (6, 208, 96),
    (8, 304, 96),
    (12, 400, 384),
    (14, 784, 384),
)
VECTORS = (
    (1, 0, 0),
    (2, 0, 1),
    (4, 1, 0),
    (7, 4, 0),
    (9, 5, 0),
    (10, 5, 1),
    (11, 5, 2),
    (13, 10, 0),
    (15, 15, 0),
    (16, 15, 1),
    (17, 15, 2),
)


def slots_of(first, count):
    runs = []
    for w in range(first, first + count):
        chip, at = divmod(w, 73)
        slot = chip * CHIP + at + (1 if at >= vector_slot(chip) else 0)
        if runs and runs[-1][0] + runs[-1][2] == slot:
            runs[-1][2] += 1
        else:
            runs.append([slot, w - first, 1])
    return runs


def vector_slot(chip):
    return 36 if chip in (0, 4, 5) else 73


def vector_at(chip):
    return chip * CHIP + vector_slot(chip)


def pieces(tiles, held, first, count, sems, base, out=False):
    made = []
    for i, (slot, at, n) in enumerate(slots_of(first, count)):
        a, b = tiles.at[pl.ds(slot, n)], held.at[pl.ds(at, n)]
        a, b = (b, a) if out else (a, b)
        made.append(pltpu.make_async_copy(a, b, sems.at[base + i]))
    return made


def matrix(tile_rows):
    return tile_rows.reshape(-1, D)


def col_sum(v):
    return jnp.sum(v.reshape(-1, 8, v.shape[-1]), axis=0)


def norm_stats(v):
    mean = jnp.mean(v, axis=-1, keepdims=True)
    center = v - mean
    spread = jnp.mean(center * center, axis=-1, keepdims=True)
    inv = lax.rsqrt(spread + norm_eps)
    return center * inv, inv


def norm_back(grad, gain, hat, inv):
    g = grad * gain
    return inv * (g - jnp.mean(g, axis=-1, keepdims=True) - hat * jnp.mean(g * hat, axis=-1, keepdims=True))


ROOT_HALF = 0.7071067811865476
ROOT_TAU = 0.3989422804014327


def middle_kernel(tiles, ctx, hidden, cot, act_out, gfi_out, gctx_out, grads,
                  wo, wup, wdn, vecs, vf, act, slope, low1, hat1, inv1, hat2, inv2, a, sums, dwo, dwup, dwdn, vgrads, lsem, ssem):
    f32, bf = jnp.float32, jnp.bfloat16
    rows = ctx.shape[0]
    R = 64
    steps = rows // R
    loads_o = pieces(tiles, wo, 304, 96, lsem, 0)
    loads_u = pieces(tiles, wup, 400, 384, lsem, 4)
    loads_d = pieces(tiles, wdn, 784, 384, lsem, 12)
    loads_v = [pltpu.make_async_copy(tiles.at[vector_at(c)], vecs.at[i], lsem.at[20 + i]) for i, c in enumerate((5, 10, 15))]
    for c in loads_v + loads_o + loads_u + loads_d:
        c.start()
    up4 = wup.reshape(96, 4, 8, D)
    dup4 = dwup.reshape(96, 4, 8, D)

    def vec(i, r):
        return vf[i, pl.ds(r, 1), :]

    def each(f):
        @pl.loop(0, steps)
        def _(i):
            f(pl.ds(pl.multiple_of(i * R, R), R))

    for c in loads_v + loads_o:
        c.wait()
    vf[...] = vecs[...].astype(f32)
    a[...] = jnp.dot(ctx[...], matrix(wo[...]), preferred_element_type=f32)

    def first(sl):
        hat, inv = norm_stats(hidden[sl, :] + a[sl, :] + vec(0, 0))
        hat1[sl, :] = hat
        inv1[sl, :] = inv
        out = hat * vec(0, 1) + vec(0, 2)
        a[sl, :] = out
        low1[sl, :] = out.astype(bf)

    each(first)
    for c in loads_u + loads_d:
        c.wait()

    def up(j, _):
        for half in range(2):
            sl = pl.ds(half * (rows // 2), rows // 2)
            u = jnp.dot(low1[sl, :], matrix(up4[:, j]), preferred_element_type=f32) + vec(1, j)
            share = 0.5 * (1.0 + lax.erf(u * ROOT_HALF))
            act[j, sl, :] = (u * share).astype(bf)
            slope[j, sl, :] = share + u * jnp.exp(-0.5 * u * u) * ROOT_TAU
        return 0

    lax.fori_loop(0, 4, up, 0)

    def down(j, _):
        a[...] += jnp.dot(act[j], matrix(wdn[pl.ds(96 * j, 96)]), preferred_element_type=f32)
        return 0

    lax.fori_loop(0, 4, down, 0)
    sums[...] = jnp.zeros_like(sums)

    def second(sl):
        hat, inv = norm_stats(a[sl, :] + vec(2, 0))
        act_out[sl, :] = (hat * vec(2, 1) + vec(2, 2)).astype(bf)
        g = cot[sl, :].astype(f32)
        sums[6] += col_sum(g * hat)
        sums[7] += col_sum(g)
        back = norm_back(g, vec(2, 1), hat, inv)
        sums[5] += col_sum(back)
        a[sl, :] = back
        hat2[sl, :] = back.astype(bf)

    each(second)
    down_back = hat2

    def back(j, _):
        for half in range(2):
            sl = pl.ds(half * (rows // 2), rows // 2)
            g = lax.dot_general(down_back[sl, :], matrix(wdn[pl.ds(96 * j, 96)]), NT, preferred_element_type=f32) * slope[j, sl, :]
            sums[8 + j] += col_sum(g)
            act_back[sl, :] = g.astype(bf)
        dwdn[pl.ds(96 * j, 96)] = lax.dot_general(act[j], down_back[...], TN, preferred_element_type=f32).astype(bf).reshape(96, 8, D)
        dup4[:, j] = lax.dot_general(low1[...], act_back[...], TN, preferred_element_type=f32).astype(bf).reshape(96, 8, D)
        a[...] += lax.dot_general(act_back[...], matrix(up4[:, j]), NT, preferred_element_type=f32)
        return 0

    act_back = inv2
    lax.fori_loop(0, 4, back, 0)
    stores = pieces(grads, dwup, 400, 384, ssem, 4, True) + pieces(grads, dwdn, 784, 384, ssem, 12, True)
    for c in stores:
        c.start()

    def third(sl):
        g = a[sl, :]
        sums[3] += col_sum(g * hat1[sl, :])
        sums[4] += col_sum(g)
        back = norm_back(g, vec(0, 1), hat1[sl, :], inv1[sl, :])
        sums[2] += col_sum(back)
        gfi_out[sl, :] = back
        hat2[sl, :] = back.astype(bf)

    each(third)
    gctx_out[...] = lax.dot_general(hat2[...], matrix(wo[...]), NT, preferred_element_type=f32).astype(bf)
    dwo[...] = lax.dot_general(ctx[...], hat2[...], TN, preferred_element_type=f32).astype(bf).reshape(96, 8, D)
    for i, held in enumerate(((2, 3, 4), (8, 9, 10, 11), (5, 6, 7))):
        lines = [jnp.sum(sums[s], axis=0, keepdims=True) for s in held]
        lines.append(jnp.zeros((8 - len(held), D), f32))
        vgrads[i] = jnp.concatenate(lines).astype(bf)
    last = pieces(grads, dwo, 304, 96, ssem, 0, True)
    quiet = [ch for ch in range(6, 15) if ch != 10]
    vgrads[3] = jnp.zeros((8, D), bf)
    last += [pltpu.make_async_copy(vgrads.at[min(i, 3)], grads.at[vector_at(ch)], ssem.at[20 + i]) for i, ch in enumerate([5, 10, 15] + quiet)]
    for c in last:
        c.start()
    for c in stores + last:
        c.wait()


def middle(tiles, ctx, hidden, cot):
    rows = ctx.shape[0]
    f32, bf = jnp.float32, jnp.bfloat16
    vm, any_ = pl.BlockSpec(memory_space=pltpu.VMEM), pl.BlockSpec(memory_space=pl.ANY)
    S = jax.ShapeDtypeStruct
    return pl.pallas_call(
        middle_kernel,
        out_shape=[S((rows, D), bf), S((rows, D), f32), S((rows, D), bf), S((16 * CHIP, 8, D), bf)],
        in_specs=[any_, vm, vm, vm],
        out_specs=[vm, vm, vm, any_],
        scratch_shapes=[
            pltpu.VMEM((96, 8, D), bf), pltpu.VMEM((384, 8, D), bf), pltpu.VMEM((384, 8, D), bf), pltpu.VMEM((3, 8, D), bf), pltpu.VMEM((3, 8, D), f32),
            pltpu.VMEM((4, rows, D), bf), pltpu.VMEM((4, rows, D), f32), pltpu.VMEM((rows, D), bf),
            pltpu.VMEM((rows, D), f32), pltpu.VMEM((rows, 1), f32), pltpu.VMEM((rows, D), bf), pltpu.VMEM((rows, D), bf),
            pltpu.VMEM((rows, D), f32), pltpu.VMEM((12, 8, D), f32),
            pltpu.VMEM((96, 8, D), bf), pltpu.VMEM((384, 8, D), bf), pltpu.VMEM((384, 8, D), bf), pltpu.VMEM((4, 8, D), bf),
            pltpu.SemaphoreType.DMA((24,)), pltpu.SemaphoreType.DMA((32,)),
        ],
        compiler_params=pltpu.CompilerParams(vmem_limit_bytes=58 << 20),
        name="middle",
    )(tiles, ctx, hidden, cot)


NT = (((1,), (1,)), ((), ()))
TN = (((0,), (0,)), ((), ()))


def half(ref_value, hh):
    lanes = lax.broadcasted_iota(jnp.int32, ref_value.shape, 1)
    keep = lanes < 64 if hh == 0 else lanes >= 64
    return jnp.where(keep, ref_value, jnp.zeros_like(ref_value))


def page_of(at, lengths):
    end, page = 0, jnp.zeros(at.shape, jnp.int32)
    for i in range(4):
        end = end + lengths[0, i]
        page = page + jnp.where(at >= end, 1, 0)
    return page


def fill_codes(code_ref, buckets, pads, lengths):
    keys, rows = code_ref.shape
    own = lax.axis_index("seq") * rows
    tag = page_of(lax.broadcasted_iota(jnp.int32, (1, keys), 1), lengths) + 1
    tag = jnp.where(jnp.concatenate([pads[0, 0:1], pads[1, 0:1]], axis=1) > 0, tag, 0)
    for i in range(rows // 128):
        at = own + 128 * i + lax.broadcasted_iota(jnp.int32, (128, 1), 0)
        page = page_of(at, lengths) + 1
        for j in range(keys // 128):
            key_at = 128 * j + lax.broadcasted_iota(jnp.int32, (1, 128), 1)
            allowed = (page == tag[:, 128 * j : 128 * j + 128]) | (key_at == at)
            code = jnp.where(allowed, buckets[128 * i : 128 * i + 128, 128 * j : 128 * j + 128], BUCKETS)
            code_ref[128 * j : 128 * j + 128, 128 * i : 128 * i + 128] = code.T


def fill_table(tab_ref, lines):
    f32 = jnp.float32
    head = lax.broadcasted_iota(jnp.int32, (16, 128), 0)
    bucket = lax.broadcasted_iota(jnp.int32, (16, 128), 1)
    place_of = bucket * H + head
    tab = jnp.full((16, 128), masked_score, f32)
    for i in range(BUCKETS * H // 128):
        row = jnp.broadcast_to(lines[1:2, 128 * i : 128 * i + 128].astype(f32), (16, 128))
        inside = jnp.clip(place_of - 128 * i, 0, 127)
        got = jnp.take_along_axis(row, inside, axis=1, mode="promise_in_bounds")
        tab = jnp.where((place_of // 128 == i) & (bucket < BUCKETS) & (head < H), got, tab)
    tab_ref[...] = tab


def soft_pair(pair, q, k, code_ref, tab_ref, s_scr, p_ref):
    keys, rows = s_scr.shape
    f32, bf = jnp.float32, jnp.bfloat16
    for hh in range(2):
        qm = half(q, hh)
        line = jnp.broadcast_to(tab_ref[pl.ds(2 * pair + hh, 1), :], (keys, 128))
        s = lax.dot_general(k, qm, NT, preferred_element_type=f32)
        cols = []
        for j in range(rows // 128):
            code = code_ref[:, 128 * j : 128 * j + 128]
            bias = jnp.take_along_axis(line, code, axis=1, mode="promise_in_bounds")
            cols.append(jnp.where(bias < 0.5 * masked_score, masked_score, s[:, 128 * j : 128 * j + 128] + bias))
        s = jnp.concatenate(cols, axis=1)
        s_scr[...] = s
        top = jnp.max(jnp.max(s.reshape(keys // 8, 8, rows), axis=0), axis=0, keepdims=True)
        e = jnp.exp(s_scr[...] - top)
        s_scr[...] = e
        inverse = 1.0 / jnp.sum(jnp.sum(e.reshape(keys // 8, 8, rows), axis=0), axis=0, keepdims=True)
        p_ref[hh] = (s_scr[...] * inverse).astype(bf)


def context_pair(v, p_ref):
    vt = v.T
    out = [jnp.dot(vt, p_ref[hh], preferred_element_type=jnp.float32) for hh in range(2)]
    sub = lax.broadcasted_iota(jnp.int32, out[0].shape, 0)
    return jnp.where(sub < 64, out[0], out[1]).T.astype(jnp.bfloat16)


def attend_kernel(lengths, q_ref, k_ref, v_ref, buckets, pads, lines, ctx_ref, p_ref, code_ref, s_scr, tab_ref):
    pair = pl.program_id(0)

    @pl.when(pair == 0)
    def _():
        fill_codes(code_ref, buckets, pads, lengths)
        fill_table(tab_ref, lines)

    soft_pair(pair, q_ref[...], k_ref[...], code_ref, tab_ref, s_scr, p_ref)
    ctx_ref[...] = context_pair(v_ref[...], p_ref)


def attend(query, key_all, value_all, buckets, page_lengths, pads, lines):
    rows, keys = query.shape[0], key_all.shape[0]
    bf = jnp.bfloat16
    const = lambda p: (0, 0)
    return pl.pallas_call(
        attend_kernel,
        grid=(H // 2,),
        out_shape=[
            jax.ShapeDtypeStruct((rows, D), bf),
            jax.ShapeDtypeStruct((H, keys, rows), bf),
            jax.ShapeDtypeStruct((keys, rows), jnp.int32),
        ],
        in_specs=[
            pl.BlockSpec(memory_space=pltpu.SMEM),
            pl.BlockSpec((rows, 128), lambda p: (0, p)),
            pl.BlockSpec((keys, 128), lambda p: (0, p)),
            pl.BlockSpec((keys, 128), lambda p: (0, p)),
            pl.BlockSpec((rows, keys), const),
            pl.BlockSpec((2, 8, rows), lambda p: (0, 0, 0)),
            pl.BlockSpec((8, D), const),
        ],
        out_specs=[pl.BlockSpec((rows, 128), lambda p: (0, p)), pl.BlockSpec((2, keys, rows), lambda p: (p, 0, 0)), pl.BlockSpec((keys, rows), const)],
        scratch_shapes=[pltpu.VMEM((keys, rows), jnp.float32), pltpu.VMEM((16, 128), jnp.float32)],
        compiler_params=pltpu.CompilerParams(vmem_limit_bytes=56 << 20),
        name="attend",
    )(page_lengths, query, key_all, value_all, buckets, pads, lines)


def table_row(acc, shape):
    f32 = jnp.float32
    a = lax.broadcasted_iota(jnp.int32, acc.shape, 0) % 8
    b = lax.broadcasted_iota(jnp.int32, acc.shape, 1) // BUCKETS
    acc = jnp.where(a == b, acc, 0.0)
    heads = jnp.sum(acc.reshape(H, 8, 8 * BUCKETS), axis=1)
    lane = lax.broadcasted_iota(jnp.int32, (8 * BUCKETS, D), 1) // H
    wide = jnp.where(lane == lax.broadcasted_iota(jnp.int32, lane.shape, 0) % BUCKETS, 1.0, 0.0)
    out = jnp.dot(heads, wide, precision=lax.Precision.HIGHEST, preferred_element_type=f32)
    mine = lax.broadcasted_iota(jnp.int32, out.shape, 1) % H == lax.broadcasted_iota(jnp.int32, out.shape, 0)
    out = jnp.sum(jnp.where(mine, out, 0.0), axis=0, keepdims=True)
    return jnp.broadcast_to(out, shape)


def attend_back_kernel(q_ref, k_ref, v_ref, do_ref, p_ref, code_ref, dq_ref, dk_ref, dv_ref, tab_ref, spread, held):
    pair = pl.program_id(0)
    keys, rows = code_ref.shape
    f32, bf = jnp.float32, jnp.bfloat16
    STEP_ROWS = keys
    kt = k_ref[...].T
    dq = []
    for hh in range(2):
        qm = half(q_ref[...], hh)
        dom = half(do_ref[...], hh)

        def inner(i, total):
            at = pl.multiple_of(i * STEP_ROWS, STEP_ROWS)
            g = lax.dot_general(v_ref[pl.ds(at, STEP_ROWS), :], dom, NT, preferred_element_type=f32)
            w = g * p_ref[hh, pl.ds(at, STEP_ROWS), :].astype(f32)
            return total + jnp.sum(w.reshape(STEP_ROWS // 8, 8, rows), axis=0)

        total = lax.fori_loop(0, keys // STEP_ROWS, inner, jnp.zeros((8, rows), f32))
        total = jnp.sum(total, axis=0, keepdims=True)

        def grads(i, acc):
            at = pl.multiple_of(i * STEP_ROWS, STEP_ROWS)
            sl = pl.ds(at, STEP_ROWS)
            g = lax.dot_general(v_ref[sl, :], dom, NT, preferred_element_type=f32)
            p = p_ref[hh, sl, :]
            ds = p.astype(f32) * (g - total)
            wide = ds.reshape(STEP_ROWS // 8, 8, rows)
            if hh == 0:
                held[...] = wide
            else:
                both = jnp.concatenate([held[...], wide], axis=1).astype(bf)
                spread[:, pl.ds(pl.multiple_of(pair * 16, 16), 16), :] = both
            ds = ds.astype(bf)
            dv = jnp.dot(p, dom, preferred_element_type=f32)
            dk = jnp.dot(ds, qm, preferred_element_type=f32)
            if hh == 0:
                dv_ref[sl, :] = dv
                dk_ref[sl, :] = dk
            else:
                dv_ref[sl, :] += dv
                dk_ref[sl, :] += dk
            return acc + lax.dot_general(k_ref[sl, :], ds, TN, preferred_element_type=f32)

        dq.append(lax.fori_loop(0, keys // STEP_ROWS, grads, jnp.zeros((128, rows), f32)))
    sub = lax.broadcasted_iota(jnp.int32, dq[0].shape, 0)
    dq_ref[...] = jnp.where(sub < 64, dq[0], dq[1]).T * 0.125

    @pl.when(pair == H // 2 - 1)
    def _():
        bucket = lax.broadcasted_iota(jnp.int32, (BUCKETS, rows), 0)

        def count(i, acc):
            code = code_ref[pl.ds(pl.multiple_of(i * 8, 8), 8), :]
            hot = jnp.concatenate(
                [jnp.where(jnp.broadcast_to(code[r : r + 1], bucket.shape) == bucket, 1.0, 0.0) for r in range(8)]
            ).astype(bf)
            return acc + lax.dot_general(spread[i], hot, NT, preferred_element_type=f32)

        acc = lax.fori_loop(0, keys // 8, count, jnp.zeros((8 * H, 8 * BUCKETS), f32), unroll=8)
        tab_ref[...] = table_row(acc, tab_ref.shape)


def soft_back(query, key_all, value_all, grad_context, soft, code):
    rows, keys = query.shape[0], key_all.shape[0]
    f32 = jnp.float32
    row = pl.BlockSpec((rows, 128), lambda p: (0, p))
    key = pl.BlockSpec((keys, 128), lambda p: (0, p))
    dq, dk, dv, tab = pl.pallas_call(
        attend_back_kernel,
        grid=(H // 2,),
        out_shape=[
            jax.ShapeDtypeStruct((rows, D), f32),
            jax.ShapeDtypeStruct((keys, D), f32),
            jax.ShapeDtypeStruct((keys, D), f32),
            jax.ShapeDtypeStruct((8, D), f32),
        ],
        in_specs=[row, key, key, row, pl.BlockSpec((2, keys, rows), lambda p: (p, 0, 0)), pl.BlockSpec((keys, rows), lambda p: (0, 0))],
        out_specs=[row, key, key, pl.BlockSpec((8, D), lambda p: (0, 0))],
        scratch_shapes=[pltpu.VMEM((keys // 8, 8 * H, rows), jnp.bfloat16), pltpu.VMEM((keys // 8, 8, rows), f32)],
        compiler_params=pltpu.CompilerParams(vmem_limit_bytes=58 << 20),
        name="attend_back",
    )(query, key_all, value_all, grad_context, soft, code)
    return dq, dk, dv, tab


def meet_partner():
    dp, c = lax.axis_index("dp"), lax.axis_index("seq")
    partner = (dp, 1 - c)
    bar = pltpu.get_barrier_semaphore()
    pl.semaphore_signal(bar, inc=1, device_id=partner, device_id_type=MESH)
    pl.semaphore_wait(bar, 1)
    return c, partner


def enter_kernel(tiles, tokens, feats, pad, hidden, low, query, keys, values, pads, wl, wq, wk, wv, vecs, vf, lsem, sends, recvs):
    f32, bf = jnp.float32, jnp.bfloat16
    rows = tokens.shape[0]
    loads = [pltpu.make_async_copy(tiles.at[vector_at(ch)], vecs.at[i], lsem.at[i]) for i, ch in enumerate((0, 1, 4))]
    loads += pieces(tiles, wl, 0, 16, lsem, 4) + pieces(tiles, wk, 112, 96, lsem, 8)
    loads += pieces(tiles, wv, 208, 96, lsem, 12) + pieces(tiles, wq, 16, 96, lsem, 16)
    for c in loads:
        c.start()
    c, partner = meet_partner()
    own = pl.ds(c * rows, rows)

    def share(ref, i):
        return rcopy(ref.at[own], ref.at[own], sends.at[i], recvs.at[i], partner)

    pads[pl.ds(c, 1)] = pad[...].reshape(1, 8, rows)
    pair_pads = rcopy(pads.at[pl.ds(c, 1)], pads.at[pl.ds(c, 1)], sends.at[2], recvs.at[2], partner)
    pair_pads.start()
    for copy in loads:
        copy.wait()
    vf[...] = vecs[...].astype(f32)
    h = tokens[...].astype(f32) + jnp.dot(feats[...], matrix(wl[...]), preferred_element_type=f32) + vf[0, 0:1, :]
    hidden[...] = h
    low[...] = h.astype(bf)
    keys[own, :] = jnp.dot(low[...], matrix(wk[...]), preferred_element_type=f32).astype(bf)
    send_keys = share(keys, 0)
    send_keys.start()
    values[own, :] = (jnp.dot(low[...], matrix(wv[...]), preferred_element_type=f32) + vf[2, 0:1, :]).astype(bf)
    send_values = share(values, 1)
    send_values.start()
    query[...] = ((jnp.dot(low[...], matrix(wq[...]), preferred_element_type=f32) + vf[1, 0:1, :]) * 0.125).astype(bf)
    for copy in (pair_pads, send_keys, send_values):
        copy.wait()


def enter(tiles, tokens, feats, pad):
    rows = tokens.shape[0]
    f32, bf = jnp.float32, jnp.bfloat16
    vm, any_ = pl.BlockSpec(memory_space=pltpu.VMEM), pl.BlockSpec(memory_space=pl.ANY)
    S, sem = jax.ShapeDtypeStruct, pltpu.SemaphoreType.DMA
    w = pltpu.VMEM((96, 8, D), bf)
    return pl.pallas_call(
        enter_kernel,
        out_shape=[S((rows, D), f32), S((rows, D), bf), S((rows, D), bf), S((2 * rows, D), bf), S((2 * rows, D), bf), S((2, 8, rows), jnp.int32)],
        in_specs=[any_, vm, vm, vm],
        out_specs=[vm] * 6,
        scratch_shapes=[pltpu.VMEM((16, 8, D), bf), w, w, w, pltpu.VMEM((3, 8, D), bf), pltpu.VMEM((3, 8, D), f32), sem((20,)), sem((3,)), sem((3,))],
        compiler_params=pltpu.CompilerParams(collective_id=2, has_side_effects=True, vmem_limit_bytes=40 << 20),
        name="enter",
    )(tiles, tokens, feats, pad)


def leave_kernel(tiles, dq, dk, dv, gfi, low, feats, table, grads_in, input_grad, grads,
                 wq, wk, wv, out, come, back, dwl, dwq, dwk, dwv, vgrads, lsem, ssem, sends, recvs):
    f32, bf = jnp.float32, jnp.bfloat16
    rows = gfi.shape[0]
    loads = pieces(tiles, wk, 112, 96, lsem, 0) + pieces(tiles, wv, 208, 96, lsem, 4) + pieces(tiles, wq, 16, 96, lsem, 8)
    for c in loads:
        c.start()
    c, partner = meet_partner()
    own, other = pl.ds(c * rows, rows), pl.ds((1 - c) * rows, rows)
    swaps = []
    for i, ref in enumerate((dk, dv)):
        out[i] = ref[other, :].astype(bf)
        swaps.append(rcopy(out.at[i], come.at[i], sends.at[i], recvs.at[i], partner))
        swaps[i].start()
    back[0] = dq[...].astype(bf)
    query_bias = jnp.sum(col_sum(dq[...]), axis=0, keepdims=True)
    for copy in loads:
        copy.wait()

    def through(i, w, dw):
        dw[...] = lax.dot_general(low[...], back[i], TN, preferred_element_type=f32).astype(bf).reshape(96, 8, D)
        return lax.dot_general(back[i], matrix(w[...]), NT, preferred_element_type=f32)

    input_grad[...] = gfi[...] + through(0, wq, dwq)
    stores = pieces(grads, dwq, 16, 96, ssem, 0, True)
    swaps[0].wait_recv()
    back[1] = (dk[own, :] + come[0].astype(f32)).astype(bf)
    input_grad[...] += through(1, wk, dwk)
    stores += pieces(grads, dwk, 112, 96, ssem, 4, True)
    swaps[1].wait_recv()
    grad_value = dv[own, :] + come[1].astype(f32)
    value_bias = jnp.sum(col_sum(grad_value), axis=0, keepdims=True)
    back[2] = grad_value.astype(bf)
    total = input_grad[...] + through(2, wv, dwv)
    stores += pieces(grads, dwv, 208, 96, ssem, 8, True)
    input_grad[...] = total
    layout_bias = jnp.sum(col_sum(total), axis=0, keepdims=True)
    dwl[...] = lax.dot_general(feats[...], total.astype(bf), TN, preferred_element_type=f32).astype(bf).reshape(16, 8, D)
    stores += pieces(grads, dwl, 0, 16, ssem, 12, True)

    def block(lines):
        return jnp.concatenate(lines + [jnp.zeros((8 - len(lines), D), f32)]).astype(bf)

    vgrads[0] = block([layout_bias, table[0:1, :]])
    vgrads[1] = block([query_bias])
    vgrads[2] = block([value_bias])
    vgrads[3] = jnp.zeros((8, D), bf)
    held = {0: 0, 1: 1, 4: 2}
    for i, chip in enumerate(ch for ch in range(5)):
        stores.append(pltpu.make_async_copy(vgrads.at[held.get(chip, 3)], grads.at[vector_at(chip)], ssem.at[16 + i]))
    for copy in stores:
        copy.start()
    for copy in stores:
        copy.wait()
    for swap in swaps:
        swap.wait_send()


def leave(tiles, dq, dk, dv, gfi, low, feats, table, grads):
    rows = gfi.shape[0]
    f32, bf = jnp.float32, jnp.bfloat16
    vm, any_ = pl.BlockSpec(memory_space=pltpu.VMEM), pl.BlockSpec(memory_space=pl.ANY)
    S, sem = jax.ShapeDtypeStruct, pltpu.SemaphoreType.DMA
    w = pltpu.VMEM((96, 8, D), bf)
    return pl.pallas_call(
        leave_kernel,
        out_shape=[S((rows, D), f32), S(grads.shape, bf)],
        in_specs=[any_] + [vm] * 7 + [any_],
        out_specs=[vm, any_],
        scratch_shapes=[w, w, w, pltpu.VMEM((2, rows, D), bf), pltpu.VMEM((2, rows, D), bf), pltpu.VMEM((3, rows, D), bf),
                        pltpu.VMEM((16, 8, D), bf), w, w, w, pltpu.VMEM((4, 8, D), bf), sem((12,)), sem((32,)), sem((2,)), sem((2,))],
        input_output_aliases={8: 1},
        compiler_params=pltpu.CompilerParams(collective_id=3, has_side_effects=True, vmem_limit_bytes=56 << 20),
        name="leave",
    )(tiles, dq, dk, dv, gfi, low, feats, table, grads)


def forward_kernel(x_ref, tokens, feats, pad, buckets, lengths,
                   g_ref, hidden, low, query, keys, values, ctx, soft, code_out,
                   xv, tail, head, win, chunk, lsem, hsend, hrecv, own,
                   zs, zr, xas, xar, xbs, xbr, yas, yar, ybs, ybr, cs, cr,
                   pads, hidden_v, low_v, query_v, keys_v, values_v, ctx_v, code, buckets_v, tokens_v, feats_v, p_v, s_scr, tab,
                   wl, wq, wk, wv, vrows, vf, ksend, krecv, wsem, isem, osem, psem):
    f32, bf = jnp.float32, jnp.bfloat16
    rows = tokens.shape[0]
    k, c, z, y, x = place()
    d = 2 * k + c
    inputs = [pltpu.make_async_copy(r, v, isem.at[i]) for i, (r, v) in enumerate(((buckets, buckets_v), (tokens, tokens_v), (feats, feats_v)))]
    for copy in inputs:
        copy.start()
    pads[pl.ds(c, 1)] = pad[...].reshape(1, 8, rows)
    greet(k, c, z, y, x)
    load = pltpu.make_async_copy(x_ref, xv, lsem)
    load.start()
    prev = (jnp.where(c == 1, k, jnp.maximum(k - 1, 0)), 1 - c)
    nxt = (jnp.where(c == 0, k, jnp.minimum(k + 1, 15)), 1 - c)
    to_next = rcopy(x_ref.at[pl.ds(ROWS - TAIL, TAIL)], tail, hsend.at[0], hrecv.at[0], nxt)
    to_prev = rcopy(x_ref.at[pl.ds(0, HEAD)], head, hsend.at[1], hrecv.at[1], prev)

    @pl.when(d < 31)
    def _():
        to_next.start()

    @pl.when(d > 0)
    def _():
        to_prev.start()

    win[...] = jnp.zeros_like(win)
    lanes = lax.broadcasted_iota(jnp.int32, (80, 128), 1)
    q, sh = shard_start(d)
    load.wait()

    @pl.loop(0, ROWS // 80)
    def _(i):
        r = pl.multiple_of(i * 80, 8)
        rolled = pltpu.roll(xv[pl.ds(r, 80), :], sh, 1)
        win[pl.ds(160 + r, 80), :] += jnp.where(lanes >= sh, rolled, 0.0)
        win[pl.ds(161 + r, 80), :] += jnp.where(lanes < sh, rolled, 0.0)

    @pl.when(d > 0)
    def _():
        to_next.wait_recv()
        qp, shp = shard_start(d - 1)
        lanes = lax.broadcasted_iota(jnp.int32, (TAIL, 128), 1)
        rolled = pltpu.roll(tail[...], shp, 1)
        at = 1760 - (q - qp)
        win[pl.ds(at, TAIL), :] += jnp.where(lanes >= shp, rolled, 0.0)
        win[pl.ds(at + 1, TAIL), :] += jnp.where(lanes < shp, rolled, 0.0)

    @pl.when(d < 31)
    def _():
        to_prev.wait_recv()
        qn, shn = shard_start(d + 1)
        lanes = lax.broadcasted_iota(jnp.int32, (HEAD, 128), 1)
        rolled = pltpu.roll(head[...], shn, 1)
        at = 160 + (qn - q)
        win[pl.ds(at, HEAD), :] += jnp.where(lanes >= shn, rolled, 0.0)
        win[pl.ds(at + 1, HEAD), :] += jnp.where(lanes < shn, rolled, 0.0)

    early = early_vectors(k)
    nw0 = jnp.where(early, 36, 37)
    vecs = early == (c == 0)
    first = jnp.where(c == 0, 73 * k, 73 * k + nw0)
    base = q - 160

    @pl.loop(0, SLOTS)
    def _(t):
        at, wide = tile_start(first + t)
        is_vec = vecs & (t == 36)
        at = jnp.where(is_vec, vector_row(k, q), at) - base
        wide = wide & jnp.logical_not(is_vec)

        @pl.when(wide)
        def _():
            parts = [win[pl.ds(at + j, 8, stride=24), :] for j in range(6)]
            chunk[t] = jnp.concatenate(parts, axis=1).astype(jnp.bfloat16)

        @pl.when(jnp.logical_not(wide))
        def _():
            parts = [win[pl.ds(at + j, 8, stride=6), :] for j in range(6)]
            chunk[t] = jnp.concatenate(parts, axis=1).astype(jnp.bfloat16)

    @pl.when(d < 31)
    def _():
        to_next.wait_send()

    @pl.when(d > 0)
    def _():
        to_prev.wait_send()

    xdev, ydev, cdev = (z * 4 + y * 2 + 1 - x, c), (z * 4 + (1 - y) * 2 + x, c), (k, 1 - c)
    zdev = {1: (jnp.minimum(k + 4, 15), c), -1: (jnp.maximum(k - 4, 0), c)}

    def gsl(chip, p):
        off, n = PARTS[p]
        return g_ref.at[chip, pl.ds(37 * c + off, n)]

    def src(chip, p, mine=False):
        off, n = PARTS[p]
        return chunk.at[pl.ds(off, n)] if mine else gsl(chip, p)

    def chip_of(zo, yo, xo):
        return zo * 4 + yo * 2 + xo

    def zcopy(zo, p, way, mine=False):
        chip = chip_of(zo, y, x)
        w = (way + 1) // 2
        return rcopy(src(chip, p, mine), gsl(chip, p), zs.at[w, zo, p], zr.at[zo, p], zdev[way])

    def xcopy(zo, yo, xo, p, mine=False):
        chip = chip_of(zo, yo, xo)
        s, r = (xas, xar) if p == 0 else (xbs, xbr)
        i = zo if p == 0 else zo * 2 + yo
        return rcopy(src(chip, p, mine), gsl(chip, p), s.at[i], r.at[i], xdev)

    def ycopy(zo, yo, xo, p, mine=False):
        chip = chip_of(zo, yo, xo)
        s, r = (ybs, ybr) if p == 1 else (yas, yar)
        i = zo if p == 1 else zo * 2 + xo
        return rcopy(src(chip, p, mine), gsl(chip, p), s.at[i], r.at[i], ydev)

    def ccopy(chip, p, mine=False):
        return rcopy(src(chip, p, mine), gsl(chip, p), cs.at[chip, p], cr.at[chip, p], cdev)

    pair_pads = rcopy(pads.at[pl.ds(c, 1)], pads.at[pl.ds(c, 1)], ksend.at[2], krecv.at[2], cdev)
    pair_pads.start()
    mine = [pltpu.make_async_copy(chunk.at[pl.ds(*PARTS[p])], gsl(k, p), own.at[p]) for p in (0, 1)]

    def own_z(way):
        for p in (0, 1):
            zcopy(z, p, way, True).start()

    def pass_on(zz, zo):
        way = 1 if zo < zz else -1
        for p in (0, 1):
            zcopy(zo, p, way).wait_recv()
            if 0 <= zz + way <= 3:
                zcopy(zo, p, way).start()

    def spread(zz, zo):
        xcopy(zo, y, x, 0).start()
        ycopy(zo, y, x, 1).start()
        ycopy(zo, y, x, 0).start()
        xcopy(zo, y, x, 1).start()
        for p in (0, 1):
            ccopy(chip_of(zo, y, x), p).start()

    def column(zz, zo):
        way = 1 if zo < zz else -1
        for p in (0, 1):
            zcopy(zo, p, way).wait_recv()
            if 0 <= zz + way <= 3:
                zcopy(zo, p, way).start()
            if p == 0:
                xcopy(zo, y, x, 0).start()
                ycopy(zo, y, x, 0).start()
            else:
                ycopy(zo, y, x, 1).start()
                xcopy(zo, y, x, 1).start()
            ccopy(chip_of(zo, y, x), p).start()

    def beside(zz, zo):
        xcopy(zo, y, 1 - x, 0).wait_recv()
        ycopy(zo, y, 1 - x, 0).start()
        ccopy(chip_of(zo, y, 1 - x), 0).start()
        ycopy(zo, 1 - y, x, 1).wait_recv()
        xcopy(zo, 1 - y, x, 1).start()
        ccopy(chip_of(zo, 1 - y, x), 1).start()

    def last(zz, zo):
        ycopy(zo, 1 - y, x, 0).wait_recv()
        ccopy(chip_of(zo, 1 - y, x), 0).start()
        xcopy(zo, y, 1 - x, 1).wait_recv()
        ccopy(chip_of(zo, y, 1 - x), 1).start()
        ycopy(zo, 1 - y, 1 - x, 0).wait_recv()
        ccopy(chip_of(zo, 1 - y, 1 - x), 0).start()
        xcopy(zo, 1 - y, 1 - x, 1).wait_recv()
        ccopy(chip_of(zo, 1 - y, 1 - x), 1).start()

    def raise_own(zz, zo):
        own_z(1)

    before = {
        0: ((beside, 0), (column, 1), (last, 0)),
        1: ((beside, 1), (column, 0), (raise_own, 1), (pass_on, 2), (last, 1), (beside, 0), (pass_on, 3), (spread, 2), (last, 0)),
        2: ((beside, 2), (pass_on, 3), (column, 0), (last, 2), (beside, 0), (column, 1), (last, 0)),
        3: ((beside, 3), (last, 3), (column, 0), (beside, 0), (column, 1), (last, 0)),
    }
    after = {
        0: {0: ((beside, 1), (column, 2)), 1: ((last, 1), (beside, 2)), 2: ((column, 3), (last, 2)), 3: ((beside, 3),), 4: ((last, 3),)},
        1: {0: ((beside, 2), (spread, 3)), 1: ((last, 2),), 2: ((beside, 3),), 3: ((last, 3),)},
        2: {0: ((beside, 1), (spread, 3)), 1: ((last, 1),), 2: ((beside, 3),), 3: ((last, 3),)},
        3: {0: ((beside, 1), (column, 2)), 1: ((last, 1),), 2: ((beside, 2),), 3: ((last, 2),)},
    }

    for way, holds in ((1, (z == 0) | (z == 2)), (-1, z > 0)):
        @pl.when(holds)
        def _():
            own_z(way)
    xcopy(z, y, x, 0, True).start()
    ycopy(z, y, x, 1, True).start()
    ycopy(z, y, x, 0, True).start()
    xcopy(z, y, x, 1, True).start()
    for p in (0, 1):
        mine[p].start()
        ccopy(k, p, True).start()
    for copy in inputs:
        copy.wait()
    pair_pads.wait()
    fill_codes(code, buckets_v, pads, lengths)
    outs = [pltpu.make_async_copy(code, code_out, osem.at[0])]
    outs[0].start()
    for zz in range(4):
        @pl.when(z == zz)
        def _():
            for f, zo in before[zz]:
                f(zz, zo)
    for p in (0, 1):
        mine[p].wait()

    def from_partner(chip):
        for p in (0, 1):
            off, n = PARTS[p]
            theirs = g_ref.at[chip, pl.ds(37 * (1 - c) + off, n)]
            rcopy(theirs, theirs, cs.at[chip, p], cr.at[chip, p], cdev).wait_recv()

    for chip in range(3):
        from_partner(chip)

    tiles = g_ref.reshape(16 * CHIP, 8, D)
    loads = [pltpu.make_async_copy(tiles.at[vector_at(ch)], vrows.at[i], wsem.at[i]) for i, ch in enumerate((0, 1))]
    loads += pieces(tiles, wl, 0, 16, wsem, 4) + pieces(tiles, wk, 112, 96, wsem, 8) + pieces(tiles, wq, 16, 96, wsem, 16)
    for copy in loads:
        copy.start()
    for copy in loads:
        copy.wait()
    vf[0] = vrows[0].astype(f32)
    vf[1] = vrows[1].astype(f32)
    fill_table(tab, vrows.at[0])
    h = tokens_v[...].astype(f32) + jnp.dot(feats_v[...], matrix(wl[...]), preferred_element_type=f32) + vf[0, 0:1, :]
    hidden_v[...] = h
    low_v[...] = h.astype(bf)
    half_rows = pl.ds(c * rows, rows)

    def share(ref, i):
        return rcopy(ref.at[half_rows], ref.at[half_rows], ksend.at[i], krecv.at[i], cdev)

    keys_v[half_rows, :] = jnp.dot(low_v[...], matrix(wk[...]), preferred_element_type=f32).astype(bf)
    share(keys_v, 0).start()
    query_v[...] = ((jnp.dot(low_v[...], matrix(wq[...]), preferred_element_type=f32) + vf[1, 0:1, :]) * 0.125).astype(bf)
    share(keys_v, 0).wait()
    outs += [pltpu.make_async_copy(v, r, osem.at[1 + i]) for i, (v, r) in enumerate(((hidden_v, hidden), (low_v, low), (query_v, query), (keys_v, keys)))]
    for copy in outs[1:]:
        copy.start()

    def make_values():
        for chip in (3, 4):
            from_partner(chip)
        copies = [pltpu.make_async_copy(tiles.at[vector_at(4)], vrows.at[2], wsem.at[2])] + pieces(tiles, wv, 208, 96, wsem, 12)
        for copy in copies:
            copy.start()
        for copy in copies:
            copy.wait()
        vf[2] = vrows[2].astype(f32)
        values_v[half_rows, :] = (jnp.dot(low_v[...], matrix(wv[...]), preferred_element_type=f32) + vf[2, 0:1, :]).astype(bf)
        share(values_v, 1).start()

    def keep(pair):
        return pltpu.make_async_copy(p_v.at[pl.ds(2 * pair, 2)], soft.at[pl.ds(2 * pair, 2)], psem.at[pair])

    def pair_of_heads(pair, _):
        lanes = pl.ds(pl.multiple_of(pair * 128, 128), 128)
        soft_pair(pair, query_v[:, lanes], keys_v[:, lanes], code, tab, s_scr, p_v.at[pl.ds(2 * pair, 2)])
        keep(pair).start()
        for i in range(5):
            for zz in range(4):
                if i in after[zz]:
                    @pl.when((pair == i) & (z == zz))
                    def _():
                        for f, zo in after[zz][i]:
                            f(zz, zo)
        pl.when(pair == 2)(make_values)
        return 0

    lax.fori_loop(0, H // 2, pair_of_heads, 0)
    share(values_v, 1).wait()
    outs.append(pltpu.make_async_copy(values_v, values, osem.at[5]))
    outs[-1].start()

    def context(pair, _):
        lanes = pl.ds(pl.multiple_of(pair * 128, 128), 128)
        ctx_v[:, lanes] = context_pair(values_v[:, lanes], p_v.at[pl.ds(2 * pair, 2)])
        return 0

    lax.fori_loop(0, H // 2, context, 0)
    outs.append(pltpu.make_async_copy(ctx_v, ctx, osem.at[6]))
    outs[-1].start()

    for p in (0, 1):
        for way in (1, -1):
            for zo in range(4):
                @pl.when(((z - zo) * way >= 0) & (z + way >= 0) & (z + way <= 3))
                def _():
                    zcopy(zo, p, way).wait_send()
    for zo in range(4):
        xcopy(zo, y, x, 0).wait_send()
        ycopy(zo, y, x, 1).wait_send()
        for o in range(2):
            ycopy(zo, y, o, 0).wait_send()
            xcopy(zo, o, x, 1).wait_send()
    for chip in range(16):
        for p in (0, 1):
            ccopy(chip, p).wait_send()
    for chip in range(5, 16):
        from_partner(chip)
    for pair in range(H // 2):
        keep(pair).wait()
    for copy in outs:
        copy.wait()


def gather_and_attend(master, tokens, feats, pad, buckets, page_lengths):
    x = jnp.pad(master, (0, ROWS * 128 - SHARD)).reshape(ROWS, 128)
    sem = pltpu.SemaphoreType.DMA
    any_, vm = pl.BlockSpec(memory_space=pl.ANY), pl.BlockSpec(memory_space=pltpu.VMEM)
    rows, key_rows = buckets.shape
    f32, bf = jnp.float32, jnp.bfloat16
    S, V = jax.ShapeDtypeStruct, pltpu.VMEM
    w = V((96, 8, D), bf)
    return pl.pallas_call(
        forward_kernel,
        out_shape=[
            S((16, CHIP, 8, D), bf), S((rows, D), f32), S((rows, D), bf), S((rows, D), bf), S((key_rows, D), bf), S((key_rows, D), bf),
            S((rows, D), bf), S((H, key_rows, rows), bf), S((key_rows, rows), jnp.int32),
        ],
        in_specs=[any_, any_, any_, vm, any_, pl.BlockSpec(memory_space=pltpu.SMEM)],
        out_specs=[any_] * 9,
        scratch_shapes=[
            V((ROWS, 128), f32), V((TAIL, 128), f32), V((HEAD, 128), f32), V((WIN, 128), f32), V((SLOTS, 8, D), bf),
            sem, sem((2,)), sem((2,)), sem((2,)),
            sem((2, 4, 2)), sem((4, 2)),
            sem((4,)), sem((4,)), sem((8,)), sem((8,)),
            sem((8,)), sem((8,)), sem((4,)), sem((4,)),
            sem((16, 2)), sem((16, 2)),
            V((2, 8, rows), jnp.int32), V((rows, D), f32), V((rows, D), bf), V((rows, D), bf), V((key_rows, D), bf), V((key_rows, D), bf),
            V((rows, D), bf), V((key_rows, rows), jnp.int32), V((rows, key_rows), jnp.int32), V((rows, D), bf), V((rows, LF), bf),
            V((H, key_rows, rows), bf), V((key_rows, rows), f32), V((16, 128), f32),
            V((16, 8, D), bf), w, w, w, V((3, 8, D), bf), V((3, 8, D), f32),
            sem((3,)), sem((3,)), sem((20,)), sem((3,)), sem((7,)), sem((H // 2,)),
        ],
        compiler_params=pltpu.CompilerParams(collective_id=0, has_side_effects=True, vmem_limit_bytes=60 << 20),
        name="gather_and_attend",
    )(x, tokens, feats, pad, buckets, page_lengths)


def guarded(cond, f):
    if cond is True:
        f()
    elif cond is not False:
        pl.when(cond)(f)


class Reducer:
    def __init__(self, where, zs, want, spare, g_ref, acc, crecv, a1, b1, a2, b2, asem, cs, cr, a1s, a1r, b1s, b1r, a2s, a2r, b2s, b2r):
        self.k, self.c, self.z, self.y, self.x = where
        self.zs, self.want, self.spare = zs, want, spare
        self.g_ref, self.acc, self.crecv = g_ref, acc, crecv
        self.bufs = (a1, b1, a2, b2)
        self.asem, self.cs, self.cr = asem, cs, cr
        self.sems = ((a1s, a1r), (b1s, b1r), (a2s, a2r), (b2s, b2r))
        z, y, x, c = self.z, self.y, self.x, self.c
        self.xdev, self.ydev, self.cdev = (z * 4 + y * 2 + 1 - x, c), (z * 4 + (1 - y) * 2 + x, c), (self.k, 1 - c)

    def at(self, zo, oy, ox):
        return zo, (1 - self.y if oy else self.y), (1 - self.x if ox else self.x)

    def chip(self, zo, yo, xo):
        return zo * 4 + yo * 2 + xo

    def local(self, zo, yo, xo):
        return self.chip(zo, yo, xo)

    def load(self, item):
        i = self.local(*item)
        return pltpu.make_async_copy(self.g_ref.at[self.chip(*item), pl.ds(37 * self.c, 37)], self.acc.at[i], self.asem.at[i])

    def ccopy(self, item):
        i = self.local(*item)
        return rcopy(self.g_ref.at[self.chip(*item), pl.ds(37 * (1 - self.c), 37)], self.crecv.at[i + self.spare], self.cs.at[i], self.cr.at[i], self.cdev)

    def hop(self, which, item, slot, p, dev):
        s, r = self.sems[which]
        return rcopy(self.acc.at[self.local(*item), pl.ds(*PARTS[p])], self.bufs[which].at[slot], s.at[slot], r.at[slot], dev)

    def a1(self, zo, xo):
        return self.hop(0, (zo, 1 - self.y, xo), self.zs.index(zo) * 2 + xo, 0, self.ydev)

    def b1(self, zo, yo):
        return self.hop(1, (zo, yo, 1 - self.x), self.zs.index(zo) * 2 + yo, 1, self.xdev)

    def a2(self, zo):
        return self.hop(2, (zo, self.y, 1 - self.x), self.zs.index(zo), 0, self.xdev)

    def b2(self, zo):
        return self.hop(3, (zo, 1 - self.y, self.x), self.zs.index(zo), 1, self.ydev)

    def gain(self, item, p, which, slot):
        off, n = PARTS[p]
        i, acc, buf = self.local(*item), self.acc, self.bufs[which]
        acc[i, pl.ds(off, n)] = acc[i, pl.ds(off, n)] + buf[slot]

    def begin(self, zo, oy, ox):
        item = self.at(zo, oy, ox)

        def go():
            self.load(item).start()
            self.ccopy(item).start()
        guarded(self.want(*item), go)

    def first(self, zo, oy, ox):
        item = self.at(zo, oy, ox)

        def go():
            self.load(item).wait()
            self.ccopy(item).wait_recv()
            i = self.local(*item)
            self.acc[i] = self.acc[i] + self.crecv[i + self.spare]
            if oy:
                self.a1(zo, item[2]).start()
            if ox:
                self.b1(zo, item[1]).start()
        guarded(self.want(*item), go)

    def second(self, zo):
        ia, ib = self.at(zo, 0, 1), self.at(zo, 1, 0)
        n = self.zs.index(zo) * 2

        def go_a():
            self.a1(zo, 1 - self.x).wait_recv()
            self.gain(ia, 0, 0, n + 1 - self.x)
            self.a2(zo).start()

        def go_b():
            self.b1(zo, 1 - self.y).wait_recv()
            self.gain(ib, 1, 1, n + 1 - self.y)
            self.b2(zo).start()
        guarded(self.want(*ia), go_a)
        guarded(self.want(*ib), go_b)

    def third(self, zo):
        item = self.at(zo, 0, 0)
        n = self.zs.index(zo)

        def go():
            self.a1(zo, self.x).wait_recv()
            self.b1(zo, self.y).wait_recv()
            self.a2(zo).wait_recv()
            self.b2(zo).wait_recv()
            i = self.local(*item)
            for p, (h, u), at in ((0, (0, 2), self.x), (1, (1, 3), self.y)):
                off, m = PARTS[p]
                self.acc[i, pl.ds(off, m)] = (self.acc[i, pl.ds(off, m)] + self.bufs[h][n * 2 + at]) + self.bufs[u][n]
        guarded(self.want(*item), go)

    def finish(self):
        for zo in self.zs:
            for oy in (0, 1):
                for ox in (0, 1):
                    item = self.at(zo, oy, ox)

                    def sent(item=item, oy=oy, ox=ox, zo=zo):
                        self.ccopy(item).wait_send()
                        if oy:
                            self.a1(zo, item[2]).wait_send()
                        if ox:
                            self.b1(zo, item[1]).wait_send()
                        if ox and not oy:
                            self.a2(zo).wait_send()
                        if oy and not ox:
                            self.b2(zo).wait_send()
                    guarded(self.want(*item), sent)


def reducer_scratch():
    bf, sem = jnp.bfloat16, pltpu.SemaphoreType.DMA
    tile = (8, D)
    return [
        pltpu.VMEM((16, 37) + tile, bf), pltpu.VMEM((11, 37) + tile, bf),
        pltpu.VMEM((8, 19) + tile, bf), pltpu.VMEM((8, 18) + tile, bf), pltpu.VMEM((4, 19) + tile, bf), pltpu.VMEM((4, 18) + tile, bf),
        sem((16,)), sem((16,)), sem((16,)),
        sem((8,)), sem((8,)), sem((8,)), sem((8,)), sem((4,)), sem((4,)), sem((4,)), sem((4,)),
    ]


def early_item(zo, yo, xo):
    return zo >= 2 if zo != 1 else yo + xo > 0


def late_item(zo, yo, xo):
    return zo == 0 if zo != 1 else yo + xo == 0


ZCUTS = ((0, 10), (10, 9), (19, 9), (28, 9))


class Chain:
    def __init__(self, where, acc, up, dn, us, ur, ds_, dr):
        self.k, self.c, self.z, self.y, self.x = where
        self.acc = acc
        self.ways = {1: (up, us, ur, (jnp.minimum(self.k + 4, 15), self.c)), -1: (dn, ds_, dr, (jnp.maximum(self.k - 4, 0), self.c))}

    def chip(self, zo):
        return zo * 4 + self.y * 2 + self.x

    def copy(self, zo, way, p):
        buf, s, r, dev = self.ways[way]
        part = pl.ds(*ZCUTS[p])
        return rcopy(self.acc.at[self.chip(zo), part], buf.at[zo, part], s.at[zo, p], r.at[zo, p], dev)

    def move(self, zs, zo, way, take=True, give=True, also=None):
        cond = self.z == zs if also is None else (self.z == zs) & also

        @pl.when(cond)
        def _():
            i = self.chip(zo)
            for p in range(4):
                if take:
                    self.copy(zo, way, p).wait_recv()
                    part = pl.ds(*ZCUTS[p])
                    self.acc[i, part] = self.acc[i, part] + self.ways[way][0][zo, part]
                if give:
                    self.copy(zo, way, p).start()

    def sent(self, zs, zo, way):
        @pl.when(self.z == zs)
        def _():
            for p in range(4):
                self.copy(zo, way, p).wait_send()


def chain_scratch():
    bf, sem = jnp.bfloat16, pltpu.SemaphoreType.DMA
    return [pltpu.VMEM((4, 37, 8, D), bf)] * 2 + [sem((4, 4))] * 4


def backward_kernel(tiles, q_ref, k_ref, v_ref, do_ref, p_hbm, code_hbm, gfi_in, low_in, feats_in, grads_in, m_ref, one_ref, two_ref,
                    grad_out, grads, step_ref, new1_ref, new2_ref, spread,
                    pbuf, qv, kv, vv, dov, psem, code_ref, csem, dsv, dssem, group, gsem, counts, dks, dvs, out, come, sends, recvs, back, bias,
                    wq, wk, wv, low, gfi, feats, dwl, dwq, dwk, dwv, vgrads, wsem, ssem, isem,
                    total, ebuf, sq, sqr, win, mv, onev, twov, lsem, es, er, qs, qr, *scratch):
    f32, bf = jnp.float32, jnp.bfloat16
    where = place()
    k, c, z, y, x = where
    d = 2 * k + c
    shared = grads.reshape(16, CHIP, 8, D)
    rs = Reducer(where, (0, 1, 2, 3), early_item, -5, shared, *scratch[:17])
    late = Reducer(where, (0, 1, 2, 3), late_item, 6, shared, *scratch[:17])
    acc = rs.acc
    zc = Chain(where, acc, *scratch[17:])
    xdev, ydev, cdev = rs.xdev, rs.ydev, rs.cdev
    column_devs = [((z + s) % 4 * 4 + y * 2 + x, c) for s in (1, 2, 3)]
    prev = (jnp.where(c == 1, k, jnp.maximum(k - 1, 0)), 1 - c)
    nxt = (jnp.where(c == 0, k, jnp.minimum(k + 1, 15)), 1 - c)
    bar = pltpu.get_barrier_semaphore()
    far_next, far_prev = (c == 1) & (k < 15), (c == 0) & (k > 0)
    for dev in [xdev, ydev, cdev] + column_devs:
        pl.semaphore_signal(bar, inc=1, device_id=dev, device_id_type=MESH)

    @pl.when(far_next)
    def _():
        pl.semaphore_signal(bar, inc=1, device_id=nxt, device_id_type=MESH)

    @pl.when(far_prev)
    def _():
        pl.semaphore_signal(bar, inc=1, device_id=prev, device_id_type=MESH)

    keys, rows = code_ref.shape

    def fetch_soft(pair, hh):
        return pltpu.make_async_copy(p_hbm.at[2 * pair + hh], pbuf.at[hh], psem.at[0, hh])

    def fetch(p):
        slot = p % 2
        lanes = pl.ds(pl.multiple_of(p * 128, 128), 128)
        return [pltpu.make_async_copy(r.at[:, lanes], v.at[slot], psem.at[1 + i, slot]) for i, (r, v) in enumerate(((q_ref, qv), (k_ref, kv), (v_ref, vv), (do_ref, dov)))]

    for copy in fetch(0) + [fetch_soft(0, 0), fetch_soft(0, 1)]:
        copy.start()
    pl.semaphore_wait(bar, 6 + jnp.where(far_next | far_prev, 1, 0))
    corners = ((1, 1), (1, 0), (0, 1), (0, 0))
    for zo in (3, 2):
        for oy, ox in corners:
            rs.begin(zo, oy, ox)
    code_copy = pltpu.make_async_copy(code_hbm, code_ref, csem.at[0])
    inputs = [pltpu.make_async_copy(r, v, isem.at[i]) for i, (r, v) in enumerate(((low_in, low), (gfi_in, gfi), (feats_in, feats)))]
    loads = pieces(tiles, wq, 16, 96, wsem, 8) + pieces(tiles, wv, 208, 96, wsem, 4) + pieces(tiles, wk, 112, 96, wsem, 0)
    shards = [pltpu.make_async_copy(r, v, lsem.at[i]) for i, (r, v) in enumerate(((m_ref, mv), (one_ref, onev), (two_ref, twov)))]
    for copy in [code_copy] + inputs + loads + shards:
        copy.start()
    own, other = pl.ds(c * rows, rows), pl.ds((1 - c) * rows, rows)

    def swap(pair):
        return rcopy(out.at[pair], come.at[pair], sends.at[pair], recvs.at[pair], cdev)

    def settle(pair):
        slot = pair % 2
        swap(pair).wait_recv()
        lanes = pl.ds(pl.multiple_of(pair * 128, 128), 128)
        dk = dks[slot, own, :] + come[pair, 0].astype(f32)
        dv = dvs[slot, own, :] + come[pair, 1].astype(f32)
        back[1, :, lanes] = dk.astype(bf)
        back[2, :, lanes] = dv.astype(bf)
        bias[1, :, lanes] = col_sum(dv)

    def lay(pair, hh):
        return pltpu.make_async_copy(dsv.at[hh], spread.at[:, 2 * pair + hh], dssem.at[hh])

    plan = {
        0: [(rs.first, 3, 1, 0), (rs.first, 3, 0, 1), (rs.first, 2, 1, 1)],
        1: [(rs.second, 3), (rs.first, 2, 1, 0), (rs.first, 2, 0, 1)],
        2: [(rs.first, 3, 0, 0), (rs.first, 2, 0, 0), (rs.begin, 1, 1, 1), (rs.begin, 1, 1, 0), (rs.begin, 1, 0, 1), (rs.begin, 1, 0, 0)],
        3: [(rs.second, 2), (rs.third, 3), (zc.move, 0, 3, 1, False)],
        4: [(rs.first, 1, 1, 1)],
        5: [(rs.first, 1, 1, 0), (rs.first, 1, 0, 1), (zc.move, 1, 3, 1)],
    }
    rs.first(3, 1, 1)

    def pair_of_heads(pair, _):
        slot = pair % 2

        @pl.when(pair < H // 2 - 1)
        def _():
            for copy in fetch(pair + 1):
                copy.start()

        for copy in fetch(pair):
            copy.wait()
        lanes = pl.ds(pl.multiple_of(pair * 128, 128), 128)
        dq = []
        for hh in range(2):
            fetch_soft(pair, hh).wait()
            qm = half(qv[slot], hh)
            dom = half(dov[slot], hh)
            g = lax.dot_general(vv[slot], dom, NT, preferred_element_type=f32)
            p = pbuf[hh]
            pf = p.astype(f32)
            inner = jnp.sum(jnp.sum((g * pf).reshape(keys // 8, 8, rows), axis=0), axis=0, keepdims=True)
            ds = (pf * (g - inner)).astype(bf)

            @pl.when(pair > 0)
            def _():
                lay(pair - 1, hh).wait()

            dsv[hh] = ds.reshape(keys // 8, 8, rows)
            lay(pair, hh).start()
            dv = jnp.dot(p, dom, preferred_element_type=f32)

            @pl.when(pair < H // 2 - 1)
            def _():
                fetch_soft(pair + 1, hh).start()

            dk = jnp.dot(ds, qm, preferred_element_type=f32)
            if hh == 0:
                dvs[slot] = dv
                dks[slot] = dk
            else:
                dvs[slot] += dv
                dks[slot] += dk
            dq.append(lax.dot_general(kv[slot], ds, TN, preferred_element_type=f32))
        out[pair, 0] = dks[slot, other, :].astype(bf)
        out[pair, 1] = dvs[slot, other, :].astype(bf)
        swap(pair).start()
        sub = lax.broadcasted_iota(jnp.int32, dq[0].shape, 0)
        dqf = jnp.where(sub < 64, dq[0], dq[1]).T * 0.125
        back[0, :, lanes] = dqf.astype(bf)
        bias[0, :, lanes] = col_sum(dqf)

        @pl.when(pair > 0)
        def _():
            settle(pair - 1)

        for i, steps in plan.items():
            @pl.when(pair == i)
            def _():
                for f, *a in steps:
                    f(*a)
        return 0

    lax.fori_loop(0, H // 2, pair_of_heads, 0)
    for hh in range(2):
        lay(H // 2 - 1, hh).wait()
    for copy in inputs + loads:
        copy.wait()

    def through(i, w, dw):
        dw[...] = lax.dot_general(low[...], back[i], TN, preferred_element_type=f32).astype(bf).reshape(96, 8, D)
        return lax.dot_general(back[i], matrix(w[...]), NT, preferred_element_type=f32)

    stores = []

    def keep(dw, first, count, base):
        made = pieces(grads, dw, first, count, ssem, base, True)
        for copy in made:
            copy.start()
        stores.extend(made)

    gfi[...] += through(0, wq, dwq)
    keep(dwq, 16, 96, 0)
    settle(H // 2 - 1)
    gfi[...] += through(2, wv, dwv)
    keep(dwv, 208, 96, 8)
    whole = gfi[...] + through(1, wk, dwk)
    keep(dwk, 112, 96, 4)
    gfi[...] = whole
    shown = pltpu.make_async_copy(gfi, grad_out, isem.at[6])
    shown.start()
    layout_bias = jnp.sum(col_sum(whole), axis=0, keepdims=True)
    dwl[...] = lax.dot_general(feats[...], whole.astype(bf), TN, preferred_element_type=f32).astype(bf).reshape(16, 8, D)
    keep(dwl, 0, 16, 12)

    def block(lines):
        return jnp.concatenate(lines + [jnp.zeros((8 - len(lines), D), f32)]).astype(bf)

    vgrads[0] = block([layout_bias])
    vgrads[1] = block([jnp.sum(bias[0], axis=0, keepdims=True)])
    vgrads[2] = block([jnp.sum(bias[1], axis=0, keepdims=True)])
    vgrads[3] = jnp.zeros((8, D), bf)
    held = {0: 0, 1: 1, 4: 2}
    for i, ch in enumerate((0, 1, 2, 3, 4)):
        copy = pltpu.make_async_copy(vgrads.at[held.get(ch, 3)], grads.at[vector_at(ch)], ssem.at[16 + i])
        copy.start()
        stores.append(copy)
    rs.third(2)
    zc.move(0, 2, 1, take=False)
    zc.move(3, 2, -1, take=False)
    for copy in stores:
        copy.wait()
    for oy, ox in corners:
        for zo in (1, 0):
            late.begin(zo, oy, ox)
    zc.move(2, 3, 1)

    GROUPS = 16

    def take_groups(i):
        return pltpu.make_async_copy(spread.at[pl.ds(i * GROUPS, GROUPS)], group.at[i % 2], gsem.at[i % 2])

    bucket = lax.broadcasted_iota(jnp.int32, (BUCKETS, rows), 0)
    steps = keys // 8 // GROUPS
    code_copy.wait()
    take_groups(0).start()
    counts[...] = jnp.zeros_like(counts)

    def count_some(first, n):
        for i in range(first, first + n):
            if i + 1 < steps:
                take_groups(i + 1).start()
            take_groups(i).wait()

            def count(j, run, i=i):
                code = code_ref[pl.ds(pl.multiple_of((i * GROUPS + j) * 8, 8), 8), :]
                hot = jnp.concatenate(
                    [jnp.where(jnp.broadcast_to(code[r : r + 1], bucket.shape) == bucket, 1.0, 0.0) for r in range(8)]
                ).astype(bf)
                return run + lax.dot_general(group[i % 2, j].reshape(8 * H, rows), hot, NT, preferred_element_type=f32)

            counts[...] = lax.fori_loop(0, GROUPS, count, counts[...], unroll=8)

    early_one, late_one = rs.want(1, y, x), late.want(1, y, x)
    for zo in (1, 0):
        late.first(zo, 1, 1)
    for oy, ox in ((1, 0), (0, 1)):
        for zo in (1, 0):
            late.first(zo, oy, ox)
    rs.second(1)
    rs.first(1, 0, 0)
    count_some(0, 2)
    zc.move(1, 2, 1)
    for zo in (1, 0):
        late.first(zo, 0, 0)
    rs.third(1)
    zc.move(0, 1, 1, take=False, also=early_one)
    zc.move(3, 1, -1, take=False, also=early_one)
    count_some(2, 2)
    for zo in (1, 0):
        late.second(zo)
    count_some(4, 2)
    zc.move(2, 1, -1, also=early_one)
    late.third(1)
    zc.move(0, 1, 1, take=False, also=late_one)
    zc.move(3, 1, -1, take=False, also=late_one)
    late.third(0)
    zc.move(3, 0, -1, take=False)
    count_some(6, 2)
    zc.move(2, 1, -1, also=late_one)
    zc.move(2, 0, -1)
    table = table_row(counts[...], (8, D))
    zc.move(1, 0, -1)

    total[...] = acc[k].astype(f32)

    def add(way, zo):
        buf = zc.ways[way][0]
        for p in range(4):
            zc.copy(zo, way, p).wait_recv()
        total[...] = total[...] + buf[zo].astype(f32)

    @pl.when(z == 0)
    def _():
        add(-1, 0)

    @pl.when(z == 1)
    def _():
        add(1, 1)
        add(-1, 1)

    @pl.when(z == 2)
    def _():
        add(1, 2)
        add(-1, 2)

    @pl.when(z == 3)
    def _():
        add(1, 3)

    early = early_vectors(k)
    nw0 = jnp.where(early, 36, 37)
    vecs = early == (c == 0)
    mine = jnp.where(vecs, 36, 37)
    to_next = rcopy(total.at[pl.ds(mine - EDGE, EDGE)], ebuf.at[0], es.at[0], er.at[0], nxt)
    to_prev = rcopy(total.at[pl.ds(0, EDGE)], ebuf.at[1], es.at[1], er.at[1], prev)

    @pl.when(d < 31)
    def _():
        to_next.start()

    @pl.when(d > 0)
    def _():
        to_prev.start()

    def square(i, run):
        t = total[i]
        t = t * t
        for j in range(6):
            run = run + t[:, 128 * j:128 * j + 128]
        return run

    squares = lax.fori_loop(0, 37, square, jnp.zeros((8, 128), f32))
    lines = [jnp.sum(squares, axis=0, keepdims=True)] + [table[0:1, 128 * i : 128 * i + 128] for i in range(3)]
    sq[0] = jnp.concatenate(lines + [jnp.zeros((4, 128), f32)])
    rounds = [rcopy(sq.at[i], sqr.at[i], qs.at[i], qr.at[i], dev) for i, dev in enumerate((cdev, xdev, ydev))]
    hops = [rcopy(sq.at[3], sqr.at[3 + i], qs.at[3 + i], qr.at[3 + i], column_devs[i]) for i in range(3)]
    rounds[0].start()
    q, sh = shard_start(d)
    base = q - FRONT

    def flatten(ref, i, at, wide):
        @pl.when(wide)
        def _():
            t = ref[i]
            for j in range(6):
                win[pl.ds(at + j, 8, stride=24), :] = t[:, 128 * j:128 * j + 128]

        @pl.when(jnp.logical_not(wide))
        def _():
            t = ref[i]
            for j in range(6):
                win[pl.ds(at + j, 8, stride=6), :] = t[:, 128 * j:128 * j + 128]

    own_vectors = vecs & (vector_row(k, -1) >= 0)

    @pl.when(own_vectors)
    def _():
        flatten(total, 36, vector_row(k, q) - base, k < 0)

    w0 = jnp.where(c == 0, 73 * k, 73 * k + nw0)

    @pl.loop(0, mine)
    def _(t):
        at, wide = tile_start(w0 + t)
        flatten(total, t, at - base, wide)

    rounds[0].wait_recv()
    sq[1] = sq[0] + sqr[0]
    rounds[1].start()
    @pl.when(d > 0)
    def _():
        to_next.wait_recv()

        @pl.loop(0, EDGE)
        def _(t):
            at, wide = tile_start(w0 - EDGE + t)
            flatten(ebuf.at[0], t, at - base, wide)

    @pl.when(d < 31)
    def _():
        to_prev.wait_recv()

        @pl.loop(0, EDGE)
        def _(t):
            at, wide = tile_start(w0 + mine + t)
            flatten(ebuf.at[1], t, at - base, wide)

    rounds[1].wait_recv()
    sq[2] = sq[1] + sqr[1]
    rounds[2].start()
    rounds[2].wait_recv()
    sq[3] = sq[2] + sqr[2]
    for h in hops:
        h.start()
    for h in hops:
        h.wait_recv()
    summed = (sq[3] + sqr[4]) + (sqr[3] + sqr[5])

    @pl.when(d == 0)
    def _():
        for i in range(3):
            win[pl.ds(FRONT + 774 + i, 1), :] = summed[1 + i : 2 + i]

    sub = lax.broadcasted_iota(jnp.int32, (8, 128), 0)
    entries = jnp.where(sub == 0, summed, jnp.where(sub < 4, summed * summed, 0.0))
    square_sum = jnp.sum(jnp.sum(entries, axis=1, keepdims=True), axis=0, keepdims=True)
    factor = jnp.minimum(1.0, lax.rsqrt(square_sum / RAW + 1e-06))
    for s in shards:
        s.wait()
    lanes = lax.broadcasted_iota(jnp.int32, (80, 128), 1)
    rowi = lax.broadcasted_iota(jnp.int32, (80, 128), 0)
    back = (128 - sh) % 128

    @pl.loop(0, ROWS // 80)
    def _(i):
        r = pl.multiple_of(i * 80, 8)
        here = pltpu.roll(win[pl.ds(FRONT + r, 80), :], back, 1)
        there = pltpu.roll(win[pl.ds(FRONT + 1 + r, 80), :], back, 1)
        grad = jnp.where(lanes < 128 - sh, here, there) * factor
        entry = (d == 0) & (rowi + r < ENTRY_ROWS)
        rate = jnp.where(entry, learn_rate * layer_decay, learn_rate)
        one = beta_one * onev[pl.ds(r, 80), :] + (1.0 - beta_one) * grad
        two = beta_two * twov[pl.ds(r, 80), :] + (1.0 - beta_two) * grad * grad
        fixed_one = one / (1.0 - beta_one ** STEP)
        fixed_two = two / (1.0 - beta_two ** STEP)
        step = -rate * (fixed_one / (jnp.sqrt(fixed_two) + adam_eps) + weight_decay * mv[pl.ds(r, 80), :])
        mv[pl.ds(r, 80), :] = step
        onev[pl.ds(r, 80), :] = one
        twov[pl.ds(r, 80), :] = two

    results = [pltpu.make_async_copy(v, r, lsem.at[i]) for i, (v, r) in enumerate(((mv, step_ref), (onev, new1_ref), (twov, new2_ref)))]
    for copy in results:
        copy.start()

    for h in rounds + hops:
        h.wait_send()

    @pl.when(d < 31)
    def _():
        to_next.wait_send()

    @pl.when(d > 0)
    def _():
        to_prev.wait_send()

    rs.finish()
    late.finish()
    for zs in (0, 1, 2):
        zc.sent(zs, 3, 1)
    for zs in (0, 1):
        zc.sent(zs, 2, 1)
    zc.sent(3, 2, -1)
    zc.sent(0, 1, 1)
    zc.sent(3, 1, -1)
    zc.sent(2, 1, -1)
    for zs in (1, 2, 3):
        zc.sent(zs, 0, -1)
    for pair in range(H // 2):
        swap(pair).wait_send()
    shown.wait()
    for copy in results:
        copy.wait()


def backward_and_step(tiles, query, key_all, value_all, grad_context, soft, code, gfi, low, feats, grads, master, first_moment, second_moment):
    def rows_of(v):
        return jnp.pad(v, (0, ROWS * 128 - SHARD)).reshape(ROWS, 128)

    rows, keys = query.shape[0], key_all.shape[0]
    f32, bf = jnp.float32, jnp.bfloat16
    any_ = pl.BlockSpec(memory_space=pl.ANY)
    S, V, sem = jax.ShapeDtypeStruct, pltpu.VMEM, pltpu.SemaphoreType.DMA
    w = V((96, 8, D), bf)
    tile = (8, D)
    line = V((ROWS, 128), f32)
    outs = pl.pallas_call(
        backward_kernel,
        out_shape=[S((rows, D), f32), S(grads.shape, bf)] + [S((ROWS, 128), f32)] * 3 + [S((keys // 8, H, 8, rows), bf)],
        in_specs=[any_] * 14,
        out_specs=[any_] * 6,
        scratch_shapes=[
            V((2, keys, rows), bf), V((2, rows, 128), bf), V((2, keys, 128), bf), V((2, keys, 128), bf), V((2, rows, 128), bf), sem((5, 2)),
            V((keys, rows), jnp.int32), sem((1,)), V((2, keys // 8, 8, rows), bf), sem((2,)), V((2, 16, H, 8, rows), bf), sem((2,)),
            V((8 * H, 8 * BUCKETS), f32),
            V((2, keys, 128), f32), V((2, keys, 128), f32), V((6, 2, rows, 128), bf), V((6, 2, rows, 128), bf), sem((6,)), sem((6,)),
            V((3, rows, D), bf), V((2, 8, D), f32),
            w, w, w, V((rows, D), bf), V((rows, D), f32), V((rows, LF), bf), V((16, 8, D), bf), w, w, w, V((4, 8, D), bf),
            sem((12,)), sem((24,)), sem((7,)),
            V((37,) + tile, f32), V((2, EDGE) + tile, f32), V((4, 8, 128), f32), V((6, 8, 128), f32),
            V((WIN2, 128), f32), line, line, line, sem((3,)), sem((2,)), sem((2,)), sem((6,)), sem((6,)),
        ] + reducer_scratch() + chain_scratch(),
        input_output_aliases={10: 1},
        compiler_params=pltpu.CompilerParams(collective_id=5, has_side_effects=True, vmem_limit_bytes=63 << 20),
        name="backward_and_step",
    )(tiles, query, key_all, value_all, grad_context, soft, code, gfi, low, feats, grads, rows_of(master), rows_of(first_moment), rows_of(second_moment))
    return outs[0], [o.reshape(-1)[:SHARD] for o in outs[2:5]]


def from_tiles(tiles):
    got = {}
    for name, first, count in WEIGHTS:
        block = jnp.concatenate([tiles[s : s + n] for s, _, n in slots_of(first, count)])
        if name == 12:
            block = block.reshape(96, 4, 8, D).transpose(0, 2, 1, 3)
        got[name] = block.reshape(-1, FF if name == 12 else D)
    for name, chip, row in VECTORS:
        block = tiles[vector_at(chip)]
        if name == 13:
            got[name] = block[row : row + 4].reshape(FF)
        elif name == 2:
            got[name] = block[row, : BUCKETS * H].reshape(BUCKETS, H)
        else:
            got[name] = block[row]
    return [got[i] for i in range(18)]


def to_tiles(whole):
    by_name = [p.astype(jnp.bfloat16) for p in whole]
    weights = []
    for name, first, count in WEIGHTS:
        got = by_name[name]
        if name == 12:
            got = got.reshape(96, 8, 4, D).transpose(0, 2, 1, 3)
        weights.append(got.reshape(count, 8, D))
    cuts = []
    for chip in range(16):
        held = [(r, by_name[n]) for n, c, r in VECTORS if c == chip]
        rows = [jnp.pad(v.reshape(-1), (0, -v.size % D)).reshape(-1, D) for _, v in held]
        block = jnp.concatenate(rows + [jnp.zeros((8 - sum(r.shape[0] for r in rows), D), jnp.bfloat16)])
        cuts.append((73 * chip + vector_slot(chip), block[None]))
    parts = []
    for (name, first, count), tiles in zip(WEIGHTS, weights):
        at = first
        for w, block in [c for c in cuts if first <= c[0] < first + count]:
            if w > at:
                parts.append(tiles[at - first : w - first])
            parts.append(block)
            at = w
        parts.append(tiles[at - first :])
    parts.extend(block for w, block in cuts if w == 1168)
    return jnp.concatenate(parts)


def per_device(
    custom, tokens, cotangent, page_boxes, page_lengths, padding, buckets, master, first_moment, second_moment
):
    rows = tokens.shape[1]
    feats = layout_features(page_boxes.reshape(4, rows)).astype(jnp.bfloat16)
    pad = jnp.broadcast_to(padding, (8, rows))
    if custom:
        tiles, hidden, low, query, keys, values, ctx, soft, code = gather_and_attend(
            master, tokens[0], feats, pad, buckets[0], page_lengths
        )
        tiles = tiles.reshape(16 * CHIP, 8, D)
    else:
        tiles = to_tiles(unpack(lax.all_gather(master.astype(jnp.bfloat16), ("dp", "seq"), axis=0, tiled=True)))
        hidden, low, query, keys, values, pads = enter(tiles, tokens[0], feats, pad)
        ctx, soft, code = attend(query, keys, values, buckets[0], page_lengths, pads, tiles[vector_at(0)])
    activations, grad_first_in, grad_context, grads = middle(tiles, ctx, hidden, cotangent[0])
    if custom:
        input_grad, stepped = backward_and_step(
            tiles, query, keys, values, grad_context, soft, code, grad_first_in, low, feats, grads, master, first_moment, second_moment
        )
    else:
        dq, dk, dv, table = soft_back(query, keys, values, grad_context, soft, code)
        input_grad, grads = leave(tiles, dq, dk, dv, grad_first_in, low, feats, table, grads)
        flat = jnp.concatenate([p.astype(jnp.float32).reshape(-1) for p in from_tiles(grads)])
        grad = lax.psum_scatter(flat, ("dp", "seq"), scatter_dimension=0, tiled=True)
        square = lax.psum(jnp.sum(grad * grad), ("dp", "seq"))
        factor = jnp.minimum(1.0, lax.rsqrt(square / RAW + 1e-06))
        size = master.shape[0]
        index = lax.axis_index(("dp", "seq")) * size + jnp.arange(size, dtype=jnp.int32)
        stepped = adam_update(master, first_moment, second_moment, grad * factor, index)
    return (activations[None], input_grad[None]) + tuple(stepped)


def solution(mesh):
    in_specs = (
        P("dp", "seq", None),
        P("dp", "seq", None),
        P(None, "dp", "seq"),
        P("dp", None),
        P("dp", "seq"),
        P("dp", "seq", None),
        P(("dp", "seq")),
        P(("dp", "seq")),
        P(("dp", "seq")),
    )
    out_specs = (
        P("dp", "seq", None),
        P("dp", "seq", None),
        P(("dp", "seq")),
        P(("dp", "seq")),
        P(("dp", "seq")),
    )
    custom = dict(mesh.shape) == {"dp": 16, "seq": 2}
    return jax.shard_map(
        functools.partial(per_device, custom), mesh=mesh, in_specs=in_specs, out_specs=out_specs, check_vma=False
    )
```

```python
import functools

import jax
import jax.numpy as jnp
from jax import lax
from jax.experimental import pallas as pl
from jax.experimental.pallas import tpu as pltpu
from jax.sharding import PartitionSpec as P

D = 768
H = 12
HD = 64
FF = 3072
BUCKETS = 32
FREQ = 16
LF = 128
LAYERS = 1
BLOCK = 1024
STEP = 10
ENTRY = 99456
LAYER_PARAMS = 7087104
RAW = 7186560


beta_one = 0.8
beta_two = 0.98
adam_eps = 1e-06
learn_rate = 0.0006
layer_decay = 0.8
weight_decay = 0.1
norm_eps = 1e-05
masked_score = -1000000000.0


SHAPES = (
    (LF, D), (D,), (BUCKETS, H),
    (D, D), (D,), (D, D), (D, D), (D,), (D, D), (D,), (D,), (D,),
    (D, FF), (FF,), (FF, D), (D,), (D,), (D,),
)


def unpack(flat_params):
    pieces, offset = [], 0
    for shape in SHAPES:
        amount = shape[0] * (shape[1] if len(shape) > 1 else 1)
        pieces.append(flat_params[offset : offset + amount].reshape(shape))
        offset = offset + amount
    return pieces


def adam_update(master, first_moment, second_moment, gradient, global_index):
    exponent = jnp.where(
        global_index < ENTRY,
        LAYERS,
        jnp.maximum(LAYERS - 1 - (global_index - ENTRY) // LAYER_PARAMS, 0),
    )
    rate = jnp.where(
        global_index < RAW, learn_rate * jnp.power(layer_decay, exponent.astype(jnp.float32)), 0.0
    )
    moment_one = beta_one * first_moment + (1.0 - beta_one) * gradient
    moment_two = beta_two * second_moment + (1.0 - beta_two) * gradient * gradient
    fixed_one = moment_one / (1.0 - beta_one**STEP)
    fixed_two = moment_two / (1.0 - beta_two**STEP)
    param_step = -rate * (fixed_one / (jnp.sqrt(fixed_two) + adam_eps) + weight_decay * master)
    return (param_step, moment_one, moment_two)


def layout_features(page_boxes):
    rates_sin = jnp.power(10000.0, -jnp.arange(FREQ, dtype=jnp.float32) / FREQ)
    angles = page_boxes.astype(jnp.float32)[:, :, None] * rates_sin
    stacked = jnp.stack([jnp.sin(angles), jnp.cos(angles)], axis=1)
    return jnp.transpose(stacked, (2, 0, 1, 3)).reshape(page_boxes.shape[1], LF)


MESH = pl.DeviceIdType.MESH
SHARD = 224580
ROWS = 1760
TAIL, HEAD = 160, 176
WIN = 2176
SLOTS = 37
CHIP = 74
PARTS = ((0, 19), (19, 18))


def place():
    k = lax.axis_index("dp")
    return k, lax.axis_index("seq"), k // 4, (k // 2) % 2, k % 2


def shard_start(d):
    return d * 1754 + (d * 68) // 128, (d * 68) % 128


def early_vectors(k):
    return (k == 0) | (k == 4) | (k == 5)


def vector_row(k, other):
    at = other
    for chip, row in ((0, 768), (1, 5385), (4, 14607), (5, 19221), (10, 37671), (15, 56127)):
        at = jnp.where(k == chip, row, at)
    return at


def tile_start(w):
    at = w * 48
    for first, shift in ((16, 777 - 16 * 48), (112, 5391 - 112 * 48), (208, 9999 - 208 * 48), (304, 14613 - 304 * 48), (784, 37695 - 784 * 48)):
        at = jnp.where(w >= first, w * 48 + shift, at)
    wide = (w >= 400) & (w < 784)
    v = w - 400
    at = jnp.where(wide, 19239 + (v // 4) * 192 + (v % 4) * 6, at)
    return at, wide


def neighbours(k, c, z, y, x):
    t = k >= 0
    return [
        (t, (k, 1 - c)),
        (t, (z * 4 + y * 2 + 1 - x, c)),
        (t, (z * 4 + (1 - y) * 2 + x, c)),
        (z < 3, (jnp.minimum(k + 4, 15), c)),
        (z > 0, (jnp.maximum(k - 4, 0), c)),
        ((c == 1) & (k < 15), (jnp.minimum(k + 1, 15), 0)),
        ((c == 0) & (k > 0), (jnp.maximum(k - 1, 0), 1)),
    ]


def greet(k, c, z, y, x):
    bar = pltpu.get_barrier_semaphore()
    for cond, dev in neighbours(k, c, z, y, x):
        @pl.when(cond)
        def _():
            pl.semaphore_signal(bar, inc=1, device_id=dev, device_id_type=MESH)
    peers = 3
    for cond, _ in neighbours(k, c, z, y, x)[3:]:
        peers = peers + jnp.where(cond, 1, 0)
    pl.semaphore_wait(bar, peers)


def rcopy(src, dst, ssem, rsem, dev):
    return pltpu.make_async_remote_copy(src_ref=src, dst_ref=dst, send_sem=ssem, recv_sem=rsem, device_id=dev, device_id_type=MESH)


FRONT = 344
WIN2 = 2464
EDGE = 4
ENTRY_ROWS = 777


WEIGHTS = (
    (0, 0, 16),
    (3, 16, 96),
    (5, 112, 96),
    (6, 208, 96),
    (8, 304, 96),
    (12, 400, 384),
    (14, 784, 384),
)
VECTORS = (
    (1, 0, 0),
    (2, 0, 1),
    (4, 1, 0),
    (7, 4, 0),
    (9, 5, 0),
    (10, 5, 1),
    (11, 5, 2),
    (13, 10, 0),
    (15, 15, 0),
    (16, 15, 1),
    (17, 15, 2),
)


def slots_of(first, count):
    runs = []
    for w in range(first, first + count):
        chip, at = divmod(w, 73)
        slot = chip * CHIP + at + (1 if at >= vector_slot(chip) else 0)
        if runs and runs[-1][0] + runs[-1][2] == slot:
            runs[-1][2] += 1
        else:
            runs.append([slot, w - first, 1])
    return runs


def vector_slot(chip):
    return 36 if chip in (0, 4, 5) else 73


def vector_at(chip):
    return chip * CHIP + vector_slot(chip)


def pieces(tiles, held, first, count, sems, base, out=False):
    made = []
    for i, (slot, at, n) in enumerate(slots_of(first, count)):
        a, b = tiles.at[pl.ds(slot, n)], held.at[pl.ds(at, n)]
        a, b = (b, a) if out else (a, b)
        made.append(pltpu.make_async_copy(a, b, sems.at[base + i]))
    return made


def matrix(tile_rows):
    return tile_rows.reshape(-1, D)


def col_sum(v):
    return jnp.sum(v.reshape(-1, 8, v.shape[-1]), axis=0)


def norm_stats(v):
    mean = jnp.mean(v, axis=-1, keepdims=True)
    center = v - mean
    spread = jnp.mean(center * center, axis=-1, keepdims=True)
    inv = lax.rsqrt(spread + norm_eps)
    return center * inv, inv


def norm_back(grad, gain, hat, inv):
    g = grad * gain
    return inv * (g - jnp.mean(g, axis=-1, keepdims=True) - hat * jnp.mean(g * hat, axis=-1, keepdims=True))


ROOT_HALF = 0.7071067811865476
ROOT_TAU = 0.3989422804014327


def middle_kernel(tiles, ctx, hidden, cot, act_out, gfi_out, gctx_out, grads,
                  wo, wup, wdn, vecs, vf, act, slope, low1, hat1, inv1, hat2, inv2, a, sums, dwo, dwup, dwdn, vgrads, lsem, ssem):
    f32, bf = jnp.float32, jnp.bfloat16
    rows = ctx.shape[0]
    R = 64
    steps = rows // R
    loads_o = pieces(tiles, wo, 304, 96, lsem, 0)
    loads_u = pieces(tiles, wup, 400, 384, lsem, 4)
    loads_d = pieces(tiles, wdn, 784, 384, lsem, 12)
    loads_v = [pltpu.make_async_copy(tiles.at[vector_at(c)], vecs.at[i], lsem.at[20 + i]) for i, c in enumerate((5, 10, 15))]
    for c in loads_v + loads_o + loads_u + loads_d:
        c.start()
    up4 = wup.reshape(96, 4, 8, D)
    dup4 = dwup.reshape(96, 4, 8, D)

    def vec(i, r):
        return vf[i, pl.ds(r, 1), :]

    def each(f):
        @pl.loop(0, steps)
        def _(i):
            f(pl.ds(pl.multiple_of(i * R, R), R))

    for c in loads_v + loads_o:
        c.wait()
    vf[...] = vecs[...].astype(f32)
    a[...] = jnp.dot(ctx[...], matrix(wo[...]), preferred_element_type=f32)

    def first(sl):
        hat, inv = norm_stats(hidden[sl, :] + a[sl, :] + vec(0, 0))
        hat1[sl, :] = hat
        inv1[sl, :] = inv
        out = hat * vec(0, 1) + vec(0, 2)
        a[sl, :] = out
        low1[sl, :] = out.astype(bf)

    each(first)
    for c in loads_u + loads_d:
        c.wait()

    def up(j, _):
        for half in range(2):
            sl = pl.ds(half * (rows // 2), rows // 2)
            u = jnp.dot(low1[sl, :], matrix(up4[:, j]), preferred_element_type=f32) + vec(1, j)
            share = 0.5 * (1.0 + lax.erf(u * ROOT_HALF))
            act[j, sl, :] = (u * share).astype(bf)
            slope[j, sl, :] = share + u * jnp.exp(-0.5 * u * u) * ROOT_TAU
        return 0

    lax.fori_loop(0, 4, up, 0)

    def down(j, _):
        a[...] += jnp.dot(act[j], matrix(wdn[pl.ds(96 * j, 96)]), preferred_element_type=f32)
        return 0

    lax.fori_loop(0, 4, down, 0)
    sums[...] = jnp.zeros_like(sums)

    def second(sl):
        hat, inv = norm_stats(a[sl, :] + vec(2, 0))
        act_out[sl, :] = (hat * vec(2, 1) + vec(2, 2)).astype(bf)
        g = cot[sl, :].astype(f32)
        sums[6] += col_sum(g * hat)
        sums[7] += col_sum(g)
        back = norm_back(g, vec(2, 1), hat, inv)
        sums[5] += col_sum(back)
        a[sl, :] = back
        hat2[sl, :] = back.astype(bf)

    each(second)
    down_back = hat2

    def back(j, _):
        for half in range(2):
            sl = pl.ds(half * (rows // 2), rows // 2)
            g = lax.dot_general(down_back[sl, :], matrix(wdn[pl.ds(96 * j, 96)]), NT, preferred_element_type=f32) * slope[j, sl, :]
            sums[8 + j] += col_sum(g)
            act_back[sl, :] = g.astype(bf)
        dwdn[pl.ds(96 * j, 96)] = lax.dot_general(act[j], down_back[...], TN, preferred_element_type=f32).astype(bf).reshape(96, 8, D)
        dup4[:, j] = lax.dot_general(low1[...], act_back[...], TN, preferred_element_type=f32).astype(bf).reshape(96, 8, D)
        a[...] += lax.dot_general(act_back[...], matrix(up4[:, j]), NT, preferred_element_type=f32)
        return 0

    act_back = inv2
    lax.fori_loop(0, 4, back, 0)
    stores = pieces(grads, dwup, 400, 384, ssem, 4, True) + pieces(grads, dwdn, 784, 384, ssem, 12, True)
    for c in stores:
        c.start()

    def third(sl):
        g = a[sl, :]
        sums[3] += col_sum(g * hat1[sl, :])
        sums[4] += col_sum(g)
        back = norm_back(g, vec(0, 1), hat1[sl, :], inv1[sl, :])
        sums[2] += col_sum(back)
        gfi_out[sl, :] = back
        hat2[sl, :] = back.astype(bf)

    each(third)
    gctx_out[...] = lax.dot_general(hat2[...], matrix(wo[...]), NT, preferred_element_type=f32).astype(bf)
    dwo[...] = lax.dot_general(ctx[...], hat2[...], TN, preferred_element_type=f32).astype(bf).reshape(96, 8, D)
    for i, held in enumerate(((2, 3, 4), (8, 9, 10, 11), (5, 6, 7))):
        lines = [jnp.sum(sums[s], axis=0, keepdims=True) for s in held]
        lines.append(jnp.zeros((8 - len(held), D), f32))
        vgrads[i] = jnp.concatenate(lines).astype(bf)
    last = pieces(grads, dwo, 304, 96, ssem, 0, True)
    quiet = [ch for ch in range(6, 15) if ch != 10]
    vgrads[3] = jnp.zeros((8, D), bf)
    last += [pltpu.make_async_copy(vgrads.at[min(i, 3)], grads.at[vector_at(ch)], ssem.at[20 + i]) for i, ch in enumerate([5, 10, 15] + quiet)]
    for c in last:
        c.start()
    for c in stores + last:
        c.wait()


def middle(tiles, ctx, hidden, cot):
    rows = ctx.shape[0]
    f32, bf = jnp.float32, jnp.bfloat16
    vm, any_ = pl.BlockSpec(memory_space=pltpu.VMEM), pl.BlockSpec(memory_space=pl.ANY)
    S = jax.ShapeDtypeStruct
    return pl.pallas_call(
        middle_kernel,
        out_shape=[S((rows, D), bf), S((rows, D), f32), S((rows, D), bf), S((16 * CHIP, 8, D), bf)],
        in_specs=[any_, vm, vm, vm],
        out_specs=[vm, vm, vm, any_],
        scratch_shapes=[
            pltpu.VMEM((96, 8, D), bf), pltpu.VMEM((384, 8, D), bf), pltpu.VMEM((384, 8, D), bf), pltpu.VMEM((3, 8, D), bf), pltpu.VMEM((3, 8, D), f32),
            pltpu.VMEM((4, rows, D), bf), pltpu.VMEM((4, rows, D), f32), pltpu.VMEM((rows, D), bf),
            pltpu.VMEM((rows, D), f32), pltpu.VMEM((rows, 1), f32), pltpu.VMEM((rows, D), bf), pltpu.VMEM((rows, D), bf),
            pltpu.VMEM((rows, D), f32), pltpu.VMEM((12, 8, D), f32),
            pltpu.VMEM((96, 8, D), bf), pltpu.VMEM((384, 8, D), bf), pltpu.VMEM((384, 8, D), bf), pltpu.VMEM((4, 8, D), bf),
            pltpu.SemaphoreType.DMA((24,)), pltpu.SemaphoreType.DMA((32,)),
        ],
        compiler_params=pltpu.CompilerParams(vmem_limit_bytes=58 << 20),
        name="middle",
    )(tiles, ctx, hidden, cot)


NT = (((1,), (1,)), ((), ()))
TN = (((0,), (0,)), ((), ()))


def half(ref_value, hh):
    lanes = lax.broadcasted_iota(jnp.int32, ref_value.shape, 1)
    keep = lanes // 64 == hh
    return jnp.where(keep, ref_value, jnp.zeros_like(ref_value))


def page_of(at, lengths):
    end, page = 0, jnp.zeros(at.shape, jnp.int32)
    for i in range(4):
        end = end + lengths[0, i]
        page = page + jnp.where(at >= end, 1, 0)
    return page


def fill_codes(code_ref, buckets, pads, lengths):
    keys, rows = code_ref.shape
    own = lax.axis_index("seq") * rows
    tag = page_of(lax.broadcasted_iota(jnp.int32, (1, keys), 1), lengths) + 1
    tag = jnp.where(jnp.concatenate([pads[0, 0:1], pads[1, 0:1]], axis=1) > 0, tag, 0)
    for i in range(rows // 128):
        at = own + 128 * i + lax.broadcasted_iota(jnp.int32, (128, 1), 0)
        page = page_of(at, lengths) + 1
        for j in range(keys // 128):
            key_at = 128 * j + lax.broadcasted_iota(jnp.int32, (1, 128), 1)
            allowed = (page == tag[:, 128 * j : 128 * j + 128]) | (key_at == at)
            code = jnp.where(allowed, buckets[128 * i : 128 * i + 128, 128 * j : 128 * j + 128], BUCKETS)
            code_ref[128 * j : 128 * j + 128, 128 * i : 128 * i + 128] = code.T


def fill_table(tab_ref, lines):
    f32 = jnp.float32
    head = lax.broadcasted_iota(jnp.int32, (16, 128), 0)
    bucket = lax.broadcasted_iota(jnp.int32, (16, 128), 1)
    place_of = bucket * H + head
    tab = jnp.full((16, 128), masked_score, f32)
    for i in range(BUCKETS * H // 128):
        row = jnp.broadcast_to(lines[1:2, 128 * i : 128 * i + 128].astype(f32), (16, 128))
        inside = jnp.clip(place_of - 128 * i, 0, 127)
        got = jnp.take_along_axis(row, inside, axis=1, mode="promise_in_bounds")
        tab = jnp.where((place_of // 128 == i) & (bucket < BUCKETS) & (head < H), got, tab)
    tab_ref[...] = tab


def soft_head(head, q, k, code_ref, tab_ref, s_scr, p_ref):
    keys, rows = s_scr.shape
    f32, bf = jnp.float32, jnp.bfloat16
    qm = half(q, head % 2)
    line = jnp.broadcast_to(tab_ref[pl.ds(head, 1), :], (keys, 128))
    s = lax.dot_general(k, qm, NT, preferred_element_type=f32)
    cols = []
    for j in range(rows // 128):
        code = code_ref[:, 128 * j : 128 * j + 128]
        bias = jnp.take_along_axis(line, code, axis=1, mode="promise_in_bounds")
        cols.append(jnp.where(bias < 0.5 * masked_score, masked_score, s[:, 128 * j : 128 * j + 128] + bias))
    s = jnp.concatenate(cols, axis=1)
    s_scr[...] = s
    top = jnp.max(jnp.max(s.reshape(keys // 8, 8, rows), axis=0), axis=0, keepdims=True)
    e = jnp.exp(s_scr[...] - top)
    s_scr[...] = e
    inverse = 1.0 / jnp.sum(jnp.sum(e.reshape(keys // 8, 8, rows), axis=0), axis=0, keepdims=True)
    p_ref[...] = (s_scr[...] * inverse).astype(bf)


def context_pair(v, p_ref):
    vt = v.T
    out = [jnp.dot(vt, p_ref[hh], preferred_element_type=jnp.float32) for hh in range(2)]
    sub = lax.broadcasted_iota(jnp.int32, out[0].shape, 0)
    return jnp.where(sub < 64, out[0], out[1]).T.astype(jnp.bfloat16)


def attend_kernel(lengths, q_ref, k_ref, v_ref, buckets, pads, lines, ctx_ref, p_ref, code_ref, s_scr, tab_ref):
    pair = pl.program_id(0)

    @pl.when(pair == 0)
    def _():
        fill_codes(code_ref, buckets, pads, lengths)
        fill_table(tab_ref, lines)

    for hh in range(2):
        soft_head(2 * pair + hh, q_ref[...], k_ref[...], code_ref, tab_ref, s_scr, p_ref.at[hh])
    ctx_ref[...] = context_pair(v_ref[...], p_ref)


def attend(query, key_all, value_all, buckets, page_lengths, pads, lines):
    rows, keys = query.shape[0], key_all.shape[0]
    bf = jnp.bfloat16
    const = lambda p: (0, 0)
    return pl.pallas_call(
        attend_kernel,
        grid=(H // 2,),
        out_shape=[
            jax.ShapeDtypeStruct((rows, D), bf),
            jax.ShapeDtypeStruct((H, keys, rows), bf),
            jax.ShapeDtypeStruct((keys, rows), jnp.int32),
        ],
        in_specs=[
            pl.BlockSpec(memory_space=pltpu.SMEM),
            pl.BlockSpec((rows, 128), lambda p: (0, p)),
            pl.BlockSpec((keys, 128), lambda p: (0, p)),
            pl.BlockSpec((keys, 128), lambda p: (0, p)),
            pl.BlockSpec((rows, keys), const),
            pl.BlockSpec((2, 8, rows), lambda p: (0, 0, 0)),
            pl.BlockSpec((8, D), const),
        ],
        out_specs=[pl.BlockSpec((rows, 128), lambda p: (0, p)), pl.BlockSpec((2, keys, rows), lambda p: (p, 0, 0)), pl.BlockSpec((keys, rows), const)],
        scratch_shapes=[pltpu.VMEM((keys, rows), jnp.float32), pltpu.VMEM((16, 128), jnp.float32)],
        compiler_params=pltpu.CompilerParams(vmem_limit_bytes=56 << 20),
        name="attend",
    )(page_lengths, query, key_all, value_all, buckets, pads, lines)


def table_row(acc, shape):
    f32 = jnp.float32
    a = lax.broadcasted_iota(jnp.int32, acc.shape, 0) % 8
    b = lax.broadcasted_iota(jnp.int32, acc.shape, 1) // BUCKETS
    acc = jnp.where(a == b, acc, 0.0)
    heads = jnp.sum(acc.reshape(H, 8, 8 * BUCKETS), axis=1)
    lane = lax.broadcasted_iota(jnp.int32, (8 * BUCKETS, D), 1) // H
    wide = jnp.where(lane == lax.broadcasted_iota(jnp.int32, lane.shape, 0) % BUCKETS, 1.0, 0.0)
    out = jnp.dot(heads, wide, precision=lax.Precision.HIGHEST, preferred_element_type=f32)
    mine = lax.broadcasted_iota(jnp.int32, out.shape, 1) % H == lax.broadcasted_iota(jnp.int32, out.shape, 0)
    out = jnp.sum(jnp.where(mine, out, 0.0), axis=0, keepdims=True)
    return jnp.broadcast_to(out, shape)


def attend_back_kernel(q_ref, k_ref, v_ref, do_ref, p_ref, code_ref, dq_ref, dk_ref, dv_ref, tab_ref, spread, held):
    pair = pl.program_id(0)
    keys, rows = code_ref.shape
    f32, bf = jnp.float32, jnp.bfloat16
    STEP_ROWS = keys
    kt = k_ref[...].T
    dq = []
    for hh in range(2):
        qm = half(q_ref[...], hh)
        dom = half(do_ref[...], hh)

        def inner(i, total):
            at = pl.multiple_of(i * STEP_ROWS, STEP_ROWS)
            g = lax.dot_general(v_ref[pl.ds(at, STEP_ROWS), :], dom, NT, preferred_element_type=f32)
            w = g * p_ref[hh, pl.ds(at, STEP_ROWS), :].astype(f32)
            return total + jnp.sum(w.reshape(STEP_ROWS // 8, 8, rows), axis=0)

        total = lax.fori_loop(0, keys // STEP_ROWS, inner, jnp.zeros((8, rows), f32))
        total = jnp.sum(total, axis=0, keepdims=True)

        def grads(i, acc):
            at = pl.multiple_of(i * STEP_ROWS, STEP_ROWS)
            sl = pl.ds(at, STEP_ROWS)
            g = lax.dot_general(v_ref[sl, :], dom, NT, preferred_element_type=f32)
            p = p_ref[hh, sl, :]
            ds = p.astype(f32) * (g - total)
            wide = ds.reshape(STEP_ROWS // 8, 8, rows)
            if hh == 0:
                held[...] = wide
            else:
                both = jnp.concatenate([held[...], wide], axis=1).astype(bf)
                spread[:, pl.ds(pl.multiple_of(pair * 16, 16), 16), :] = both
            ds = ds.astype(bf)
            dv = jnp.dot(p, dom, preferred_element_type=f32)
            dk = jnp.dot(ds, qm, preferred_element_type=f32)
            if hh == 0:
                dv_ref[sl, :] = dv
                dk_ref[sl, :] = dk
            else:
                dv_ref[sl, :] += dv
                dk_ref[sl, :] += dk
            return acc + lax.dot_general(k_ref[sl, :], ds, TN, preferred_element_type=f32)

        dq.append(lax.fori_loop(0, keys // STEP_ROWS, grads, jnp.zeros((128, rows), f32)))
    sub = lax.broadcasted_iota(jnp.int32, dq[0].shape, 0)
    dq_ref[...] = jnp.where(sub < 64, dq[0], dq[1]).T * 0.125

    @pl.when(pair == H // 2 - 1)
    def _():
        bucket = lax.broadcasted_iota(jnp.int32, (BUCKETS, rows), 0)

        def count(i, acc):
            code = code_ref[pl.ds(pl.multiple_of(i * 8, 8), 8), :]
            hot = jnp.concatenate(
                [jnp.where(jnp.broadcast_to(code[r : r + 1], bucket.shape) == bucket, 1.0, 0.0) for r in range(8)]
            ).astype(bf)
            return acc + lax.dot_general(spread[i], hot, NT, preferred_element_type=f32)

        acc = lax.fori_loop(0, keys // 8, count, jnp.zeros((8 * H, 8 * BUCKETS), f32), unroll=8)
        tab_ref[...] = table_row(acc, tab_ref.shape)


def soft_back(query, key_all, value_all, grad_context, soft, code):
    rows, keys = query.shape[0], key_all.shape[0]
    f32 = jnp.float32
    row = pl.BlockSpec((rows, 128), lambda p: (0, p))
    key = pl.BlockSpec((keys, 128), lambda p: (0, p))
    dq, dk, dv, tab = pl.pallas_call(
        attend_back_kernel,
        grid=(H // 2,),
        out_shape=[
            jax.ShapeDtypeStruct((rows, D), f32),
            jax.ShapeDtypeStruct((keys, D), f32),
            jax.ShapeDtypeStruct((keys, D), f32),
            jax.ShapeDtypeStruct((8, D), f32),
        ],
        in_specs=[row, key, key, row, pl.BlockSpec((2, keys, rows), lambda p: (p, 0, 0)), pl.BlockSpec((keys, rows), lambda p: (0, 0))],
        out_specs=[row, key, key, pl.BlockSpec((8, D), lambda p: (0, 0))],
        scratch_shapes=[pltpu.VMEM((keys // 8, 8 * H, rows), jnp.bfloat16), pltpu.VMEM((keys // 8, 8, rows), f32)],
        compiler_params=pltpu.CompilerParams(vmem_limit_bytes=58 << 20),
        name="attend_back",
    )(query, key_all, value_all, grad_context, soft, code)
    return dq, dk, dv, tab


def meet_partner():
    dp, c = lax.axis_index("dp"), lax.axis_index("seq")
    partner = (dp, 1 - c)
    bar = pltpu.get_barrier_semaphore()
    pl.semaphore_signal(bar, inc=1, device_id=partner, device_id_type=MESH)
    pl.semaphore_wait(bar, 1)
    return c, partner


def enter_kernel(tiles, tokens, feats, pad, hidden, low, query, keys, values, pads, wl, wq, wk, wv, vecs, vf, lsem, sends, recvs):
    f32, bf = jnp.float32, jnp.bfloat16
    rows = tokens.shape[0]
    loads = [pltpu.make_async_copy(tiles.at[vector_at(ch)], vecs.at[i], lsem.at[i]) for i, ch in enumerate((0, 1, 4))]
    loads += pieces(tiles, wl, 0, 16, lsem, 4) + pieces(tiles, wk, 112, 96, lsem, 8)
    loads += pieces(tiles, wv, 208, 96, lsem, 12) + pieces(tiles, wq, 16, 96, lsem, 16)
    for c in loads:
        c.start()
    c, partner = meet_partner()
    own = pl.ds(c * rows, rows)

    def share(ref, i):
        return rcopy(ref.at[own], ref.at[own], sends.at[i], recvs.at[i], partner)

    pads[pl.ds(c, 1)] = pad[...].reshape(1, 8, rows)
    pair_pads = rcopy(pads.at[pl.ds(c, 1)], pads.at[pl.ds(c, 1)], sends.at[2], recvs.at[2], partner)
    pair_pads.start()
    for copy in loads:
        copy.wait()
    vf[...] = vecs[...].astype(f32)
    h = tokens[...].astype(f32) + jnp.dot(feats[...], matrix(wl[...]), preferred_element_type=f32) + vf[0, 0:1, :]
    hidden[...] = h
    low[...] = h.astype(bf)
    keys[own, :] = jnp.dot(low[...], matrix(wk[...]), preferred_element_type=f32).astype(bf)
    send_keys = share(keys, 0)
    send_keys.start()
    values[own, :] = (jnp.dot(low[...], matrix(wv[...]), preferred_element_type=f32) + vf[2, 0:1, :]).astype(bf)
    send_values = share(values, 1)
    send_values.start()
    query[...] = ((jnp.dot(low[...], matrix(wq[...]), preferred_element_type=f32) + vf[1, 0:1, :]) * 0.125).astype(bf)
    for copy in (pair_pads, send_keys, send_values):
        copy.wait()


def enter(tiles, tokens, feats, pad):
    rows = tokens.shape[0]
    f32, bf = jnp.float32, jnp.bfloat16
    vm, any_ = pl.BlockSpec(memory_space=pltpu.VMEM), pl.BlockSpec(memory_space=pl.ANY)
    S, sem = jax.ShapeDtypeStruct, pltpu.SemaphoreType.DMA
    w = pltpu.VMEM((96, 8, D), bf)
    return pl.pallas_call(
        enter_kernel,
        out_shape=[S((rows, D), f32), S((rows, D), bf), S((rows, D), bf), S((2 * rows, D), bf), S((2 * rows, D), bf), S((2, 8, rows), jnp.int32)],
        in_specs=[any_, vm, vm, vm],
        out_specs=[vm] * 6,
        scratch_shapes=[pltpu.VMEM((16, 8, D), bf), w, w, w, pltpu.VMEM((3, 8, D), bf), pltpu.VMEM((3, 8, D), f32), sem((20,)), sem((3,)), sem((3,))],
        compiler_params=pltpu.CompilerParams(collective_id=2, has_side_effects=True, vmem_limit_bytes=40 << 20),
        name="enter",
    )(tiles, tokens, feats, pad)


def leave_kernel(tiles, dq, dk, dv, gfi, low, feats, table, grads_in, input_grad, grads,
                 wq, wk, wv, out, come, back, dwl, dwq, dwk, dwv, vgrads, lsem, ssem, sends, recvs):
    f32, bf = jnp.float32, jnp.bfloat16
    rows = gfi.shape[0]
    loads = pieces(tiles, wk, 112, 96, lsem, 0) + pieces(tiles, wv, 208, 96, lsem, 4) + pieces(tiles, wq, 16, 96, lsem, 8)
    for c in loads:
        c.start()
    c, partner = meet_partner()
    own, other = pl.ds(c * rows, rows), pl.ds((1 - c) * rows, rows)
    swaps = []
    for i, ref in enumerate((dk, dv)):
        out[i] = ref[other, :].astype(bf)
        swaps.append(rcopy(out.at[i], come.at[i], sends.at[i], recvs.at[i], partner))
        swaps[i].start()
    back[0] = dq[...].astype(bf)
    query_bias = jnp.sum(col_sum(dq[...]), axis=0, keepdims=True)
    for copy in loads:
        copy.wait()

    def through(i, w, dw):
        dw[...] = lax.dot_general(low[...], back[i], TN, preferred_element_type=f32).astype(bf).reshape(96, 8, D)
        return lax.dot_general(back[i], matrix(w[...]), NT, preferred_element_type=f32)

    input_grad[...] = gfi[...] + through(0, wq, dwq)
    stores = pieces(grads, dwq, 16, 96, ssem, 0, True)
    swaps[0].wait_recv()
    back[1] = (dk[own, :] + come[0].astype(f32)).astype(bf)
    input_grad[...] += through(1, wk, dwk)
    stores += pieces(grads, dwk, 112, 96, ssem, 4, True)
    swaps[1].wait_recv()
    grad_value = dv[own, :] + come[1].astype(f32)
    value_bias = jnp.sum(col_sum(grad_value), axis=0, keepdims=True)
    back[2] = grad_value.astype(bf)
    total = input_grad[...] + through(2, wv, dwv)
    stores += pieces(grads, dwv, 208, 96, ssem, 8, True)
    input_grad[...] = total
    layout_bias = jnp.sum(col_sum(total), axis=0, keepdims=True)
    dwl[...] = lax.dot_general(feats[...], total.astype(bf), TN, preferred_element_type=f32).astype(bf).reshape(16, 8, D)
    stores += pieces(grads, dwl, 0, 16, ssem, 12, True)

    def block(lines):
        return jnp.concatenate(lines + [jnp.zeros((8 - len(lines), D), f32)]).astype(bf)

    vgrads[0] = block([layout_bias, table[0:1, :]])
    vgrads[1] = block([query_bias])
    vgrads[2] = block([value_bias])
    vgrads[3] = jnp.zeros((8, D), bf)
    held = {0: 0, 1: 1, 4: 2}
    for i, chip in enumerate(ch for ch in range(5)):
        stores.append(pltpu.make_async_copy(vgrads.at[held.get(chip, 3)], grads.at[vector_at(chip)], ssem.at[16 + i]))
    for copy in stores:
        copy.start()
    for copy in stores:
        copy.wait()
    for swap in swaps:
        swap.wait_send()


def leave(tiles, dq, dk, dv, gfi, low, feats, table, grads):
    rows = gfi.shape[0]
    f32, bf = jnp.float32, jnp.bfloat16
    vm, any_ = pl.BlockSpec(memory_space=pltpu.VMEM), pl.BlockSpec(memory_space=pl.ANY)
    S, sem = jax.ShapeDtypeStruct, pltpu.SemaphoreType.DMA
    w = pltpu.VMEM((96, 8, D), bf)
    return pl.pallas_call(
        leave_kernel,
        out_shape=[S((rows, D), f32), S(grads.shape, bf)],
        in_specs=[any_] + [vm] * 7 + [any_],
        out_specs=[vm, any_],
        scratch_shapes=[w, w, w, pltpu.VMEM((2, rows, D), bf), pltpu.VMEM((2, rows, D), bf), pltpu.VMEM((3, rows, D), bf),
                        pltpu.VMEM((16, 8, D), bf), w, w, w, pltpu.VMEM((4, 8, D), bf), sem((12,)), sem((32,)), sem((2,)), sem((2,))],
        input_output_aliases={8: 1},
        compiler_params=pltpu.CompilerParams(collective_id=3, has_side_effects=True, vmem_limit_bytes=56 << 20),
        name="leave",
    )(tiles, dq, dk, dv, gfi, low, feats, table, grads)


def forward_kernel(x_ref, tokens, feats, pad, buckets, lengths,
                   g_ref, hidden, low, query, keys, values, ctx, soft, code_out,
                   xv, tail, head, win, chunk, lsem, hsend, hrecv, own,
                   zs, zr, xas, xar, xbs, xbr, yas, yar, ybs, ybr, cs, cr,
                   pads, hidden_v, low_v, query_v, keys_v, values_v, ctx_v, code, buckets_v, tokens_v, feats_v, p_v, s_scr, tab,
                   wl, wq, wk, wv, vrows, vf, ksend, krecv, wsem, isem, osem, psem):
    f32, bf = jnp.float32, jnp.bfloat16
    rows = tokens.shape[0]
    k, c, z, y, x = place()
    d = 2 * k + c
    inputs = [pltpu.make_async_copy(r, v, isem.at[i]) for i, (r, v) in enumerate(((buckets, buckets_v), (tokens, tokens_v), (feats, feats_v)))]
    for copy in inputs:
        copy.start()
    pads[pl.ds(c, 1)] = pad[...].reshape(1, 8, rows)
    greet(k, c, z, y, x)
    load = pltpu.make_async_copy(x_ref, xv, lsem)
    load.start()
    prev = (jnp.where(c == 1, k, jnp.maximum(k - 1, 0)), 1 - c)
    nxt = (jnp.where(c == 0, k, jnp.minimum(k + 1, 15)), 1 - c)
    to_next = rcopy(x_ref.at[pl.ds(ROWS - TAIL, TAIL)], tail, hsend.at[0], hrecv.at[0], nxt)
    to_prev = rcopy(x_ref.at[pl.ds(0, HEAD)], head, hsend.at[1], hrecv.at[1], prev)

    @pl.when(d < 31)
    def _():
        to_next.start()

    @pl.when(d > 0)
    def _():
        to_prev.start()

    win[...] = jnp.zeros_like(win)
    lanes = lax.broadcasted_iota(jnp.int32, (80, 128), 1)
    q, sh = shard_start(d)
    load.wait()

    @pl.loop(0, ROWS // 80)
    def _(i):
        r = pl.multiple_of(i * 80, 8)
        rolled = pltpu.roll(xv[pl.ds(r, 80), :], sh, 1)
        win[pl.ds(160 + r, 80), :] += jnp.where(lanes >= sh, rolled, 0.0)
        win[pl.ds(161 + r, 80), :] += jnp.where(lanes < sh, rolled, 0.0)

    @pl.when(d > 0)
    def _():
        to_next.wait_recv()
        qp, shp = shard_start(d - 1)
        lanes = lax.broadcasted_iota(jnp.int32, (TAIL, 128), 1)
        rolled = pltpu.roll(tail[...], shp, 1)
        at = 1760 - (q - qp)
        win[pl.ds(at, TAIL), :] += jnp.where(lanes >= shp, rolled, 0.0)
        win[pl.ds(at + 1, TAIL), :] += jnp.where(lanes < shp, rolled, 0.0)

    @pl.when(d < 31)
    def _():
        to_prev.wait_recv()
        qn, shn = shard_start(d + 1)
        lanes = lax.broadcasted_iota(jnp.int32, (HEAD, 128), 1)
        rolled = pltpu.roll(head[...], shn, 1)
        at = 160 + (qn - q)
        win[pl.ds(at, HEAD), :] += jnp.where(lanes >= shn, rolled, 0.0)
        win[pl.ds(at + 1, HEAD), :] += jnp.where(lanes < shn, rolled, 0.0)

    early = early_vectors(k)
    nw0 = jnp.where(early, 36, 37)
    vecs = early == (c == 0)
    first = jnp.where(c == 0, 73 * k, 73 * k + nw0)
    base = q - 160

    @pl.loop(0, SLOTS)
    def _(t):
        at, wide = tile_start(first + t)
        is_vec = vecs & (t == 36)
        at = jnp.where(is_vec, vector_row(k, q), at) - base
        wide = wide & jnp.logical_not(is_vec)

        @pl.when(wide)
        def _():
            parts = [win[pl.ds(at + j, 8, stride=24), :] for j in range(6)]
            chunk[t] = jnp.concatenate(parts, axis=1).astype(jnp.bfloat16)

        @pl.when(jnp.logical_not(wide))
        def _():
            parts = [win[pl.ds(at + j, 8, stride=6), :] for j in range(6)]
            chunk[t] = jnp.concatenate(parts, axis=1).astype(jnp.bfloat16)

    @pl.when(d < 31)
    def _():
        to_next.wait_send()

    @pl.when(d > 0)
    def _():
        to_prev.wait_send()

    xdev, ydev, cdev = (z * 4 + y * 2 + 1 - x, c), (z * 4 + (1 - y) * 2 + x, c), (k, 1 - c)
    zdev = {1: (jnp.minimum(k + 4, 15), c), -1: (jnp.maximum(k - 4, 0), c)}

    def gsl(chip, p):
        off, n = PARTS[p]
        return g_ref.at[chip, pl.ds(37 * c + off, n)]

    def src(chip, p, mine=False):
        off, n = PARTS[p]
        return chunk.at[pl.ds(off, n)] if mine else gsl(chip, p)

    def chip_of(zo, yo, xo):
        return zo * 4 + yo * 2 + xo

    def zcopy(zo, p, way, mine=False):
        chip = chip_of(zo, y, x)
        w = (way + 1) // 2
        return rcopy(src(chip, p, mine), gsl(chip, p), zs.at[w, zo, p], zr.at[zo, p], zdev[way])

    def xcopy(zo, yo, xo, p, mine=False):
        chip = chip_of(zo, yo, xo)
        s, r = (xas, xar) if p == 0 else (xbs, xbr)
        i = zo if p == 0 else zo * 2 + yo
        return rcopy(src(chip, p, mine), gsl(chip, p), s.at[i], r.at[i], xdev)

    def ycopy(zo, yo, xo, p, mine=False):
        chip = chip_of(zo, yo, xo)
        s, r = (ybs, ybr) if p == 1 else (yas, yar)
        i = zo if p == 1 else zo * 2 + xo
        return rcopy(src(chip, p, mine), gsl(chip, p), s.at[i], r.at[i], ydev)

    def ccopy(chip, p, mine=False):
        return rcopy(src(chip, p, mine), gsl(chip, p), cs.at[chip, p], cr.at[chip, p], cdev)

    pair_pads = rcopy(pads.at[pl.ds(c, 1)], pads.at[pl.ds(c, 1)], ksend.at[2], krecv.at[2], cdev)
    pair_pads.start()
    mine = [pltpu.make_async_copy(chunk.at[pl.ds(*PARTS[p])], gsl(k, p), own.at[p]) for p in (0, 1)]

    def own_z(way):
        for p in (0, 1):
            zcopy(z, p, way, True).start()

    def pass_on(zz, zo):
        way = 1 if zo < zz else -1
        for p in (0, 1):
            zcopy(zo, p, way).wait_recv()
            if 0 <= zz + way <= 3:
                zcopy(zo, p, way).start()

    def spread(zz, zo):
        xcopy(zo, y, x, 0).start()
        ycopy(zo, y, x, 1).start()
        ycopy(zo, y, x, 0).start()
        xcopy(zo, y, x, 1).start()
        for p in (0, 1):
            ccopy(chip_of(zo, y, x), p).start()

    def column(zz, zo):
        way = 1 if zo < zz else -1
        for p in (0, 1):
            zcopy(zo, p, way).wait_recv()
            if 0 <= zz + way <= 3:
                zcopy(zo, p, way).start()
            if p == 0:
                xcopy(zo, y, x, 0).start()
                ycopy(zo, y, x, 0).start()
            else:
                ycopy(zo, y, x, 1).start()
                xcopy(zo, y, x, 1).start()
            ccopy(chip_of(zo, y, x), p).start()

    def beside(zz, zo):
        xcopy(zo, y, 1 - x, 0).wait_recv()
        ycopy(zo, y, 1 - x, 0).start()
        ccopy(chip_of(zo, y, 1 - x), 0).start()
        ycopy(zo, 1 - y, x, 1).wait_recv()
        xcopy(zo, 1 - y, x, 1).start()
        ccopy(chip_of(zo, 1 - y, x), 1).start()

    def last(zz, zo):
        ycopy(zo, 1 - y, x, 0).wait_recv()
        ccopy(chip_of(zo, 1 - y, x), 0).start()
        xcopy(zo, y, 1 - x, 1).wait_recv()
        ccopy(chip_of(zo, y, 1 - x), 1).start()
        ycopy(zo, 1 - y, 1 - x, 0).wait_recv()
        ccopy(chip_of(zo, 1 - y, 1 - x), 0).start()
        xcopy(zo, 1 - y, 1 - x, 1).wait_recv()
        ccopy(chip_of(zo, 1 - y, 1 - x), 1).start()

    def raise_own(zz, zo):
        own_z(1)

    before = {
        0: ((beside, 0), (column, 1), (last, 0)),
        1: ((beside, 1), (column, 0), (raise_own, 1), (pass_on, 2), (last, 1), (beside, 0), (pass_on, 3), (spread, 2), (last, 0)),
        2: ((beside, 2), (pass_on, 3), (column, 0), (last, 2), (beside, 0), (column, 1), (last, 0)),
        3: ((beside, 3), (last, 3), (column, 0), (beside, 0), (column, 1), (last, 0)),
    }
    after = {
        0: {0: ((beside, 1), (column, 2)), 1: ((last, 1), (beside, 2)), 2: ((column, 3), (last, 2)), 3: ((beside, 3),), 4: ((last, 3),)},
        1: {0: ((beside, 2), (spread, 3)), 1: ((last, 2),), 2: ((beside, 3),), 3: ((last, 3),)},
        2: {0: ((beside, 1), (spread, 3)), 1: ((last, 1),), 2: ((beside, 3),), 3: ((last, 3),)},
        3: {0: ((beside, 1), (column, 2)), 1: ((last, 1),), 2: ((beside, 2),), 3: ((last, 2),)},
    }

    for way, holds in ((1, (z == 0) | (z == 2)), (-1, z > 0)):
        @pl.when(holds)
        def _():
            own_z(way)
    xcopy(z, y, x, 0, True).start()
    ycopy(z, y, x, 1, True).start()
    ycopy(z, y, x, 0, True).start()
    xcopy(z, y, x, 1, True).start()
    for p in (0, 1):
        mine[p].start()
        ccopy(k, p, True).start()
    for copy in inputs:
        copy.wait()
    pair_pads.wait()
    fill_codes(code, buckets_v, pads, lengths)
    outs = [pltpu.make_async_copy(code, code_out, osem.at[0])]
    outs[0].start()
    for zz in range(4):
        @pl.when(z == zz)
        def _():
            for f, zo in before[zz]:
                f(zz, zo)
    for p in (0, 1):
        mine[p].wait()

    def from_partner(chip):
        for p in (0, 1):
            off, n = PARTS[p]
            theirs = g_ref.at[chip, pl.ds(37 * (1 - c) + off, n)]
            rcopy(theirs, theirs, cs.at[chip, p], cr.at[chip, p], cdev).wait_recv()

    for chip in range(3):
        from_partner(chip)

    tiles = g_ref.reshape(16 * CHIP, 8, D)
    loads = [pltpu.make_async_copy(tiles.at[vector_at(ch)], vrows.at[i], wsem.at[i]) for i, ch in enumerate((0, 1))]
    loads += pieces(tiles, wl, 0, 16, wsem, 4) + pieces(tiles, wk, 112, 96, wsem, 8) + pieces(tiles, wq, 16, 96, wsem, 16)
    for copy in loads:
        copy.start()
    for copy in loads:
        copy.wait()
    vf[0] = vrows[0].astype(f32)
    vf[1] = vrows[1].astype(f32)
    fill_table(tab, vrows.at[0])
    h = tokens_v[...].astype(f32) + jnp.dot(feats_v[...], matrix(wl[...]), preferred_element_type=f32) + vf[0, 0:1, :]
    hidden_v[...] = h
    low_v[...] = h.astype(bf)
    half_rows = pl.ds(c * rows, rows)

    def share(ref, i):
        return rcopy(ref.at[half_rows], ref.at[half_rows], ksend.at[i], krecv.at[i], cdev)

    keys_v[half_rows, :] = jnp.dot(low_v[...], matrix(wk[...]), preferred_element_type=f32).astype(bf)
    share(keys_v, 0).start()
    query_v[...] = ((jnp.dot(low_v[...], matrix(wq[...]), preferred_element_type=f32) + vf[1, 0:1, :]) * 0.125).astype(bf)
    share(keys_v, 0).wait()
    outs += [pltpu.make_async_copy(v, r, osem.at[1 + i]) for i, (v, r) in enumerate(((hidden_v, hidden), (low_v, low), (query_v, query), (keys_v, keys)))]
    for copy in outs[1:]:
        copy.start()

    def make_values():
        for chip in (3, 4):
            from_partner(chip)
        copies = [pltpu.make_async_copy(tiles.at[vector_at(4)], vrows.at[2], wsem.at[2])] + pieces(tiles, wv, 208, 96, wsem, 12)
        for copy in copies:
            copy.start()
        for copy in copies:
            copy.wait()
        vf[2] = vrows[2].astype(f32)
        values_v[half_rows, :] = (jnp.dot(low_v[...], matrix(wv[...]), preferred_element_type=f32) + vf[2, 0:1, :]).astype(bf)
        share(values_v, 1).start()

    def keep(pair):
        return pltpu.make_async_copy(p_v.at[pl.ds(2 * pair, 2)], soft.at[pl.ds(2 * pair, 2)], psem.at[pair])

    def pair_of_heads(pair, _):
        lanes = pl.ds(pl.multiple_of(pair * 128, 128), 128)
        for hh in range(2):
            soft_head(2 * pair + hh, query_v[:, lanes], keys_v[:, lanes], code, tab, s_scr, p_v.at[2 * pair + hh])
        keep(pair).start()
        for i in range(5):
            for zz in range(4):
                if i in after[zz]:
                    @pl.when((pair == i) & (z == zz))
                    def _():
                        for f, zo in after[zz][i]:
                            f(zz, zo)
        pl.when(pair == 2)(make_values)
        return 0

    lax.fori_loop(0, H // 2, pair_of_heads, 0)
    share(values_v, 1).wait()
    outs.append(pltpu.make_async_copy(values_v, values, osem.at[5]))
    outs[-1].start()

    def context(pair, _):
        lanes = pl.ds(pl.multiple_of(pair * 128, 128), 128)
        ctx_v[:, lanes] = context_pair(values_v[:, lanes], p_v.at[pl.ds(2 * pair, 2)])
        return 0

    lax.fori_loop(0, H // 2, context, 0)
    outs.append(pltpu.make_async_copy(ctx_v, ctx, osem.at[6]))
    outs[-1].start()

    for p in (0, 1):
        for way in (1, -1):
            for zo in range(4):
                @pl.when(((z - zo) * way >= 0) & (z + way >= 0) & (z + way <= 3))
                def _():
                    zcopy(zo, p, way).wait_send()
    for zo in range(4):
        xcopy(zo, y, x, 0).wait_send()
        ycopy(zo, y, x, 1).wait_send()
        for o in range(2):
            ycopy(zo, y, o, 0).wait_send()
            xcopy(zo, o, x, 1).wait_send()
    for chip in range(16):
        for p in (0, 1):
            ccopy(chip, p).wait_send()
    for chip in range(5, 16):
        from_partner(chip)
    for pair in range(H // 2):
        keep(pair).wait()
    for copy in outs:
        copy.wait()


def gather_and_attend(master, tokens, feats, pad, buckets, page_lengths):
    x = jnp.pad(master, (0, ROWS * 128 - SHARD)).reshape(ROWS, 128)
    sem = pltpu.SemaphoreType.DMA
    any_, vm = pl.BlockSpec(memory_space=pl.ANY), pl.BlockSpec(memory_space=pltpu.VMEM)
    rows, key_rows = buckets.shape
    f32, bf = jnp.float32, jnp.bfloat16
    S, V = jax.ShapeDtypeStruct, pltpu.VMEM
    w = V((96, 8, D), bf)
    return pl.pallas_call(
        forward_kernel,
        out_shape=[
            S((16, CHIP, 8, D), bf), S((rows, D), f32), S((rows, D), bf), S((rows, D), bf), S((key_rows, D), bf), S((key_rows, D), bf),
            S((rows, D), bf), S((H, key_rows, rows), bf), S((key_rows, rows), jnp.int32),
        ],
        in_specs=[any_, any_, any_, vm, any_, pl.BlockSpec(memory_space=pltpu.SMEM)],
        out_specs=[any_] * 9,
        scratch_shapes=[
            V((ROWS, 128), f32), V((TAIL, 128), f32), V((HEAD, 128), f32), V((WIN, 128), f32), V((SLOTS, 8, D), bf),
            sem, sem((2,)), sem((2,)), sem((2,)),
            sem((2, 4, 2)), sem((4, 2)),
            sem((4,)), sem((4,)), sem((8,)), sem((8,)),
            sem((8,)), sem((8,)), sem((4,)), sem((4,)),
            sem((16, 2)), sem((16, 2)),
            V((2, 8, rows), jnp.int32), V((rows, D), f32), V((rows, D), bf), V((rows, D), bf), V((key_rows, D), bf), V((key_rows, D), bf),
            V((rows, D), bf), V((key_rows, rows), jnp.int32), V((rows, key_rows), jnp.int32), V((rows, D), bf), V((rows, LF), bf),
            V((H, key_rows, rows), bf), V((key_rows, rows), f32), V((16, 128), f32),
            V((16, 8, D), bf), w, w, w, V((3, 8, D), bf), V((3, 8, D), f32),
            sem((3,)), sem((3,)), sem((20,)), sem((3,)), sem((7,)), sem((H // 2,)),
        ],
        compiler_params=pltpu.CompilerParams(collective_id=0, has_side_effects=True, vmem_limit_bytes=60 << 20),
        name="gather_and_attend",
    )(x, tokens, feats, pad, buckets, page_lengths)


def guarded(cond, f):
    if cond is True:
        f()
    elif cond is not False:
        pl.when(cond)(f)


class Reducer:
    def __init__(self, where, zs, want, spare, g_ref, acc, crecv, a1, b1, a2, b2, asem, cs, cr, a1s, a1r, b1s, b1r, a2s, a2r, b2s, b2r):
        self.k, self.c, self.z, self.y, self.x = where
        self.zs, self.want, self.spare = zs, want, spare
        self.g_ref, self.acc, self.crecv = g_ref, acc, crecv
        self.bufs = (a1, b1, a2, b2)
        self.asem, self.cs, self.cr = asem, cs, cr
        self.sems = ((a1s, a1r), (b1s, b1r), (a2s, a2r), (b2s, b2r))
        z, y, x, c = self.z, self.y, self.x, self.c
        self.xdev, self.ydev, self.cdev = (z * 4 + y * 2 + 1 - x, c), (z * 4 + (1 - y) * 2 + x, c), (self.k, 1 - c)

    def at(self, zo, oy, ox):
        return zo, (1 - self.y if oy else self.y), (1 - self.x if ox else self.x)

    def chip(self, zo, yo, xo):
        return zo * 4 + yo * 2 + xo

    def local(self, zo, yo, xo):
        return self.chip(zo, yo, xo)

    def load(self, item):
        i = self.local(*item)
        return pltpu.make_async_copy(self.g_ref.at[self.chip(*item), pl.ds(37 * self.c, 37)], self.acc.at[i], self.asem.at[i])

    def ccopy(self, item):
        i = self.local(*item)
        return rcopy(self.g_ref.at[self.chip(*item), pl.ds(37 * (1 - self.c), 37)], self.crecv.at[i + self.spare], self.cs.at[i], self.cr.at[i], self.cdev)

    def hop(self, which, item, slot, p, dev):
        s, r = self.sems[which]
        return rcopy(self.acc.at[self.local(*item), pl.ds(*PARTS[p])], self.bufs[which].at[slot], s.at[slot], r.at[slot], dev)

    def a1(self, zo, xo):
        return self.hop(0, (zo, 1 - self.y, xo), self.zs.index(zo) * 2 + xo, 0, self.ydev)

    def b1(self, zo, yo):
        return self.hop(1, (zo, yo, 1 - self.x), self.zs.index(zo) * 2 + yo, 1, self.xdev)

    def a2(self, zo):
        return self.hop(2, (zo, self.y, 1 - self.x), self.zs.index(zo), 0, self.xdev)

    def b2(self, zo):
        return self.hop(3, (zo, 1 - self.y, self.x), self.zs.index(zo), 1, self.ydev)

    def gain(self, item, p, which, slot):
        off, n = PARTS[p]
        i, acc, buf = self.local(*item), self.acc, self.bufs[which]
        acc[i, pl.ds(off, n)] = acc[i, pl.ds(off, n)] + buf[slot]

    def begin(self, zo, oy, ox):
        item = self.at(zo, oy, ox)

        def go():
            self.load(item).start()
            self.ccopy(item).start()
        guarded(self.want(*item), go)

    def first(self, zo, oy, ox):
        item = self.at(zo, oy, ox)

        def go():
            self.load(item).wait()
            self.ccopy(item).wait_recv()
            i = self.local(*item)
            self.acc[i] = self.acc[i] + self.crecv[i + self.spare]
            if oy:
                self.a1(zo, item[2]).start()
            if ox:
                self.b1(zo, item[1]).start()
        guarded(self.want(*item), go)

    def second(self, zo):
        ia, ib = self.at(zo, 0, 1), self.at(zo, 1, 0)
        n = self.zs.index(zo) * 2

        def go_a():
            self.a1(zo, 1 - self.x).wait_recv()
            self.gain(ia, 0, 0, n + 1 - self.x)
            self.a2(zo).start()

        def go_b():
            self.b1(zo, 1 - self.y).wait_recv()
            self.gain(ib, 1, 1, n + 1 - self.y)
            self.b2(zo).start()
        guarded(self.want(*ia), go_a)
        guarded(self.want(*ib), go_b)

    def third(self, zo):
        item = self.at(zo, 0, 0)
        n = self.zs.index(zo)

        def go():
            self.a1(zo, self.x).wait_recv()
            self.b1(zo, self.y).wait_recv()
            self.a2(zo).wait_recv()
            self.b2(zo).wait_recv()
            i = self.local(*item)
            for p, (h, u), at in ((0, (0, 2), self.x), (1, (1, 3), self.y)):
                off, m = PARTS[p]
                self.acc[i, pl.ds(off, m)] = (self.acc[i, pl.ds(off, m)] + self.bufs[h][n * 2 + at]) + self.bufs[u][n]
        guarded(self.want(*item), go)

    def finish(self):
        for zo in self.zs:
            for oy in (0, 1):
                for ox in (0, 1):
                    item = self.at(zo, oy, ox)

                    def sent(item=item, oy=oy, ox=ox, zo=zo):
                        self.ccopy(item).wait_send()
                        if oy:
                            self.a1(zo, item[2]).wait_send()
                        if ox:
                            self.b1(zo, item[1]).wait_send()
                        if ox and not oy:
                            self.a2(zo).wait_send()
                        if oy and not ox:
                            self.b2(zo).wait_send()
                    guarded(self.want(*item), sent)


def reducer_scratch():
    bf, sem = jnp.bfloat16, pltpu.SemaphoreType.DMA
    tile = (8, D)
    return [
        pltpu.VMEM((16, 37) + tile, bf), pltpu.VMEM((11, 37) + tile, bf),
        pltpu.VMEM((8, 19) + tile, bf), pltpu.VMEM((8, 18) + tile, bf), pltpu.VMEM((4, 19) + tile, bf), pltpu.VMEM((4, 18) + tile, bf),
        sem((16,)), sem((16,)), sem((16,)),
        sem((8,)), sem((8,)), sem((8,)), sem((8,)), sem((4,)), sem((4,)), sem((4,)), sem((4,)),
    ]


def early_item(zo, yo, xo):
    return zo >= 2 if zo != 1 else yo + xo > 0


def late_item(zo, yo, xo):
    return zo == 0 if zo != 1 else yo + xo == 0


ZCUTS = ((0, 10), (10, 9), (19, 9), (28, 9))


class Chain:
    def __init__(self, where, acc, up, dn, us, ur, ds_, dr):
        self.k, self.c, self.z, self.y, self.x = where
        self.acc = acc
        self.ways = {1: (up, us, ur, (jnp.minimum(self.k + 4, 15), self.c)), -1: (dn, ds_, dr, (jnp.maximum(self.k - 4, 0), self.c))}

    def chip(self, zo):
        return zo * 4 + self.y * 2 + self.x

    def copy(self, zo, way, p):
        buf, s, r, dev = self.ways[way]
        part = pl.ds(*ZCUTS[p])
        return rcopy(self.acc.at[self.chip(zo), part], buf.at[zo, part], s.at[zo, p], r.at[zo, p], dev)

    def move(self, zs, zo, way, take=True, give=True, also=None):
        cond = self.z == zs if also is None else (self.z == zs) & also

        @pl.when(cond)
        def _():
            i = self.chip(zo)
            for p in range(4):
                if take:
                    self.copy(zo, way, p).wait_recv()
                    part = pl.ds(*ZCUTS[p])
                    self.acc[i, part] = self.acc[i, part] + self.ways[way][0][zo, part]
                if give:
                    self.copy(zo, way, p).start()

    def sent(self, zs, zo, way):
        @pl.when(self.z == zs)
        def _():
            for p in range(4):
                self.copy(zo, way, p).wait_send()


def chain_scratch():
    bf, sem = jnp.bfloat16, pltpu.SemaphoreType.DMA
    return [pltpu.VMEM((4, 37, 8, D), bf)] * 2 + [sem((4, 4))] * 4


def backward_kernel(tiles, q_ref, k_ref, v_ref, do_ref, p_hbm, code_hbm, gfi_in, low_in, feats_in, grads_in, m_ref, one_ref, two_ref,
                    grad_out, grads, step_ref, new1_ref, new2_ref, spread,
                    pbuf, qv, kv, vv, dov, psem, code_ref, csem, dsv, dssem, group, gsem, counts, dks, dvs, out, come, sends, recvs, back, bias,
                    wq, wk, wv, low, gfi, feats, dwl, dwq, dwk, dwv, vgrads, wsem, ssem, isem,
                    total, ebuf, sq, sqr, win, mv, onev, twov, lsem, es, er, qs, qr, *scratch):
    f32, bf = jnp.float32, jnp.bfloat16
    where = place()
    k, c, z, y, x = where
    d = 2 * k + c
    shared = grads.reshape(16, CHIP, 8, D)
    rs = Reducer(where, (0, 1, 2, 3), early_item, -5, shared, *scratch[:17])
    late = Reducer(where, (0, 1, 2, 3), late_item, 6, shared, *scratch[:17])
    acc = rs.acc
    zc = Chain(where, acc, *scratch[17:])
    xdev, ydev, cdev = rs.xdev, rs.ydev, rs.cdev
    column_devs = [((z + s) % 4 * 4 + y * 2 + x, c) for s in (1, 2, 3)]
    prev = (jnp.where(c == 1, k, jnp.maximum(k - 1, 0)), 1 - c)
    nxt = (jnp.where(c == 0, k, jnp.minimum(k + 1, 15)), 1 - c)
    bar = pltpu.get_barrier_semaphore()
    far_next, far_prev = (c == 1) & (k < 15), (c == 0) & (k > 0)
    for dev in [xdev, ydev, cdev] + column_devs:
        pl.semaphore_signal(bar, inc=1, device_id=dev, device_id_type=MESH)

    @pl.when(far_next)
    def _():
        pl.semaphore_signal(bar, inc=1, device_id=nxt, device_id_type=MESH)

    @pl.when(far_prev)
    def _():
        pl.semaphore_signal(bar, inc=1, device_id=prev, device_id_type=MESH)

    keys, rows = code_ref.shape

    def fetch_soft(pair, hh):
        return pltpu.make_async_copy(p_hbm.at[2 * pair + hh], pbuf.at[hh], psem.at[0, hh])

    def fetch(p):
        slot = p % 2
        lanes = pl.ds(pl.multiple_of(p * 128, 128), 128)
        return [pltpu.make_async_copy(r.at[:, lanes], v.at[slot], psem.at[1 + i, slot]) for i, (r, v) in enumerate(((q_ref, qv), (k_ref, kv), (v_ref, vv), (do_ref, dov)))]

    for copy in fetch(0) + [fetch_soft(0, 0), fetch_soft(0, 1)]:
        copy.start()
    pl.semaphore_wait(bar, 6 + jnp.where(far_next | far_prev, 1, 0))
    corners = ((1, 1), (1, 0), (0, 1), (0, 0))
    for zo in (3, 2):
        for oy, ox in corners:
            rs.begin(zo, oy, ox)
    code_copy = pltpu.make_async_copy(code_hbm, code_ref, csem.at[0])
    inputs = [pltpu.make_async_copy(r, v, isem.at[i]) for i, (r, v) in enumerate(((low_in, low), (gfi_in, gfi), (feats_in, feats)))]
    loads = pieces(tiles, wq, 16, 96, wsem, 8) + pieces(tiles, wv, 208, 96, wsem, 4) + pieces(tiles, wk, 112, 96, wsem, 0)
    shards = [pltpu.make_async_copy(r, v, lsem.at[i]) for i, (r, v) in enumerate(((m_ref, mv), (one_ref, onev), (two_ref, twov)))]
    for copy in [code_copy] + inputs + loads + shards:
        copy.start()
    own, other = pl.ds(c * rows, rows), pl.ds((1 - c) * rows, rows)

    def swap(pair):
        return rcopy(out.at[pair], come.at[pair], sends.at[pair], recvs.at[pair], cdev)

    def settle(pair):
        slot = pair % 2
        swap(pair).wait_recv()
        lanes = pl.ds(pl.multiple_of(pair * 128, 128), 128)
        dk = dks[slot, own, :] + come[pair, 0].astype(f32)
        dv = dvs[slot, own, :] + come[pair, 1].astype(f32)
        back[1, :, lanes] = dk.astype(bf)
        back[2, :, lanes] = dv.astype(bf)
        bias[1, :, lanes] = col_sum(dv)

    def lay(pair, hh):
        return pltpu.make_async_copy(dsv.at[hh], spread.at[:, 2 * pair + hh], dssem.at[hh])

    plan = {
        0: [(rs.first, 3, 1, 0), (rs.first, 3, 0, 1), (rs.first, 2, 1, 1)],
        1: [(rs.second, 3), (rs.first, 2, 1, 0), (rs.first, 2, 0, 1)],
        2: [(rs.first, 3, 0, 0), (rs.first, 2, 0, 0), (rs.begin, 1, 1, 1), (rs.begin, 1, 1, 0), (rs.begin, 1, 0, 1), (rs.begin, 1, 0, 0)],
        3: [(rs.second, 2), (rs.third, 3), (zc.move, 0, 3, 1, False)],
        5: [(rs.third, 2), (zc.move, 0, 2, 1, False), (zc.move, 3, 2, -1, False), (zc.move, 1, 3, 1)],
    }
    rs.first(3, 1, 1)

    def pair_of_heads(pair, _):
        slot = pair % 2

        @pl.when(pair < H // 2 - 1)
        def _():
            for copy in fetch(pair + 1):
                copy.start()

        for copy in fetch(pair):
            copy.wait()
        lanes = pl.ds(pl.multiple_of(pair * 128, 128), 128)
        dq = []
        for hh in range(2):
            fetch_soft(pair, hh).wait()
            qm = half(qv[slot], hh)
            dom = half(dov[slot], hh)
            g = lax.dot_general(vv[slot], dom, NT, preferred_element_type=f32)
            p = pbuf[hh]
            pf = p.astype(f32)
            inner = jnp.sum(jnp.sum((g * pf).reshape(keys // 8, 8, rows), axis=0), axis=0, keepdims=True)
            ds = (pf * (g - inner)).astype(bf)

            @pl.when(pair > 0)
            def _():
                lay(pair - 1, hh).wait()

            dsv[hh] = ds.reshape(keys // 8, 8, rows)
            lay(pair, hh).start()
            dv = jnp.dot(p, dom, preferred_element_type=f32)

            @pl.when(pair < H // 2 - 1)
            def _():
                fetch_soft(pair + 1, hh).start()

            dk = jnp.dot(ds, qm, preferred_element_type=f32)
            if hh == 0:
                dvs[slot] = dv
                dks[slot] = dk
            else:
                dvs[slot] += dv
                dks[slot] += dk
            dq.append(lax.dot_general(kv[slot], ds, TN, preferred_element_type=f32))
        out[pair, 0] = dks[slot, other, :].astype(bf)
        out[pair, 1] = dvs[slot, other, :].astype(bf)
        swap(pair).start()
        sub = lax.broadcasted_iota(jnp.int32, dq[0].shape, 0)
        dqf = jnp.where(sub < 64, dq[0], dq[1]).T * 0.125
        back[0, :, lanes] = dqf.astype(bf)
        bias[0, :, lanes] = col_sum(dqf)

        @pl.when(pair > 0)
        def _():
            settle(pair - 1)

        for i, steps in plan.items():
            @pl.when(pair == i)
            def _():
                for f, *a in steps:
                    f(*a)
        return 0

    lax.fori_loop(0, H // 2, pair_of_heads, 0)
    for hh in range(2):
        lay(H // 2 - 1, hh).wait()
    for copy in inputs + loads:
        copy.wait()

    def through(i, w, dw):
        dw[...] = lax.dot_general(low[...], back[i], TN, preferred_element_type=f32).astype(bf).reshape(96, 8, D)
        return lax.dot_general(back[i], matrix(w[...]), NT, preferred_element_type=f32)

    stores = []

    def keep(dw, first, count, base):
        made = pieces(grads, dw, first, count, ssem, base, True)
        for copy in made:
            copy.start()
        stores.extend(made)

    gfi[...] += through(0, wq, dwq)
    keep(dwq, 16, 96, 0)
    settle(H // 2 - 1)
    gfi[...] += through(2, wv, dwv)
    keep(dwv, 208, 96, 8)
    whole = gfi[...] + through(1, wk, dwk)
    keep(dwk, 112, 96, 4)
    gfi[...] = whole
    shown = pltpu.make_async_copy(gfi, grad_out, isem.at[6])
    shown.start()
    layout_bias = jnp.sum(col_sum(whole), axis=0, keepdims=True)
    dwl[...] = lax.dot_general(feats[...], whole.astype(bf), TN, preferred_element_type=f32).astype(bf).reshape(16, 8, D)
    keep(dwl, 0, 16, 12)

    def block(lines):
        return jnp.concatenate(lines + [jnp.zeros((8 - len(lines), D), f32)]).astype(bf)

    vgrads[0] = block([layout_bias])
    vgrads[1] = block([jnp.sum(bias[0], axis=0, keepdims=True)])
    vgrads[2] = block([jnp.sum(bias[1], axis=0, keepdims=True)])
    vgrads[3] = jnp.zeros((8, D), bf)
    held = {0: 0, 1: 1, 4: 2}
    for i, ch in enumerate((0, 1, 2, 3, 4)):
        copy = pltpu.make_async_copy(vgrads.at[held.get(ch, 3)], grads.at[vector_at(ch)], ssem.at[16 + i])
        copy.start()
        stores.append(copy)
    for copy in stores:
        copy.wait()
    for oy, ox in corners:
        for zo in (0, 1):
            late.begin(zo, oy, ox)

    GROUPS = 16

    def take_groups(i):
        return pltpu.make_async_copy(spread.at[pl.ds(i * GROUPS, GROUPS)], group.at[i % 2], gsem.at[i % 2])

    bucket = lax.broadcasted_iota(jnp.int32, (BUCKETS, rows), 0)
    steps = keys // 8 // GROUPS
    code_copy.wait()
    take_groups(0).start()
    counts[...] = jnp.zeros_like(counts)

    def count_some(first, n):
        for i in range(first, first + n):
            if i + 1 < steps:
                take_groups(i + 1).start()
            take_groups(i).wait()

            def count(j, run, i=i):
                code = code_ref[pl.ds(pl.multiple_of((i * GROUPS + j) * 8, 8), 8), :]
                hot = jnp.concatenate(
                    [jnp.where(jnp.broadcast_to(code[r : r + 1], bucket.shape) == bucket, 1.0, 0.0) for r in range(8)]
                ).astype(bf)
                return run + lax.dot_general(group[i % 2, j].reshape(8 * H, rows), hot, NT, preferred_element_type=f32)

            counts[...] = lax.fori_loop(0, GROUPS, count, counts[...], unroll=8)

    early_one, late_one = rs.want(1, y, x), late.want(1, y, x)
    for oy, ox in corners[:3]:
        late.first(0, oy, ox)
    for oy, ox in corners[:3]:
        late.first(1, oy, ox)
    late.second(0)
    late.second(1)
    rs.first(1, 1, 1)
    rs.first(1, 1, 0)
    rs.first(1, 0, 1)
    late.first(0, 0, 0)
    zc.move(2, 3, 1)
    count_some(0, 1)
    late.third(0)
    zc.move(3, 0, -1, take=False)
    late.first(1, 0, 0)
    late.third(1)
    zc.move(0, 1, 1, take=False, also=late_one)
    zc.move(3, 1, -1, take=False, also=late_one)
    rs.second(1)
    rs.first(1, 0, 0)
    zc.move(1, 2, 1)
    count_some(1, 1)
    zc.move(2, 0, -1)
    zc.move(2, 1, -1, also=late_one)
    count_some(2, 2)
    zc.move(1, 0, -1)
    rs.third(1)
    zc.move(0, 1, 1, take=False, also=early_one)
    zc.move(3, 1, -1, take=False, also=early_one)
    count_some(4, 3)
    zc.move(2, 1, -1, also=early_one)
    count_some(7, 1)
    table = table_row(counts[...], (8, D))

    total[...] = acc[k].astype(f32)

    def add(way, zo):
        buf = zc.ways[way][0]
        for p in range(4):
            zc.copy(zo, way, p).wait_recv()
        total[...] = total[...] + buf[zo].astype(f32)

    @pl.when(z == 0)
    def _():
        add(-1, 0)

    @pl.when(z == 1)
    def _():
        add(1, 1)
        add(-1, 1)

    @pl.when(z == 2)
    def _():
        add(1, 2)
        add(-1, 2)

    @pl.when(z == 3)
    def _():
        add(1, 3)

    early = early_vectors(k)
    nw0 = jnp.where(early, 36, 37)
    vecs = early == (c == 0)
    mine = jnp.where(vecs, 36, 37)
    to_next = rcopy(total.at[pl.ds(mine - EDGE, EDGE)], ebuf.at[0], es.at[0], er.at[0], nxt)
    to_prev = rcopy(total.at[pl.ds(0, EDGE)], ebuf.at[1], es.at[1], er.at[1], prev)

    @pl.when(d < 31)
    def _():
        to_next.start()

    @pl.when(d > 0)
    def _():
        to_prev.start()

    def square(i, run):
        t = total[i]
        t = t * t
        for j in range(6):
            run = run + t[:, 128 * j:128 * j + 128]
        return run

    squares = lax.fori_loop(0, 37, square, jnp.zeros((8, 128), f32))
    lines = [jnp.sum(squares, axis=0, keepdims=True)] + [table[0:1, 128 * i : 128 * i + 128] for i in range(3)]
    sq[0] = jnp.concatenate(lines + [jnp.zeros((4, 128), f32)])
    rounds = [rcopy(sq.at[i], sqr.at[i], qs.at[i], qr.at[i], dev) for i, dev in enumerate((cdev, xdev, ydev))]
    hops = [rcopy(sq.at[3], sqr.at[3 + i], qs.at[3 + i], qr.at[3 + i], column_devs[i]) for i in range(3)]
    rounds[0].start()
    q, sh = shard_start(d)
    base = q - FRONT

    def flatten(ref, i, at, wide):
        @pl.when(wide)
        def _():
            t = ref[i]
            for j in range(6):
                win[pl.ds(at + j, 8, stride=24), :] = t[:, 128 * j:128 * j + 128]

        @pl.when(jnp.logical_not(wide))
        def _():
            t = ref[i]
            for j in range(6):
                win[pl.ds(at + j, 8, stride=6), :] = t[:, 128 * j:128 * j + 128]

    own_vectors = vecs & (vector_row(k, -1) >= 0)

    @pl.when(own_vectors)
    def _():
        flatten(total, 36, vector_row(k, q) - base, k < 0)

    w0 = jnp.where(c == 0, 73 * k, 73 * k + nw0)

    @pl.loop(0, mine)
    def _(t):
        at, wide = tile_start(w0 + t)
        flatten(total, t, at - base, wide)

    rounds[0].wait_recv()
    sq[1] = sq[0] + sqr[0]
    rounds[1].start()
    @pl.when(d > 0)
    def _():
        to_next.wait_recv()

        @pl.loop(0, EDGE)
        def _(t):
            at, wide = tile_start(w0 - EDGE + t)
            flatten(ebuf.at[0], t, at - base, wide)

    @pl.when(d < 31)
    def _():
        to_prev.wait_recv()

        @pl.loop(0, EDGE)
        def _(t):
            at, wide = tile_start(w0 + mine + t)
            flatten(ebuf.at[1], t, at - base, wide)

    rounds[1].wait_recv()
    sq[2] = sq[1] + sqr[1]
    rounds[2].start()
    rounds[2].wait_recv()
    sq[3] = sq[2] + sqr[2]
    for h in hops:
        h.start()
    for h in hops:
        h.wait_recv()
    summed = (sq[3] + sqr[4]) + (sqr[3] + sqr[5])

    @pl.when(d == 0)
    def _():
        for i in range(3):
            win[pl.ds(FRONT + 774 + i, 1), :] = summed[1 + i : 2 + i]

    sub = lax.broadcasted_iota(jnp.int32, (8, 128), 0)
    entries = jnp.where(sub == 0, summed, jnp.where(sub < 4, summed * summed, 0.0))
    square_sum = jnp.sum(jnp.sum(entries, axis=1, keepdims=True), axis=0, keepdims=True)
    factor = jnp.minimum(1.0, lax.rsqrt(square_sum / RAW + 1e-06))
    for s in shards:
        s.wait()
    lanes = lax.broadcasted_iota(jnp.int32, (80, 128), 1)
    rowi = lax.broadcasted_iota(jnp.int32, (80, 128), 0)
    back = (128 - sh) % 128

    @pl.loop(0, ROWS // 80)
    def _(i):
        r = pl.multiple_of(i * 80, 8)
        here = pltpu.roll(win[pl.ds(FRONT + r, 80), :], back, 1)
        there = pltpu.roll(win[pl.ds(FRONT + 1 + r, 80), :], back, 1)
        grad = jnp.where(lanes < 128 - sh, here, there) * factor
        entry = (d == 0) & (rowi + r < ENTRY_ROWS)
        rate = jnp.where(entry, learn_rate * layer_decay, learn_rate)
        one = beta_one * onev[pl.ds(r, 80), :] + (1.0 - beta_one) * grad
        two = beta_two * twov[pl.ds(r, 80), :] + (1.0 - beta_two) * grad * grad
        fixed_one = one / (1.0 - beta_one ** STEP)
        fixed_two = two / (1.0 - beta_two ** STEP)
        step = -rate * (fixed_one / (jnp.sqrt(fixed_two) + adam_eps) + weight_decay * mv[pl.ds(r, 80), :])
        mv[pl.ds(r, 80), :] = step
        onev[pl.ds(r, 80), :] = one
        twov[pl.ds(r, 80), :] = two

    results = [pltpu.make_async_copy(v, r, lsem.at[i]) for i, (v, r) in enumerate(((mv, step_ref), (onev, new1_ref), (twov, new2_ref)))]
    for copy in results:
        copy.start()

    for h in rounds + hops:
        h.wait_send()

    @pl.when(d < 31)
    def _():
        to_next.wait_send()

    @pl.when(d > 0)
    def _():
        to_prev.wait_send()

    rs.finish()
    late.finish()
    for zs in (0, 1, 2):
        zc.sent(zs, 3, 1)
    for zs in (0, 1):
        zc.sent(zs, 2, 1)
    zc.sent(3, 2, -1)
    zc.sent(0, 1, 1)
    zc.sent(3, 1, -1)
    zc.sent(2, 1, -1)
    for zs in (1, 2, 3):
        zc.sent(zs, 0, -1)
    for pair in range(H // 2):
        swap(pair).wait_send()
    shown.wait()
    for copy in results:
        copy.wait()


def backward_and_step(tiles, query, key_all, value_all, grad_context, soft, code, gfi, low, feats, grads, master, first_moment, second_moment):
    def rows_of(v):
        return jnp.pad(v, (0, ROWS * 128 - SHARD)).reshape(ROWS, 128)

    rows, keys = query.shape[0], key_all.shape[0]
    f32, bf = jnp.float32, jnp.bfloat16
    any_ = pl.BlockSpec(memory_space=pl.ANY)
    S, V, sem = jax.ShapeDtypeStruct, pltpu.VMEM, pltpu.SemaphoreType.DMA
    w = V((96, 8, D), bf)
    tile = (8, D)
    line = V((ROWS, 128), f32)
    outs = pl.pallas_call(
        backward_kernel,
        out_shape=[S((rows, D), f32), S(grads.shape, bf)] + [S((ROWS, 128), f32)] * 3 + [S((keys // 8, H, 8, rows), bf)],
        in_specs=[any_] * 14,
        out_specs=[any_] * 6,
        scratch_shapes=[
            V((2, keys, rows), bf), V((2, rows, 128), bf), V((2, keys, 128), bf), V((2, keys, 128), bf), V((2, rows, 128), bf), sem((5, 2)),
            V((keys, rows), jnp.int32), sem((1,)), V((2, keys // 8, 8, rows), bf), sem((2,)), V((2, 16, H, 8, rows), bf), sem((2,)),
            V((8 * H, 8 * BUCKETS), f32),
            V((2, keys, 128), f32), V((2, keys, 128), f32), V((6, 2, rows, 128), bf), V((6, 2, rows, 128), bf), sem((6,)), sem((6,)),
            V((3, rows, D), bf), V((2, 8, D), f32),
            w, w, w, V((rows, D), bf), V((rows, D), f32), V((rows, LF), bf), V((16, 8, D), bf), w, w, w, V((4, 8, D), bf),
            sem((12,)), sem((24,)), sem((7,)),
            V((37,) + tile, f32), V((2, EDGE) + tile, f32), V((4, 8, 128), f32), V((6, 8, 128), f32),
            V((WIN2, 128), f32), line, line, line, sem((3,)), sem((2,)), sem((2,)), sem((6,)), sem((6,)),
        ] + reducer_scratch() + chain_scratch(),
        input_output_aliases={10: 1},
        compiler_params=pltpu.CompilerParams(collective_id=5, has_side_effects=True, vmem_limit_bytes=63 << 20),
        name="backward_and_step",
    )(tiles, query, key_all, value_all, grad_context, soft, code, gfi, low, feats, grads, rows_of(master), rows_of(first_moment), rows_of(second_moment))
    return outs[0], [o.reshape(-1)[:SHARD] for o in outs[2:5]]


def from_tiles(tiles):
    got = {}
    for name, first, count in WEIGHTS:
        block = jnp.concatenate([tiles[s : s + n] for s, _, n in slots_of(first, count)])
        if name == 12:
            block = block.reshape(96, 4, 8, D).transpose(0, 2, 1, 3)
        got[name] = block.reshape(-1, FF if name == 12 else D)
    for name, chip, row in VECTORS:
        block = tiles[vector_at(chip)]
        if name == 13:
            got[name] = block[row : row + 4].reshape(FF)
        elif name == 2:
            got[name] = block[row, : BUCKETS * H].reshape(BUCKETS, H)
        else:
            got[name] = block[row]
    return [got[i] for i in range(18)]


def to_tiles(whole):
    by_name = [p.astype(jnp.bfloat16) for p in whole]
    weights = []
    for name, first, count in WEIGHTS:
        got = by_name[name]
        if name == 12:
            got = got.reshape(96, 8, 4, D).transpose(0, 2, 1, 3)
        weights.append(got.reshape(count, 8, D))
    cuts = []
    for chip in range(16):
        held = [(r, by_name[n]) for n, c, r in VECTORS if c == chip]
        rows = [jnp.pad(v.reshape(-1), (0, -v.size % D)).reshape(-1, D) for _, v in held]
        block = jnp.concatenate(rows + [jnp.zeros((8 - sum(r.shape[0] for r in rows), D), jnp.bfloat16)])
        cuts.append((73 * chip + vector_slot(chip), block[None]))
    parts = []
    for (name, first, count), tiles in zip(WEIGHTS, weights):
        at = first
        for w, block in [c for c in cuts if first <= c[0] < first + count]:
            if w > at:
                parts.append(tiles[at - first : w - first])
            parts.append(block)
            at = w
        parts.append(tiles[at - first :])
    parts.extend(block for w, block in cuts if w == 1168)
    return jnp.concatenate(parts)


def per_device(
    custom, tokens, cotangent, page_boxes, page_lengths, padding, buckets, master, first_moment, second_moment
):
    rows = tokens.shape[1]
    feats = layout_features(page_boxes.reshape(4, rows)).astype(jnp.bfloat16)
    pad = jnp.broadcast_to(padding, (8, rows))
    if custom:
        tiles, hidden, low, query, keys, values, ctx, soft, code = gather_and_attend(
            master, tokens[0], feats, pad, buckets[0], page_lengths
        )
        tiles = tiles.reshape(16 * CHIP, 8, D)
    else:
        tiles = to_tiles(unpack(lax.all_gather(master.astype(jnp.bfloat16), ("dp", "seq"), axis=0, tiled=True)))
        hidden, low, query, keys, values, pads = enter(tiles, tokens[0], feats, pad)
        ctx, soft, code = attend(query, keys, values, buckets[0], page_lengths, pads, tiles[vector_at(0)])
    activations, grad_first_in, grad_context, grads = middle(tiles, ctx, hidden, cotangent[0])
    if custom:
        input_grad, stepped = backward_and_step(
            tiles, query, keys, values, grad_context, soft, code, grad_first_in, low, feats, grads, master, first_moment, second_moment
        )
    else:
        dq, dk, dv, table = soft_back(query, keys, values, grad_context, soft, code)
        input_grad, grads = leave(tiles, dq, dk, dv, grad_first_in, low, feats, table, grads)
        flat = jnp.concatenate([p.astype(jnp.float32).reshape(-1) for p in from_tiles(grads)])
        grad = lax.psum_scatter(flat, ("dp", "seq"), scatter_dimension=0, tiled=True)
        square = lax.psum(jnp.sum(grad * grad), ("dp", "seq"))
        factor = jnp.minimum(1.0, lax.rsqrt(square / RAW + 1e-06))
        size = master.shape[0]
        index = lax.axis_index(("dp", "seq")) * size + jnp.arange(size, dtype=jnp.int32)
        stepped = adam_update(master, first_moment, second_moment, grad * factor, index)
    return (activations[None], input_grad[None]) + tuple(stepped)


def solution(mesh):
    in_specs = (
        P("dp", "seq", None),
        P("dp", "seq", None),
        P(None, "dp", "seq"),
        P("dp", None),
        P("dp", "seq"),
        P("dp", "seq", None),
        P(("dp", "seq")),
        P(("dp", "seq")),
        P(("dp", "seq")),
    )
    out_specs = (
        P("dp", "seq", None),
        P("dp", "seq", None),
        P(("dp", "seq")),
        P(("dp", "seq")),
        P(("dp", "seq")),
    )
    custom = dict(mesh.shape) == {"dp": 16, "seq": 2}
    return jax.shard_map(
        functools.partial(per_device, custom), mesh=mesh, in_specs=in_specs, out_specs=out_specs, check_vma=False
    )
```

```python
import functools

import jax
import jax.numpy as jnp
from jax import lax
from jax.experimental import pallas as pl
from jax.experimental.pallas import tpu as pltpu
from jax.sharding import PartitionSpec as P

D = 768
H = 12
HD = 64
FF = 3072
BUCKETS = 32
FREQ = 16
LF = 128
LAYERS = 1
BLOCK = 1024
STEP = 10
ENTRY = 99456
LAYER_PARAMS = 7087104
RAW = 7186560


beta_one = 0.8
beta_two = 0.98
adam_eps = 1e-06
learn_rate = 0.0006
layer_decay = 0.8
weight_decay = 0.1
norm_eps = 1e-05
masked_score = -1000000000.0


SHAPES = (
    (LF, D), (D,), (BUCKETS, H),
    (D, D), (D,), (D, D), (D, D), (D,), (D, D), (D,), (D,), (D,),
    (D, FF), (FF,), (FF, D), (D,), (D,), (D,),
)


def unpack(flat_params):
    pieces, offset = [], 0
    for shape in SHAPES:
        amount = shape[0] * (shape[1] if len(shape) > 1 else 1)
        pieces.append(flat_params[offset : offset + amount].reshape(shape))
        offset = offset + amount
    return pieces


def adam_update(master, first_moment, second_moment, gradient, global_index):
    exponent = jnp.where(
        global_index < ENTRY,
        LAYERS,
        jnp.maximum(LAYERS - 1 - (global_index - ENTRY) // LAYER_PARAMS, 0),
    )
    rate = jnp.where(
        global_index < RAW, learn_rate * jnp.power(layer_decay, exponent.astype(jnp.float32)), 0.0
    )
    moment_one = beta_one * first_moment + (1.0 - beta_one) * gradient
    moment_two = beta_two * second_moment + (1.0 - beta_two) * gradient * gradient
    fixed_one = moment_one / (1.0 - beta_one**STEP)
    fixed_two = moment_two / (1.0 - beta_two**STEP)
    param_step = -rate * (fixed_one / (jnp.sqrt(fixed_two) + adam_eps) + weight_decay * master)
    return (param_step, moment_one, moment_two)


def layout_features(page_boxes):
    rates_sin = jnp.power(10000.0, -jnp.arange(FREQ, dtype=jnp.float32) / FREQ)
    angles = page_boxes.astype(jnp.float32)[:, :, None] * rates_sin
    stacked = jnp.stack([jnp.sin(angles), jnp.cos(angles)], axis=1)
    return jnp.transpose(stacked, (2, 0, 1, 3)).reshape(page_boxes.shape[1], LF)


MESH = pl.DeviceIdType.MESH
SHARD = 224580
ROWS = 1760
TAIL, HEAD = 160, 176
WIN = 2176
SLOTS = 37
CHIP = 74
PARTS = ((0, 19), (19, 18))


def place():
    k = lax.axis_index("dp")
    return k, lax.axis_index("seq"), k // 4, (k // 2) % 2, k % 2


def shard_start(d):
    return d * 1754 + (d * 68) // 128, (d * 68) % 128


def early_vectors(k):
    return (k == 0) | (k == 4) | (k == 5)


def vector_row(k, other):
    at = other
    for chip, row in ((0, 768), (1, 5385), (4, 14607), (5, 19221), (10, 37671), (15, 56127)):
        at = jnp.where(k == chip, row, at)
    return at


def tile_start(w):
    at = w * 48
    for first, shift in ((16, 777 - 16 * 48), (112, 5391 - 112 * 48), (208, 9999 - 208 * 48), (304, 14613 - 304 * 48), (784, 37695 - 784 * 48)):
        at = jnp.where(w >= first, w * 48 + shift, at)
    wide = (w >= 400) & (w < 784)
    v = w - 400
    at = jnp.where(wide, 19239 + (v // 4) * 192 + (v % 4) * 6, at)
    return at, wide


def neighbours(k, c, z, y, x):
    t = k >= 0
    return [
        (t, (k, 1 - c)),
        (t, (z * 4 + y * 2 + 1 - x, c)),
        (t, (z * 4 + (1 - y) * 2 + x, c)),
        (z < 3, (jnp.minimum(k + 4, 15), c)),
        (z > 0, (jnp.maximum(k - 4, 0), c)),
        ((c == 1) & (k < 15), (jnp.minimum(k + 1, 15), 0)),
        ((c == 0) & (k > 0), (jnp.maximum(k - 1, 0), 1)),
    ]


def greet(k, c, z, y, x):
    bar = pltpu.get_barrier_semaphore()
    for cond, dev in neighbours(k, c, z, y, x):
        @pl.when(cond)
        def _():
            pl.semaphore_signal(bar, inc=1, device_id=dev, device_id_type=MESH)
    peers = 3
    for cond, _ in neighbours(k, c, z, y, x)[3:]:
        peers = peers + jnp.where(cond, 1, 0)
    pl.semaphore_wait(bar, peers)


def rcopy(src, dst, ssem, rsem, dev):
    return pltpu.make_async_remote_copy(src_ref=src, dst_ref=dst, send_sem=ssem, recv_sem=rsem, device_id=dev, device_id_type=MESH)


FRONT = 344
WIN2 = 2464
EDGE = 4
ENTRY_ROWS = 777


WEIGHTS = (
    (0, 0, 16),
    (3, 16, 96),
    (5, 112, 96),
    (6, 208, 96),
    (8, 304, 96),
    (12, 400, 384),
    (14, 784, 384),
)
VECTORS = (
    (1, 0, 0),
    (2, 0, 1),
    (4, 1, 0),
    (7, 4, 0),
    (9, 5, 0),
    (10, 5, 1),
    (11, 5, 2),
    (13, 10, 0),
    (15, 15, 0),
    (16, 15, 1),
    (17, 15, 2),
)


def slots_of(first, count):
    runs = []
    for w in range(first, first + count):
        chip, at = divmod(w, 73)
        slot = chip * CHIP + at + (1 if at >= vector_slot(chip) else 0)
        if runs and runs[-1][0] + runs[-1][2] == slot:
            runs[-1][2] += 1
        else:
            runs.append([slot, w - first, 1])
    return runs


def vector_slot(chip):
    return 36 if chip in (0, 4, 5) else 73


def vector_at(chip):
    return chip * CHIP + vector_slot(chip)


def pieces(tiles, held, first, count, sems, base, out=False):
    made = []
    for i, (slot, at, n) in enumerate(slots_of(first, count)):
        a, b = tiles.at[pl.ds(slot, n)], held.at[pl.ds(at, n)]
        a, b = (b, a) if out else (a, b)
        made.append(pltpu.make_async_copy(a, b, sems.at[base + i]))
    return made


def matrix(tile_rows):
    return tile_rows.reshape(-1, D)


def col_sum(v):
    return jnp.sum(v.reshape(-1, 8, v.shape[-1]), axis=0)


def norm_stats(v):
    mean = jnp.mean(v, axis=-1, keepdims=True)
    center = v - mean
    spread = jnp.mean(center * center, axis=-1, keepdims=True)
    inv = lax.rsqrt(spread + norm_eps)
    return center * inv, inv


def norm_back(grad, gain, hat, inv):
    g = grad * gain
    return inv * (g - jnp.mean(g, axis=-1, keepdims=True) - hat * jnp.mean(g * hat, axis=-1, keepdims=True))


ROOT_HALF = 0.7071067811865476
ROOT_TAU = 0.3989422804014327


def middle_kernel(tiles, ctx, hidden, cot, act_out, gfi_out, gctx_out, grads,
                  wo, wup, wdn, vecs, vf, act, slope, low1, hat1, inv1, hat2, inv2, a, sums, dwo, dwup, dwdn, vgrads, lsem, ssem):
    f32, bf = jnp.float32, jnp.bfloat16
    rows = ctx.shape[0]
    R = 64
    steps = rows // R
    loads_o = pieces(tiles, wo, 304, 96, lsem, 0)
    loads_u = pieces(tiles, wup, 400, 384, lsem, 4)
    loads_d = pieces(tiles, wdn, 784, 384, lsem, 12)
    loads_v = [pltpu.make_async_copy(tiles.at[vector_at(c)], vecs.at[i], lsem.at[20 + i]) for i, c in enumerate((5, 10, 15))]
    for c in loads_v + loads_o + loads_u + loads_d:
        c.start()
    up4 = wup.reshape(96, 4, 8, D)
    dup4 = dwup.reshape(96, 4, 8, D)

    def vec(i, r):
        return vf[i, pl.ds(r, 1), :]

    def each(f):
        @pl.loop(0, steps)
        def _(i):
            f(pl.ds(pl.multiple_of(i * R, R), R))

    for c in loads_v + loads_o:
        c.wait()
    vf[...] = vecs[...].astype(f32)
    a[...] = jnp.dot(ctx[...], matrix(wo[...]), preferred_element_type=f32)

    def first(sl):
        hat, inv = norm_stats(hidden[sl, :] + a[sl, :] + vec(0, 0))
        hat1[sl, :] = hat
        inv1[sl, :] = inv
        out = hat * vec(0, 1) + vec(0, 2)
        a[sl, :] = out
        low1[sl, :] = out.astype(bf)

    each(first)
    for c in loads_u + loads_d:
        c.wait()

    def up(j, _):
        for half in range(2):
            sl = pl.ds(half * (rows // 2), rows // 2)
            u = jnp.dot(low1[sl, :], matrix(up4[:, j]), preferred_element_type=f32) + vec(1, j)
            share = 0.5 * (1.0 + lax.erf(u * ROOT_HALF))
            act[j, sl, :] = (u * share).astype(bf)
            slope[j, sl, :] = share + u * jnp.exp(-0.5 * u * u) * ROOT_TAU
        return 0

    lax.fori_loop(0, 4, up, 0)

    def down(j, _):
        a[...] += jnp.dot(act[j], matrix(wdn[pl.ds(96 * j, 96)]), preferred_element_type=f32)
        return 0

    lax.fori_loop(0, 4, down, 0)
    sums[...] = jnp.zeros_like(sums)

    def second(sl):
        hat, inv = norm_stats(a[sl, :] + vec(2, 0))
        act_out[sl, :] = (hat * vec(2, 1) + vec(2, 2)).astype(bf)
        g = cot[sl, :].astype(f32)
        sums[6] += col_sum(g * hat)
        sums[7] += col_sum(g)
        back = norm_back(g, vec(2, 1), hat, inv)
        sums[5] += col_sum(back)
        a[sl, :] = back
        hat2[sl, :] = back.astype(bf)

    each(second)
    down_back = hat2

    def back(j, _):
        for half in range(2):
            sl = pl.ds(half * (rows // 2), rows // 2)
            g = lax.dot_general(down_back[sl, :], matrix(wdn[pl.ds(96 * j, 96)]), NT, preferred_element_type=f32) * slope[j, sl, :]
            sums[8 + j] += col_sum(g)
            act_back[sl, :] = g.astype(bf)
        dwdn[pl.ds(96 * j, 96)] = lax.dot_general(act[j], down_back[...], TN, preferred_element_type=f32).astype(bf).reshape(96, 8, D)
        dup4[:, j] = lax.dot_general(low1[...], act_back[...], TN, preferred_element_type=f32).astype(bf).reshape(96, 8, D)
        a[...] += lax.dot_general(act_back[...], matrix(up4[:, j]), NT, preferred_element_type=f32)
        return 0

    act_back = inv2
    lax.fori_loop(0, 4, back, 0)
    stores = pieces(grads, dwup, 400, 384, ssem, 4, True) + pieces(grads, dwdn, 784, 384, ssem, 12, True)
    for c in stores:
        c.start()

    def third(sl):
        g = a[sl, :]
        sums[3] += col_sum(g * hat1[sl, :])
        sums[4] += col_sum(g)
        back = norm_back(g, vec(0, 1), hat1[sl, :], inv1[sl, :])
        sums[2] += col_sum(back)
        gfi_out[sl, :] = back
        hat2[sl, :] = back.astype(bf)

    each(third)
    gctx_out[...] = lax.dot_general(hat2[...], matrix(wo[...]), NT, preferred_element_type=f32).astype(bf)
    dwo[...] = lax.dot_general(ctx[...], hat2[...], TN, preferred_element_type=f32).astype(bf).reshape(96, 8, D)
    for i, held in enumerate(((2, 3, 4), (8, 9, 10, 11), (5, 6, 7))):
        lines = [jnp.sum(sums[s], axis=0, keepdims=True) for s in held]
        lines.append(jnp.zeros((8 - len(held), D), f32))
        vgrads[i] = jnp.concatenate(lines).astype(bf)
    last = pieces(grads, dwo, 304, 96, ssem, 0, True)
    quiet = [ch for ch in range(6, 15) if ch != 10]
    vgrads[3] = jnp.zeros((8, D), bf)
    last += [pltpu.make_async_copy(vgrads.at[min(i, 3)], grads.at[vector_at(ch)], ssem.at[20 + i]) for i, ch in enumerate([5, 10, 15] + quiet)]
    for c in last:
        c.start()
    for c in stores + last:
        c.wait()


def middle(tiles, ctx, hidden, cot):
    rows = ctx.shape[0]
    f32, bf = jnp.float32, jnp.bfloat16
    vm, any_ = pl.BlockSpec(memory_space=pltpu.VMEM), pl.BlockSpec(memory_space=pl.ANY)
    S = jax.ShapeDtypeStruct
    return pl.pallas_call(
        middle_kernel,
        out_shape=[S((rows, D), bf), S((rows, D), f32), S((rows, D), bf), S((16 * CHIP, 8, D), bf)],
        in_specs=[any_, vm, vm, vm],
        out_specs=[vm, vm, vm, any_],
        scratch_shapes=[
            pltpu.VMEM((96, 8, D), bf), pltpu.VMEM((384, 8, D), bf), pltpu.VMEM((384, 8, D), bf), pltpu.VMEM((3, 8, D), bf), pltpu.VMEM((3, 8, D), f32),
            pltpu.VMEM((4, rows, D), bf), pltpu.VMEM((4, rows, D), f32), pltpu.VMEM((rows, D), bf),
            pltpu.VMEM((rows, D), f32), pltpu.VMEM((rows, 1), f32), pltpu.VMEM((rows, D), bf), pltpu.VMEM((rows, D), bf),
            pltpu.VMEM((rows, D), f32), pltpu.VMEM((12, 8, D), f32),
            pltpu.VMEM((96, 8, D), bf), pltpu.VMEM((384, 8, D), bf), pltpu.VMEM((384, 8, D), bf), pltpu.VMEM((4, 8, D), bf),
            pltpu.SemaphoreType.DMA((24,)), pltpu.SemaphoreType.DMA((32,)),
        ],
        compiler_params=pltpu.CompilerParams(vmem_limit_bytes=58 << 20),
        name="middle",
    )(tiles, ctx, hidden, cot)


NT = (((1,), (1,)), ((), ()))
TN = (((0,), (0,)), ((), ()))


def half(ref_value, hh):
    lanes = lax.broadcasted_iota(jnp.int32, ref_value.shape, 1)
    keep = lanes // 64 == hh
    return jnp.where(keep, ref_value, jnp.zeros_like(ref_value))


def page_of(at, lengths):
    end, page = 0, jnp.zeros(at.shape, jnp.int32)
    for i in range(4):
        end = end + lengths[0, i]
        page = page + jnp.where(at >= end, 1, 0)
    return page


def fill_codes(code_ref, buckets, pads, lengths):
    keys, rows = code_ref.shape
    own = lax.axis_index("seq") * rows
    tag = page_of(lax.broadcasted_iota(jnp.int32, (1, keys), 1), lengths) + 1
    tag = jnp.where(jnp.concatenate([pads[0, 0:1], pads[1, 0:1]], axis=1) > 0, tag, 0)
    for i in range(rows // 128):
        at = own + 128 * i + lax.broadcasted_iota(jnp.int32, (128, 1), 0)
        page = page_of(at, lengths) + 1
        for j in range(keys // 128):
            key_at = 128 * j + lax.broadcasted_iota(jnp.int32, (1, 128), 1)
            allowed = (page == tag[:, 128 * j : 128 * j + 128]) | (key_at == at)
            code = jnp.where(allowed, buckets[128 * i : 128 * i + 128, 128 * j : 128 * j + 128], BUCKETS)
            code_ref[128 * j : 128 * j + 128, 128 * i : 128 * i + 128] = code.T


def fill_table(tab_ref, lines):
    f32 = jnp.float32
    head = lax.broadcasted_iota(jnp.int32, (16, 128), 0)
    bucket = lax.broadcasted_iota(jnp.int32, (16, 128), 1)
    place_of = bucket * H + head
    tab = jnp.full((16, 128), masked_score, f32)
    for i in range(BUCKETS * H // 128):
        row = jnp.broadcast_to(lines[1:2, 128 * i : 128 * i + 128].astype(f32), (16, 128))
        inside = jnp.clip(place_of - 128 * i, 0, 127)
        got = jnp.take_along_axis(row, inside, axis=1, mode="promise_in_bounds")
        tab = jnp.where((place_of // 128 == i) & (bucket < BUCKETS) & (head < H), got, tab)
    tab_ref[...] = tab


def soft_head(head, q, k, code_ref, tab_ref, s_scr, p_ref):
    keys, rows = s_scr.shape
    f32, bf = jnp.float32, jnp.bfloat16
    qm = half(q, head % 2)
    line = jnp.broadcast_to(tab_ref[pl.ds(head, 1), :], (keys, 128))
    s = lax.dot_general(k, qm, NT, preferred_element_type=f32)
    cols = []
    for j in range(rows // 128):
        code = code_ref[:, 128 * j : 128 * j + 128]
        bias = jnp.take_along_axis(line, code, axis=1, mode="promise_in_bounds")
        cols.append(jnp.where(bias < 0.5 * masked_score, masked_score, s[:, 128 * j : 128 * j + 128] + bias))
    s = jnp.concatenate(cols, axis=1)
    s_scr[...] = s
    top = jnp.max(jnp.max(s.reshape(keys // 8, 8, rows), axis=0), axis=0, keepdims=True)
    e = jnp.exp(s_scr[...] - top)
    s_scr[...] = e
    inverse = 1.0 / jnp.sum(jnp.sum(e.reshape(keys // 8, 8, rows), axis=0), axis=0, keepdims=True)
    p_ref[...] = (s_scr[...] * inverse).astype(bf)


def context_pair(v, p_ref):
    vt = v.T
    out = [jnp.dot(vt, p_ref[hh], preferred_element_type=jnp.float32) for hh in range(2)]
    sub = lax.broadcasted_iota(jnp.int32, out[0].shape, 0)
    return jnp.where(sub < 64, out[0], out[1]).T.astype(jnp.bfloat16)


def attend_kernel(lengths, q_ref, k_ref, v_ref, buckets, pads, lines, ctx_ref, p_ref, code_ref, s_scr, tab_ref):
    pair = pl.program_id(0)

    @pl.when(pair == 0)
    def _():
        fill_codes(code_ref, buckets, pads, lengths)
        fill_table(tab_ref, lines)

    for hh in range(2):
        soft_head(2 * pair + hh, q_ref[...], k_ref[...], code_ref, tab_ref, s_scr, p_ref.at[hh])
    ctx_ref[...] = context_pair(v_ref[...], p_ref)


def attend(query, key_all, value_all, buckets, page_lengths, pads, lines):
    rows, keys = query.shape[0], key_all.shape[0]
    bf = jnp.bfloat16
    const = lambda p: (0, 0)
    return pl.pallas_call(
        attend_kernel,
        grid=(H // 2,),
        out_shape=[
            jax.ShapeDtypeStruct((rows, D), bf),
            jax.ShapeDtypeStruct((H, keys, rows), bf),
            jax.ShapeDtypeStruct((keys, rows), jnp.int32),
        ],
        in_specs=[
            pl.BlockSpec(memory_space=pltpu.SMEM),
            pl.BlockSpec((rows, 128), lambda p: (0, p)),
            pl.BlockSpec((keys, 128), lambda p: (0, p)),
            pl.BlockSpec((keys, 128), lambda p: (0, p)),
            pl.BlockSpec((rows, keys), const),
            pl.BlockSpec((2, 8, rows), lambda p: (0, 0, 0)),
            pl.BlockSpec((8, D), const),
        ],
        out_specs=[pl.BlockSpec((rows, 128), lambda p: (0, p)), pl.BlockSpec((2, keys, rows), lambda p: (p, 0, 0)), pl.BlockSpec((keys, rows), const)],
        scratch_shapes=[pltpu.VMEM((keys, rows), jnp.float32), pltpu.VMEM((16, 128), jnp.float32)],
        compiler_params=pltpu.CompilerParams(vmem_limit_bytes=56 << 20),
        name="attend",
    )(page_lengths, query, key_all, value_all, buckets, pads, lines)


def table_row(acc, shape):
    f32 = jnp.float32
    a = lax.broadcasted_iota(jnp.int32, acc.shape, 0) % 8
    b = lax.broadcasted_iota(jnp.int32, acc.shape, 1) // BUCKETS
    acc = jnp.where(a == b, acc, 0.0)
    heads = jnp.sum(acc.reshape(H, 8, 8 * BUCKETS), axis=1)
    lane = lax.broadcasted_iota(jnp.int32, (8 * BUCKETS, D), 1) // H
    wide = jnp.where(lane == lax.broadcasted_iota(jnp.int32, lane.shape, 0) % BUCKETS, 1.0, 0.0)
    out = jnp.dot(heads, wide, precision=lax.Precision.HIGHEST, preferred_element_type=f32)
    mine = lax.broadcasted_iota(jnp.int32, out.shape, 1) % H == lax.broadcasted_iota(jnp.int32, out.shape, 0)
    out = jnp.sum(jnp.where(mine, out, 0.0), axis=0, keepdims=True)
    return jnp.broadcast_to(out, shape)


def attend_back_kernel(q_ref, k_ref, v_ref, do_ref, p_ref, code_ref, dq_ref, dk_ref, dv_ref, tab_ref, spread, held):
    pair = pl.program_id(0)
    keys, rows = code_ref.shape
    f32, bf = jnp.float32, jnp.bfloat16
    STEP_ROWS = keys
    kt = k_ref[...].T
    dq = []
    for hh in range(2):
        qm = half(q_ref[...], hh)
        dom = half(do_ref[...], hh)

        def inner(i, total):
            at = pl.multiple_of(i * STEP_ROWS, STEP_ROWS)
            g = lax.dot_general(v_ref[pl.ds(at, STEP_ROWS), :], dom, NT, preferred_element_type=f32)
            w = g * p_ref[hh, pl.ds(at, STEP_ROWS), :].astype(f32)
            return total + jnp.sum(w.reshape(STEP_ROWS // 8, 8, rows), axis=0)

        total = lax.fori_loop(0, keys // STEP_ROWS, inner, jnp.zeros((8, rows), f32))
        total = jnp.sum(total, axis=0, keepdims=True)

        def grads(i, acc):
            at = pl.multiple_of(i * STEP_ROWS, STEP_ROWS)
            sl = pl.ds(at, STEP_ROWS)
            g = lax.dot_general(v_ref[sl, :], dom, NT, preferred_element_type=f32)
            p = p_ref[hh, sl, :]
            ds = p.astype(f32) * (g - total)
            wide = ds.reshape(STEP_ROWS // 8, 8, rows)
            if hh == 0:
                held[...] = wide
            else:
                both = jnp.concatenate([held[...], wide], axis=1).astype(bf)
                spread[:, pl.ds(pl.multiple_of(pair * 16, 16), 16), :] = both
            ds = ds.astype(bf)
            dv = jnp.dot(p, dom, preferred_element_type=f32)
            dk = jnp.dot(ds, qm, preferred_element_type=f32)
            if hh == 0:
                dv_ref[sl, :] = dv
                dk_ref[sl, :] = dk
            else:
                dv_ref[sl, :] += dv
                dk_ref[sl, :] += dk
            return acc + lax.dot_general(k_ref[sl, :], ds, TN, preferred_element_type=f32)

        dq.append(lax.fori_loop(0, keys // STEP_ROWS, grads, jnp.zeros((128, rows), f32)))
    sub = lax.broadcasted_iota(jnp.int32, dq[0].shape, 0)
    dq_ref[...] = jnp.where(sub < 64, dq[0], dq[1]).T * 0.125

    @pl.when(pair == H // 2 - 1)
    def _():
        bucket = lax.broadcasted_iota(jnp.int32, (BUCKETS, rows), 0)

        def count(i, acc):
            code = code_ref[pl.ds(pl.multiple_of(i * 8, 8), 8), :]
            hot = jnp.concatenate(
                [jnp.where(jnp.broadcast_to(code[r : r + 1], bucket.shape) == bucket, 1.0, 0.0) for r in range(8)]
            ).astype(bf)
            return acc + lax.dot_general(spread[i], hot, NT, preferred_element_type=f32)

        acc = lax.fori_loop(0, keys // 8, count, jnp.zeros((8 * H, 8 * BUCKETS), f32), unroll=8)
        tab_ref[...] = table_row(acc, tab_ref.shape)


def soft_back(query, key_all, value_all, grad_context, soft, code):
    rows, keys = query.shape[0], key_all.shape[0]
    f32 = jnp.float32
    row = pl.BlockSpec((rows, 128), lambda p: (0, p))
    key = pl.BlockSpec((keys, 128), lambda p: (0, p))
    dq, dk, dv, tab = pl.pallas_call(
        attend_back_kernel,
        grid=(H // 2,),
        out_shape=[
            jax.ShapeDtypeStruct((rows, D), f32),
            jax.ShapeDtypeStruct((keys, D), f32),
            jax.ShapeDtypeStruct((keys, D), f32),
            jax.ShapeDtypeStruct((8, D), f32),
        ],
        in_specs=[row, key, key, row, pl.BlockSpec((2, keys, rows), lambda p: (p, 0, 0)), pl.BlockSpec((keys, rows), lambda p: (0, 0))],
        out_specs=[row, key, key, pl.BlockSpec((8, D), lambda p: (0, 0))],
        scratch_shapes=[pltpu.VMEM((keys // 8, 8 * H, rows), jnp.bfloat16), pltpu.VMEM((keys // 8, 8, rows), f32)],
        compiler_params=pltpu.CompilerParams(vmem_limit_bytes=58 << 20),
        name="attend_back",
    )(query, key_all, value_all, grad_context, soft, code)
    return dq, dk, dv, tab


def meet_partner():
    dp, c = lax.axis_index("dp"), lax.axis_index("seq")
    partner = (dp, 1 - c)
    bar = pltpu.get_barrier_semaphore()
    pl.semaphore_signal(bar, inc=1, device_id=partner, device_id_type=MESH)
    pl.semaphore_wait(bar, 1)
    return c, partner


def enter_kernel(tiles, tokens, feats, pad, hidden, low, query, keys, values, pads, wl, wq, wk, wv, vecs, vf, lsem, sends, recvs):
    f32, bf = jnp.float32, jnp.bfloat16
    rows = tokens.shape[0]
    loads = [pltpu.make_async_copy(tiles.at[vector_at(ch)], vecs.at[i], lsem.at[i]) for i, ch in enumerate((0, 1, 4))]
    loads += pieces(tiles, wl, 0, 16, lsem, 4) + pieces(tiles, wk, 112, 96, lsem, 8)
    loads += pieces(tiles, wv, 208, 96, lsem, 12) + pieces(tiles, wq, 16, 96, lsem, 16)
    for c in loads:
        c.start()
    c, partner = meet_partner()
    own = pl.ds(c * rows, rows)

    def share(ref, i):
        return rcopy(ref.at[own], ref.at[own], sends.at[i], recvs.at[i], partner)

    pads[pl.ds(c, 1)] = pad[...].reshape(1, 8, rows)
    pair_pads = rcopy(pads.at[pl.ds(c, 1)], pads.at[pl.ds(c, 1)], sends.at[2], recvs.at[2], partner)
    pair_pads.start()
    for copy in loads:
        copy.wait()
    vf[...] = vecs[...].astype(f32)
    h = tokens[...].astype(f32) + jnp.dot(feats[...], matrix(wl[...]), preferred_element_type=f32) + vf[0, 0:1, :]
    hidden[...] = h
    low[...] = h.astype(bf)
    keys[own, :] = jnp.dot(low[...], matrix(wk[...]), preferred_element_type=f32).astype(bf)
    send_keys = share(keys, 0)
    send_keys.start()
    values[own, :] = (jnp.dot(low[...], matrix(wv[...]), preferred_element_type=f32) + vf[2, 0:1, :]).astype(bf)
    send_values = share(values, 1)
    send_values.start()
    query[...] = ((jnp.dot(low[...], matrix(wq[...]), preferred_element_type=f32) + vf[1, 0:1, :]) * 0.125).astype(bf)
    for copy in (pair_pads, send_keys, send_values):
        copy.wait()


def enter(tiles, tokens, feats, pad):
    rows = tokens.shape[0]
    f32, bf = jnp.float32, jnp.bfloat16
    vm, any_ = pl.BlockSpec(memory_space=pltpu.VMEM), pl.BlockSpec(memory_space=pl.ANY)
    S, sem = jax.ShapeDtypeStruct, pltpu.SemaphoreType.DMA
    w = pltpu.VMEM((96, 8, D), bf)
    return pl.pallas_call(
        enter_kernel,
        out_shape=[S((rows, D), f32), S((rows, D), bf), S((rows, D), bf), S((2 * rows, D), bf), S((2 * rows, D), bf), S((2, 8, rows), jnp.int32)],
        in_specs=[any_, vm, vm, vm],
        out_specs=[vm] * 6,
        scratch_shapes=[pltpu.VMEM((16, 8, D), bf), w, w, w, pltpu.VMEM((3, 8, D), bf), pltpu.VMEM((3, 8, D), f32), sem((20,)), sem((3,)), sem((3,))],
        compiler_params=pltpu.CompilerParams(collective_id=2, has_side_effects=True, vmem_limit_bytes=40 << 20),
        name="enter",
    )(tiles, tokens, feats, pad)


def leave_kernel(tiles, dq, dk, dv, gfi, low, feats, table, grads_in, input_grad, grads,
                 wq, wk, wv, out, come, back, dwl, dwq, dwk, dwv, vgrads, lsem, ssem, sends, recvs):
    f32, bf = jnp.float32, jnp.bfloat16
    rows = gfi.shape[0]
    loads = pieces(tiles, wk, 112, 96, lsem, 0) + pieces(tiles, wv, 208, 96, lsem, 4) + pieces(tiles, wq, 16, 96, lsem, 8)
    for c in loads:
        c.start()
    c, partner = meet_partner()
    own, other = pl.ds(c * rows, rows), pl.ds((1 - c) * rows, rows)
    swaps = []
    for i, ref in enumerate((dk, dv)):
        out[i] = ref[other, :].astype(bf)
        swaps.append(rcopy(out.at[i], come.at[i], sends.at[i], recvs.at[i], partner))
        swaps[i].start()
    back[0] = dq[...].astype(bf)
    query_bias = jnp.sum(col_sum(dq[...]), axis=0, keepdims=True)
    for copy in loads:
        copy.wait()

    def through(i, w, dw):
        dw[...] = lax.dot_general(low[...], back[i], TN, preferred_element_type=f32).astype(bf).reshape(96, 8, D)
        return lax.dot_general(back[i], matrix(w[...]), NT, preferred_element_type=f32)

    input_grad[...] = gfi[...] + through(0, wq, dwq)
    stores = pieces(grads, dwq, 16, 96, ssem, 0, True)
    swaps[0].wait_recv()
    back[1] = (dk[own, :] + come[0].astype(f32)).astype(bf)
    input_grad[...] += through(1, wk, dwk)
    stores += pieces(grads, dwk, 112, 96, ssem, 4, True)
    swaps[1].wait_recv()
    grad_value = dv[own, :] + come[1].astype(f32)
    value_bias = jnp.sum(col_sum(grad_value), axis=0, keepdims=True)
    back[2] = grad_value.astype(bf)
    total = input_grad[...] + through(2, wv, dwv)
    stores += pieces(grads, dwv, 208, 96, ssem, 8, True)
    input_grad[...] = total
    layout_bias = jnp.sum(col_sum(total), axis=0, keepdims=True)
    dwl[...] = lax.dot_general(feats[...], total.astype(bf), TN, preferred_element_type=f32).astype(bf).reshape(16, 8, D)
    stores += pieces(grads, dwl, 0, 16, ssem, 12, True)

    def block(lines):
        return jnp.concatenate(lines + [jnp.zeros((8 - len(lines), D), f32)]).astype(bf)

    vgrads[0] = block([layout_bias, table[0:1, :]])
    vgrads[1] = block([query_bias])
    vgrads[2] = block([value_bias])
    vgrads[3] = jnp.zeros((8, D), bf)
    held = {0: 0, 1: 1, 4: 2}
    for i, chip in enumerate(ch for ch in range(5)):
        stores.append(pltpu.make_async_copy(vgrads.at[held.get(chip, 3)], grads.at[vector_at(chip)], ssem.at[16 + i]))
    for copy in stores:
        copy.start()
    for copy in stores:
        copy.wait()
    for swap in swaps:
        swap.wait_send()


def leave(tiles, dq, dk, dv, gfi, low, feats, table, grads):
    rows = gfi.shape[0]
    f32, bf = jnp.float32, jnp.bfloat16
    vm, any_ = pl.BlockSpec(memory_space=pltpu.VMEM), pl.BlockSpec(memory_space=pl.ANY)
    S, sem = jax.ShapeDtypeStruct, pltpu.SemaphoreType.DMA
    w = pltpu.VMEM((96, 8, D), bf)
    return pl.pallas_call(
        leave_kernel,
        out_shape=[S((rows, D), f32), S(grads.shape, bf)],
        in_specs=[any_] + [vm] * 7 + [any_],
        out_specs=[vm, any_],
        scratch_shapes=[w, w, w, pltpu.VMEM((2, rows, D), bf), pltpu.VMEM((2, rows, D), bf), pltpu.VMEM((3, rows, D), bf),
                        pltpu.VMEM((16, 8, D), bf), w, w, w, pltpu.VMEM((4, 8, D), bf), sem((12,)), sem((32,)), sem((2,)), sem((2,))],
        input_output_aliases={8: 1},
        compiler_params=pltpu.CompilerParams(collective_id=3, has_side_effects=True, vmem_limit_bytes=56 << 20),
        name="leave",
    )(tiles, dq, dk, dv, gfi, low, feats, table, grads)


def forward_kernel(x_ref, tokens, feats, pad, buckets, lengths,
                   g_ref, hidden, low, query, keys, values, ctx, soft, code_out,
                   xv, tail, head, win, chunk, lsem, hsend, hrecv, own,
                   zs, zr, xas, xar, xbs, xbr, yas, yar, ybs, ybr, cs, cr,
                   pads, hidden_v, low_v, query_v, keys_v, values_v, ctx_v, code, buckets_v, tokens_v, feats_v, p_v, s_scr, tab,
                   wl, wq, wk, wv, vrows, vf, ksend, krecv, wsem, isem, osem, psem):
    f32, bf = jnp.float32, jnp.bfloat16
    rows = tokens.shape[0]
    k, c, z, y, x = place()
    d = 2 * k + c
    inputs = [pltpu.make_async_copy(r, v, isem.at[i]) for i, (r, v) in enumerate(((buckets, buckets_v), (tokens, tokens_v), (feats, feats_v)))]
    for copy in inputs:
        copy.start()
    pads[pl.ds(c, 1)] = pad[...].reshape(1, 8, rows)
    greet(k, c, z, y, x)
    load = pltpu.make_async_copy(x_ref, xv, lsem)
    load.start()
    prev = (jnp.where(c == 1, k, jnp.maximum(k - 1, 0)), 1 - c)
    nxt = (jnp.where(c == 0, k, jnp.minimum(k + 1, 15)), 1 - c)
    to_next = rcopy(x_ref.at[pl.ds(ROWS - TAIL, TAIL)], tail, hsend.at[0], hrecv.at[0], nxt)
    to_prev = rcopy(x_ref.at[pl.ds(0, HEAD)], head, hsend.at[1], hrecv.at[1], prev)

    @pl.when(d < 31)
    def _():
        to_next.start()

    @pl.when(d > 0)
    def _():
        to_prev.start()

    win[...] = jnp.zeros_like(win)
    lanes = lax.broadcasted_iota(jnp.int32, (80, 128), 1)
    q, sh = shard_start(d)
    load.wait()

    @pl.loop(0, ROWS // 80)
    def _(i):
        r = pl.multiple_of(i * 80, 8)
        rolled = pltpu.roll(xv[pl.ds(r, 80), :], sh, 1)
        win[pl.ds(160 + r, 80), :] += jnp.where(lanes >= sh, rolled, 0.0)
        win[pl.ds(161 + r, 80), :] += jnp.where(lanes < sh, rolled, 0.0)

    @pl.when(d > 0)
    def _():
        to_next.wait_recv()
        qp, shp = shard_start(d - 1)
        lanes = lax.broadcasted_iota(jnp.int32, (TAIL, 128), 1)
        rolled = pltpu.roll(tail[...], shp, 1)
        at = 1760 - (q - qp)
        win[pl.ds(at, TAIL), :] += jnp.where(lanes >= shp, rolled, 0.0)
        win[pl.ds(at + 1, TAIL), :] += jnp.where(lanes < shp, rolled, 0.0)

    @pl.when(d < 31)
    def _():
        to_prev.wait_recv()
        qn, shn = shard_start(d + 1)
        lanes = lax.broadcasted_iota(jnp.int32, (HEAD, 128), 1)
        rolled = pltpu.roll(head[...], shn, 1)
        at = 160 + (qn - q)
        win[pl.ds(at, HEAD), :] += jnp.where(lanes >= shn, rolled, 0.0)
        win[pl.ds(at + 1, HEAD), :] += jnp.where(lanes < shn, rolled, 0.0)

    early = early_vectors(k)
    nw0 = jnp.where(early, 36, 37)
    vecs = early == (c == 0)
    first = jnp.where(c == 0, 73 * k, 73 * k + nw0)
    base = q - 160

    @pl.loop(0, SLOTS)
    def _(t):
        at, wide = tile_start(first + t)
        is_vec = vecs & (t == 36)
        at = jnp.where(is_vec, vector_row(k, q), at) - base
        wide = wide & jnp.logical_not(is_vec)

        @pl.when(wide)
        def _():
            parts = [win[pl.ds(at + j, 8, stride=24), :] for j in range(6)]
            chunk[t] = jnp.concatenate(parts, axis=1).astype(jnp.bfloat16)

        @pl.when(jnp.logical_not(wide))
        def _():
            parts = [win[pl.ds(at + j, 8, stride=6), :] for j in range(6)]
            chunk[t] = jnp.concatenate(parts, axis=1).astype(jnp.bfloat16)

    @pl.when(d < 31)
    def _():
        to_next.wait_send()

    @pl.when(d > 0)
    def _():
        to_prev.wait_send()

    xdev, ydev, cdev = (z * 4 + y * 2 + 1 - x, c), (z * 4 + (1 - y) * 2 + x, c), (k, 1 - c)
    zdev = {1: (jnp.minimum(k + 4, 15), c), -1: (jnp.maximum(k - 4, 0), c)}

    def gsl(chip, p):
        off, n = PARTS[p]
        return g_ref.at[chip, pl.ds(37 * c + off, n)]

    def src(chip, p, mine=False):
        off, n = PARTS[p]
        return chunk.at[pl.ds(off, n)] if mine else gsl(chip, p)

    def chip_of(zo, yo, xo):
        return zo * 4 + yo * 2 + xo

    def zcopy(zo, p, way, mine=False):
        chip = chip_of(zo, y, x)
        w = (way + 1) // 2
        return rcopy(src(chip, p, mine), gsl(chip, p), zs.at[w, zo, p], zr.at[zo, p], zdev[way])

    def xcopy(zo, yo, xo, p, mine=False):
        chip = chip_of(zo, yo, xo)
        s, r = (xas, xar) if p == 0 else (xbs, xbr)
        i = zo if p == 0 else zo * 2 + yo
        return rcopy(src(chip, p, mine), gsl(chip, p), s.at[i], r.at[i], xdev)

    def ycopy(zo, yo, xo, p, mine=False):
        chip = chip_of(zo, yo, xo)
        s, r = (ybs, ybr) if p == 1 else (yas, yar)
        i = zo if p == 1 else zo * 2 + xo
        return rcopy(src(chip, p, mine), gsl(chip, p), s.at[i], r.at[i], ydev)

    def ccopy(chip, p, mine=False):
        return rcopy(src(chip, p, mine), gsl(chip, p), cs.at[chip, p], cr.at[chip, p], cdev)

    pair_pads = rcopy(pads.at[pl.ds(c, 1)], pads.at[pl.ds(c, 1)], ksend.at[2], krecv.at[2], cdev)
    pair_pads.start()
    mine = [pltpu.make_async_copy(chunk.at[pl.ds(*PARTS[p])], gsl(k, p), own.at[p]) for p in (0, 1)]

    def own_z(way):
        for p in (0, 1):
            zcopy(z, p, way, True).start()

    def pass_on(zz, zo):
        way = 1 if zo < zz else -1
        for p in (0, 1):
            zcopy(zo, p, way).wait_recv()
            if 0 <= zz + way <= 3:
                zcopy(zo, p, way).start()

    def spread(zz, zo):
        xcopy(zo, y, x, 0).start()
        ycopy(zo, y, x, 1).start()
        ycopy(zo, y, x, 0).start()
        xcopy(zo, y, x, 1).start()
        for p in (0, 1):
            ccopy(chip_of(zo, y, x), p).start()

    def column(zz, zo):
        way = 1 if zo < zz else -1
        for p in (0, 1):
            zcopy(zo, p, way).wait_recv()
            if 0 <= zz + way <= 3:
                zcopy(zo, p, way).start()
            if p == 0:
                xcopy(zo, y, x, 0).start()
                ycopy(zo, y, x, 0).start()
            else:
                ycopy(zo, y, x, 1).start()
                xcopy(zo, y, x, 1).start()
            ccopy(chip_of(zo, y, x), p).start()

    def beside(zz, zo):
        xcopy(zo, y, 1 - x, 0).wait_recv()
        ycopy(zo, y, 1 - x, 0).start()
        ccopy(chip_of(zo, y, 1 - x), 0).start()
        ycopy(zo, 1 - y, x, 1).wait_recv()
        xcopy(zo, 1 - y, x, 1).start()
        ccopy(chip_of(zo, 1 - y, x), 1).start()

    def last(zz, zo):
        ycopy(zo, 1 - y, x, 0).wait_recv()
        ccopy(chip_of(zo, 1 - y, x), 0).start()
        xcopy(zo, y, 1 - x, 1).wait_recv()
        ccopy(chip_of(zo, y, 1 - x), 1).start()
        ycopy(zo, 1 - y, 1 - x, 0).wait_recv()
        ccopy(chip_of(zo, 1 - y, 1 - x), 0).start()
        xcopy(zo, 1 - y, 1 - x, 1).wait_recv()
        ccopy(chip_of(zo, 1 - y, 1 - x), 1).start()

    def own_first(zz, zo):
        xcopy(z, y, x, 0, True).start()
        ycopy(z, y, x, 1, True).start()

    def own_second(zz, zo):
        ycopy(z, y, x, 0, True).start()
        xcopy(z, y, x, 1, True).start()
        for p in (0, 1):
            ccopy(k, p, True).start()

    def values_now(zz, zo):
        make_values()

    def own_up(zz, zo):
        own_z(1)

    def own_down(zz, zo):
        own_z(-1)

    begin = {
        0: ((own_up, 0), (own_first, 0), (own_second, 0)),
        1: ((own_first, 1), (own_down, 1)),
        2: ((own_up, 2), (own_down, 2), (own_first, 2)),
        3: ((own_down, 3), (own_first, 3)),
    }
    before = {
        0: ((beside, 0), (column, 1), (last, 0)),
        1: ((column, 0), (own_up, 1), (beside, 0), (column, 3), (column, 2), (last, 0)),
        2: ((column, 3), (pass_on, 0), (spread, 0), (beside, 0), (column, 1), (own_second, 2), (last, 0)),
        3: ((column, 2), (column, 0), (beside, 0), (beside, 2), (last, 0), (column, 1), (beside, 3)),
    }
    after = {
        0: {-1: ((column, 3), (beside, 1)), 1: ((beside, 3),), 2: ((last, 1), (column, 2)), 8: ((values_now, 0), (beside, 2)), 10: ((last, 3),), 11: ((last, 2),)},
        1: {4: ((own_second, 1),), 6: ((beside, 1), (beside, 3)), 7: ((beside, 2),), 8: ((last, 1), (values_now, 0)), 10: ((last, 3),), 11: ((last, 2),)},
        2: {2: ((beside, 1),), 4: ((beside, 2),), 6: ((last, 1), (beside, 3)), 10: ((last, 2),), 11: ((values_now, 0), (last, 3))},
        3: {5: ((last, 2), (beside, 1)), 8: ((own_second, 3),), 9: ((last, 1),), 11: ((last, 3), (values_now, 0))},
    }

    for p in (0, 1):
        mine[p].start()
    for zz in range(4):
        @pl.when(z == zz)
        def _():
            for f, zo in begin[zz]:
                f(zz, zo)
    for copy in inputs:
        copy.wait()
    pair_pads.wait()
    fill_codes(code, buckets_v, pads, lengths)
    outs = [pltpu.make_async_copy(code, code_out, osem.at[0])]
    outs[0].start()
    for zz in range(4):
        @pl.when(z == zz)
        def _():
            for f, zo in before[zz]:
                f(zz, zo)
    for p in (0, 1):
        mine[p].wait()

    def from_partner(chip):
        for p in (0, 1):
            off, n = PARTS[p]
            theirs = g_ref.at[chip, pl.ds(37 * (1 - c) + off, n)]
            rcopy(theirs, theirs, cs.at[chip, p], cr.at[chip, p], cdev).wait_recv()

    for chip in range(3):
        from_partner(chip)

    tiles = g_ref.reshape(16 * CHIP, 8, D)
    loads = [pltpu.make_async_copy(tiles.at[vector_at(ch)], vrows.at[i], wsem.at[i]) for i, ch in enumerate((0, 1))]
    loads += pieces(tiles, wl, 0, 16, wsem, 4) + pieces(tiles, wk, 112, 96, wsem, 8) + pieces(tiles, wq, 16, 96, wsem, 16)
    for copy in loads:
        copy.start()
    for copy in loads:
        copy.wait()
    vf[0] = vrows[0].astype(f32)
    vf[1] = vrows[1].astype(f32)
    fill_table(tab, vrows.at[0])
    h = tokens_v[...].astype(f32) + jnp.dot(feats_v[...], matrix(wl[...]), preferred_element_type=f32) + vf[0, 0:1, :]
    hidden_v[...] = h
    low_v[...] = h.astype(bf)
    half_rows = pl.ds(c * rows, rows)

    def share(ref, i):
        return rcopy(ref.at[half_rows], ref.at[half_rows], ksend.at[i], krecv.at[i], cdev)

    keys_v[half_rows, :] = jnp.dot(low_v[...], matrix(wk[...]), preferred_element_type=f32).astype(bf)
    share(keys_v, 0).start()
    query_v[...] = ((jnp.dot(low_v[...], matrix(wq[...]), preferred_element_type=f32) + vf[1, 0:1, :]) * 0.125).astype(bf)
    share(keys_v, 0).wait()
    outs += [pltpu.make_async_copy(v, r, osem.at[1 + i]) for i, (v, r) in enumerate(((hidden_v, hidden), (low_v, low), (query_v, query), (keys_v, keys)))]
    for copy in outs[1:]:
        copy.start()

    def make_values():
        for chip in (3, 4):
            from_partner(chip)
        copies = [pltpu.make_async_copy(tiles.at[vector_at(4)], vrows.at[2], wsem.at[2])] + pieces(tiles, wv, 208, 96, wsem, 12)
        for copy in copies:
            copy.start()
        for copy in copies:
            copy.wait()
        vf[2] = vrows[2].astype(f32)
        values_v[half_rows, :] = (jnp.dot(low_v[...], matrix(wv[...]), preferred_element_type=f32) + vf[2, 0:1, :]).astype(bf)
        share(values_v, 1).start()

    def keep(pair):
        return pltpu.make_async_copy(p_v.at[pl.ds(2 * pair, 2)], soft.at[pl.ds(2 * pair, 2)], psem.at[pair])

    for zz in range(4):
        if -1 in after[zz]:
            @pl.when(z == zz)
            def _():
                for f, zo in after[zz][-1]:
                    f(zz, zo)

    def one_head(head, _):
        lanes = pl.ds(pl.multiple_of(head // 2 * 128, 128), 128)
        soft_head(head, query_v[:, lanes], keys_v[:, lanes], code, tab, s_scr, p_v.at[head])

        @pl.when(head % 2 == 1)
        def _():
            keep(head // 2).start()

        for zz in range(4):
            for i in range(H):
                if i in after[zz]:
                    @pl.when((head == i) & (z == zz))
                    def _():
                        for f, zo in after[zz][i]:
                            f(zz, zo)
        return 0

    lax.fori_loop(0, H, one_head, 0)
    share(values_v, 1).wait()
    outs.append(pltpu.make_async_copy(values_v, values, osem.at[5]))
    outs[-1].start()

    def context(pair, _):
        lanes = pl.ds(pl.multiple_of(pair * 128, 128), 128)
        ctx_v[:, lanes] = context_pair(values_v[:, lanes], p_v.at[pl.ds(2 * pair, 2)])
        return 0

    lax.fori_loop(0, H // 2, context, 0)
    outs.append(pltpu.make_async_copy(ctx_v, ctx, osem.at[6]))
    outs[-1].start()

    for p in (0, 1):
        for way in (1, -1):
            for zo in range(4):
                @pl.when(((z - zo) * way >= 0) & (z + way >= 0) & (z + way <= 3))
                def _():
                    zcopy(zo, p, way).wait_send()
    for zo in range(4):
        xcopy(zo, y, x, 0).wait_send()
        ycopy(zo, y, x, 1).wait_send()
        for o in range(2):
            ycopy(zo, y, o, 0).wait_send()
            xcopy(zo, o, x, 1).wait_send()
    for chip in range(16):
        for p in (0, 1):
            ccopy(chip, p).wait_send()
    for chip in range(5, 16):
        from_partner(chip)
    for pair in range(H // 2):
        keep(pair).wait()
    for copy in outs:
        copy.wait()


def gather_and_attend(master, tokens, feats, pad, buckets, page_lengths):
    x = jnp.pad(master, (0, ROWS * 128 - SHARD)).reshape(ROWS, 128)
    sem = pltpu.SemaphoreType.DMA
    any_, vm = pl.BlockSpec(memory_space=pl.ANY), pl.BlockSpec(memory_space=pltpu.VMEM)
    rows, key_rows = buckets.shape
    f32, bf = jnp.float32, jnp.bfloat16
    S, V = jax.ShapeDtypeStruct, pltpu.VMEM
    w = V((96, 8, D), bf)
    return pl.pallas_call(
        forward_kernel,
        out_shape=[
            S((16, CHIP, 8, D), bf), S((rows, D), f32), S((rows, D), bf), S((rows, D), bf), S((key_rows, D), bf), S((key_rows, D), bf),
            S((rows, D), bf), S((H, key_rows, rows), bf), S((key_rows, rows), jnp.int32),
        ],
        in_specs=[any_, any_, any_, vm, any_, pl.BlockSpec(memory_space=pltpu.SMEM)],
        out_specs=[any_] * 9,
        scratch_shapes=[
            V((ROWS, 128), f32), V((TAIL, 128), f32), V((HEAD, 128), f32), V((WIN, 128), f32), V((SLOTS, 8, D), bf),
            sem, sem((2,)), sem((2,)), sem((2,)),
            sem((2, 4, 2)), sem((4, 2)),
            sem((4,)), sem((4,)), sem((8,)), sem((8,)),
            sem((8,)), sem((8,)), sem((4,)), sem((4,)),
            sem((16, 2)), sem((16, 2)),
            V((2, 8, rows), jnp.int32), V((rows, D), f32), V((rows, D), bf), V((rows, D), bf), V((key_rows, D), bf), V((key_rows, D), bf),
            V((rows, D), bf), V((key_rows, rows), jnp.int32), V((rows, key_rows), jnp.int32), V((rows, D), bf), V((rows, LF), bf),
            V((H, key_rows, rows), bf), V((key_rows, rows), f32), V((16, 128), f32),
            V((16, 8, D), bf), w, w, w, V((3, 8, D), bf), V((3, 8, D), f32),
            sem((3,)), sem((3,)), sem((20,)), sem((3,)), sem((7,)), sem((H // 2,)),
        ],
        compiler_params=pltpu.CompilerParams(collective_id=0, has_side_effects=True, vmem_limit_bytes=60 << 20),
        name="gather_and_attend",
    )(x, tokens, feats, pad, buckets, page_lengths)


def guarded(cond, f):
    if cond is True:
        f()
    elif cond is not False:
        pl.when(cond)(f)


class Reducer:
    def __init__(self, where, zs, want, spare, g_ref, acc, crecv, a1, b1, a2, b2, asem, cs, cr, a1s, a1r, b1s, b1r, a2s, a2r, b2s, b2r):
        self.k, self.c, self.z, self.y, self.x = where
        self.zs, self.want, self.spare = zs, want, spare
        self.g_ref, self.acc, self.crecv = g_ref, acc, crecv
        self.bufs = (a1, b1, a2, b2)
        self.asem, self.cs, self.cr = asem, cs, cr
        self.sems = ((a1s, a1r), (b1s, b1r), (a2s, a2r), (b2s, b2r))
        z, y, x, c = self.z, self.y, self.x, self.c
        self.xdev, self.ydev, self.cdev = (z * 4 + y * 2 + 1 - x, c), (z * 4 + (1 - y) * 2 + x, c), (self.k, 1 - c)

    def at(self, zo, oy, ox):
        return zo, (1 - self.y if oy else self.y), (1 - self.x if ox else self.x)

    def chip(self, zo, yo, xo):
        return zo * 4 + yo * 2 + xo

    def local(self, zo, yo, xo):
        return self.chip(zo, yo, xo)

    def load(self, item):
        i = self.local(*item)
        return pltpu.make_async_copy(self.g_ref.at[self.chip(*item), pl.ds(37 * self.c, 37)], self.acc.at[i], self.asem.at[i])

    def ccopy(self, item):
        i = self.local(*item)
        return rcopy(self.g_ref.at[self.chip(*item), pl.ds(37 * (1 - self.c), 37)], self.crecv.at[i + self.spare], self.cs.at[i], self.cr.at[i], self.cdev)

    def hop(self, which, item, slot, p, dev):
        s, r = self.sems[which]
        return rcopy(self.acc.at[self.local(*item), pl.ds(*PARTS[p])], self.bufs[which].at[slot], s.at[slot], r.at[slot], dev)

    def a1(self, zo, xo):
        return self.hop(0, (zo, 1 - self.y, xo), self.zs.index(zo) * 2 + xo, 0, self.ydev)

    def b1(self, zo, yo):
        return self.hop(1, (zo, yo, 1 - self.x), self.zs.index(zo) * 2 + yo, 1, self.xdev)

    def a2(self, zo):
        return self.hop(2, (zo, self.y, 1 - self.x), self.zs.index(zo), 0, self.xdev)

    def b2(self, zo):
        return self.hop(3, (zo, 1 - self.y, self.x), self.zs.index(zo), 1, self.ydev)

    def gain(self, item, p, which, slot):
        off, n = PARTS[p]
        i, acc, buf = self.local(*item), self.acc, self.bufs[which]
        acc[i, pl.ds(off, n)] = acc[i, pl.ds(off, n)] + buf[slot]

    def begin(self, zo, oy, ox):
        item = self.at(zo, oy, ox)

        def go():
            self.load(item).start()
            self.ccopy(item).start()
        guarded(self.want(*item), go)

    def first(self, zo, oy, ox):
        item = self.at(zo, oy, ox)

        def go():
            self.load(item).wait()
            self.ccopy(item).wait_recv()
            i = self.local(*item)
            self.acc[i] = self.acc[i] + self.crecv[i + self.spare]
            if oy:
                self.a1(zo, item[2]).start()
            if ox:
                self.b1(zo, item[1]).start()
        guarded(self.want(*item), go)

    def second(self, zo):
        ia, ib = self.at(zo, 0, 1), self.at(zo, 1, 0)
        n = self.zs.index(zo) * 2

        def go_a():
            self.a1(zo, 1 - self.x).wait_recv()
            self.gain(ia, 0, 0, n + 1 - self.x)
            self.a2(zo).start()

        def go_b():
            self.b1(zo, 1 - self.y).wait_recv()
            self.gain(ib, 1, 1, n + 1 - self.y)
            self.b2(zo).start()
        guarded(self.want(*ia), go_a)
        guarded(self.want(*ib), go_b)

    def third(self, zo):
        item = self.at(zo, 0, 0)
        n = self.zs.index(zo)

        def go():
            self.a1(zo, self.x).wait_recv()
            self.b1(zo, self.y).wait_recv()
            self.a2(zo).wait_recv()
            self.b2(zo).wait_recv()
            i = self.local(*item)
            for p, (h, u), at in ((0, (0, 2), self.x), (1, (1, 3), self.y)):
                off, m = PARTS[p]
                self.acc[i, pl.ds(off, m)] = (self.acc[i, pl.ds(off, m)] + self.bufs[h][n * 2 + at]) + self.bufs[u][n]
        guarded(self.want(*item), go)

    def finish(self):
        for zo in self.zs:
            for oy in (0, 1):
                for ox in (0, 1):
                    item = self.at(zo, oy, ox)

                    def sent(item=item, oy=oy, ox=ox, zo=zo):
                        self.ccopy(item).wait_send()
                        if oy:
                            self.a1(zo, item[2]).wait_send()
                        if ox:
                            self.b1(zo, item[1]).wait_send()
                        if ox and not oy:
                            self.a2(zo).wait_send()
                        if oy and not ox:
                            self.b2(zo).wait_send()
                    guarded(self.want(*item), sent)


def reducer_scratch():
    bf, sem = jnp.bfloat16, pltpu.SemaphoreType.DMA
    tile = (8, D)
    return [
        pltpu.VMEM((16, 37) + tile, bf), pltpu.VMEM((11, 37) + tile, bf),
        pltpu.VMEM((8, 19) + tile, bf), pltpu.VMEM((8, 18) + tile, bf), pltpu.VMEM((4, 19) + tile, bf), pltpu.VMEM((4, 18) + tile, bf),
        sem((16,)), sem((16,)), sem((16,)),
        sem((8,)), sem((8,)), sem((8,)), sem((8,)), sem((4,)), sem((4,)), sem((4,)), sem((4,)),
    ]


def early_item(zo, yo, xo):
    return zo >= 2 if zo != 1 else yo + xo > 0


def late_item(zo, yo, xo):
    return zo == 0 if zo != 1 else yo + xo == 0


ZCUTS = ((0, 10), (10, 9), (19, 9), (28, 9))


class Chain:
    def __init__(self, where, acc, up, dn, us, ur, ds_, dr):
        self.k, self.c, self.z, self.y, self.x = where
        self.acc = acc
        self.ways = {1: (up, us, ur, (jnp.minimum(self.k + 4, 15), self.c)), -1: (dn, ds_, dr, (jnp.maximum(self.k - 4, 0), self.c))}

    def chip(self, zo):
        return zo * 4 + self.y * 2 + self.x

    def copy(self, zo, way, p):
        buf, s, r, dev = self.ways[way]
        part = pl.ds(*ZCUTS[p])
        return rcopy(self.acc.at[self.chip(zo), part], buf.at[zo, part], s.at[zo, p], r.at[zo, p], dev)

    def move(self, zs, zo, way, take=True, give=True, also=None):
        cond = self.z == zs if also is None else (self.z == zs) & also

        @pl.when(cond)
        def _():
            i = self.chip(zo)
            for p in range(4):
                if take:
                    self.copy(zo, way, p).wait_recv()
                    part = pl.ds(*ZCUTS[p])
                    self.acc[i, part] = self.acc[i, part] + self.ways[way][0][zo, part]
                if give:
                    self.copy(zo, way, p).start()

    def sent(self, zs, zo, way):
        @pl.when(self.z == zs)
        def _():
            for p in range(4):
                self.copy(zo, way, p).wait_send()


def chain_scratch():
    bf, sem = jnp.bfloat16, pltpu.SemaphoreType.DMA
    return [pltpu.VMEM((4, 37, 8, D), bf)] * 2 + [sem((4, 4))] * 4


def backward_kernel(tiles, q_ref, k_ref, v_ref, do_ref, p_hbm, code_hbm, gfi_in, low_in, feats_in, grads_in, m_ref, one_ref, two_ref,
                    grad_out, grads, step_ref, new1_ref, new2_ref, spread,
                    pbuf, qv, kv, vv, dov, psem, code_ref, csem, dsv, dssem, group, gsem, counts, dks, dvs, out, come, sends, recvs, back, bias,
                    wq, wk, wv, low, gfi, feats, dwl, dwq, dwk, dwv, vgrads, wsem, ssem, isem,
                    total, ebuf, sq, sqr, win, mv, onev, twov, lsem, es, er, qs, qr, *scratch):
    f32, bf = jnp.float32, jnp.bfloat16
    where = place()
    k, c, z, y, x = where
    d = 2 * k + c
    shared = grads.reshape(16, CHIP, 8, D)
    rs = Reducer(where, (0, 1, 2, 3), early_item, -5, shared, *scratch[:17])
    late = Reducer(where, (0, 1, 2, 3), late_item, 6, shared, *scratch[:17])
    acc = rs.acc
    zc = Chain(where, acc, *scratch[17:])
    xdev, ydev, cdev = rs.xdev, rs.ydev, rs.cdev
    column_devs = [((z + s) % 4 * 4 + y * 2 + x, c) for s in (1, 2, 3)]
    prev = (jnp.where(c == 1, k, jnp.maximum(k - 1, 0)), 1 - c)
    nxt = (jnp.where(c == 0, k, jnp.minimum(k + 1, 15)), 1 - c)
    bar = pltpu.get_barrier_semaphore()
    far_next, far_prev = (c == 1) & (k < 15), (c == 0) & (k > 0)
    for dev in [xdev, ydev, cdev] + column_devs:
        pl.semaphore_signal(bar, inc=1, device_id=dev, device_id_type=MESH)

    @pl.when(far_next)
    def _():
        pl.semaphore_signal(bar, inc=1, device_id=nxt, device_id_type=MESH)

    @pl.when(far_prev)
    def _():
        pl.semaphore_signal(bar, inc=1, device_id=prev, device_id_type=MESH)

    keys, rows = code_ref.shape

    def fetch_soft(pair, hh):
        return pltpu.make_async_copy(p_hbm.at[2 * pair + hh], pbuf.at[hh], psem.at[0, hh])

    def fetch(p):
        slot = p % 2
        lanes = pl.ds(pl.multiple_of(p * 128, 128), 128)
        return [pltpu.make_async_copy(r.at[:, lanes], v.at[slot], psem.at[1 + i, slot]) for i, (r, v) in enumerate(((q_ref, qv), (k_ref, kv), (v_ref, vv), (do_ref, dov)))]

    for copy in fetch(0) + [fetch_soft(0, 0), fetch_soft(0, 1)]:
        copy.start()
    pl.semaphore_wait(bar, 6 + jnp.where(far_next | far_prev, 1, 0))
    corners = ((1, 1), (1, 0), (0, 1), (0, 0))
    for oy, ox in corners:
        rs.begin(2, oy, ox)
    code_copy = pltpu.make_async_copy(code_hbm, code_ref, csem.at[0])
    inputs = [pltpu.make_async_copy(r, v, isem.at[i]) for i, (r, v) in enumerate(((low_in, low), (gfi_in, gfi), (feats_in, feats)))]
    loads = pieces(tiles, wq, 16, 96, wsem, 8) + pieces(tiles, wv, 208, 96, wsem, 4) + pieces(tiles, wk, 112, 96, wsem, 0)
    shards = [pltpu.make_async_copy(r, v, lsem.at[i]) for i, (r, v) in enumerate(((m_ref, mv), (one_ref, onev), (two_ref, twov)))]
    for copy in [code_copy] + inputs + loads + shards:
        copy.start()
    own, other = pl.ds(c * rows, rows), pl.ds((1 - c) * rows, rows)

    def swap(pair):
        return rcopy(out.at[pair], come.at[pair], sends.at[pair], recvs.at[pair], cdev)

    def settle(pair):
        slot = pair % 2
        swap(pair).wait_recv()
        lanes = pl.ds(pl.multiple_of(pair * 128, 128), 128)
        dk = dks[slot, own, :] + come[pair, 0].astype(f32)
        dv = dvs[slot, own, :] + come[pair, 1].astype(f32)
        back[1, :, lanes] = dk.astype(bf)
        back[2, :, lanes] = dv.astype(bf)
        bias[1, :, lanes] = col_sum(dv)

    def lay(pair, hh):
        return pltpu.make_async_copy(dsv.at[hh], spread.at[:, 2 * pair + hh], dssem.at[hh])

    plan = {
        0: [(rs.first, 2, 0, 0), (rs.first, 2, 0, 1), (rs.first, 2, 1, 0), (rs.first, 3, 1, 1), (rs.begin, 1, 1, 1), (rs.begin, 1, 1, 0), (rs.begin, 1, 0, 1), (rs.begin, 1, 0, 0)],
        1: [(rs.first, 3, 1, 0), (rs.first, 3, 0, 0), (rs.second, 2), (rs.first, 1, 1, 1), (rs.first, 3, 0, 1)],
        5: [(rs.second, 3)],
    }
    rs.begin(3, 1, 1)
    rs.begin(3, 1, 0)
    rs.begin(3, 0, 1)
    rs.begin(3, 0, 0)
    rs.first(2, 1, 1)

    def pair_of_heads(pair, _):
        slot = pair % 2

        @pl.when(pair < H // 2 - 1)
        def _():
            for copy in fetch(pair + 1):
                copy.start()

        for copy in fetch(pair):
            copy.wait()
        lanes = pl.ds(pl.multiple_of(pair * 128, 128), 128)
        dq = []
        for hh in range(2):
            fetch_soft(pair, hh).wait()
            qm = half(qv[slot], hh)
            dom = half(dov[slot], hh)
            g = lax.dot_general(vv[slot], dom, NT, preferred_element_type=f32)
            p = pbuf[hh]
            pf = p.astype(f32)
            inner = jnp.sum(jnp.sum((g * pf).reshape(keys // 8, 8, rows), axis=0), axis=0, keepdims=True)
            ds = (pf * (g - inner)).astype(bf)

            @pl.when(pair > 0)
            def _():
                lay(pair - 1, hh).wait()

            dsv[hh] = ds.reshape(keys // 8, 8, rows)
            lay(pair, hh).start()
            dv = jnp.dot(p, dom, preferred_element_type=f32)

            @pl.when(pair < H // 2 - 1)
            def _():
                fetch_soft(pair + 1, hh).start()

            dk = jnp.dot(ds, qm, preferred_element_type=f32)
            if hh == 0:
                dvs[slot] = dv
                dks[slot] = dk
            else:
                dvs[slot] += dv
                dks[slot] += dk
            dq.append(lax.dot_general(kv[slot], ds, TN, preferred_element_type=f32))
        out[pair, 0] = dks[slot, other, :].astype(bf)
        out[pair, 1] = dvs[slot, other, :].astype(bf)
        swap(pair).start()
        sub = lax.broadcasted_iota(jnp.int32, dq[0].shape, 0)
        dqf = jnp.where(sub < 64, dq[0], dq[1]).T * 0.125
        back[0, :, lanes] = dqf.astype(bf)
        bias[0, :, lanes] = col_sum(dqf)

        @pl.when(pair > 0)
        def _():
            settle(pair - 1)

        for i, steps in plan.items():
            @pl.when(pair == i)
            def _():
                for f, *a in steps:
                    f(*a)
        return 0

    lax.fori_loop(0, H // 2, pair_of_heads, 0)
    for hh in range(2):
        lay(H // 2 - 1, hh).wait()
    for copy in inputs + loads:
        copy.wait()

    def through(i, w, dw):
        dw[...] = lax.dot_general(low[...], back[i], TN, preferred_element_type=f32).astype(bf).reshape(96, 8, D)
        return lax.dot_general(back[i], matrix(w[...]), NT, preferred_element_type=f32)

    stores = []

    def keep(dw, first, count, base):
        made = pieces(grads, dw, first, count, ssem, base, True)
        for copy in made:
            copy.start()
        stores.extend(made)

    gfi[...] += through(0, wq, dwq)
    keep(dwq, 16, 96, 0)
    settle(H // 2 - 1)
    gfi[...] += through(2, wv, dwv)
    keep(dwv, 208, 96, 8)
    whole = gfi[...] + through(1, wk, dwk)
    keep(dwk, 112, 96, 4)
    gfi[...] = whole
    shown = pltpu.make_async_copy(gfi, grad_out, isem.at[6])
    shown.start()
    layout_bias = jnp.sum(col_sum(whole), axis=0, keepdims=True)
    dwl[...] = lax.dot_general(feats[...], whole.astype(bf), TN, preferred_element_type=f32).astype(bf).reshape(16, 8, D)
    keep(dwl, 0, 16, 12)

    def block(lines):
        return jnp.concatenate(lines + [jnp.zeros((8 - len(lines), D), f32)]).astype(bf)

    vgrads[0] = block([layout_bias])
    vgrads[1] = block([jnp.sum(bias[0], axis=0, keepdims=True)])
    vgrads[2] = block([jnp.sum(bias[1], axis=0, keepdims=True)])
    vgrads[3] = jnp.zeros((8, D), bf)
    held = {0: 0, 1: 1, 4: 2}
    for i, ch in enumerate((0, 1, 2, 3, 4)):
        copy = pltpu.make_async_copy(vgrads.at[held.get(ch, 3)], grads.at[vector_at(ch)], ssem.at[16 + i])
        copy.start()
        stores.append(copy)
    for copy in stores:
        copy.wait()
    for oy, ox in corners:
        for zo in (0, 1):
            late.begin(zo, oy, ox)

    GROUPS = 16

    def take_groups(i):
        return pltpu.make_async_copy(spread.at[pl.ds(i * GROUPS, GROUPS)], group.at[i % 2], gsem.at[i % 2])

    bucket = lax.broadcasted_iota(jnp.int32, (BUCKETS, rows), 0)
    steps = keys // 8 // GROUPS
    code_copy.wait()
    take_groups(0).start()
    counts[...] = jnp.zeros_like(counts)

    def count_some(first, n):
        for i in range(first, first + n):
            if i + 1 < steps:
                take_groups(i + 1).start()
            take_groups(i).wait()

            def count(j, run, i=i):
                code = code_ref[pl.ds(pl.multiple_of((i * GROUPS + j) * 8, 8), 8), :]
                hot = jnp.concatenate(
                    [jnp.where(jnp.broadcast_to(code[r : r + 1], bucket.shape) == bucket, 1.0, 0.0) for r in range(8)]
                ).astype(bf)
                return run + lax.dot_general(group[i % 2, j].reshape(8 * H, rows), hot, NT, preferred_element_type=f32)

            counts[...] = lax.fori_loop(0, GROUPS, count, counts[...], unroll=8)

    early_one, late_one = rs.want(1, y, x), late.want(1, y, x)
    count_some(0, 1)
    late.first(0, 1, 1)
    late.first(1, 1, 1)
    late.first(0, 1, 0)
    late.first(1, 1, 0)
    rs.third(3)
    zc.move(0, 3, 1, take=False)
    late.first(0, 0, 1)
    late.first(1, 0, 1)
    rs.third(2)
    count_some(1, 1)
    zc.move(1, 3, 1)
    count_some(2, 1)
    zc.move(3, 2, -1, take=False)
    count_some(3, 1)
    late.second(0)
    late.second(1)
    rs.first(1, 0, 0)
    count_some(4, 1)
    rs.first(1, 1, 0)
    rs.first(1, 0, 1)
    rs.second(1)
    late.first(0, 0, 0)
    late.first(1, 0, 0)
    count_some(5, 1)
    zc.move(0, 2, 1, take=False)
    count_some(6, 1)
    zc.move(1, 2, 1)
    zc.move(2, 3, 1)
    late.third(0)
    zc.move(1, 0, -1)
    zc.move(2, 0, -1)
    zc.move(3, 0, -1, take=False)
    late.third(1)
    zc.move(0, 1, 1, take=False, also=late_one)
    zc.move(3, 1, -1, take=False, also=late_one)
    zc.move(2, 1, -1, also=late_one)
    rs.third(1)
    zc.move(0, 1, 1, take=False, also=early_one)
    zc.move(3, 1, -1, take=False, also=early_one)
    count_some(7, 1)
    zc.move(2, 1, -1, also=early_one)
    table = table_row(counts[...], (8, D))

    total[...] = acc[k].astype(f32)

    def add(way, zo):
        buf = zc.ways[way][0]
        for p in range(4):
            zc.copy(zo, way, p).wait_recv()
        total[...] = total[...] + buf[zo].astype(f32)

    @pl.when(z == 0)
    def _():
        add(-1, 0)

    @pl.when(z == 1)
    def _():
        add(1, 1)
        add(-1, 1)

    @pl.when(z == 2)
    def _():
        add(1, 2)
        add(-1, 2)

    @pl.when(z == 3)
    def _():
        add(1, 3)

    early = early_vectors(k)
    nw0 = jnp.where(early, 36, 37)
    vecs = early == (c == 0)
    mine = jnp.where(vecs, 36, 37)
    to_next = rcopy(total.at[pl.ds(mine - EDGE, EDGE)], ebuf.at[0], es.at[0], er.at[0], nxt)
    to_prev = rcopy(total.at[pl.ds(0, EDGE)], ebuf.at[1], es.at[1], er.at[1], prev)

    @pl.when(d < 31)
    def _():
        to_next.start()

    @pl.when(d > 0)
    def _():
        to_prev.start()

    def square(i, run):
        t = total[i]
        t = t * t
        for j in range(6):
            run = run + t[:, 128 * j:128 * j + 128]
        return run

    squares = lax.fori_loop(0, 37, square, jnp.zeros((8, 128), f32))
    lines = [jnp.sum(squares, axis=0, keepdims=True)] + [table[0:1, 128 * i : 128 * i + 128] for i in range(3)]
    sq[0] = jnp.concatenate(lines + [jnp.zeros((4, 128), f32)])
    rounds = [rcopy(sq.at[i], sqr.at[i], qs.at[i], qr.at[i], dev) for i, dev in enumerate((cdev, xdev, ydev))]
    hops = [rcopy(sq.at[3], sqr.at[3 + i], qs.at[3 + i], qr.at[3 + i], column_devs[i]) for i in range(3)]
    rounds[0].start()
    q, sh = shard_start(d)
    base = q - FRONT

    def flatten(ref, i, at, wide):
        @pl.when(wide)
        def _():
            t = ref[i]
            for j in range(6):
                win[pl.ds(at + j, 8, stride=24), :] = t[:, 128 * j:128 * j + 128]

        @pl.when(jnp.logical_not(wide))
        def _():
            t = ref[i]
            for j in range(6):
                win[pl.ds(at + j, 8, stride=6), :] = t[:, 128 * j:128 * j + 128]

    own_vectors = vecs & (vector_row(k, -1) >= 0)

    @pl.when(own_vectors)
    def _():
        flatten(total, 36, vector_row(k, q) - base, k < 0)

    w0 = jnp.where(c == 0, 73 * k, 73 * k + nw0)

    @pl.loop(0, mine)
    def _(t):
        at, wide = tile_start(w0 + t)
        flatten(total, t, at - base, wide)

    rounds[0].wait_recv()
    sq[1] = sq[0] + sqr[0]
    rounds[1].start()
    @pl.when(d > 0)
    def _():
        to_next.wait_recv()

        @pl.loop(0, EDGE)
        def _(t):
            at, wide = tile_start(w0 - EDGE + t)
            flatten(ebuf.at[0], t, at - base, wide)

    @pl.when(d < 31)
    def _():
        to_prev.wait_recv()

        @pl.loop(0, EDGE)
        def _(t):
            at, wide = tile_start(w0 + mine + t)
            flatten(ebuf.at[1], t, at - base, wide)

    rounds[1].wait_recv()
    sq[2] = sq[1] + sqr[1]
    rounds[2].start()
    rounds[2].wait_recv()
    sq[3] = sq[2] + sqr[2]
    for h in hops:
        h.start()
    for h in hops:
        h.wait_recv()
    summed = (sq[3] + sqr[4]) + (sqr[3] + sqr[5])

    @pl.when(d == 0)
    def _():
        for i in range(3):
            win[pl.ds(FRONT + 774 + i, 1), :] = summed[1 + i : 2 + i]

    sub = lax.broadcasted_iota(jnp.int32, (8, 128), 0)
    entries = jnp.where(sub == 0, summed, jnp.where(sub < 4, summed * summed, 0.0))
    square_sum = jnp.sum(jnp.sum(entries, axis=1, keepdims=True), axis=0, keepdims=True)
    factor = jnp.minimum(1.0, lax.rsqrt(square_sum / RAW + 1e-06))
    for s in shards:
        s.wait()
    lanes = lax.broadcasted_iota(jnp.int32, (80, 128), 1)
    rowi = lax.broadcasted_iota(jnp.int32, (80, 128), 0)
    back = (128 - sh) % 128

    @pl.loop(0, ROWS // 80)
    def _(i):
        r = pl.multiple_of(i * 80, 8)
        here = pltpu.roll(win[pl.ds(FRONT + r, 80), :], back, 1)
        there = pltpu.roll(win[pl.ds(FRONT + 1 + r, 80), :], back, 1)
        grad = jnp.where(lanes < 128 - sh, here, there) * factor
        entry = (d == 0) & (rowi + r < ENTRY_ROWS)
        rate = jnp.where(entry, learn_rate * layer_decay, learn_rate)
        one = beta_one * onev[pl.ds(r, 80), :] + (1.0 - beta_one) * grad
        two = beta_two * twov[pl.ds(r, 80), :] + (1.0 - beta_two) * grad * grad
        fixed_one = one / (1.0 - beta_one ** STEP)
        fixed_two = two / (1.0 - beta_two ** STEP)
        step = -rate * (fixed_one / (jnp.sqrt(fixed_two) + adam_eps) + weight_decay * mv[pl.ds(r, 80), :])
        mv[pl.ds(r, 80), :] = step
        onev[pl.ds(r, 80), :] = one
        twov[pl.ds(r, 80), :] = two

    results = [pltpu.make_async_copy(v, r, lsem.at[i]) for i, (v, r) in enumerate(((mv, step_ref), (onev, new1_ref), (twov, new2_ref)))]
    for copy in results:
        copy.start()

    for h in rounds + hops:
        h.wait_send()

    @pl.when(d < 31)
    def _():
        to_next.wait_send()

    @pl.when(d > 0)
    def _():
        to_prev.wait_send()

    rs.finish()
    late.finish()
    for zs in (0, 1, 2):
        zc.sent(zs, 3, 1)
    for zs in (0, 1):
        zc.sent(zs, 2, 1)
    zc.sent(3, 2, -1)
    zc.sent(0, 1, 1)
    zc.sent(3, 1, -1)
    zc.sent(2, 1, -1)
    for zs in (1, 2, 3):
        zc.sent(zs, 0, -1)
    for pair in range(H // 2):
        swap(pair).wait_send()
    shown.wait()
    for copy in results:
        copy.wait()


def backward_and_step(tiles, query, key_all, value_all, grad_context, soft, code, gfi, low, feats, grads, master, first_moment, second_moment):
    def rows_of(v):
        return jnp.pad(v, (0, ROWS * 128 - SHARD)).reshape(ROWS, 128)

    rows, keys = query.shape[0], key_all.shape[0]
    f32, bf = jnp.float32, jnp.bfloat16
    any_ = pl.BlockSpec(memory_space=pl.ANY)
    S, V, sem = jax.ShapeDtypeStruct, pltpu.VMEM, pltpu.SemaphoreType.DMA
    w = V((96, 8, D), bf)
    tile = (8, D)
    line = V((ROWS, 128), f32)
    outs = pl.pallas_call(
        backward_kernel,
        out_shape=[S((rows, D), f32), S(grads.shape, bf)] + [S((ROWS, 128), f32)] * 3 + [S((keys // 8, H, 8, rows), bf)],
        in_specs=[any_] * 14,
        out_specs=[any_] * 6,
        scratch_shapes=[
            V((2, keys, rows), bf), V((2, rows, 128), bf), V((2, keys, 128), bf), V((2, keys, 128), bf), V((2, rows, 128), bf), sem((5, 2)),
            V((keys, rows), jnp.int32), sem((1,)), V((2, keys // 8, 8, rows), bf), sem((2,)), V((2, 16, H, 8, rows), bf), sem((2,)),
            V((8 * H, 8 * BUCKETS), f32),
            V((2, keys, 128), f32), V((2, keys, 128), f32), V((6, 2, rows, 128), bf), V((6, 2, rows, 128), bf), sem((6,)), sem((6,)),
            V((3, rows, D), bf), V((2, 8, D), f32),
            w, w, w, V((rows, D), bf), V((rows, D), f32), V((rows, LF), bf), V((16, 8, D), bf), w, w, w, V((4, 8, D), bf),
            sem((12,)), sem((24,)), sem((7,)),
            V((37,) + tile, f32), V((2, EDGE) + tile, f32), V((4, 8, 128), f32), V((6, 8, 128), f32),
            V((WIN2, 128), f32), line, line, line, sem((3,)), sem((2,)), sem((2,)), sem((6,)), sem((6,)),
        ] + reducer_scratch() + chain_scratch(),
        input_output_aliases={10: 1},
        compiler_params=pltpu.CompilerParams(collective_id=5, has_side_effects=True, vmem_limit_bytes=63 << 20),
        name="backward_and_step",
    )(tiles, query, key_all, value_all, grad_context, soft, code, gfi, low, feats, grads, rows_of(master), rows_of(first_moment), rows_of(second_moment))
    return outs[0], [o.reshape(-1)[:SHARD] for o in outs[2:5]]


def from_tiles(tiles):
    got = {}
    for name, first, count in WEIGHTS:
        block = jnp.concatenate([tiles[s : s + n] for s, _, n in slots_of(first, count)])
        if name == 12:
            block = block.reshape(96, 4, 8, D).transpose(0, 2, 1, 3)
        got[name] = block.reshape(-1, FF if name == 12 else D)
    for name, chip, row in VECTORS:
        block = tiles[vector_at(chip)]
        if name == 13:
            got[name] = block[row : row + 4].reshape(FF)
        elif name == 2:
            got[name] = block[row, : BUCKETS * H].reshape(BUCKETS, H)
        else:
            got[name] = block[row]
    return [got[i] for i in range(18)]


def to_tiles(whole):
    by_name = [p.astype(jnp.bfloat16) for p in whole]
    weights = []
    for name, first, count in WEIGHTS:
        got = by_name[name]
        if name == 12:
            got = got.reshape(96, 8, 4, D).transpose(0, 2, 1, 3)
        weights.append(got.reshape(count, 8, D))
    cuts = []
    for chip in range(16):
        held = [(r, by_name[n]) for n, c, r in VECTORS if c == chip]
        rows = [jnp.pad(v.reshape(-1), (0, -v.size % D)).reshape(-1, D) for _, v in held]
        block = jnp.concatenate(rows + [jnp.zeros((8 - sum(r.shape[0] for r in rows), D), jnp.bfloat16)])
        cuts.append((73 * chip + vector_slot(chip), block[None]))
    parts = []
    for (name, first, count), tiles in zip(WEIGHTS, weights):
        at = first
        for w, block in [c for c in cuts if first <= c[0] < first + count]:
            if w > at:
                parts.append(tiles[at - first : w - first])
            parts.append(block)
            at = w
        parts.append(tiles[at - first :])
    parts.extend(block for w, block in cuts if w == 1168)
    return jnp.concatenate(parts)


def per_device(
    custom, tokens, cotangent, page_boxes, page_lengths, padding, buckets, master, first_moment, second_moment
):
    rows = tokens.shape[1]
    feats = layout_features(page_boxes.reshape(4, rows)).astype(jnp.bfloat16)
    pad = jnp.broadcast_to(padding, (8, rows))
    if custom:
        tiles, hidden, low, query, keys, values, ctx, soft, code = gather_and_attend(
            master, tokens[0], feats, pad, buckets[0], page_lengths
        )
        tiles = tiles.reshape(16 * CHIP, 8, D)
    else:
        tiles = to_tiles(unpack(lax.all_gather(master.astype(jnp.bfloat16), ("dp", "seq"), axis=0, tiled=True)))
        hidden, low, query, keys, values, pads = enter(tiles, tokens[0], feats, pad)
        ctx, soft, code = attend(query, keys, values, buckets[0], page_lengths, pads, tiles[vector_at(0)])
    activations, grad_first_in, grad_context, grads = middle(tiles, ctx, hidden, cotangent[0])
    if custom:
        input_grad, stepped = backward_and_step(
            tiles, query, keys, values, grad_context, soft, code, grad_first_in, low, feats, grads, master, first_moment, second_moment
        )
    else:
        dq, dk, dv, table = soft_back(query, keys, values, grad_context, soft, code)
        input_grad, grads = leave(tiles, dq, dk, dv, grad_first_in, low, feats, table, grads)
        flat = jnp.concatenate([p.astype(jnp.float32).reshape(-1) for p in from_tiles(grads)])
        grad = lax.psum_scatter(flat, ("dp", "seq"), scatter_dimension=0, tiled=True)
        square = lax.psum(jnp.sum(grad * grad), ("dp", "seq"))
        factor = jnp.minimum(1.0, lax.rsqrt(square / RAW + 1e-06))
        size = master.shape[0]
        index = lax.axis_index(("dp", "seq")) * size + jnp.arange(size, dtype=jnp.int32)
        stepped = adam_update(master, first_moment, second_moment, grad * factor, index)
    return (activations[None], input_grad[None]) + tuple(stepped)


def solution(mesh):
    in_specs = (
        P("dp", "seq", None),
        P("dp", "seq", None),
        P(None, "dp", "seq"),
        P("dp", None),
        P("dp", "seq"),
        P("dp", "seq", None),
        P(("dp", "seq")),
        P(("dp", "seq")),
        P(("dp", "seq")),
    )
    out_specs = (
        P("dp", "seq", None),
        P("dp", "seq", None),
        P(("dp", "seq")),
        P(("dp", "seq")),
        P(("dp", "seq")),
    )
    custom = dict(mesh.shape) == {"dp": 16, "seq": 2}
    return jax.shard_map(
        functools.partial(per_device, custom), mesh=mesh, in_specs=in_specs, out_specs=out_specs, check_vma=False
    )
```

```python
import functools

import jax
import jax.numpy as jnp
from jax import lax
from jax.experimental import pallas as pl
from jax.experimental.pallas import tpu as pltpu
from jax.sharding import PartitionSpec as P

D = 768
H = 12
HD = 64
FF = 3072
BUCKETS = 32
FREQ = 16
LF = 128
LAYERS = 1
BLOCK = 1024
STEP = 10
ENTRY = 99456
LAYER_PARAMS = 7087104
RAW = 7186560


beta_one = 0.8
beta_two = 0.98
adam_eps = 1e-06
learn_rate = 0.0006
layer_decay = 0.8
weight_decay = 0.1
norm_eps = 1e-05
masked_score = -1000000000.0


SHAPES = (
    (LF, D), (D,), (BUCKETS, H),
    (D, D), (D,), (D, D), (D, D), (D,), (D, D), (D,), (D,), (D,),
    (D, FF), (FF,), (FF, D), (D,), (D,), (D,),
)


def unpack(flat_params):
    pieces, offset = [], 0
    for shape in SHAPES:
        amount = shape[0] * (shape[1] if len(shape) > 1 else 1)
        pieces.append(flat_params[offset : offset + amount].reshape(shape))
        offset = offset + amount
    return pieces


def adam_update(master, first_moment, second_moment, gradient, global_index):
    exponent = jnp.where(
        global_index < ENTRY,
        LAYERS,
        jnp.maximum(LAYERS - 1 - (global_index - ENTRY) // LAYER_PARAMS, 0),
    )
    rate = jnp.where(
        global_index < RAW, learn_rate * jnp.power(layer_decay, exponent.astype(jnp.float32)), 0.0
    )
    moment_one = beta_one * first_moment + (1.0 - beta_one) * gradient
    moment_two = beta_two * second_moment + (1.0 - beta_two) * gradient * gradient
    fixed_one = moment_one / (1.0 - beta_one**STEP)
    fixed_two = moment_two / (1.0 - beta_two**STEP)
    param_step = -rate * (fixed_one / (jnp.sqrt(fixed_two) + adam_eps) + weight_decay * master)
    return (param_step, moment_one, moment_two)


def layout_features(page_boxes):
    rates_sin = jnp.power(10000.0, -jnp.arange(FREQ, dtype=jnp.float32) / FREQ)
    angles = page_boxes.astype(jnp.float32)[:, :, None] * rates_sin
    stacked = jnp.stack([jnp.sin(angles), jnp.cos(angles)], axis=1)
    return jnp.transpose(stacked, (2, 0, 1, 3)).reshape(page_boxes.shape[1], LF)


MESH = pl.DeviceIdType.MESH
SHARD = 224580
ROWS = 1760
TAIL, HEAD = 160, 176
WIN = 2176
SLOTS = 37
CHIP = 74
PARTS = ((0, 19), (19, 18))


def place():
    k = lax.axis_index("dp")
    return k, lax.axis_index("seq"), k // 4, (k // 2) % 2, k % 2


def shard_start(d):
    return d * 1754 + (d * 68) // 128, (d * 68) % 128


def early_vectors(k):
    return (k == 0) | (k == 4) | (k == 5)


def vector_row(k, other):
    at = other
    for chip, row in ((0, 768), (1, 5385), (4, 14607), (5, 19221), (10, 37671), (15, 56127)):
        at = jnp.where(k == chip, row, at)
    return at


def tile_start(w):
    at = w * 48
    for first, shift in ((16, 777 - 16 * 48), (112, 5391 - 112 * 48), (208, 9999 - 208 * 48), (304, 14613 - 304 * 48), (784, 37695 - 784 * 48)):
        at = jnp.where(w >= first, w * 48 + shift, at)
    wide = (w >= 400) & (w < 784)
    v = w - 400
    at = jnp.where(wide, 19239 + (v // 4) * 192 + (v % 4) * 6, at)
    return at, wide


def neighbours(k, c, z, y, x):
    t = k >= 0
    return [
        (t, (k, 1 - c)),
        (t, (z * 4 + y * 2 + 1 - x, c)),
        (t, (z * 4 + (1 - y) * 2 + x, c)),
        (z < 3, (jnp.minimum(k + 4, 15), c)),
        (z > 0, (jnp.maximum(k - 4, 0), c)),
        ((c == 1) & (k < 15), (jnp.minimum(k + 1, 15), 0)),
        ((c == 0) & (k > 0), (jnp.maximum(k - 1, 0), 1)),
    ]


def greet(k, c, z, y, x):
    bar = pltpu.get_barrier_semaphore()
    for cond, dev in neighbours(k, c, z, y, x):
        @pl.when(cond)
        def _():
            pl.semaphore_signal(bar, inc=1, device_id=dev, device_id_type=MESH)
    peers = 3
    for cond, _ in neighbours(k, c, z, y, x)[3:]:
        peers = peers + jnp.where(cond, 1, 0)
    pl.semaphore_wait(bar, peers)


def rcopy(src, dst, ssem, rsem, dev):
    return pltpu.make_async_remote_copy(src_ref=src, dst_ref=dst, send_sem=ssem, recv_sem=rsem, device_id=dev, device_id_type=MESH)


FRONT = 344
WIN2 = 2464
EDGE = 4
ENTRY_ROWS = 777


WEIGHTS = (
    (0, 0, 16),
    (3, 16, 96),
    (5, 112, 96),
    (6, 208, 96),
    (8, 304, 96),
    (12, 400, 384),
    (14, 784, 384),
)
VECTORS = (
    (1, 0, 0),
    (2, 0, 1),
    (4, 1, 0),
    (7, 4, 0),
    (9, 5, 0),
    (10, 5, 1),
    (11, 5, 2),
    (13, 10, 0),
    (15, 15, 0),
    (16, 15, 1),
    (17, 15, 2),
)


def slots_of(first, count):
    runs = []
    for w in range(first, first + count):
        chip, at = divmod(w, 73)
        slot = chip * CHIP + at + (1 if at >= vector_slot(chip) else 0)
        if runs and runs[-1][0] + runs[-1][2] == slot:
            runs[-1][2] += 1
        else:
            runs.append([slot, w - first, 1])
    return runs


def vector_slot(chip):
    return 36 if chip in (0, 4, 5) else 73


def vector_at(chip):
    return chip * CHIP + vector_slot(chip)


def pieces(tiles, held, first, count, sems, base, out=False):
    made = []
    for i, (slot, at, n) in enumerate(slots_of(first, count)):
        a, b = tiles.at[pl.ds(slot, n)], held.at[pl.ds(at, n)]
        a, b = (b, a) if out else (a, b)
        made.append(pltpu.make_async_copy(a, b, sems.at[base + i]))
    return made


def matrix(tile_rows):
    return tile_rows.reshape(-1, D)


def col_sum(v):
    return jnp.sum(v.reshape(-1, 8, v.shape[-1]), axis=0)


def norm_stats(v):
    mean = jnp.mean(v, axis=-1, keepdims=True)
    center = v - mean
    spread = jnp.mean(center * center, axis=-1, keepdims=True)
    inv = lax.rsqrt(spread + norm_eps)
    return center * inv, inv


def norm_back(grad, gain, hat, inv):
    g = grad * gain
    return inv * (g - jnp.mean(g, axis=-1, keepdims=True) - hat * jnp.mean(g * hat, axis=-1, keepdims=True))


ROOT_HALF = 0.7071067811865476
ROOT_TAU = 0.3989422804014327


def middle_kernel(tiles, ctx, hidden, cot, act_out, gfi_out, gctx_out, grads,
                  wo, wup, wdn, vecs, vf, act, slope, low1, hat1, inv1, hat2, inv2, a, sums, dwo, dwup, dwdn, vgrads, lsem, ssem):
    f32, bf = jnp.float32, jnp.bfloat16
    rows = ctx.shape[0]
    R = 64
    steps = rows // R
    loads_o = pieces(tiles, wo, 304, 96, lsem, 0)
    loads_u = pieces(tiles, wup, 400, 384, lsem, 4)
    loads_d = pieces(tiles, wdn, 784, 384, lsem, 12)
    loads_v = [pltpu.make_async_copy(tiles.at[vector_at(c)], vecs.at[i], lsem.at[20 + i]) for i, c in enumerate((5, 10, 15))]
    for c in loads_v + loads_o + loads_u + loads_d:
        c.start()
    up4 = wup.reshape(96, 4, 8, D)
    dup4 = dwup.reshape(96, 4, 8, D)

    def vec(i, r):
        return vf[i, pl.ds(r, 1), :]

    def each(f):
        @pl.loop(0, steps)
        def _(i):
            f(pl.ds(pl.multiple_of(i * R, R), R))

    for c in loads_v + loads_o:
        c.wait()
    vf[...] = vecs[...].astype(f32)
    a[...] = jnp.dot(ctx[...], matrix(wo[...]), preferred_element_type=f32)

    def first(sl):
        hat, inv = norm_stats(hidden[sl, :] + a[sl, :] + vec(0, 0))
        hat1[sl, :] = hat
        inv1[sl, :] = inv
        out = hat * vec(0, 1) + vec(0, 2)
        a[sl, :] = out
        low1[sl, :] = out.astype(bf)

    each(first)
    for c in loads_u + loads_d:
        c.wait()

    def up(j, _):
        for half in range(2):
            sl = pl.ds(half * (rows // 2), rows // 2)
            u = jnp.dot(low1[sl, :], matrix(up4[:, j]), preferred_element_type=f32) + vec(1, j)
            share = 0.5 * (1.0 + lax.erf(u * ROOT_HALF))
            act[j, sl, :] = (u * share).astype(bf)
            slope[j, sl, :] = share + u * jnp.exp(-0.5 * u * u) * ROOT_TAU
        return 0

    lax.fori_loop(0, 4, up, 0)

    def down(j, _):
        a[...] += jnp.dot(act[j], matrix(wdn[pl.ds(96 * j, 96)]), preferred_element_type=f32)
        return 0

    lax.fori_loop(0, 4, down, 0)
    sums[...] = jnp.zeros_like(sums)

    def second(sl):
        hat, inv = norm_stats(a[sl, :] + vec(2, 0))
        act_out[sl, :] = (hat * vec(2, 1) + vec(2, 2)).astype(bf)
        g = cot[sl, :].astype(f32)
        sums[6] += col_sum(g * hat)
        sums[7] += col_sum(g)
        back = norm_back(g, vec(2, 1), hat, inv)
        sums[5] += col_sum(back)
        a[sl, :] = back
        hat2[sl, :] = back.astype(bf)

    each(second)
    down_back = hat2

    def back(j, _):
        for half in range(2):
            sl = pl.ds(half * (rows // 2), rows // 2)
            g = lax.dot_general(down_back[sl, :], matrix(wdn[pl.ds(96 * j, 96)]), NT, preferred_element_type=f32) * slope[j, sl, :]
            sums[8 + j] += col_sum(g)
            act_back[sl, :] = g.astype(bf)
        dwdn[pl.ds(96 * j, 96)] = lax.dot_general(act[j], down_back[...], TN, preferred_element_type=f32).astype(bf).reshape(96, 8, D)
        dup4[:, j] = lax.dot_general(low1[...], act_back[...], TN, preferred_element_type=f32).astype(bf).reshape(96, 8, D)
        a[...] += lax.dot_general(act_back[...], matrix(up4[:, j]), NT, preferred_element_type=f32)
        return 0

    act_back = inv2
    lax.fori_loop(0, 4, back, 0)
    stores = pieces(grads, dwup, 400, 384, ssem, 4, True) + pieces(grads, dwdn, 784, 384, ssem, 12, True)
    for c in stores:
        c.start()

    def third(sl):
        g = a[sl, :]
        sums[3] += col_sum(g * hat1[sl, :])
        sums[4] += col_sum(g)
        back = norm_back(g, vec(0, 1), hat1[sl, :], inv1[sl, :])
        sums[2] += col_sum(back)
        gfi_out[sl, :] = back
        hat2[sl, :] = back.astype(bf)

    each(third)
    gctx_out[...] = lax.dot_general(hat2[...], matrix(wo[...]), NT, preferred_element_type=f32).astype(bf)
    dwo[...] = lax.dot_general(ctx[...], hat2[...], TN, preferred_element_type=f32).astype(bf).reshape(96, 8, D)
    for i, held in enumerate(((2, 3, 4), (8, 9, 10, 11), (5, 6, 7))):
        lines = [jnp.sum(sums[s], axis=0, keepdims=True) for s in held]
        lines.append(jnp.zeros((8 - len(held), D), f32))
        vgrads[i] = jnp.concatenate(lines).astype(bf)
    last = pieces(grads, dwo, 304, 96, ssem, 0, True)
    quiet = [ch for ch in range(6, 15) if ch != 10]
    vgrads[3] = jnp.zeros((8, D), bf)
    last += [pltpu.make_async_copy(vgrads.at[min(i, 3)], grads.at[vector_at(ch)], ssem.at[20 + i]) for i, ch in enumerate([5, 10, 15] + quiet)]
    for c in last:
        c.start()
    for c in stores + last:
        c.wait()


def middle(tiles, ctx, hidden, cot):
    rows = ctx.shape[0]
    f32, bf = jnp.float32, jnp.bfloat16
    vm, any_ = pl.BlockSpec(memory_space=pltpu.VMEM), pl.BlockSpec(memory_space=pl.ANY)
    S = jax.ShapeDtypeStruct
    return pl.pallas_call(
        middle_kernel,
        out_shape=[S((rows, D), bf), S((rows, D), f32), S((rows, D), bf), S((16 * CHIP, 8, D), bf)],
        in_specs=[any_, vm, vm, vm],
        out_specs=[vm, vm, vm, any_],
        scratch_shapes=[
            pltpu.VMEM((96, 8, D), bf), pltpu.VMEM((384, 8, D), bf), pltpu.VMEM((384, 8, D), bf), pltpu.VMEM((3, 8, D), bf), pltpu.VMEM((3, 8, D), f32),
            pltpu.VMEM((4, rows, D), bf), pltpu.VMEM((4, rows, D), f32), pltpu.VMEM((rows, D), bf),
            pltpu.VMEM((rows, D), f32), pltpu.VMEM((rows, 1), f32), pltpu.VMEM((rows, D), bf), pltpu.VMEM((rows, D), bf),
            pltpu.VMEM((rows, D), f32), pltpu.VMEM((12, 8, D), f32),
            pltpu.VMEM((96, 8, D), bf), pltpu.VMEM((384, 8, D), bf), pltpu.VMEM((384, 8, D), bf), pltpu.VMEM((4, 8, D), bf),
            pltpu.SemaphoreType.DMA((24,)), pltpu.SemaphoreType.DMA((32,)),
        ],
        compiler_params=pltpu.CompilerParams(vmem_limit_bytes=58 << 20),
        name="middle",
    )(tiles, ctx, hidden, cot)


NT = (((1,), (1,)), ((), ()))
TN = (((0,), (0,)), ((), ()))


def half(ref_value, hh):
    lanes = lax.broadcasted_iota(jnp.int32, ref_value.shape, 1)
    keep = lanes // 64 == hh
    return jnp.where(keep, ref_value, jnp.zeros_like(ref_value))


def page_of(at, lengths):
    end, page = 0, jnp.zeros(at.shape, jnp.int32)
    for i in range(4):
        end = end + lengths[0, i]
        page = page + jnp.where(at >= end, 1, 0)
    return page


def fill_codes(code_ref, buckets, pads, lengths):
    keys, rows = code_ref.shape
    own = lax.axis_index("seq") * rows
    tag = page_of(lax.broadcasted_iota(jnp.int32, (1, keys), 1), lengths) + 1
    tag = jnp.where(jnp.concatenate([pads[0, 0:1], pads[1, 0:1]], axis=1) > 0, tag, 0)
    for i in range(rows // 128):
        at = own + 128 * i + lax.broadcasted_iota(jnp.int32, (128, 1), 0)
        page = page_of(at, lengths) + 1
        for j in range(keys // 128):
            key_at = 128 * j + lax.broadcasted_iota(jnp.int32, (1, 128), 1)
            allowed = (page == tag[:, 128 * j : 128 * j + 128]) | (key_at == at)
            code = jnp.where(allowed, buckets[128 * i : 128 * i + 128, 128 * j : 128 * j + 128], BUCKETS)
            code_ref[128 * j : 128 * j + 128, 128 * i : 128 * i + 128] = code.T


def fill_table(tab_ref, lines):
    f32 = jnp.float32
    head = lax.broadcasted_iota(jnp.int32, (16, 128), 0)
    bucket = lax.broadcasted_iota(jnp.int32, (16, 128), 1)
    place_of = bucket * H + head
    tab = jnp.full((16, 128), masked_score, f32)
    for i in range(BUCKETS * H // 128):
        row = jnp.broadcast_to(lines[1:2, 128 * i : 128 * i + 128].astype(f32), (16, 128))
        inside = jnp.clip(place_of - 128 * i, 0, 127)
        got = jnp.take_along_axis(row, inside, axis=1, mode="promise_in_bounds")
        tab = jnp.where((place_of // 128 == i) & (bucket < BUCKETS) & (head < H), got, tab)
    tab_ref[...] = tab


def soft_head(head, q, k, code_ref, tab_ref, s_scr, p_ref):
    keys, rows = s_scr.shape
    f32, bf = jnp.float32, jnp.bfloat16
    qm = half(q, head % 2)
    line = jnp.broadcast_to(tab_ref[pl.ds(head, 1), :], (keys, 128))
    s = lax.dot_general(k, qm, NT, preferred_element_type=f32)
    cols = []
    for j in range(rows // 128):
        code = code_ref[:, 128 * j : 128 * j + 128]
        bias = jnp.take_along_axis(line, code, axis=1, mode="promise_in_bounds")
        cols.append(jnp.where(bias < 0.5 * masked_score, masked_score, s[:, 128 * j : 128 * j + 128] + bias))
    s = jnp.concatenate(cols, axis=1)
    s_scr[...] = s
    top = jnp.max(jnp.max(s.reshape(keys // 8, 8, rows), axis=0), axis=0, keepdims=True)
    e = jnp.exp(s_scr[...] - top)
    s_scr[...] = e
    inverse = 1.0 / jnp.sum(jnp.sum(e.reshape(keys // 8, 8, rows), axis=0), axis=0, keepdims=True)
    p_ref[...] = (s_scr[...] * inverse).astype(bf)


def context_pair(v, p_ref):
    vt = v.T
    out = [jnp.dot(vt, p_ref[hh], preferred_element_type=jnp.float32) for hh in range(2)]
    sub = lax.broadcasted_iota(jnp.int32, out[0].shape, 0)
    return jnp.where(sub < 64, out[0], out[1]).T.astype(jnp.bfloat16)


def attend_kernel(lengths, q_ref, k_ref, v_ref, buckets, pads, lines, ctx_ref, p_ref, code_ref, s_scr, tab_ref):
    pair = pl.program_id(0)

    @pl.when(pair == 0)
    def _():
        fill_codes(code_ref, buckets, pads, lengths)
        fill_table(tab_ref, lines)

    for hh in range(2):
        soft_head(2 * pair + hh, q_ref[...], k_ref[...], code_ref, tab_ref, s_scr, p_ref.at[hh])
    ctx_ref[...] = context_pair(v_ref[...], p_ref)


def attend(query, key_all, value_all, buckets, page_lengths, pads, lines):
    rows, keys = query.shape[0], key_all.shape[0]
    bf = jnp.bfloat16
    const = lambda p: (0, 0)
    return pl.pallas_call(
        attend_kernel,
        grid=(H // 2,),
        out_shape=[
            jax.ShapeDtypeStruct((rows, D), bf),
            jax.ShapeDtypeStruct((H, keys, rows), bf),
            jax.ShapeDtypeStruct((keys, rows), jnp.int32),
        ],
        in_specs=[
            pl.BlockSpec(memory_space=pltpu.SMEM),
            pl.BlockSpec((rows, 128), lambda p: (0, p)),
            pl.BlockSpec((keys, 128), lambda p: (0, p)),
            pl.BlockSpec((keys, 128), lambda p: (0, p)),
            pl.BlockSpec((rows, keys), const),
            pl.BlockSpec((2, 8, rows), lambda p: (0, 0, 0)),
            pl.BlockSpec((8, D), const),
        ],
        out_specs=[pl.BlockSpec((rows, 128), lambda p: (0, p)), pl.BlockSpec((2, keys, rows), lambda p: (p, 0, 0)), pl.BlockSpec((keys, rows), const)],
        scratch_shapes=[pltpu.VMEM((keys, rows), jnp.float32), pltpu.VMEM((16, 128), jnp.float32)],
        compiler_params=pltpu.CompilerParams(vmem_limit_bytes=56 << 20),
        name="attend",
    )(page_lengths, query, key_all, value_all, buckets, pads, lines)


def table_row(acc, shape):
    f32 = jnp.float32
    a = lax.broadcasted_iota(jnp.int32, acc.shape, 0) % 8
    b = lax.broadcasted_iota(jnp.int32, acc.shape, 1) // BUCKETS
    acc = jnp.where(a == b, acc, 0.0)
    heads = jnp.sum(acc.reshape(H, 8, 8 * BUCKETS), axis=1)
    lane = lax.broadcasted_iota(jnp.int32, (8 * BUCKETS, D), 1) // H
    wide = jnp.where(lane == lax.broadcasted_iota(jnp.int32, lane.shape, 0) % BUCKETS, 1.0, 0.0)
    out = jnp.dot(heads, wide, precision=lax.Precision.HIGHEST, preferred_element_type=f32)
    mine = lax.broadcasted_iota(jnp.int32, out.shape, 1) % H == lax.broadcasted_iota(jnp.int32, out.shape, 0)
    out = jnp.sum(jnp.where(mine, out, 0.0), axis=0, keepdims=True)
    return jnp.broadcast_to(out, shape)


def attend_back_kernel(q_ref, k_ref, v_ref, do_ref, p_ref, code_ref, dq_ref, dk_ref, dv_ref, tab_ref, spread, held):
    pair = pl.program_id(0)
    keys, rows = code_ref.shape
    f32, bf = jnp.float32, jnp.bfloat16
    STEP_ROWS = keys
    kt = k_ref[...].T
    dq = []
    for hh in range(2):
        qm = half(q_ref[...], hh)
        dom = half(do_ref[...], hh)

        def inner(i, total):
            at = pl.multiple_of(i * STEP_ROWS, STEP_ROWS)
            g = lax.dot_general(v_ref[pl.ds(at, STEP_ROWS), :], dom, NT, preferred_element_type=f32)
            w = g * p_ref[hh, pl.ds(at, STEP_ROWS), :].astype(f32)
            return total + jnp.sum(w.reshape(STEP_ROWS // 8, 8, rows), axis=0)

        total = lax.fori_loop(0, keys // STEP_ROWS, inner, jnp.zeros((8, rows), f32))
        total = jnp.sum(total, axis=0, keepdims=True)

        def grads(i, acc):
            at = pl.multiple_of(i * STEP_ROWS, STEP_ROWS)
            sl = pl.ds(at, STEP_ROWS)
            g = lax.dot_general(v_ref[sl, :], dom, NT, preferred_element_type=f32)
            p = p_ref[hh, sl, :]
            ds = p.astype(f32) * (g - total)
            wide = ds.reshape(STEP_ROWS // 8, 8, rows)
            if hh == 0:
                held[...] = wide
            else:
                both = jnp.concatenate([held[...], wide], axis=1).astype(bf)
                spread[:, pl.ds(pl.multiple_of(pair * 16, 16), 16), :] = both
            ds = ds.astype(bf)
            dv = jnp.dot(p, dom, preferred_element_type=f32)
            dk = jnp.dot(ds, qm, preferred_element_type=f32)
            if hh == 0:
                dv_ref[sl, :] = dv
                dk_ref[sl, :] = dk
            else:
                dv_ref[sl, :] += dv
                dk_ref[sl, :] += dk
            return acc + lax.dot_general(k_ref[sl, :], ds, TN, preferred_element_type=f32)

        dq.append(lax.fori_loop(0, keys // STEP_ROWS, grads, jnp.zeros((128, rows), f32)))
    sub = lax.broadcasted_iota(jnp.int32, dq[0].shape, 0)
    dq_ref[...] = jnp.where(sub < 64, dq[0], dq[1]).T * 0.125

    @pl.when(pair == H // 2 - 1)
    def _():
        bucket = lax.broadcasted_iota(jnp.int32, (BUCKETS, rows), 0)

        def count(i, acc):
            code = code_ref[pl.ds(pl.multiple_of(i * 8, 8), 8), :]
            hot = jnp.concatenate(
                [jnp.where(jnp.broadcast_to(code[r : r + 1], bucket.shape) == bucket, 1.0, 0.0) for r in range(8)]
            ).astype(bf)
            return acc + lax.dot_general(spread[i], hot, NT, preferred_element_type=f32)

        acc = lax.fori_loop(0, keys // 8, count, jnp.zeros((8 * H, 8 * BUCKETS), f32), unroll=8)
        tab_ref[...] = table_row(acc, tab_ref.shape)


def soft_back(query, key_all, value_all, grad_context, soft, code):
    rows, keys = query.shape[0], key_all.shape[0]
    f32 = jnp.float32
    row = pl.BlockSpec((rows, 128), lambda p: (0, p))
    key = pl.BlockSpec((keys, 128), lambda p: (0, p))
    dq, dk, dv, tab = pl.pallas_call(
        attend_back_kernel,
        grid=(H // 2,),
        out_shape=[
            jax.ShapeDtypeStruct((rows, D), f32),
            jax.ShapeDtypeStruct((keys, D), f32),
            jax.ShapeDtypeStruct((keys, D), f32),
            jax.ShapeDtypeStruct((8, D), f32),
        ],
        in_specs=[row, key, key, row, pl.BlockSpec((2, keys, rows), lambda p: (p, 0, 0)), pl.BlockSpec((keys, rows), lambda p: (0, 0))],
        out_specs=[row, key, key, pl.BlockSpec((8, D), lambda p: (0, 0))],
        scratch_shapes=[pltpu.VMEM((keys // 8, 8 * H, rows), jnp.bfloat16), pltpu.VMEM((keys // 8, 8, rows), f32)],
        compiler_params=pltpu.CompilerParams(vmem_limit_bytes=58 << 20),
        name="attend_back",
    )(query, key_all, value_all, grad_context, soft, code)
    return dq, dk, dv, tab


def meet_partner():
    dp, c = lax.axis_index("dp"), lax.axis_index("seq")
    partner = (dp, 1 - c)
    bar = pltpu.get_barrier_semaphore()
    pl.semaphore_signal(bar, inc=1, device_id=partner, device_id_type=MESH)
    pl.semaphore_wait(bar, 1)
    return c, partner


def enter_kernel(tiles, tokens, feats, pad, hidden, low, query, keys, values, pads, wl, wq, wk, wv, vecs, vf, lsem, sends, recvs):
    f32, bf = jnp.float32, jnp.bfloat16
    rows = tokens.shape[0]
    loads = [pltpu.make_async_copy(tiles.at[vector_at(ch)], vecs.at[i], lsem.at[i]) for i, ch in enumerate((0, 1, 4))]
    loads += pieces(tiles, wl, 0, 16, lsem, 4) + pieces(tiles, wk, 112, 96, lsem, 8)
    loads += pieces(tiles, wv, 208, 96, lsem, 12) + pieces(tiles, wq, 16, 96, lsem, 16)
    for c in loads:
        c.start()
    c, partner = meet_partner()
    own = pl.ds(c * rows, rows)

    def share(ref, i):
        return rcopy(ref.at[own], ref.at[own], sends.at[i], recvs.at[i], partner)

    pads[pl.ds(c, 1)] = pad[...].reshape(1, 8, rows)
    pair_pads = rcopy(pads.at[pl.ds(c, 1)], pads.at[pl.ds(c, 1)], sends.at[2], recvs.at[2], partner)
    pair_pads.start()
    for copy in loads:
        copy.wait()
    vf[...] = vecs[...].astype(f32)
    h = tokens[...].astype(f32) + jnp.dot(feats[...], matrix(wl[...]), preferred_element_type=f32) + vf[0, 0:1, :]
    hidden[...] = h
    low[...] = h.astype(bf)
    keys[own, :] = jnp.dot(low[...], matrix(wk[...]), preferred_element_type=f32).astype(bf)
    send_keys = share(keys, 0)
    send_keys.start()
    values[own, :] = (jnp.dot(low[...], matrix(wv[...]), preferred_element_type=f32) + vf[2, 0:1, :]).astype(bf)
    send_values = share(values, 1)
    send_values.start()
    query[...] = ((jnp.dot(low[...], matrix(wq[...]), preferred_element_type=f32) + vf[1, 0:1, :]) * 0.125).astype(bf)
    for copy in (pair_pads, send_keys, send_values):
        copy.wait()


def enter(tiles, tokens, feats, pad):
    rows = tokens.shape[0]
    f32, bf = jnp.float32, jnp.bfloat16
    vm, any_ = pl.BlockSpec(memory_space=pltpu.VMEM), pl.BlockSpec(memory_space=pl.ANY)
    S, sem = jax.ShapeDtypeStruct, pltpu.SemaphoreType.DMA
    w = pltpu.VMEM((96, 8, D), bf)
    return pl.pallas_call(
        enter_kernel,
        out_shape=[S((rows, D), f32), S((rows, D), bf), S((rows, D), bf), S((2 * rows, D), bf), S((2 * rows, D), bf), S((2, 8, rows), jnp.int32)],
        in_specs=[any_, vm, vm, vm],
        out_specs=[vm] * 6,
        scratch_shapes=[pltpu.VMEM((16, 8, D), bf), w, w, w, pltpu.VMEM((3, 8, D), bf), pltpu.VMEM((3, 8, D), f32), sem((20,)), sem((3,)), sem((3,))],
        compiler_params=pltpu.CompilerParams(collective_id=2, has_side_effects=True, vmem_limit_bytes=40 << 20),
        name="enter",
    )(tiles, tokens, feats, pad)


def leave_kernel(tiles, dq, dk, dv, gfi, low, feats, table, grads_in, input_grad, grads,
                 wq, wk, wv, out, come, back, dwl, dwq, dwk, dwv, vgrads, lsem, ssem, sends, recvs):
    f32, bf = jnp.float32, jnp.bfloat16
    rows = gfi.shape[0]
    loads = pieces(tiles, wk, 112, 96, lsem, 0) + pieces(tiles, wv, 208, 96, lsem, 4) + pieces(tiles, wq, 16, 96, lsem, 8)
    for c in loads:
        c.start()
    c, partner = meet_partner()
    own, other = pl.ds(c * rows, rows), pl.ds((1 - c) * rows, rows)
    swaps = []
    for i, ref in enumerate((dk, dv)):
        out[i] = ref[other, :].astype(bf)
        swaps.append(rcopy(out.at[i], come.at[i], sends.at[i], recvs.at[i], partner))
        swaps[i].start()
    back[0] = dq[...].astype(bf)
    query_bias = jnp.sum(col_sum(dq[...]), axis=0, keepdims=True)
    for copy in loads:
        copy.wait()

    def through(i, w, dw):
        dw[...] = lax.dot_general(low[...], back[i], TN, preferred_element_type=f32).astype(bf).reshape(96, 8, D)
        return lax.dot_general(back[i], matrix(w[...]), NT, preferred_element_type=f32)

    input_grad[...] = gfi[...] + through(0, wq, dwq)
    stores = pieces(grads, dwq, 16, 96, ssem, 0, True)
    swaps[0].wait_recv()
    back[1] = (dk[own, :] + come[0].astype(f32)).astype(bf)
    input_grad[...] += through(1, wk, dwk)
    stores += pieces(grads, dwk, 112, 96, ssem, 4, True)
    swaps[1].wait_recv()
    grad_value = dv[own, :] + come[1].astype(f32)
    value_bias = jnp.sum(col_sum(grad_value), axis=0, keepdims=True)
    back[2] = grad_value.astype(bf)
    total = input_grad[...] + through(2, wv, dwv)
    stores += pieces(grads, dwv, 208, 96, ssem, 8, True)
    input_grad[...] = total
    layout_bias = jnp.sum(col_sum(total), axis=0, keepdims=True)
    dwl[...] = lax.dot_general(feats[...], total.astype(bf), TN, preferred_element_type=f32).astype(bf).reshape(16, 8, D)
    stores += pieces(grads, dwl, 0, 16, ssem, 12, True)

    def block(lines):
        return jnp.concatenate(lines + [jnp.zeros((8 - len(lines), D), f32)]).astype(bf)

    vgrads[0] = block([layout_bias, table[0:1, :]])
    vgrads[1] = block([query_bias])
    vgrads[2] = block([value_bias])
    vgrads[3] = jnp.zeros((8, D), bf)
    held = {0: 0, 1: 1, 4: 2}
    for i, chip in enumerate(ch for ch in range(5)):
        stores.append(pltpu.make_async_copy(vgrads.at[held.get(chip, 3)], grads.at[vector_at(chip)], ssem.at[16 + i]))
    for copy in stores:
        copy.start()
    for copy in stores:
        copy.wait()
    for swap in swaps:
        swap.wait_send()


def leave(tiles, dq, dk, dv, gfi, low, feats, table, grads):
    rows = gfi.shape[0]
    f32, bf = jnp.float32, jnp.bfloat16
    vm, any_ = pl.BlockSpec(memory_space=pltpu.VMEM), pl.BlockSpec(memory_space=pl.ANY)
    S, sem = jax.ShapeDtypeStruct, pltpu.SemaphoreType.DMA
    w = pltpu.VMEM((96, 8, D), bf)
    return pl.pallas_call(
        leave_kernel,
        out_shape=[S((rows, D), f32), S(grads.shape, bf)],
        in_specs=[any_] + [vm] * 7 + [any_],
        out_specs=[vm, any_],
        scratch_shapes=[w, w, w, pltpu.VMEM((2, rows, D), bf), pltpu.VMEM((2, rows, D), bf), pltpu.VMEM((3, rows, D), bf),
                        pltpu.VMEM((16, 8, D), bf), w, w, w, pltpu.VMEM((4, 8, D), bf), sem((12,)), sem((32,)), sem((2,)), sem((2,))],
        input_output_aliases={8: 1},
        compiler_params=pltpu.CompilerParams(collective_id=3, has_side_effects=True, vmem_limit_bytes=56 << 20),
        name="leave",
    )(tiles, dq, dk, dv, gfi, low, feats, table, grads)


GATHER_PARTS = ((0, 8), (8, 7), (15, 7), (22, 7), (29, 4), (33, 4))
GATHER_STEPS = (
    ((647, 384, 128, 256, 385, 129, 257, 386, 130, 258, 387, 131, 259, 388, 132, 260, 389, 133, 261),
     (17, 145, 8, 264, 19, 147, 12, 396, 20, 404, 10, 266, 9, 11, 13, 655, 397, 16, 18, 21, 663, 32, 33, 34, 35, 36, 37, 679, 405, 149, 268, 160, 288, 161, 289, 29, 413, 24, 25, 26, 27, 28, 671, 412, 162, 290),
     {-1: (163, 291), 0: (49, 177, 40, 296, 64, 65, 66, 67, 68, 69, 711), 1: (42, 298, 51, 179, 192), 2: (320,), 3: (41, 43, 44, 45, 687, 193, 321, 48, 50, 52, 53, 695), 4: (194, 322), 5: (195, 323, 56, 57, 58, 59, 60, 61, 703), 6: (96, 224, 352), 7: (97, 225, 353), 8: (81, 209, 72, 328, 98, 99, 100, 101, 743), 9: (226, 74, 330), 10: (227, 354, -1), 11: (73, 75, 76, 77, 719, 83, 211, 355, 113, 241, 104, 360, 105, 106, 107, 108, 109, 751, 80, 82, 84, 85, 727, 362, 112, 114, 115, 116, 117, 759, 243, 120, 121, 122, 123, 124, 125, 767, 88, 89, 90, 91, 92, 93, 735)}),
    ((679, 544, 416, 160, 288, 545, 417, 161, 289, 546),
     (0, 384, 128, 256, 547, 1, 385, 129, 257, 548, 549, 2, 386, 130, 258, 64, 576, 8, 264, 3, 387, 131, 17, 145, 4, 388, 65, 577, 259, 5, 647, 66, 67, 68, 69, 711, 389, 162, 578, 10, 266, 12, 396, 20, 404, 579, 290, 9, 11, 13, 655, 397, 19, 147, 163, 16, 18, 21, 663, 405, 580, 291, 418, 581, 164, 292, 96, 608, 29, 413, 165, 293, 24, 25, 26, 27, 28, 671, 412, 49, 177, 40, 296, 419),
     {-1: (97, 98, 99, 100, 101, 743, 51, 179, 44, 556, 52, 564, 42, 298, 420, 41, 43, 45, 687, 557, 48, 50, 53, 695, 565, 421, 181), 0: (300, 609, 428, 192, 320, 436), 1: (429, 193, 321, 61, 573), 2: (437, 56, 57, 58, 59, 60, 703, 572, 610, 194, 445, 322), 3: (444, 611, 195, 323), 4: (612, 224, 352), 5: (613, 108, 620, 225, 353), 6: (76, 588, 72, 73, 74, 75, 77, 719, 226, 116, 628, 354), 7: (589, 227, 109, 621, 355), 8: (84, 596, 81, 209, 80, 82, 83, 85, 727, 328, 117, 629), 9: (597, 211, 330), 10: (104, 105, 106, 107, 751, 112, 113, 114, 115, 759, 241, 360, -1), 11: (243, 362, 125, 637, 124, 636, 93, 605, 88, 89, 90, 91, 92, 735, 604, 120, 121, 122, 123, 767)}),
    ((711, 576, 448, 192, 320, 577, 449, 193, 321, 578),
     (32, 416, 160, 288, 579, 33, 417, 161, 289, 580, 581, 0, 384, 128, 256, 96, 608, 1, 385, 129, 257, 97, 609, 98, 99, 100, 101, 743, 2, 386, 130, 258, 610, 8, 264, 3, 387, 131, 611, 17, 145, 4, 388, 259, 5, 647, 389, 612, 49, 177, 10, 266, 12, 396, 613, 20, 404, 40, 296, 9, 11, 13, 655, 397, 19, 147, 16, 18, 21, 663, 405, 34, 162, 290, 418, 194, 322, 29, 413, 195, 24, 25, 26, 27, 28, 671, 412, 42, 298),
     {-1: (35, 419, 163, 291, 36, 420, 196, 37, 679, 421, 323), 0: (197, 44, 428, 324, 52, 436), 1: (108, 620, 325, 41, 43, 45, 687, 429, 51, 179, 224, 76, 588, 72, 328), 2: (48, 50, 53, 695, 437, 116, 628, 73, 74, 75, 77, 719, 589, 61, 445, 81, 209, 109, 621), 3: (84, 596, 352, 60, 444, 56, 57, 58, 59, 703, 117, 629, 80, 82, 83, 85, 727, 450, 225), 4: (597, 353, 451, 226), 5: (354, 452, 227), 6: (453, 355, 460, 211), 7: (330, 461, 213, 468), 8: (332, 113, 241, 104, 105, 106, 107, 751, 469, 360, 112, 114, 115, 759), 9: (125, 637, 243, 124, 636, 362, 93, 477, 605), 10: (88, 89, 90, 91, 92, 735, 476, 604, -1), 11: (120, 121, 122, 123, 767)}),
    ((743, 608, 224, 352, 609, 225, 353, 610, 226, 354, 611, 227, 355, 612, 613),
     (32, 160, 288, 33, 161, 289, 0, 128, 256, 1, 129, 257, 2, 130, 8, 264, 258, 17, 145, 3, 131, 259, 4, 5, 647, 49, 177, 10, 266, 40, 296, 9, 11, 12, 13, 655, 19, 147, 228, 16, 18, 20, 21, 663, 34, 290, 162, 356, 229, 357, 64, 192, 24, 25, 26, 27, 28, 29, 671, 108, 620),
     {-1: (42, 298, 35, 163, 291, 116, 628, 104, 105, 106, 107, 109, 751, 621, 117, 629, 112, 113, 114, 115, 759, 65, 193, 36, 37, 679, 320), 0: (360,), 1: (41, 43, 44, 45, 687, 51, 179, 241), 2: (48, 50, 52, 53, 695, 321, 243), 3: (362, 56, 57, 58, 59, 60, 61, 703, 245), 4: (364, 66, 194, 72, 328), 5: (81, 209, 322, 125, 637), 6: (67, 195, 120, 121, 122, 123, 124, 767, 636, 68, 69, 711, 323), 7: (74, 330), 8: (73, 75, 76, 77, 719), 9: (83, 211, 80, 82, 84, 85, 727), 10: (-1,), 11: (88, 89, 90, 91, 92, 93, 735)}),
)


def forward_kernel(x_ref, tokens, feats, pad, buckets, lengths,
                   g_ref, hidden, low, query, keys, values, ctx, soft, code_out,
                   xv, tail, head, win, chunk, lsem, hsend, hrecv, own,
                   ssem, rsem, cr,
                   pads, hidden_v, low_v, query_v, keys_v, values_v, ctx_v, code, buckets_v, tokens_v, feats_v, p_v, s_scr, tab,
                   wl, wq, wk, wv, vrows, vf, ksend, krecv, wsem, isem, osem, psem):
    f32, bf = jnp.float32, jnp.bfloat16
    rows = tokens.shape[0]
    k, c, z, y, x = place()
    d = 2 * k + c
    inputs = [pltpu.make_async_copy(r, v, isem.at[i]) for i, (r, v) in enumerate(((buckets, buckets_v), (tokens, tokens_v), (feats, feats_v)))]
    for copy in inputs:
        copy.start()
    pads[pl.ds(c, 1)] = pad[...].reshape(1, 8, rows)
    greet(k, c, z, y, x)
    load = pltpu.make_async_copy(x_ref, xv, lsem)
    load.start()
    prev = (jnp.where(c == 1, k, jnp.maximum(k - 1, 0)), 1 - c)
    nxt = (jnp.where(c == 0, k, jnp.minimum(k + 1, 15)), 1 - c)
    to_next = rcopy(x_ref.at[pl.ds(ROWS - TAIL, TAIL)], tail, hsend.at[0], hrecv.at[0], nxt)
    to_prev = rcopy(x_ref.at[pl.ds(0, HEAD)], head, hsend.at[1], hrecv.at[1], prev)

    @pl.when(d < 31)
    def _():
        to_next.start()

    @pl.when(d > 0)
    def _():
        to_prev.start()

    win[...] = jnp.zeros_like(win)
    lanes = lax.broadcasted_iota(jnp.int32, (80, 128), 1)
    q, sh = shard_start(d)
    load.wait()

    @pl.loop(0, ROWS // 80)
    def _(i):
        r = pl.multiple_of(i * 80, 8)
        rolled = pltpu.roll(xv[pl.ds(r, 80), :], sh, 1)
        win[pl.ds(160 + r, 80), :] += jnp.where(lanes >= sh, rolled, 0.0)
        win[pl.ds(161 + r, 80), :] += jnp.where(lanes < sh, rolled, 0.0)

    @pl.when(d > 0)
    def _():
        to_next.wait_recv()
        qp, shp = shard_start(d - 1)
        lanes = lax.broadcasted_iota(jnp.int32, (TAIL, 128), 1)
        rolled = pltpu.roll(tail[...], shp, 1)
        at = 1760 - (q - qp)
        win[pl.ds(at, TAIL), :] += jnp.where(lanes >= shp, rolled, 0.0)
        win[pl.ds(at + 1, TAIL), :] += jnp.where(lanes < shp, rolled, 0.0)

    @pl.when(d < 31)
    def _():
        to_prev.wait_recv()
        qn, shn = shard_start(d + 1)
        lanes = lax.broadcasted_iota(jnp.int32, (HEAD, 128), 1)
        rolled = pltpu.roll(head[...], shn, 1)
        at = 160 + (qn - q)
        win[pl.ds(at, HEAD), :] += jnp.where(lanes >= shn, rolled, 0.0)
        win[pl.ds(at + 1, HEAD), :] += jnp.where(lanes < shn, rolled, 0.0)

    early = early_vectors(k)
    nw0 = jnp.where(early, 36, 37)
    vecs = early == (c == 0)
    first = jnp.where(c == 0, 73 * k, 73 * k + nw0)
    base = q - 160

    @pl.loop(0, SLOTS)
    def _(t):
        at, wide = tile_start(first + t)
        is_vec = vecs & (t == 36)
        at = jnp.where(is_vec, vector_row(k, q), at) - base
        wide = wide & jnp.logical_not(is_vec)

        @pl.when(wide)
        def _():
            parts = [win[pl.ds(at + j, 8, stride=24), :] for j in range(6)]
            chunk[t] = jnp.concatenate(parts, axis=1).astype(jnp.bfloat16)

        @pl.when(jnp.logical_not(wide))
        def _():
            parts = [win[pl.ds(at + j, 8, stride=6), :] for j in range(6)]
            chunk[t] = jnp.concatenate(parts, axis=1).astype(jnp.bfloat16)

    @pl.when(d < 31)
    def _():
        to_next.wait_send()

    @pl.when(d > 0)
    def _():
        to_prev.wait_send()

    xdev, ydev, cdev = (z * 4 + y * 2 + 1 - x, c), (z * 4 + (1 - y) * 2 + x, c), (k, 1 - c)
    targets = {1: xdev, 2: ydev, 3: (jnp.minimum(k + 4, 15), c), 4: (jnp.maximum(k - 4, 0), c), 5: cdev}
    tiles = g_ref.reshape(16 * CHIP, 8, D)

    def step(zz, op):
        if op < 0:
            make_values()
            return
        link, item, p = op // 128, op // 8 % 16, op % 8
        chip = item // 4 * 4 + (1 - y if item // 2 % 2 else y) * 2 + (1 - x if item % 2 else x)
        off, n = (0, 37) if link == 5 else GATHER_PARTS[p]
        there = g_ref.at[chip, pl.ds(37 * c + off, n)]
        if link == 0:
            rcopy(there, there, ssem.at[0], rsem.at[chip, p], xdev).wait_recv()
            return
        here = chunk.at[pl.ds(off, n)] if item == zz * 4 else there
        rcopy(here, there, ssem.at[link - 1], cr.at[chip] if link == 5 else rsem.at[chip, p], targets[link]).start()

    def steps_of(zz, which, head=0):
        for op in GATHER_STEPS[zz][which] if which < 2 else GATHER_STEPS[zz][2].get(head, ()):
            step(zz, op)

    def sent_rows(zz, link):
        ops = [op for w in (0, 1) for op in GATHER_STEPS[zz][w]] + [op for v in GATHER_STEPS[zz][2].values() for op in v]
        return sum(37 if link == 5 else GATHER_PARTS[op % 8][1] for op in ops if op // 128 == link)

    pair_pads = rcopy(pads.at[pl.ds(c, 1)], pads.at[pl.ds(c, 1)], ksend.at[2], krecv.at[2], cdev)
    pair_pads.start()
    mine = pltpu.make_async_copy(chunk, g_ref.at[k, pl.ds(37 * c, 37)], own.at[0])

    for zz in range(4):
        @pl.when(z == zz)
        def _():
            steps_of(zz, 0)
    mine.start()
    for copy in inputs:
        copy.wait()
    pair_pads.wait()
    fill_codes(code, buckets_v, pads, lengths)
    outs = [pltpu.make_async_copy(code, code_out, osem.at[0])]
    outs[0].start()
    for zz in range(4):
        @pl.when(z == zz)
        def _():
            steps_of(zz, 1)
    mine.wait()

    def from_partner(chip):
        theirs = g_ref.at[chip, pl.ds(37 * (1 - c), 37)]
        rcopy(theirs, theirs, ssem.at[4], cr.at[chip], cdev).wait_recv()

    for chip in range(3):
        from_partner(chip)

    loads = [pltpu.make_async_copy(tiles.at[vector_at(ch)], vrows.at[i], wsem.at[i]) for i, ch in enumerate((0, 1))]
    loads += pieces(tiles, wl, 0, 16, wsem, 4) + pieces(tiles, wk, 112, 96, wsem, 8) + pieces(tiles, wq, 16, 96, wsem, 16)
    for copy in loads:
        copy.start()
    for copy in loads:
        copy.wait()
    vf[0] = vrows[0].astype(f32)
    vf[1] = vrows[1].astype(f32)
    fill_table(tab, vrows.at[0])
    h = tokens_v[...].astype(f32) + jnp.dot(feats_v[...], matrix(wl[...]), preferred_element_type=f32) + vf[0, 0:1, :]
    hidden_v[...] = h
    low_v[...] = h.astype(bf)
    half_rows = pl.ds(c * rows, rows)

    def share(ref, i):
        return rcopy(ref.at[half_rows], ref.at[half_rows], ksend.at[i], krecv.at[i], cdev)

    keys_v[half_rows, :] = jnp.dot(low_v[...], matrix(wk[...]), preferred_element_type=f32).astype(bf)
    share(keys_v, 0).start()
    query_v[...] = ((jnp.dot(low_v[...], matrix(wq[...]), preferred_element_type=f32) + vf[1, 0:1, :]) * 0.125).astype(bf)
    share(keys_v, 0).wait()
    outs += [pltpu.make_async_copy(v, r, osem.at[1 + i]) for i, (v, r) in enumerate(((hidden_v, hidden), (low_v, low), (query_v, query), (keys_v, keys)))]
    for copy in outs[1:]:
        copy.start()

    def make_values():
        for chip in (3, 4):
            from_partner(chip)
        copies = [pltpu.make_async_copy(tiles.at[vector_at(4)], vrows.at[2], wsem.at[2])] + pieces(tiles, wv, 208, 96, wsem, 12)
        for copy in copies:
            copy.start()
        for copy in copies:
            copy.wait()
        vf[2] = vrows[2].astype(f32)
        values_v[half_rows, :] = (jnp.dot(low_v[...], matrix(wv[...]), preferred_element_type=f32) + vf[2, 0:1, :]).astype(bf)
        share(values_v, 1).start()

    def keep(pair):
        return pltpu.make_async_copy(p_v.at[pl.ds(2 * pair, 2)], soft.at[pl.ds(2 * pair, 2)], psem.at[pair])

    for zz in range(4):
        if -1 in GATHER_STEPS[zz][2]:
            @pl.when(z == zz)
            def _():
                steps_of(zz, 2, -1)

    def one_head(head, _):
        lanes = pl.ds(pl.multiple_of(head // 2 * 128, 128), 128)
        soft_head(head, query_v[:, lanes], keys_v[:, lanes], code, tab, s_scr, p_v.at[head])

        @pl.when(head % 2 == 1)
        def _():
            keep(head // 2).start()

        for zz in range(4):
            for i in range(H):
                if i in GATHER_STEPS[zz][2]:
                    @pl.when((head == i) & (z == zz))
                    def _():
                        steps_of(zz, 2, i)
        return 0

    lax.fori_loop(0, H, one_head, 0)
    share(values_v, 1).wait()
    outs.append(pltpu.make_async_copy(values_v, values, osem.at[5]))
    outs[-1].start()

    def context(pair, _):
        lanes = pl.ds(pl.multiple_of(pair * 128, 128), 128)
        ctx_v[:, lanes] = context_pair(values_v[:, lanes], p_v.at[pl.ds(2 * pair, 2)])
        return 0

    lax.fori_loop(0, H // 2, context, 0)
    outs.append(pltpu.make_async_copy(ctx_v, ctx, osem.at[6]))
    outs[-1].start()

    for zz in range(4):
        @pl.when(z == zz)
        def _():
            for link in range(1, 6):
                n = sent_rows(zz, link)
                if n:
                    whole = tiles.at[pl.ds(0, n)]
                    rcopy(whole, whole, ssem.at[link - 1], cr.at[0], targets[link]).wait_send()
    for chip in range(5, 16):
        from_partner(chip)
    for pair in range(H // 2):
        keep(pair).wait()
    for copy in outs:
        copy.wait()


def gather_and_attend(master, tokens, feats, pad, buckets, page_lengths):
    x = jnp.pad(master, (0, ROWS * 128 - SHARD)).reshape(ROWS, 128)
    sem = pltpu.SemaphoreType.DMA
    any_, vm = pl.BlockSpec(memory_space=pl.ANY), pl.BlockSpec(memory_space=pltpu.VMEM)
    rows, key_rows = buckets.shape
    f32, bf = jnp.float32, jnp.bfloat16
    S, V = jax.ShapeDtypeStruct, pltpu.VMEM
    w = V((96, 8, D), bf)
    return pl.pallas_call(
        forward_kernel,
        out_shape=[
            S((16, CHIP, 8, D), bf), S((rows, D), f32), S((rows, D), bf), S((rows, D), bf), S((key_rows, D), bf), S((key_rows, D), bf),
            S((rows, D), bf), S((H, key_rows, rows), bf), S((key_rows, rows), jnp.int32),
        ],
        in_specs=[any_, any_, any_, vm, any_, pl.BlockSpec(memory_space=pltpu.SMEM)],
        out_specs=[any_] * 9,
        scratch_shapes=[
            V((ROWS, 128), f32), V((TAIL, 128), f32), V((HEAD, 128), f32), V((WIN, 128), f32), V((SLOTS, 8, D), bf),
            sem, sem((2,)), sem((2,)), sem((2,)),
            sem((5,)), sem((16, 6)), sem((16,)),
            V((2, 8, rows), jnp.int32), V((rows, D), f32), V((rows, D), bf), V((rows, D), bf), V((key_rows, D), bf), V((key_rows, D), bf),
            V((rows, D), bf), V((key_rows, rows), jnp.int32), V((rows, key_rows), jnp.int32), V((rows, D), bf), V((rows, LF), bf),
            V((H, key_rows, rows), bf), V((key_rows, rows), f32), V((16, 128), f32),
            V((16, 8, D), bf), w, w, w, V((3, 8, D), bf), V((3, 8, D), f32),
            sem((3,)), sem((3,)), sem((20,)), sem((3,)), sem((7,)), sem((H // 2,)),
        ],
        compiler_params=pltpu.CompilerParams(collective_id=0, has_side_effects=True, vmem_limit_bytes=60 << 20),
        name="gather_and_attend",
    )(x, tokens, feats, pad, buckets, page_lengths)


def guarded(cond, f):
    if cond is True:
        f()
    elif cond is not False:
        pl.when(cond)(f)


class Reducer:
    def __init__(self, where, zs, want, spare, g_ref, acc, crecv, a1, b1, a2, b2, asem, cs, cr, a1s, a1r, b1s, b1r, a2s, a2r, b2s, b2r):
        self.k, self.c, self.z, self.y, self.x = where
        self.zs, self.want, self.spare = zs, want, spare
        self.g_ref, self.acc, self.crecv = g_ref, acc, crecv
        self.bufs = (a1, b1, a2, b2)
        self.asem, self.cs, self.cr = asem, cs, cr
        self.sems = ((a1s, a1r), (b1s, b1r), (a2s, a2r), (b2s, b2r))
        z, y, x, c = self.z, self.y, self.x, self.c
        self.xdev, self.ydev, self.cdev = (z * 4 + y * 2 + 1 - x, c), (z * 4 + (1 - y) * 2 + x, c), (self.k, 1 - c)

    def at(self, zo, oy, ox):
        return zo, (1 - self.y if oy else self.y), (1 - self.x if ox else self.x)

    def chip(self, zo, yo, xo):
        return zo * 4 + yo * 2 + xo

    def local(self, zo, yo, xo):
        return self.chip(zo, yo, xo)

    def load(self, item):
        i = self.local(*item)
        return pltpu.make_async_copy(self.g_ref.at[self.chip(*item), pl.ds(37 * self.c, 37)], self.acc.at[i], self.asem.at[i])

    def ccopy(self, item):
        i = self.local(*item)
        return rcopy(self.g_ref.at[self.chip(*item), pl.ds(37 * (1 - self.c), 37)], self.crecv.at[i + self.spare], self.cs.at[i], self.cr.at[i], self.cdev)

    def hop(self, which, item, slot, p, dev):
        s, r = self.sems[which]
        return rcopy(self.acc.at[self.local(*item), pl.ds(*PARTS[p])], self.bufs[which].at[slot], s.at[slot], r.at[slot], dev)

    def a1(self, zo, xo):
        return self.hop(0, (zo, 1 - self.y, xo), self.zs.index(zo) * 2 + xo, 0, self.ydev)

    def b1(self, zo, yo):
        return self.hop(1, (zo, yo, 1 - self.x), self.zs.index(zo) * 2 + yo, 1, self.xdev)

    def a2(self, zo):
        return self.hop(2, (zo, self.y, 1 - self.x), self.zs.index(zo), 0, self.xdev)

    def b2(self, zo):
        return self.hop(3, (zo, 1 - self.y, self.x), self.zs.index(zo), 1, self.ydev)

    def gain(self, item, p, which, slot):
        off, n = PARTS[p]
        i, acc, buf = self.local(*item), self.acc, self.bufs[which]
        acc[i, pl.ds(off, n)] = acc[i, pl.ds(off, n)] + buf[slot]

    def begin(self, zo, oy, ox):
        item = self.at(zo, oy, ox)

        def go():
            self.load(item).start()
            self.ccopy(item).start()
        guarded(self.want(*item), go)

    def first(self, zo, oy, ox):
        item = self.at(zo, oy, ox)

        def go():
            self.load(item).wait()
            self.ccopy(item).wait_recv()
            i = self.local(*item)
            self.acc[i] = self.acc[i] + self.crecv[i + self.spare]
            if oy:
                self.a1(zo, item[2]).start()
            if ox:
                self.b1(zo, item[1]).start()
        guarded(self.want(*item), go)

    def second(self, zo):
        ia, ib = self.at(zo, 0, 1), self.at(zo, 1, 0)
        n = self.zs.index(zo) * 2

        def go_a():
            self.a1(zo, 1 - self.x).wait_recv()
            self.gain(ia, 0, 0, n + 1 - self.x)
            self.a2(zo).start()

        def go_b():
            self.b1(zo, 1 - self.y).wait_recv()
            self.gain(ib, 1, 1, n + 1 - self.y)
            self.b2(zo).start()
        guarded(self.want(*ia), go_a)
        guarded(self.want(*ib), go_b)

    def third(self, zo):
        item = self.at(zo, 0, 0)
        n = self.zs.index(zo)

        def go():
            self.a1(zo, self.x).wait_recv()
            self.b1(zo, self.y).wait_recv()
            self.a2(zo).wait_recv()
            self.b2(zo).wait_recv()
            i = self.local(*item)
            for p, (h, u), at in ((0, (0, 2), self.x), (1, (1, 3), self.y)):
                off, m = PARTS[p]
                self.acc[i, pl.ds(off, m)] = (self.acc[i, pl.ds(off, m)] + self.bufs[h][n * 2 + at]) + self.bufs[u][n]
        guarded(self.want(*item), go)

    def finish(self):
        for zo in self.zs:
            for oy in (0, 1):
                for ox in (0, 1):
                    item = self.at(zo, oy, ox)

                    def sent(item=item, oy=oy, ox=ox, zo=zo):
                        self.ccopy(item).wait_send()
                        if oy:
                            self.a1(zo, item[2]).wait_send()
                        if ox:
                            self.b1(zo, item[1]).wait_send()
                        if ox and not oy:
                            self.a2(zo).wait_send()
                        if oy and not ox:
                            self.b2(zo).wait_send()
                    guarded(self.want(*item), sent)


def reducer_scratch():
    bf, sem = jnp.bfloat16, pltpu.SemaphoreType.DMA
    tile = (8, D)
    return [
        pltpu.VMEM((16, 37) + tile, bf), pltpu.VMEM((11, 37) + tile, bf),
        pltpu.VMEM((8, 19) + tile, bf), pltpu.VMEM((8, 18) + tile, bf), pltpu.VMEM((4, 19) + tile, bf), pltpu.VMEM((4, 18) + tile, bf),
        sem((16,)), sem((16,)), sem((16,)),
        sem((8,)), sem((8,)), sem((8,)), sem((8,)), sem((4,)), sem((4,)), sem((4,)), sem((4,)),
    ]


def early_item(zo, yo, xo):
    return zo >= 2 if zo != 1 else yo + xo > 0


def late_item(zo, yo, xo):
    return zo == 0 if zo != 1 else yo + xo == 0


ZCUTS = ((0, 10), (10, 9), (19, 9), (28, 9))


class Chain:
    def __init__(self, where, acc, up, dn, us, ur, ds_, dr):
        self.k, self.c, self.z, self.y, self.x = where
        self.acc = acc
        self.ways = {1: (up, us, ur, (jnp.minimum(self.k + 4, 15), self.c)), -1: (dn, ds_, dr, (jnp.maximum(self.k - 4, 0), self.c))}

    def chip(self, zo):
        return zo * 4 + self.y * 2 + self.x

    def copy(self, zo, way, p):
        buf, s, r, dev = self.ways[way]
        part = pl.ds(*ZCUTS[p])
        return rcopy(self.acc.at[self.chip(zo), part], buf.at[zo, part], s.at[zo, p], r.at[zo, p], dev)

    def move(self, zs, zo, way, take=True, give=True, also=None):
        cond = self.z == zs if also is None else (self.z == zs) & also

        @pl.when(cond)
        def _():
            i = self.chip(zo)
            for p in range(4):
                if take:
                    self.copy(zo, way, p).wait_recv()
                    part = pl.ds(*ZCUTS[p])
                    self.acc[i, part] = self.acc[i, part] + self.ways[way][0][zo, part]
                if give:
                    self.copy(zo, way, p).start()

    def sent(self, zs, zo, way):
        @pl.when(self.z == zs)
        def _():
            for p in range(4):
                self.copy(zo, way, p).wait_send()


def chain_scratch():
    bf, sem = jnp.bfloat16, pltpu.SemaphoreType.DMA
    return [pltpu.VMEM((4, 37, 8, D), bf)] * 2 + [sem((4, 4))] * 4


def backward_kernel(tiles, q_ref, k_ref, v_ref, do_ref, p_hbm, code_hbm, gfi_in, low_in, feats_in, grads_in, m_ref, one_ref, two_ref,
                    grad_out, grads, step_ref, new1_ref, new2_ref, spread,
                    pbuf, qv, kv, vv, dov, psem, code_ref, csem, dsv, dssem, group, gsem, counts, dks, dvs, out, come, sends, recvs, back, bias,
                    wq, wk, wv, low, gfi, feats, dwl, dwq, dwk, dwv, vgrads, wsem, ssem, isem,
                    total, ebuf, sq, sqr, win, mv, onev, twov, lsem, es, er, qs, qr, *scratch):
    f32, bf = jnp.float32, jnp.bfloat16
    where = place()
    k, c, z, y, x = where
    d = 2 * k + c
    shared = grads.reshape(16, CHIP, 8, D)
    rs = Reducer(where, (0, 1, 2, 3), early_item, -5, shared, *scratch[:17])
    late = Reducer(where, (0, 1, 2, 3), late_item, 6, shared, *scratch[:17])
    acc = rs.acc
    zc = Chain(where, acc, *scratch[17:])
    xdev, ydev, cdev = rs.xdev, rs.ydev, rs.cdev
    column_devs = [((z + s) % 4 * 4 + y * 2 + x, c) for s in (1, 2, 3)]
    prev = (jnp.where(c == 1, k, jnp.maximum(k - 1, 0)), 1 - c)
    nxt = (jnp.where(c == 0, k, jnp.minimum(k + 1, 15)), 1 - c)
    bar = pltpu.get_barrier_semaphore()
    far_next, far_prev = (c == 1) & (k < 15), (c == 0) & (k > 0)
    plane_devs = [(z * 4 + (1 - y if oy else y) * 2 + (1 - x if ox else x), 1 - c if oc else c) for oc in (0, 1) for oy in (0, 1) for ox in (0, 1)][1:]
    for dev in plane_devs + column_devs:
        pl.semaphore_signal(bar, inc=1, device_id=dev, device_id_type=MESH)

    @pl.when(far_next)
    def _():
        pl.semaphore_signal(bar, inc=1, device_id=nxt, device_id_type=MESH)

    @pl.when(far_prev)
    def _():
        pl.semaphore_signal(bar, inc=1, device_id=prev, device_id_type=MESH)

    keys, rows = code_ref.shape

    def fetch_soft(pair, hh):
        return pltpu.make_async_copy(p_hbm.at[2 * pair + hh], pbuf.at[hh], psem.at[0, hh])

    def fetch(p):
        slot = p % 2
        lanes = pl.ds(pl.multiple_of(p * 128, 128), 128)
        return [pltpu.make_async_copy(r.at[:, lanes], v.at[slot], psem.at[1 + i, slot]) for i, (r, v) in enumerate(((q_ref, qv), (k_ref, kv), (v_ref, vv), (do_ref, dov)))]

    for copy in fetch(0) + [fetch_soft(0, 0), fetch_soft(0, 1)]:
        copy.start()
    pl.semaphore_wait(bar, 10 + jnp.where(far_next | far_prev, 1, 0))
    corners = ((1, 1), (1, 0), (0, 1), (0, 0))
    for oy, ox in corners:
        rs.begin(2, oy, ox)
    code_copy = pltpu.make_async_copy(code_hbm, code_ref, csem.at[0])
    inputs = [pltpu.make_async_copy(r, v, isem.at[i]) for i, (r, v) in enumerate(((low_in, low), (gfi_in, gfi), (feats_in, feats)))]
    loads = pieces(tiles, wq, 16, 96, wsem, 8) + pieces(tiles, wv, 208, 96, wsem, 4) + pieces(tiles, wk, 112, 96, wsem, 0)
    shards = [pltpu.make_async_copy(r, v, lsem.at[i]) for i, (r, v) in enumerate(((m_ref, mv), (one_ref, onev), (two_ref, twov)))]
    for copy in [code_copy] + inputs + loads + shards:
        copy.start()
    own, other = pl.ds(c * rows, rows), pl.ds((1 - c) * rows, rows)

    def swap(pair):
        return rcopy(out.at[pair], come.at[pair], sends.at[pair], recvs.at[pair], cdev)

    def settle(pair):
        slot = pair % 2
        swap(pair).wait_recv()
        lanes = pl.ds(pl.multiple_of(pair * 128, 128), 128)
        dk = dks[slot, own, :] + come[pair, 0].astype(f32)
        dv = dvs[slot, own, :] + come[pair, 1].astype(f32)
        back[1, :, lanes] = dk.astype(bf)
        back[2, :, lanes] = dv.astype(bf)
        bias[1, :, lanes] = col_sum(dv)

    def lay(pair, hh):
        return pltpu.make_async_copy(dsv.at[hh], spread.at[:, 2 * pair + hh], dssem.at[hh])

    plan = {
        0: [(rs.first, 2, 0, 0), (rs.first, 2, 0, 1), (rs.first, 2, 1, 0), (rs.first, 3, 1, 1), (rs.begin, 1, 1, 1), (rs.begin, 1, 1, 0), (rs.begin, 1, 0, 1), (rs.begin, 1, 0, 0)],
        1: [(rs.first, 3, 1, 0), (rs.first, 3, 0, 0), (rs.second, 2), (rs.first, 1, 1, 1), (rs.first, 3, 0, 1)],
        5: [(rs.second, 3)],
    }
    rs.begin(3, 1, 1)
    rs.begin(3, 1, 0)
    rs.begin(3, 0, 1)
    rs.begin(3, 0, 0)
    rs.first(2, 1, 1)

    def pair_of_heads(pair, _):
        slot = pair % 2

        @pl.when(pair < H // 2 - 1)
        def _():
            for copy in fetch(pair + 1):
                copy.start()

        for copy in fetch(pair):
            copy.wait()
        lanes = pl.ds(pl.multiple_of(pair * 128, 128), 128)
        dq = []
        for hh in range(2):
            fetch_soft(pair, hh).wait()
            qm = half(qv[slot], hh)
            dom = half(dov[slot], hh)
            g = lax.dot_general(vv[slot], dom, NT, preferred_element_type=f32)
            p = pbuf[hh]
            pf = p.astype(f32)
            inner = jnp.sum(jnp.sum((g * pf).reshape(keys // 8, 8, rows), axis=0), axis=0, keepdims=True)
            ds = (pf * (g - inner)).astype(bf)

            @pl.when(pair > 0)
            def _():
                lay(pair - 1, hh).wait()

            dsv[hh] = ds.reshape(keys // 8, 8, rows)
            lay(pair, hh).start()
            dv = jnp.dot(p, dom, preferred_element_type=f32)

            @pl.when(pair < H // 2 - 1)
            def _():
                fetch_soft(pair + 1, hh).start()

            dk = jnp.dot(ds, qm, preferred_element_type=f32)
            if hh == 0:
                dvs[slot] = dv
                dks[slot] = dk
            else:
                dvs[slot] += dv
                dks[slot] += dk
            dq.append(lax.dot_general(kv[slot], ds, TN, preferred_element_type=f32))
        out[pair, 0] = dks[slot, other, :].astype(bf)
        out[pair, 1] = dvs[slot, other, :].astype(bf)
        swap(pair).start()
        sub = lax.broadcasted_iota(jnp.int32, dq[0].shape, 0)
        dqf = jnp.where(sub < 64, dq[0], dq[1]).T * 0.125
        back[0, :, lanes] = dqf.astype(bf)
        bias[0, :, lanes] = col_sum(dqf)

        @pl.when(pair > 0)
        def _():
            settle(pair - 1)

        for i, steps in plan.items():
            @pl.when(pair == i)
            def _():
                for f, *a in steps:
                    f(*a)
        return 0

    lax.fori_loop(0, H // 2, pair_of_heads, 0)
    for hh in range(2):
        lay(H // 2 - 1, hh).wait()
    for copy in inputs + loads:
        copy.wait()

    def through(i, w, dw):
        dw[...] = lax.dot_general(low[...], back[i], TN, preferred_element_type=f32).astype(bf).reshape(96, 8, D)
        return lax.dot_general(back[i], matrix(w[...]), NT, preferred_element_type=f32)

    stores = []

    def keep(dw, first, count, base):
        made = pieces(grads, dw, first, count, ssem, base, True)
        for copy in made:
            copy.start()
        stores.extend(made)

    gfi[...] += through(0, wq, dwq)
    keep(dwq, 16, 96, 0)
    settle(H // 2 - 1)
    gfi[...] += through(2, wv, dwv)
    keep(dwv, 208, 96, 8)
    whole = gfi[...] + through(1, wk, dwk)
    keep(dwk, 112, 96, 4)
    gfi[...] = whole
    shown = pltpu.make_async_copy(gfi, grad_out, isem.at[6])
    shown.start()
    layout_bias = jnp.sum(col_sum(whole), axis=0, keepdims=True)
    dwl[...] = lax.dot_general(feats[...], whole.astype(bf), TN, preferred_element_type=f32).astype(bf).reshape(16, 8, D)
    keep(dwl, 0, 16, 12)

    def block(lines):
        return jnp.concatenate(lines + [jnp.zeros((8 - len(lines), D), f32)]).astype(bf)

    vgrads[0] = block([layout_bias])
    vgrads[1] = block([jnp.sum(bias[0], axis=0, keepdims=True)])
    vgrads[2] = block([jnp.sum(bias[1], axis=0, keepdims=True)])
    vgrads[3] = jnp.zeros((8, D), bf)
    held = {0: 0, 1: 1, 4: 2}
    for i, ch in enumerate((0, 1, 2, 3, 4)):
        copy = pltpu.make_async_copy(vgrads.at[held.get(ch, 3)], grads.at[vector_at(ch)], ssem.at[16 + i])
        copy.start()
        stores.append(copy)
    for copy in stores:
        copy.wait()
    for oy, ox in corners:
        for zo in (0, 1):
            late.begin(zo, oy, ox)

    GROUPS = 16

    def take_groups(i):
        return pltpu.make_async_copy(spread.at[pl.ds(i * GROUPS, GROUPS)], group.at[i % 2], gsem.at[i % 2])

    bucket = lax.broadcasted_iota(jnp.int32, (BUCKETS, rows), 0)
    steps = keys // 8 // GROUPS
    code_copy.wait()
    take_groups(0).start()
    counts[...] = jnp.zeros_like(counts)

    def count_some(first, n):
        for i in range(first, first + n):
            if i + 1 < steps:
                take_groups(i + 1).start()
            take_groups(i).wait()

            def count(j, run, i=i):
                code = code_ref[pl.ds(pl.multiple_of((i * GROUPS + j) * 8, 8), 8), :]
                hot = jnp.concatenate(
                    [jnp.where(jnp.broadcast_to(code[r : r + 1], bucket.shape) == bucket, 1.0, 0.0) for r in range(8)]
                ).astype(bf)
                return run + lax.dot_general(group[i % 2, j].reshape(8 * H, rows), hot, NT, preferred_element_type=f32)

            counts[...] = lax.fori_loop(0, GROUPS, count, counts[...], unroll=8)

    early_one, late_one = rs.want(1, y, x), late.want(1, y, x)
    count_some(0, 1)
    late.first(0, 1, 1)
    late.first(1, 1, 1)
    late.first(0, 1, 0)
    late.first(1, 1, 0)
    rs.third(3)
    zc.move(0, 3, 1, take=False)
    late.first(0, 0, 1)
    late.first(1, 0, 1)
    rs.third(2)
    count_some(1, 1)
    zc.move(1, 3, 1)
    count_some(2, 1)
    zc.move(3, 2, -1, take=False)
    count_some(3, 1)
    late.second(0)
    late.second(1)
    rs.first(1, 0, 0)
    count_some(4, 1)
    rs.first(1, 1, 0)
    rs.first(1, 0, 1)
    rs.second(1)
    late.first(0, 0, 0)
    late.first(1, 0, 0)
    count_some(5, 1)
    zc.move(0, 2, 1, take=False)
    count_some(6, 1)
    zc.move(1, 2, 1)
    zc.move(2, 3, 1)
    late.third(0)
    zc.move(1, 0, -1)
    zc.move(2, 0, -1)
    zc.move(3, 0, -1, take=False)
    late.third(1)
    zc.move(0, 1, 1, take=False, also=late_one)
    zc.move(3, 1, -1, take=False, also=late_one)
    zc.move(2, 1, -1, also=late_one)
    rs.third(1)
    zc.move(0, 1, 1, take=False, also=early_one)
    zc.move(3, 1, -1, take=False, also=early_one)
    count_some(7, 1)
    zc.move(2, 1, -1, also=early_one)
    table = table_row(counts[...], (8, D))

    total[...] = acc[k].astype(f32)

    def add(way, zo):
        buf = zc.ways[way][0]
        for p in range(4):
            zc.copy(zo, way, p).wait_recv()
        total[...] = total[...] + buf[zo].astype(f32)

    @pl.when(z == 0)
    def _():
        add(-1, 0)

    @pl.when(z == 1)
    def _():
        add(1, 1)
        add(-1, 1)

    @pl.when(z == 2)
    def _():
        add(1, 2)
        add(-1, 2)

    @pl.when(z == 3)
    def _():
        add(1, 3)

    early = early_vectors(k)
    nw0 = jnp.where(early, 36, 37)
    vecs = early == (c == 0)
    mine = jnp.where(vecs, 36, 37)
    to_next = rcopy(total.at[pl.ds(mine - EDGE, EDGE)], ebuf.at[0], es.at[0], er.at[0], nxt)
    to_prev = rcopy(total.at[pl.ds(0, EDGE)], ebuf.at[1], es.at[1], er.at[1], prev)

    @pl.when(d < 31)
    def _():
        to_next.start()

    @pl.when(d > 0)
    def _():
        to_prev.start()

    def square(i, run):
        t = total[i]
        t = t * t
        for j in range(6):
            run = run + t[:, 128 * j:128 * j + 128]
        return run

    squares = lax.fori_loop(0, 37, square, jnp.zeros((8, 128), f32))
    lines = [jnp.sum(squares, axis=0, keepdims=True)] + [table[0:1, 128 * i : 128 * i + 128] for i in range(3)]
    place_in = c * 4 + y * 2 + x
    sq[0] = jnp.concatenate(lines + [jnp.zeros((4, 128), f32)])
    sqr[place_in] = sq[0]
    rounds = [rcopy(sq.at[0], sqr.at[place_in], qs.at[i], qr.at[place_in], dev) for i, dev in enumerate(plane_devs)]
    hops = [rcopy(sq.at[1], sqr.at[8 + z], qs.at[7 + i], qr.at[8 + z], dev) for i, dev in enumerate(column_devs)]
    for h in rounds:
        h.start()

    def arrived(slot):
        return rcopy(sqr.at[slot], sqr.at[slot], qs.at[0], qr.at[slot], cdev)

    rs.finish()
    late.finish()
    for zs in (0, 1, 2):
        zc.sent(zs, 3, 1)
    for zs in (0, 1):
        zc.sent(zs, 2, 1)
    zc.sent(3, 2, -1)
    zc.sent(0, 1, 1)
    zc.sent(3, 1, -1)
    zc.sent(2, 1, -1)
    for zs in (1, 2, 3):
        zc.sent(zs, 0, -1)
    for pair in range(H // 2):
        swap(pair).wait_send()
    q, sh = shard_start(d)
    base = q - FRONT

    def flatten(ref, i, at, wide):
        @pl.when(wide)
        def _():
            t = ref[i]
            for j in range(6):
                win[pl.ds(at + j, 8, stride=24), :] = t[:, 128 * j:128 * j + 128]

        @pl.when(jnp.logical_not(wide))
        def _():
            t = ref[i]
            for j in range(6):
                win[pl.ds(at + j, 8, stride=6), :] = t[:, 128 * j:128 * j + 128]

    own_vectors = vecs & (vector_row(k, -1) >= 0)

    @pl.when(own_vectors)
    def _():
        flatten(total, 36, vector_row(k, q) - base, k < 0)

    w0 = jnp.where(c == 0, 73 * k, 73 * k + nw0)

    @pl.loop(0, mine)
    def _(t):
        at, wide = tile_start(w0 + t)
        flatten(total, t, at - base, wide)

    for i in range(8):
        @pl.when(place_in != i)
        def _():
            arrived(i).wait_recv()
    layer = sqr[0]
    for i in range(1, 8):
        layer = layer + sqr[i]
    sq[1] = layer
    sqr[8 + z] = layer
    for h in hops:
        h.start()
    @pl.when(d > 0)
    def _():
        to_next.wait_recv()

        @pl.loop(0, EDGE)
        def _(t):
            at, wide = tile_start(w0 - EDGE + t)
            flatten(ebuf.at[0], t, at - base, wide)

    @pl.when(d < 31)
    def _():
        to_prev.wait_recv()

        @pl.loop(0, EDGE)
        def _(t):
            at, wide = tile_start(w0 + mine + t)
            flatten(ebuf.at[1], t, at - base, wide)

    for i in range(4):
        @pl.when(z != i)
        def _():
            arrived(8 + i).wait_recv()
    summed = (sqr[8] + sqr[9]) + (sqr[10] + sqr[11])

    @pl.when(d == 0)
    def _():
        for i in range(3):
            win[pl.ds(FRONT + 774 + i, 1), :] = summed[1 + i : 2 + i]

    sub = lax.broadcasted_iota(jnp.int32, (8, 128), 0)
    entries = jnp.where(sub == 0, summed, jnp.where(sub < 4, summed * summed, 0.0))
    square_sum = jnp.sum(jnp.sum(entries, axis=1, keepdims=True), axis=0, keepdims=True)
    factor = jnp.minimum(1.0, lax.rsqrt(square_sum / RAW + 1e-06))
    for s in shards:
        s.wait()
    lanes = lax.broadcasted_iota(jnp.int32, (80, 128), 1)
    rowi = lax.broadcasted_iota(jnp.int32, (80, 128), 0)
    back = (128 - sh) % 128

    @pl.loop(0, ROWS // 80)
    def _(i):
        r = pl.multiple_of(i * 80, 8)
        here = pltpu.roll(win[pl.ds(FRONT + r, 80), :], back, 1)
        there = pltpu.roll(win[pl.ds(FRONT + 1 + r, 80), :], back, 1)
        grad = jnp.where(lanes < 128 - sh, here, there) * factor
        entry = (d == 0) & (rowi + r < ENTRY_ROWS)
        rate = jnp.where(entry, learn_rate * layer_decay, learn_rate)
        one = beta_one * onev[pl.ds(r, 80), :] + (1.0 - beta_one) * grad
        two = beta_two * twov[pl.ds(r, 80), :] + (1.0 - beta_two) * grad * grad
        fixed_one = one / (1.0 - beta_one ** STEP)
        fixed_two = two / (1.0 - beta_two ** STEP)
        step = -rate * (fixed_one / (jnp.sqrt(fixed_two) + adam_eps) + weight_decay * mv[pl.ds(r, 80), :])
        mv[pl.ds(r, 80), :] = step
        onev[pl.ds(r, 80), :] = one
        twov[pl.ds(r, 80), :] = two

    results = [pltpu.make_async_copy(v, r, lsem.at[i]) for i, (v, r) in enumerate(((mv, step_ref), (onev, new1_ref), (twov, new2_ref)))]
    for copy in results:
        copy.start()

    for h in rounds + hops:
        h.wait_send()

    @pl.when(d < 31)
    def _():
        to_next.wait_send()

    @pl.when(d > 0)
    def _():
        to_prev.wait_send()

    shown.wait()
    for copy in results:
        copy.wait()


def backward_and_step(tiles, query, key_all, value_all, grad_context, soft, code, gfi, low, feats, grads, master, first_moment, second_moment):
    def rows_of(v):
        return jnp.pad(v, (0, ROWS * 128 - SHARD)).reshape(ROWS, 128)

    rows, keys = query.shape[0], key_all.shape[0]
    f32, bf = jnp.float32, jnp.bfloat16
    any_ = pl.BlockSpec(memory_space=pl.ANY)
    S, V, sem = jax.ShapeDtypeStruct, pltpu.VMEM, pltpu.SemaphoreType.DMA
    w = V((96, 8, D), bf)
    tile = (8, D)
    line = V((ROWS, 128), f32)
    outs = pl.pallas_call(
        backward_kernel,
        out_shape=[S((rows, D), f32), S(grads.shape, bf)] + [S((ROWS, 128), f32)] * 3 + [S((keys // 8, H, 8, rows), bf)],
        in_specs=[any_] * 14,
        out_specs=[any_] * 6,
        scratch_shapes=[
            V((2, keys, rows), bf), V((2, rows, 128), bf), V((2, keys, 128), bf), V((2, keys, 128), bf), V((2, rows, 128), bf), sem((5, 2)),
            V((keys, rows), jnp.int32), sem((1,)), V((2, keys // 8, 8, rows), bf), sem((2,)), V((2, 16, H, 8, rows), bf), sem((2,)),
            V((8 * H, 8 * BUCKETS), f32),
            V((2, keys, 128), f32), V((2, keys, 128), f32), V((6, 2, rows, 128), bf), V((6, 2, rows, 128), bf), sem((6,)), sem((6,)),
            V((3, rows, D), bf), V((2, 8, D), f32),
            w, w, w, V((rows, D), bf), V((rows, D), f32), V((rows, LF), bf), V((16, 8, D), bf), w, w, w, V((4, 8, D), bf),
            sem((12,)), sem((24,)), sem((7,)),
            V((37,) + tile, f32), V((2, EDGE) + tile, f32), V((2, 8, 128), f32), V((12, 8, 128), f32),
            V((WIN2, 128), f32), line, line, line, sem((3,)), sem((2,)), sem((2,)), sem((10,)), sem((12,)),
        ] + reducer_scratch() + chain_scratch(),
        input_output_aliases={10: 1},
        compiler_params=pltpu.CompilerParams(collective_id=5, has_side_effects=True, vmem_limit_bytes=63 << 20),
        name="backward_and_step",
    )(tiles, query, key_all, value_all, grad_context, soft, code, gfi, low, feats, grads, rows_of(master), rows_of(first_moment), rows_of(second_moment))
    return outs[0], [o.reshape(-1)[:SHARD] for o in outs[2:5]]


def from_tiles(tiles):
    got = {}
    for name, first, count in WEIGHTS:
        block = jnp.concatenate([tiles[s : s + n] for s, _, n in slots_of(first, count)])
        if name == 12:
            block = block.reshape(96, 4, 8, D).transpose(0, 2, 1, 3)
        got[name] = block.reshape(-1, FF if name == 12 else D)
    for name, chip, row in VECTORS:
        block = tiles[vector_at(chip)]
        if name == 13:
            got[name] = block[row : row + 4].reshape(FF)
        elif name == 2:
            got[name] = block[row, : BUCKETS * H].reshape(BUCKETS, H)
        else:
            got[name] = block[row]
    return [got[i] for i in range(18)]


def to_tiles(whole):
    by_name = [p.astype(jnp.bfloat16) for p in whole]
    weights = []
    for name, first, count in WEIGHTS:
        got = by_name[name]
        if name == 12:
            got = got.reshape(96, 8, 4, D).transpose(0, 2, 1, 3)
        weights.append(got.reshape(count, 8, D))
    cuts = []
    for chip in range(16):
        held = [(r, by_name[n]) for n, c, r in VECTORS if c == chip]
        rows = [jnp.pad(v.reshape(-1), (0, -v.size % D)).reshape(-1, D) for _, v in held]
        block = jnp.concatenate(rows + [jnp.zeros((8 - sum(r.shape[0] for r in rows), D), jnp.bfloat16)])
        cuts.append((73 * chip + vector_slot(chip), block[None]))
    parts = []
    for (name, first, count), tiles in zip(WEIGHTS, weights):
        at = first
        for w, block in [c for c in cuts if first <= c[0] < first + count]:
            if w > at:
                parts.append(tiles[at - first : w - first])
            parts.append(block)
            at = w
        parts.append(tiles[at - first :])
    parts.extend(block for w, block in cuts if w == 1168)
    return jnp.concatenate(parts)


def per_device(
    custom, tokens, cotangent, page_boxes, page_lengths, padding, buckets, master, first_moment, second_moment
):
    rows = tokens.shape[1]
    feats = layout_features(page_boxes.reshape(4, rows)).astype(jnp.bfloat16)
    pad = jnp.broadcast_to(padding, (8, rows))
    if custom:
        tiles, hidden, low, query, keys, values, ctx, soft, code = gather_and_attend(
            master, tokens[0], feats, pad, buckets[0], page_lengths
        )
        tiles = tiles.reshape(16 * CHIP, 8, D)
    else:
        tiles = to_tiles(unpack(lax.all_gather(master.astype(jnp.bfloat16), ("dp", "seq"), axis=0, tiled=True)))
        hidden, low, query, keys, values, pads = enter(tiles, tokens[0], feats, pad)
        ctx, soft, code = attend(query, keys, values, buckets[0], page_lengths, pads, tiles[vector_at(0)])
    activations, grad_first_in, grad_context, grads = middle(tiles, ctx, hidden, cotangent[0])
    if custom:
        input_grad, stepped = backward_and_step(
            tiles, query, keys, values, grad_context, soft, code, grad_first_in, low, feats, grads, master, first_moment, second_moment
        )
    else:
        dq, dk, dv, table = soft_back(query, keys, values, grad_context, soft, code)
        input_grad, grads = leave(tiles, dq, dk, dv, grad_first_in, low, feats, table, grads)
        flat = jnp.concatenate([p.astype(jnp.float32).reshape(-1) for p in from_tiles(grads)])
        grad = lax.psum_scatter(flat, ("dp", "seq"), scatter_dimension=0, tiled=True)
        square = lax.psum(jnp.sum(grad * grad), ("dp", "seq"))
        factor = jnp.minimum(1.0, lax.rsqrt(square / RAW + 1e-06))
        size = master.shape[0]
        index = lax.axis_index(("dp", "seq")) * size + jnp.arange(size, dtype=jnp.int32)
        stepped = adam_update(master, first_moment, second_moment, grad * factor, index)
    return (activations[None], input_grad[None]) + tuple(stepped)


def solution(mesh):
    in_specs = (
        P("dp", "seq", None),
        P("dp", "seq", None),
        P(None, "dp", "seq"),
        P("dp", None),
        P("dp", "seq"),
        P("dp", "seq", None),
        P(("dp", "seq")),
        P(("dp", "seq")),
        P(("dp", "seq")),
    )
    out_specs = (
        P("dp", "seq", None),
        P("dp", "seq", None),
        P(("dp", "seq")),
        P(("dp", "seq")),
        P(("dp", "seq")),
    )
    custom = dict(mesh.shape) == {"dp": 16, "seq": 2}
    return jax.shard_map(
        functools.partial(per_device, custom), mesh=mesh, in_specs=in_specs, out_specs=out_specs, check_vma=False
    )
```

```python
import functools
import math

import jax
import jax.numpy as jnp
from jax import lax
from jax.experimental import pallas as pl
from jax.experimental.pallas import tpu as pltpu
from jax.sharding import PartitionSpec as P

D = 768
H = 12
HD = 64
FF = 3072
BUCKETS = 32
FREQ = 16
LF = 128
LAYERS = 1
BLOCK = 1024
STEP = 10
ENTRY = 99456
LAYER_PARAMS = 7087104
RAW = 7186560


beta_one = 0.8
beta_two = 0.98
adam_eps = 1e-06
learn_rate = 0.0006
layer_decay = 0.8
weight_decay = 0.1
norm_eps = 1e-05
masked_score = -1000000000.0


SHAPES = (
    (LF, D), (D,), (BUCKETS, H),
    (D, D), (D,), (D, D), (D, D), (D,), (D, D), (D,), (D,), (D,),
    (D, FF), (FF,), (FF, D), (D,), (D,), (D,),
)


def unpack(flat_params):
    pieces, offset = [], 0
    for shape in SHAPES:
        amount = shape[0] * (shape[1] if len(shape) > 1 else 1)
        pieces.append(flat_params[offset : offset + amount].reshape(shape))
        offset = offset + amount
    return pieces


def adam_update(master, first_moment, second_moment, gradient, global_index):
    exponent = jnp.where(
        global_index < ENTRY,
        LAYERS,
        jnp.maximum(LAYERS - 1 - (global_index - ENTRY) // LAYER_PARAMS, 0),
    )
    rate = jnp.where(
        global_index < RAW, learn_rate * jnp.power(layer_decay, exponent.astype(jnp.float32)), 0.0
    )
    moment_one = beta_one * first_moment + (1.0 - beta_one) * gradient
    moment_two = beta_two * second_moment + (1.0 - beta_two) * gradient * gradient
    fixed_one = moment_one / (1.0 - beta_one**STEP)
    fixed_two = moment_two / (1.0 - beta_two**STEP)
    param_step = -rate * (fixed_one / (jnp.sqrt(fixed_two) + adam_eps) + weight_decay * master)
    return (param_step, moment_one, moment_two)


def layout_features(page_boxes):
    rates_sin = jnp.power(10000.0, -jnp.arange(FREQ, dtype=jnp.float32) / FREQ)
    angles = page_boxes.astype(jnp.float32)[:, :, None] * rates_sin
    stacked = jnp.stack([jnp.sin(angles), jnp.cos(angles)], axis=1)
    return jnp.transpose(stacked, (2, 0, 1, 3)).reshape(page_boxes.shape[1], LF)


MESH = pl.DeviceIdType.MESH
SHARD = 224580
ROWS = 1760
TAIL, HEAD = 160, 176
WIN = 2176
SLOTS = 37
CHIP = 74
PARTS = ((0, 19), (19, 18))


def place():
    k = lax.axis_index("dp")
    return k, lax.axis_index("seq"), k // 4, (k // 2) % 2, k % 2


def shard_start(d):
    return d * 1754 + (d * 68) // 128, (d * 68) % 128


def early_vectors(k):
    return (k == 0) | (k == 4) | (k == 5)


def vector_row(k, other):
    at = other
    for chip, row in ((0, 768), (1, 5385), (4, 14607), (5, 19221), (10, 37671), (15, 56127)):
        at = jnp.where(k == chip, row, at)
    return at


def tile_start(w):
    at = w * 48
    for first, shift in ((16, 777 - 16 * 48), (112, 5391 - 112 * 48), (208, 9999 - 208 * 48), (304, 14613 - 304 * 48), (784, 37695 - 784 * 48)):
        at = jnp.where(w >= first, w * 48 + shift, at)
    wide = (w >= 400) & (w < 784)
    v = w - 400
    at = jnp.where(wide, 19239 + (v // 4) * 192 + (v % 4) * 6, at)
    return at, wide


def neighbours(k, c, z, y, x):
    t = k >= 0
    return [
        (t, (k, 1 - c)),
        (t, (z * 4 + y * 2 + 1 - x, c)),
        (t, (z * 4 + (1 - y) * 2 + x, c)),
        (z < 3, (jnp.minimum(k + 4, 15), c)),
        (z > 0, (jnp.maximum(k - 4, 0), c)),
        ((c == 1) & (k < 15), (jnp.minimum(k + 1, 15), 0)),
        ((c == 0) & (k > 0), (jnp.maximum(k - 1, 0), 1)),
    ]


def greet(k, c, z, y, x):
    bar = pltpu.get_barrier_semaphore()
    for cond, dev in neighbours(k, c, z, y, x):
        @pl.when(cond)
        def _():
            pl.semaphore_signal(bar, inc=1, device_id=dev, device_id_type=MESH)
    peers = 3
    for cond, _ in neighbours(k, c, z, y, x)[3:]:
        peers = peers + jnp.where(cond, 1, 0)
    pl.semaphore_wait(bar, peers)


def rcopy(src, dst, ssem, rsem, dev):
    return pltpu.make_async_remote_copy(src_ref=src, dst_ref=dst, send_sem=ssem, recv_sem=rsem, device_id=dev, device_id_type=MESH)


FRONT = 344
WIN2 = 2464
EDGE = 4
ENTRY_ROWS = 777


WEIGHTS = (
    (0, 0, 16),
    (3, 16, 96),
    (5, 112, 96),
    (6, 208, 96),
    (8, 304, 96),
    (12, 400, 384),
    (14, 784, 384),
)
VECTORS = (
    (1, 0, 0),
    (2, 0, 1),
    (4, 1, 0),
    (7, 4, 0),
    (9, 5, 0),
    (10, 5, 1),
    (11, 5, 2),
    (13, 10, 0),
    (15, 15, 0),
    (16, 15, 1),
    (17, 15, 2),
)


def slots_of(first, count):
    runs = []
    for w in range(first, first + count):
        chip, at = divmod(w, 73)
        slot = chip * CHIP + at + (1 if at >= vector_slot(chip) else 0)
        if runs and runs[-1][0] + runs[-1][2] == slot:
            runs[-1][2] += 1
        else:
            runs.append([slot, w - first, 1])
    return runs


def vector_slot(chip):
    return 36 if chip in (0, 4, 5) else 73


def vector_at(chip):
    return chip * CHIP + vector_slot(chip)


def pieces(tiles, held, first, count, sems, base, out=False):
    made = []
    for i, (slot, at, n) in enumerate(slots_of(first, count)):
        a, b = tiles.at[pl.ds(slot, n)], held.at[pl.ds(at, n)]
        a, b = (b, a) if out else (a, b)
        made.append(pltpu.make_async_copy(a, b, sems.at[base + i]))
    return made


def matrix(tile_rows):
    return tile_rows.reshape(-1, D)


def col_sum(v):
    return jnp.sum(v.reshape(-1, 8, v.shape[-1]), axis=0)


def norm_stats(v):
    mean = jnp.mean(v, axis=-1, keepdims=True)
    center = v - mean
    spread = jnp.mean(center * center, axis=-1, keepdims=True)
    inv = lax.rsqrt(spread + norm_eps)
    return center * inv, inv


def norm_back(grad, gain, hat, inv):
    g = grad * gain
    return inv * (g - jnp.mean(g, axis=-1, keepdims=True) - hat * jnp.mean(g * hat, axis=-1, keepdims=True))


ROOT_HALF = 0.7071067811865476
ROOT_TAU = 0.3989422804014327


def middle_kernel(tiles, ctx, hidden, cot, act_out, gfi_out, gctx_out, grads,
                  wo, wup, wdn, vecs, vf, act, slope, low1, hat1, inv1, hat2, inv2, a, sums, dwo, dwup, dwdn, vgrads, lsem, ssem):
    f32, bf = jnp.float32, jnp.bfloat16
    rows = ctx.shape[0]
    R = 128
    steps = rows // R
    loads_o = pieces(tiles, wo, 304, 96, lsem, 0)
    loads_u = pieces(tiles, wup, 400, 384, lsem, 4)
    loads_d = pieces(tiles, wdn, 784, 384, lsem, 12)
    loads_v = [pltpu.make_async_copy(tiles.at[vector_at(c)], vecs.at[i], lsem.at[20 + i]) for i, c in enumerate((5, 10, 15))]
    for c in loads_v + loads_o + loads_u + loads_d:
        c.start()
    up4 = wup.reshape(96, 4, 8, D)
    dup4 = dwup.reshape(96, 4, 8, D)

    def vec(i, r):
        return vf[i, pl.ds(r, 1), :]

    def each(f):
        @pl.loop(0, steps)
        def _(i):
            f(pl.ds(pl.multiple_of(i * R, R), R))

    for c in loads_v + loads_o:
        c.wait()
    vf[...] = vecs[...].astype(f32)
    a[...] = jnp.dot(ctx[...], matrix(wo[...]), preferred_element_type=f32)

    def first(sl):
        hat, inv = norm_stats(hidden[sl, :] + a[sl, :] + vec(0, 0))
        hat1[sl, :] = hat
        inv1[sl, :] = inv
        out = hat * vec(0, 1) + vec(0, 2)
        a[sl, :] = out
        low1[sl, :] = out.astype(bf)

    each(first)
    for c in loads_u + loads_d:
        c.wait()

    def up(j, _):
        for half in range(2):
            sl = pl.ds(half * (rows // 2), rows // 2)
            u = jnp.dot(low1[sl, :], matrix(up4[:, j]), preferred_element_type=f32) + vec(1, j)
            share = 0.5 * (1.0 + lax.erf(u * ROOT_HALF))
            act[j, sl, :] = (u * share).astype(bf)
            slope[j, sl, :] = share + u * jnp.exp(-0.5 * u * u) * ROOT_TAU
        return 0

    lax.fori_loop(0, 4, up, 0)

    def down(j, _):
        a[...] += jnp.dot(act[j], matrix(wdn[pl.ds(96 * j, 96)]), preferred_element_type=f32)
        return 0

    lax.fori_loop(0, 4, down, 0)
    sums[...] = jnp.zeros_like(sums)

    def second(sl):
        hat, inv = norm_stats(a[sl, :] + vec(2, 0))
        act_out[sl, :] = (hat * vec(2, 1) + vec(2, 2)).astype(bf)
        g = cot[sl, :].astype(f32)
        sums[6] += col_sum(g * hat)
        sums[7] += col_sum(g)
        back = norm_back(g, vec(2, 1), hat, inv)
        sums[5] += col_sum(back)
        a[sl, :] = back
        hat2[sl, :] = back.astype(bf)

    each(second)
    down_back = hat2

    def back(j, _):
        for half in range(2):
            sl = pl.ds(half * (rows // 2), rows // 2)
            g = lax.dot_general(down_back[sl, :], matrix(wdn[pl.ds(96 * j, 96)]), NT, preferred_element_type=f32) * slope[j, sl, :]
            sums[8 + j] += col_sum(g)
            act_back[sl, :] = g.astype(bf)
        dwdn[pl.ds(96 * j, 96)] = lax.dot_general(act[j], down_back[...], TN, preferred_element_type=f32).astype(bf).reshape(96, 8, D)
        dup4[:, j] = lax.dot_general(low1[...], act_back[...], TN, preferred_element_type=f32).astype(bf).reshape(96, 8, D)
        a[...] += lax.dot_general(act_back[...], matrix(up4[:, j]), NT, preferred_element_type=f32)
        return 0

    act_back = inv2
    lax.fori_loop(0, 4, back, 0)
    stores = pieces(grads, dwup, 400, 384, ssem, 4, True) + pieces(grads, dwdn, 784, 384, ssem, 12, True)
    for c in stores:
        c.start()

    def third(sl):
        g = a[sl, :]
        sums[3] += col_sum(g * hat1[sl, :])
        sums[4] += col_sum(g)
        back = norm_back(g, vec(0, 1), hat1[sl, :], inv1[sl, :])
        sums[2] += col_sum(back)
        gfi_out[sl, :] = back
        hat2[sl, :] = back.astype(bf)

    each(third)
    gctx_out[...] = lax.dot_general(hat2[...], matrix(wo[...]), NT, preferred_element_type=f32).astype(bf)
    dwo[...] = lax.dot_general(ctx[...], hat2[...], TN, preferred_element_type=f32).astype(bf).reshape(96, 8, D)
    for i, held in enumerate(((2, 3, 4), (8, 9, 10, 11), (5, 6, 7))):
        lines = [jnp.sum(sums[s], axis=0, keepdims=True) for s in held]
        lines.append(jnp.zeros((8 - len(held), D), f32))
        vgrads[i] = jnp.concatenate(lines).astype(bf)
    last = pieces(grads, dwo, 304, 96, ssem, 0, True)
    quiet = [ch for ch in range(6, 15) if ch != 10]
    vgrads[3] = jnp.zeros((8, D), bf)
    last += [pltpu.make_async_copy(vgrads.at[min(i, 3)], grads.at[vector_at(ch)], ssem.at[20 + i]) for i, ch in enumerate([5, 10, 15] + quiet)]
    for c in last:
        c.start()
    for c in stores + last:
        c.wait()


def middle(tiles, ctx, hidden, cot):
    rows = ctx.shape[0]
    f32, bf = jnp.float32, jnp.bfloat16
    vm, any_ = pl.BlockSpec(memory_space=pltpu.VMEM), pl.BlockSpec(memory_space=pl.ANY)
    S = jax.ShapeDtypeStruct
    return pl.pallas_call(
        middle_kernel,
        out_shape=[S((rows, D), bf), S((rows, D), f32), S((rows, D), bf), S((16 * CHIP, 8, D), bf)],
        in_specs=[any_, vm, vm, vm],
        out_specs=[vm, vm, vm, any_],
        scratch_shapes=[
            pltpu.VMEM((96, 8, D), bf), pltpu.VMEM((384, 8, D), bf), pltpu.VMEM((384, 8, D), bf), pltpu.VMEM((3, 8, D), bf), pltpu.VMEM((3, 8, D), f32),
            pltpu.VMEM((4, rows, D), bf), pltpu.VMEM((4, rows, D), f32), pltpu.VMEM((rows, D), bf),
            pltpu.VMEM((rows, D), f32), pltpu.VMEM((rows, 1), f32), pltpu.VMEM((rows, D), bf), pltpu.VMEM((rows, D), bf),
            pltpu.VMEM((rows, D), f32), pltpu.VMEM((12, 8, D), f32),
            pltpu.VMEM((96, 8, D), bf), pltpu.VMEM((384, 8, D), bf), pltpu.VMEM((384, 8, D), bf), pltpu.VMEM((4, 8, D), bf),
            pltpu.SemaphoreType.DMA((24,)), pltpu.SemaphoreType.DMA((32,)),
        ],
        compiler_params=pltpu.CompilerParams(vmem_limit_bytes=58 << 20),
        name="middle",
    )(tiles, ctx, hidden, cot)


NT = (((1,), (1,)), ((), ()))
TN = (((0,), (0,)), ((), ()))


def half(ref_value, hh):
    lanes = lax.broadcasted_iota(jnp.int32, ref_value.shape, 1)
    keep = lanes // 64 == hh
    return jnp.where(keep, ref_value, jnp.zeros_like(ref_value))


def page_of(at, lengths):
    end, page = 0, jnp.zeros(at.shape, jnp.int32)
    for i in range(4):
        end = end + lengths[0, i]
        page = page + jnp.where(at >= end, 1, 0)
    return page


def fill_codes(code_ref, buckets, pads, lengths):
    keys, rows = code_ref.shape
    own = lax.axis_index("seq") * rows
    tag = page_of(lax.broadcasted_iota(jnp.int32, (1, keys), 1), lengths) + 1
    tag = jnp.where(jnp.concatenate([pads[0, 0:1], pads[1, 0:1]], axis=1) > 0, tag, 0)
    for i in range(rows // 128):
        at = own + 128 * i + lax.broadcasted_iota(jnp.int32, (128, 1), 0)
        page = page_of(at, lengths) + 1
        for j in range(keys // 128):
            key_at = 128 * j + lax.broadcasted_iota(jnp.int32, (1, 128), 1)
            allowed = (page == tag[:, 128 * j : 128 * j + 128]) | (key_at == at)
            code = jnp.where(allowed, buckets[128 * i : 128 * i + 128, 128 * j : 128 * j + 128], BUCKETS)
            code_ref[128 * j : 128 * j + 128, 128 * i : 128 * i + 128] = code.T


def fill_table(tab_ref, lines):
    f32 = jnp.float32
    head = lax.broadcasted_iota(jnp.int32, (16, 128), 0)
    bucket = lax.broadcasted_iota(jnp.int32, (16, 128), 1)
    place_of = bucket * H + head
    tab = jnp.full((16, 128), masked_score, f32)
    for i in range(BUCKETS * H // 128):
        row = jnp.broadcast_to(lines[1:2, 128 * i : 128 * i + 128].astype(f32), (16, 128))
        inside = jnp.clip(place_of - 128 * i, 0, 127)
        got = jnp.take_along_axis(row, inside, axis=1, mode="promise_in_bounds")
        tab = jnp.where((place_of // 128 == i) & (bucket < BUCKETS) & (head < H), got, tab)
    tab_ref[...] = tab


def soft_head(head, q, k, code_ref, tab_ref, s_scr, p_ref):
    keys, rows = s_scr.shape
    f32, bf = jnp.float32, jnp.bfloat16
    qm = half(q, head % 2)
    line = jnp.broadcast_to(tab_ref[pl.ds(head, 1), :], (keys, 128))
    s = lax.dot_general(k, qm, NT, preferred_element_type=f32)
    cols = []
    for j in range(rows // 128):
        code = code_ref[:, 128 * j : 128 * j + 128]
        bias = jnp.take_along_axis(line, code, axis=1, mode="promise_in_bounds")
        cols.append(jnp.where(bias < 0.5 * masked_score, masked_score, s[:, 128 * j : 128 * j + 128] + bias))
    s = jnp.concatenate(cols, axis=1)
    s_scr[...] = s
    top = jnp.max(jnp.max(s.reshape(keys // 8, 8, rows), axis=0), axis=0, keepdims=True)
    e = jnp.exp(s_scr[...] - top)
    s_scr[...] = e
    inverse = 1.0 / jnp.sum(jnp.sum(e.reshape(keys // 8, 8, rows), axis=0), axis=0, keepdims=True)
    p_ref[...] = (s_scr[...] * inverse).astype(bf)


def context_pair(v, p_ref):
    vt = v.T
    out = [jnp.dot(vt, p_ref[hh], preferred_element_type=jnp.float32) for hh in range(2)]
    sub = lax.broadcasted_iota(jnp.int32, out[0].shape, 0)
    return jnp.where(sub < 64, out[0], out[1]).T.astype(jnp.bfloat16)


def attend_kernel(lengths, q_ref, k_ref, v_ref, buckets, pads, lines, ctx_ref, p_ref, code_ref, s_scr, tab_ref):
    pair = pl.program_id(0)

    @pl.when(pair == 0)
    def _():
        fill_codes(code_ref, buckets, pads, lengths)
        fill_table(tab_ref, lines)

    for hh in range(2):
        soft_head(2 * pair + hh, q_ref[...], k_ref[...], code_ref, tab_ref, s_scr, p_ref.at[hh])
    ctx_ref[...] = context_pair(v_ref[...], p_ref)


def attend(query, key_all, value_all, buckets, page_lengths, pads, lines):
    rows, keys = query.shape[0], key_all.shape[0]
    bf = jnp.bfloat16
    const = lambda p: (0, 0)
    return pl.pallas_call(
        attend_kernel,
        grid=(H // 2,),
        out_shape=[
            jax.ShapeDtypeStruct((rows, D), bf),
            jax.ShapeDtypeStruct((H, keys, rows), bf),
            jax.ShapeDtypeStruct((keys, rows), jnp.int32),
        ],
        in_specs=[
            pl.BlockSpec(memory_space=pltpu.SMEM),
            pl.BlockSpec((rows, 128), lambda p: (0, p)),
            pl.BlockSpec((keys, 128), lambda p: (0, p)),
            pl.BlockSpec((keys, 128), lambda p: (0, p)),
            pl.BlockSpec((rows, keys), const),
            pl.BlockSpec((2, 8, rows), lambda p: (0, 0, 0)),
            pl.BlockSpec((8, D), const),
        ],
        out_specs=[pl.BlockSpec((rows, 128), lambda p: (0, p)), pl.BlockSpec((2, keys, rows), lambda p: (p, 0, 0)), pl.BlockSpec((keys, rows), const)],
        scratch_shapes=[pltpu.VMEM((keys, rows), jnp.float32), pltpu.VMEM((16, 128), jnp.float32)],
        compiler_params=pltpu.CompilerParams(vmem_limit_bytes=56 << 20),
        name="attend",
    )(page_lengths, query, key_all, value_all, buckets, pads, lines)


def table_row(acc, shape):
    f32 = jnp.float32
    a = lax.broadcasted_iota(jnp.int32, acc.shape, 0) % 8
    b = lax.broadcasted_iota(jnp.int32, acc.shape, 1) // BUCKETS
    acc = jnp.where(a == b, acc, 0.0)
    heads = jnp.sum(acc.reshape(H, 8, 8 * BUCKETS), axis=1)
    lane = lax.broadcasted_iota(jnp.int32, (8 * BUCKETS, D), 1) // H
    wide = jnp.where(lane == lax.broadcasted_iota(jnp.int32, lane.shape, 0) % BUCKETS, 1.0, 0.0)
    out = jnp.dot(heads, wide, precision=lax.Precision.HIGHEST, preferred_element_type=f32)
    mine = lax.broadcasted_iota(jnp.int32, out.shape, 1) % H == lax.broadcasted_iota(jnp.int32, out.shape, 0)
    out = jnp.sum(jnp.where(mine, out, 0.0), axis=0, keepdims=True)
    return jnp.broadcast_to(out, shape)


def attend_back_kernel(q_ref, k_ref, v_ref, do_ref, p_ref, code_ref, dq_ref, dk_ref, dv_ref, tab_ref, spread, held):
    pair = pl.program_id(0)
    keys, rows = code_ref.shape
    f32, bf = jnp.float32, jnp.bfloat16
    STEP_ROWS = keys
    kt = k_ref[...].T
    dq = []
    for hh in range(2):
        qm = half(q_ref[...], hh)
        dom = half(do_ref[...], hh)

        def inner(i, total):
            at = pl.multiple_of(i * STEP_ROWS, STEP_ROWS)
            g = lax.dot_general(v_ref[pl.ds(at, STEP_ROWS), :], dom, NT, preferred_element_type=f32)
            w = g * p_ref[hh, pl.ds(at, STEP_ROWS), :].astype(f32)
            return total + jnp.sum(w.reshape(STEP_ROWS // 8, 8, rows), axis=0)

        total = lax.fori_loop(0, keys // STEP_ROWS, inner, jnp.zeros((8, rows), f32))
        total = jnp.sum(total, axis=0, keepdims=True)

        def grads(i, acc):
            at = pl.multiple_of(i * STEP_ROWS, STEP_ROWS)
            sl = pl.ds(at, STEP_ROWS)
            g = lax.dot_general(v_ref[sl, :], dom, NT, preferred_element_type=f32)
            p = p_ref[hh, sl, :]
            ds = p.astype(f32) * (g - total)
            wide = ds.reshape(STEP_ROWS // 8, 8, rows)
            if hh == 0:
                held[...] = wide
            else:
                both = jnp.concatenate([held[...], wide], axis=1).astype(bf)
                spread[:, pl.ds(pl.multiple_of(pair * 16, 16), 16), :] = both
            ds = ds.astype(bf)
            dv = jnp.dot(p, dom, preferred_element_type=f32)
            dk = jnp.dot(ds, qm, preferred_element_type=f32)
            if hh == 0:
                dv_ref[sl, :] = dv
                dk_ref[sl, :] = dk
            else:
                dv_ref[sl, :] += dv
                dk_ref[sl, :] += dk
            return acc + lax.dot_general(k_ref[sl, :], ds, TN, preferred_element_type=f32)

        dq.append(lax.fori_loop(0, keys // STEP_ROWS, grads, jnp.zeros((128, rows), f32)))
    sub = lax.broadcasted_iota(jnp.int32, dq[0].shape, 0)
    dq_ref[...] = jnp.where(sub < 64, dq[0], dq[1]).T * 0.125

    @pl.when(pair == H // 2 - 1)
    def _():
        bucket = lax.broadcasted_iota(jnp.int32, (BUCKETS, rows), 0)

        def count(i, acc):
            code = code_ref[pl.ds(pl.multiple_of(i * 8, 8), 8), :]
            hot = jnp.concatenate(
                [jnp.where(jnp.broadcast_to(code[r : r + 1], bucket.shape) == bucket, 1.0, 0.0) for r in range(8)]
            ).astype(bf)
            return acc + lax.dot_general(spread[i], hot, NT, preferred_element_type=f32)

        acc = lax.fori_loop(0, keys // 8, count, jnp.zeros((8 * H, 8 * BUCKETS), f32), unroll=8)
        tab_ref[...] = table_row(acc, tab_ref.shape)


def soft_back(query, key_all, value_all, grad_context, soft, code):
    rows, keys = query.shape[0], key_all.shape[0]
    f32 = jnp.float32
    row = pl.BlockSpec((rows, 128), lambda p: (0, p))
    key = pl.BlockSpec((keys, 128), lambda p: (0, p))
    dq, dk, dv, tab = pl.pallas_call(
        attend_back_kernel,
        grid=(H // 2,),
        out_shape=[
            jax.ShapeDtypeStruct((rows, D), f32),
            jax.ShapeDtypeStruct((keys, D), f32),
            jax.ShapeDtypeStruct((keys, D), f32),
            jax.ShapeDtypeStruct((8, D), f32),
        ],
        in_specs=[row, key, key, row, pl.BlockSpec((2, keys, rows), lambda p: (p, 0, 0)), pl.BlockSpec((keys, rows), lambda p: (0, 0))],
        out_specs=[row, key, key, pl.BlockSpec((8, D), lambda p: (0, 0))],
        scratch_shapes=[pltpu.VMEM((keys // 8, 8 * H, rows), jnp.bfloat16), pltpu.VMEM((keys // 8, 8, rows), f32)],
        compiler_params=pltpu.CompilerParams(vmem_limit_bytes=58 << 20),
        name="attend_back",
    )(query, key_all, value_all, grad_context, soft, code)
    return dq, dk, dv, tab


def meet_partner():
    dp, c = lax.axis_index("dp"), lax.axis_index("seq")
    partner = (dp, 1 - c)
    bar = pltpu.get_barrier_semaphore()
    pl.semaphore_signal(bar, inc=1, device_id=partner, device_id_type=MESH)
    pl.semaphore_wait(bar, 1)
    return c, partner


def enter_kernel(tiles, tokens, feats, pad, hidden, low, query, keys, values, pads, wl, wq, wk, wv, vecs, vf, lsem, sends, recvs):
    f32, bf = jnp.float32, jnp.bfloat16
    rows = tokens.shape[0]
    loads = [pltpu.make_async_copy(tiles.at[vector_at(ch)], vecs.at[i], lsem.at[i]) for i, ch in enumerate((0, 1, 4))]
    loads += pieces(tiles, wl, 0, 16, lsem, 4) + pieces(tiles, wk, 112, 96, lsem, 8)
    loads += pieces(tiles, wv, 208, 96, lsem, 12) + pieces(tiles, wq, 16, 96, lsem, 16)
    for c in loads:
        c.start()
    c, partner = meet_partner()
    own = pl.ds(c * rows, rows)

    def share(ref, i):
        return rcopy(ref.at[own], ref.at[own], sends.at[i], recvs.at[i], partner)

    pads[pl.ds(c, 1)] = pad[...].reshape(1, 8, rows)
    pair_pads = rcopy(pads.at[pl.ds(c, 1)], pads.at[pl.ds(c, 1)], sends.at[2], recvs.at[2], partner)
    pair_pads.start()
    for copy in loads:
        copy.wait()
    vf[...] = vecs[...].astype(f32)
    h = tokens[...].astype(f32) + jnp.dot(feats[...], matrix(wl[...]), preferred_element_type=f32) + vf[0, 0:1, :]
    hidden[...] = h
    low[...] = h.astype(bf)
    keys[own, :] = jnp.dot(low[...], matrix(wk[...]), preferred_element_type=f32).astype(bf)
    send_keys = share(keys, 0)
    send_keys.start()
    values[own, :] = (jnp.dot(low[...], matrix(wv[...]), preferred_element_type=f32) + vf[2, 0:1, :]).astype(bf)
    send_values = share(values, 1)
    send_values.start()
    query[...] = ((jnp.dot(low[...], matrix(wq[...]), preferred_element_type=f32) + vf[1, 0:1, :]) * 0.125).astype(bf)
    for copy in (pair_pads, send_keys, send_values):
        copy.wait()


def enter(tiles, tokens, feats, pad):
    rows = tokens.shape[0]
    f32, bf = jnp.float32, jnp.bfloat16
    vm, any_ = pl.BlockSpec(memory_space=pltpu.VMEM), pl.BlockSpec(memory_space=pl.ANY)
    S, sem = jax.ShapeDtypeStruct, pltpu.SemaphoreType.DMA
    w = pltpu.VMEM((96, 8, D), bf)
    return pl.pallas_call(
        enter_kernel,
        out_shape=[S((rows, D), f32), S((rows, D), bf), S((rows, D), bf), S((2 * rows, D), bf), S((2 * rows, D), bf), S((2, 8, rows), jnp.int32)],
        in_specs=[any_, vm, vm, vm],
        out_specs=[vm] * 6,
        scratch_shapes=[pltpu.VMEM((16, 8, D), bf), w, w, w, pltpu.VMEM((3, 8, D), bf), pltpu.VMEM((3, 8, D), f32), sem((20,)), sem((3,)), sem((3,))],
        compiler_params=pltpu.CompilerParams(collective_id=2, has_side_effects=True, vmem_limit_bytes=40 << 20),
        name="enter",
    )(tiles, tokens, feats, pad)


def leave_kernel(tiles, dq, dk, dv, gfi, low, feats, table, grads_in, input_grad, grads,
                 wq, wk, wv, out, come, back, dwl, dwq, dwk, dwv, vgrads, lsem, ssem, sends, recvs):
    f32, bf = jnp.float32, jnp.bfloat16
    rows = gfi.shape[0]
    loads = pieces(tiles, wk, 112, 96, lsem, 0) + pieces(tiles, wv, 208, 96, lsem, 4) + pieces(tiles, wq, 16, 96, lsem, 8)
    for c in loads:
        c.start()
    c, partner = meet_partner()
    own, other = pl.ds(c * rows, rows), pl.ds((1 - c) * rows, rows)
    swaps = []
    for i, ref in enumerate((dk, dv)):
        out[i] = ref[other, :].astype(bf)
        swaps.append(rcopy(out.at[i], come.at[i], sends.at[i], recvs.at[i], partner))
        swaps[i].start()
    back[0] = dq[...].astype(bf)
    query_bias = jnp.sum(col_sum(dq[...]), axis=0, keepdims=True)
    for copy in loads:
        copy.wait()

    def through(i, w, dw):
        dw[...] = lax.dot_general(low[...], back[i], TN, preferred_element_type=f32).astype(bf).reshape(96, 8, D)
        return lax.dot_general(back[i], matrix(w[...]), NT, preferred_element_type=f32)

    input_grad[...] = gfi[...] + through(0, wq, dwq)
    stores = pieces(grads, dwq, 16, 96, ssem, 0, True)
    swaps[0].wait_recv()
    back[1] = (dk[own, :] + come[0].astype(f32)).astype(bf)
    input_grad[...] += through(1, wk, dwk)
    stores += pieces(grads, dwk, 112, 96, ssem, 4, True)
    swaps[1].wait_recv()
    grad_value = dv[own, :] + come[1].astype(f32)
    value_bias = jnp.sum(col_sum(grad_value), axis=0, keepdims=True)
    back[2] = grad_value.astype(bf)
    total = input_grad[...] + through(2, wv, dwv)
    stores += pieces(grads, dwv, 208, 96, ssem, 8, True)
    input_grad[...] = total
    layout_bias = jnp.sum(col_sum(total), axis=0, keepdims=True)
    dwl[...] = lax.dot_general(feats[...], total.astype(bf), TN, preferred_element_type=f32).astype(bf).reshape(16, 8, D)
    stores += pieces(grads, dwl, 0, 16, ssem, 12, True)

    def block(lines):
        return jnp.concatenate(lines + [jnp.zeros((8 - len(lines), D), f32)]).astype(bf)

    vgrads[0] = block([layout_bias, table[0:1, :]])
    vgrads[1] = block([query_bias])
    vgrads[2] = block([value_bias])
    vgrads[3] = jnp.zeros((8, D), bf)
    held = {0: 0, 1: 1, 4: 2}
    for i, chip in enumerate(ch for ch in range(5)):
        stores.append(pltpu.make_async_copy(vgrads.at[held.get(chip, 3)], grads.at[vector_at(chip)], ssem.at[16 + i]))
    for copy in stores:
        copy.start()
    for copy in stores:
        copy.wait()
    for swap in swaps:
        swap.wait_send()


def leave(tiles, dq, dk, dv, gfi, low, feats, table, grads):
    rows = gfi.shape[0]
    f32, bf = jnp.float32, jnp.bfloat16
    vm, any_ = pl.BlockSpec(memory_space=pltpu.VMEM), pl.BlockSpec(memory_space=pl.ANY)
    S, sem = jax.ShapeDtypeStruct, pltpu.SemaphoreType.DMA
    w = pltpu.VMEM((96, 8, D), bf)
    return pl.pallas_call(
        leave_kernel,
        out_shape=[S((rows, D), f32), S(grads.shape, bf)],
        in_specs=[any_] + [vm] * 7 + [any_],
        out_specs=[vm, any_],
        scratch_shapes=[w, w, w, pltpu.VMEM((2, rows, D), bf), pltpu.VMEM((2, rows, D), bf), pltpu.VMEM((3, rows, D), bf),
                        pltpu.VMEM((16, 8, D), bf), w, w, w, pltpu.VMEM((4, 8, D), bf), sem((12,)), sem((32,)), sem((2,)), sem((2,))],
        input_output_aliases={8: 1},
        compiler_params=pltpu.CompilerParams(collective_id=3, has_side_effects=True, vmem_limit_bytes=56 << 20),
        name="leave",
    )(tiles, dq, dk, dv, gfi, low, feats, table, grads)


GATHER_PARTS = ((0, 8), (8, 7), (15, 7), (22, 7), (29, 4), (33, 4))
GATHER_STEPS = (
    ((647, 384, 128, 256, 385, 129, 257, 386, 130, 258, 387, 131, 259, 388, 132, 260, 389, 133, 261),
     (17, 145, 8, 264, 19, 147, 12, 396, 20, 404, 10, 266, 9, 11, 13, 655, 397, 16, 18, 21, 663, 32, 33, 34, 35, 36, 37, 679, 405, 149, 268, 160, 288, 161, 289, 29, 413, 24, 25, 26, 27, 28, 671, 412, 162, 290),
     {-1: (163, 291), 0: (49, 177, 40, 296, 64, 65, 66, 67, 68, 69, 711), 1: (42, 298, 51, 179, 192), 2: (320,), 3: (41, 43, 44, 45, 687, 193, 321, 48, 50, 52, 53, 695), 4: (194, 322), 5: (195, 323, 56, 57, 58, 59, 60, 61, 703), 6: (96, 224, 352), 7: (97, 225, 353), 8: (81, 209, 72, 328, 98, 99, 100, 101, 743), 9: (226, 74, 330), 10: (227, 354, -1), 11: (73, 75, 76, 77, 719, 83, 211, 355, 113, 241, 104, 360, 105, 106, 107, 108, 109, 751, 80, 82, 84, 85, 727, 362, 112, 114, 115, 116, 117, 759, 243, 120, 121, 122, 123, 124, 125, 767, 88, 89, 90, 91, 92, 93, 735)}),
    ((679, 544, 416, 160, 288, 545, 417, 161, 289, 546),
     (0, 384, 128, 256, 547, 1, 385, 129, 257, 548, 549, 2, 386, 130, 258, 64, 576, 8, 264, 3, 387, 131, 17, 145, 4, 388, 65, 577, 259, 5, 647, 66, 67, 68, 69, 711, 389, 162, 578, 10, 266, 12, 396, 20, 404, 579, 290, 9, 11, 13, 655, 397, 19, 147, 163, 16, 18, 21, 663, 405, 580, 291, 418, 581, 164, 292, 96, 608, 29, 413, 165, 293, 24, 25, 26, 27, 28, 671, 412, 49, 177, 40, 296, 419),
     {-1: (97, 98, 99, 100, 101, 743, 51, 179, 44, 556, 52, 564, 42, 298, 420, 41, 43, 45, 687, 557, 48, 50, 53, 695, 565, 421, 181), 0: (300, 609, 428, 192, 320, 436), 1: (429, 193, 321, 61, 573), 2: (437, 56, 57, 58, 59, 60, 703, 572, 610, 194, 445, 322), 3: (444, 611, 195, 323), 4: (612, 224, 352), 5: (613, 108, 620, 225, 353), 6: (76, 588, 72, 73, 74, 75, 77, 719, 226, 116, 628, 354), 7: (589, 227, 109, 621, 355), 8: (84, 596, 81, 209, 80, 82, 83, 85, 727, 328, 117, 629), 9: (597, 211, 330), 10: (104, 105, 106, 107, 751, 112, 113, 114, 115, 759, 241, 360, -1), 11: (243, 362, 125, 637, 124, 636, 93, 605, 88, 89, 90, 91, 92, 735, 604, 120, 121, 122, 123, 767)}),
    ((711, 576, 448, 192, 320, 577, 449, 193, 321, 578),
     (32, 416, 160, 288, 579, 33, 417, 161, 289, 580, 581, 0, 384, 128, 256, 96, 608, 1, 385, 129, 257, 97, 609, 98, 99, 100, 101, 743, 2, 386, 130, 258, 610, 8, 264, 3, 387, 131, 611, 17, 145, 4, 388, 259, 5, 647, 389, 612, 49, 177, 10, 266, 12, 396, 613, 20, 404, 40, 296, 9, 11, 13, 655, 397, 19, 147, 16, 18, 21, 663, 405, 34, 162, 290, 418, 194, 322, 29, 413, 195, 24, 25, 26, 27, 28, 671, 412, 42, 298),
     {-1: (35, 419, 163, 291, 36, 420, 196, 37, 679, 421, 323), 0: (197, 44, 428, 324, 52, 436), 1: (108, 620, 325, 41, 43, 45, 687, 429, 51, 179, 224, 76, 588, 72, 328), 2: (48, 50, 53, 695, 437, 116, 628, 73, 74, 75, 77, 719, 589, 61, 445, 81, 209, 109, 621), 3: (84, 596, 352, 60, 444, 56, 57, 58, 59, 703, 117, 629, 80, 82, 83, 85, 727, 450, 225), 4: (597, 353, 451, 226), 5: (354, 452, 227), 6: (453, 355, 460, 211), 7: (330, 461, 213, 468), 8: (332, 113, 241, 104, 105, 106, 107, 751, 469, 360, 112, 114, 115, 759), 9: (125, 637, 243, 124, 636, 362, 93, 477, 605), 10: (88, 89, 90, 91, 92, 735, 476, 604, -1), 11: (120, 121, 122, 123, 767)}),
    ((743, 608, 224, 352, 609, 225, 353, 610, 226, 354, 611, 227, 355, 612, 613),
     (32, 160, 288, 33, 161, 289, 0, 128, 256, 1, 129, 257, 2, 130, 8, 264, 258, 17, 145, 3, 131, 259, 4, 5, 647, 49, 177, 10, 266, 40, 296, 9, 11, 12, 13, 655, 19, 147, 228, 16, 18, 20, 21, 663, 34, 290, 162, 356, 229, 357, 64, 192, 24, 25, 26, 27, 28, 29, 671, 108, 620),
     {-1: (42, 298, 35, 163, 291, 116, 628, 104, 105, 106, 107, 109, 751, 621, 117, 629, 112, 113, 114, 115, 759, 65, 193, 36, 37, 679, 320), 0: (360,), 1: (41, 43, 44, 45, 687, 51, 179, 241), 2: (48, 50, 52, 53, 695, 321, 243), 3: (362, 56, 57, 58, 59, 60, 61, 703, 245), 4: (364, 66, 194, 72, 328), 5: (81, 209, 322, 125, 637), 6: (67, 195, 120, 121, 122, 123, 124, 767, 636, 68, 69, 711, 323), 7: (74, 330), 8: (73, 75, 76, 77, 719), 9: (83, 211, 80, 82, 84, 85, 727), 10: (-1,), 11: (88, 89, 90, 91, 92, 93, 735)}),
)


def fill_features(out, boxes):
    rows = out.shape[0]
    f32 = jnp.float32
    cols = jnp.concatenate([boxes[i].astype(f32) for i in range(4)] + [jnp.zeros((4, rows), f32)]).T
    lane = lax.broadcasted_iota(jnp.int32, (rows, LF), 1)
    rate = jnp.exp((lane % FREQ).astype(f32) * (-math.log(10000.0) / FREQ))
    coordinate = lane // (2 * FREQ)
    at = cols[:, 3:4]
    for i in range(3):
        at = jnp.where(coordinate == i, cols[:, i : i + 1], at)
    angle = at * rate
    out[...] = jnp.where(lane // FREQ % 2 == 0, jnp.sin(angle), jnp.cos(angle)).astype(jnp.bfloat16)


def forward_kernel(x_ref, tokens, boxes, pad, buckets, lengths,
                   g_ref, hidden, low, query, keys, values, ctx, soft, code_out, feats,
                   xv, tail, head, win, chunk, lsem, hsend, hrecv, own,
                   ssem, rsem, cr,
                   pads, hidden_v, low_v, query_v, keys_v, values_v, ctx_v, code, buckets_v, tokens_v, feats_v, p_v, s_scr, tab,
                   wl, wq, wk, wv, vrows, vf, ksend, krecv, wsem, isem, osem, psem):
    f32, bf = jnp.float32, jnp.bfloat16
    rows = tokens.shape[0]
    k, c, z, y, x = place()
    d = 2 * k + c
    inputs = [pltpu.make_async_copy(r, v, isem.at[i]) for i, (r, v) in enumerate(((buckets, buckets_v), (tokens, tokens_v)))]
    for copy in inputs:
        copy.start()
    pads[pl.ds(c, 1)] = jnp.broadcast_to(pad[...], (8, rows)).reshape(1, 8, rows)
    greet(k, c, z, y, x)
    load = pltpu.make_async_copy(x_ref, xv, lsem)
    load.start()
    prev = (jnp.where(c == 1, k, jnp.maximum(k - 1, 0)), 1 - c)
    nxt = (jnp.where(c == 0, k, jnp.minimum(k + 1, 15)), 1 - c)
    to_next = rcopy(x_ref.at[pl.ds(ROWS - TAIL, TAIL)], tail, hsend.at[0], hrecv.at[0], nxt)
    to_prev = rcopy(x_ref.at[pl.ds(0, HEAD)], head, hsend.at[1], hrecv.at[1], prev)

    @pl.when(d < 31)
    def _():
        to_next.start()

    @pl.when(d > 0)
    def _():
        to_prev.start()

    win[...] = jnp.zeros_like(win)
    lanes = lax.broadcasted_iota(jnp.int32, (80, 128), 1)
    q, sh = shard_start(d)
    load.wait()

    @pl.loop(0, ROWS // 80)
    def _(i):
        r = pl.multiple_of(i * 80, 8)
        rolled = pltpu.roll(xv[pl.ds(r, 80), :], sh, 1)
        win[pl.ds(160 + r, 80), :] += jnp.where(lanes >= sh, rolled, 0.0)
        win[pl.ds(161 + r, 80), :] += jnp.where(lanes < sh, rolled, 0.0)

    @pl.when(d > 0)
    def _():
        to_next.wait_recv()
        qp, shp = shard_start(d - 1)
        lanes = lax.broadcasted_iota(jnp.int32, (TAIL, 128), 1)
        rolled = pltpu.roll(tail[...], shp, 1)
        at = 1760 - (q - qp)
        win[pl.ds(at, TAIL), :] += jnp.where(lanes >= shp, rolled, 0.0)
        win[pl.ds(at + 1, TAIL), :] += jnp.where(lanes < shp, rolled, 0.0)

    @pl.when(d < 31)
    def _():
        to_prev.wait_recv()
        qn, shn = shard_start(d + 1)
        lanes = lax.broadcasted_iota(jnp.int32, (HEAD, 128), 1)
        rolled = pltpu.roll(head[...], shn, 1)
        at = 160 + (qn - q)
        win[pl.ds(at, HEAD), :] += jnp.where(lanes >= shn, rolled, 0.0)
        win[pl.ds(at + 1, HEAD), :] += jnp.where(lanes < shn, rolled, 0.0)

    early = early_vectors(k)
    nw0 = jnp.where(early, 36, 37)
    vecs = early == (c == 0)
    first = jnp.where(c == 0, 73 * k, 73 * k + nw0)
    base = q - 160

    @pl.loop(0, SLOTS)
    def _(t):
        at, wide = tile_start(first + t)
        is_vec = vecs & (t == 36)
        at = jnp.where(is_vec, vector_row(k, q), at) - base
        wide = wide & jnp.logical_not(is_vec)

        @pl.when(wide)
        def _():
            parts = [win[pl.ds(at + j, 8, stride=24), :] for j in range(6)]
            chunk[t] = jnp.concatenate(parts, axis=1).astype(jnp.bfloat16)

        @pl.when(jnp.logical_not(wide))
        def _():
            parts = [win[pl.ds(at + j, 8, stride=6), :] for j in range(6)]
            chunk[t] = jnp.concatenate(parts, axis=1).astype(jnp.bfloat16)

    @pl.when(d < 31)
    def _():
        to_next.wait_send()

    @pl.when(d > 0)
    def _():
        to_prev.wait_send()

    xdev, ydev, cdev = (z * 4 + y * 2 + 1 - x, c), (z * 4 + (1 - y) * 2 + x, c), (k, 1 - c)
    targets = {1: xdev, 2: ydev, 3: (jnp.minimum(k + 4, 15), c), 4: (jnp.maximum(k - 4, 0), c), 5: cdev}
    tiles = g_ref.reshape(16 * CHIP, 8, D)

    def step(zz, op):
        if op < 0:
            make_values()
            return
        link, item, p = op // 128, op // 8 % 16, op % 8
        chip = item // 4 * 4 + (1 - y if item // 2 % 2 else y) * 2 + (1 - x if item % 2 else x)
        off, n = (0, 37) if link == 5 else GATHER_PARTS[p]
        there = g_ref.at[chip, pl.ds(37 * c + off, n)]
        if link == 0:
            rcopy(there, there, ssem.at[0], rsem.at[chip, p], xdev).wait_recv()
            return
        here = chunk.at[pl.ds(off, n)] if item == zz * 4 else there
        rcopy(here, there, ssem.at[link - 1], cr.at[chip] if link == 5 else rsem.at[chip, p], targets[link]).start()

    def steps_of(zz, which, head=0):
        for op in GATHER_STEPS[zz][which] if which < 2 else GATHER_STEPS[zz][2].get(head, ()):
            step(zz, op)

    def sent_rows(zz, link):
        ops = [op for w in (0, 1) for op in GATHER_STEPS[zz][w]] + [op for v in GATHER_STEPS[zz][2].values() for op in v]
        return sum(37 if link == 5 else GATHER_PARTS[op % 8][1] for op in ops if op // 128 == link)

    pair_pads = rcopy(pads.at[pl.ds(c, 1)], pads.at[pl.ds(c, 1)], ksend.at[2], krecv.at[2], cdev)
    pair_pads.start()
    mine = pltpu.make_async_copy(chunk, g_ref.at[k, pl.ds(37 * c, 37)], own.at[0])

    for zz in range(4):
        @pl.when(z == zz)
        def _():
            steps_of(zz, 0)
    mine.start()
    for copy in inputs:
        copy.wait()
    pair_pads.wait()
    fill_codes(code, buckets_v, pads, lengths)
    fill_features(feats_v, boxes)
    outs = [pltpu.make_async_copy(code, code_out, osem.at[0]), pltpu.make_async_copy(feats_v, feats, osem.at[7])]
    for copy in outs:
        copy.start()
    for zz in range(4):
        @pl.when(z == zz)
        def _():
            steps_of(zz, 1)
    mine.wait()

    def from_partner(chip):
        theirs = g_ref.at[chip, pl.ds(37 * (1 - c), 37)]
        rcopy(theirs, theirs, ssem.at[4], cr.at[chip], cdev).wait_recv()

    for chip in range(3):
        from_partner(chip)

    loads = [pltpu.make_async_copy(tiles.at[vector_at(ch)], vrows.at[i], wsem.at[i]) for i, ch in enumerate((0, 1))]
    loads += pieces(tiles, wl, 0, 16, wsem, 4) + pieces(tiles, wk, 112, 96, wsem, 8) + pieces(tiles, wq, 16, 96, wsem, 16)
    for copy in loads:
        copy.start()
    for copy in loads:
        copy.wait()
    vf[0] = vrows[0].astype(f32)
    vf[1] = vrows[1].astype(f32)
    fill_table(tab, vrows.at[0])
    h = tokens_v[...].astype(f32) + jnp.dot(feats_v[...], matrix(wl[...]), preferred_element_type=f32) + vf[0, 0:1, :]
    hidden_v[...] = h
    low_v[...] = h.astype(bf)
    half_rows = pl.ds(c * rows, rows)

    def share(ref, i):
        return rcopy(ref.at[half_rows], ref.at[half_rows], ksend.at[i], krecv.at[i], cdev)

    keys_v[half_rows, :] = jnp.dot(low_v[...], matrix(wk[...]), preferred_element_type=f32).astype(bf)
    share(keys_v, 0).start()
    query_v[...] = ((jnp.dot(low_v[...], matrix(wq[...]), preferred_element_type=f32) + vf[1, 0:1, :]) * 0.125).astype(bf)
    share(keys_v, 0).wait()
    outs += [pltpu.make_async_copy(v, r, osem.at[1 + i]) for i, (v, r) in enumerate(((hidden_v, hidden), (low_v, low), (query_v, query), (keys_v, keys)))]
    for copy in outs[2:]:
        copy.start()

    def make_values():
        for chip in (3, 4):
            from_partner(chip)
        copies = [pltpu.make_async_copy(tiles.at[vector_at(4)], vrows.at[2], wsem.at[2])] + pieces(tiles, wv, 208, 96, wsem, 12)
        for copy in copies:
            copy.start()
        for copy in copies:
            copy.wait()
        vf[2] = vrows[2].astype(f32)
        values_v[half_rows, :] = (jnp.dot(low_v[...], matrix(wv[...]), preferred_element_type=f32) + vf[2, 0:1, :]).astype(bf)
        share(values_v, 1).start()

    def keep(pair):
        return pltpu.make_async_copy(p_v.at[pl.ds(2 * pair, 2)], soft.at[pl.ds(2 * pair, 2)], psem.at[pair])

    for zz in range(4):
        if -1 in GATHER_STEPS[zz][2]:
            @pl.when(z == zz)
            def _():
                steps_of(zz, 2, -1)

    def one_head(head, _):
        lanes = pl.ds(pl.multiple_of(head // 2 * 128, 128), 128)
        soft_head(head, query_v[:, lanes], keys_v[:, lanes], code, tab, s_scr, p_v.at[head])

        @pl.when(head % 2 == 1)
        def _():
            keep(head // 2).start()

        for zz in range(4):
            for i in range(H):
                if i in GATHER_STEPS[zz][2]:
                    @pl.when((head == i) & (z == zz))
                    def _():
                        steps_of(zz, 2, i)
        return 0

    lax.fori_loop(0, H, one_head, 0)
    share(values_v, 1).wait()
    outs.append(pltpu.make_async_copy(values_v, values, osem.at[5]))
    outs[-1].start()

    def context(pair, _):
        lanes = pl.ds(pl.multiple_of(pair * 128, 128), 128)
        ctx_v[:, lanes] = context_pair(values_v[:, lanes], p_v.at[pl.ds(2 * pair, 2)])
        return 0

    lax.fori_loop(0, H // 2, context, 0)
    outs.append(pltpu.make_async_copy(ctx_v, ctx, osem.at[6]))
    outs[-1].start()

    for zz in range(4):
        @pl.when(z == zz)
        def _():
            for link in range(1, 6):
                n = sent_rows(zz, link)
                if n:
                    whole = tiles.at[pl.ds(0, n)]
                    rcopy(whole, whole, ssem.at[link - 1], cr.at[0], targets[link]).wait_send()
    for chip in range(5, 16):
        from_partner(chip)
    for pair in range(H // 2):
        keep(pair).wait()
    for copy in outs:
        copy.wait()


def gather_and_attend(master, tokens, boxes, pad, buckets, page_lengths):
    x = jnp.pad(master, (0, ROWS * 128 - SHARD)).reshape(ROWS, 128)
    sem = pltpu.SemaphoreType.DMA
    any_, vm = pl.BlockSpec(memory_space=pl.ANY), pl.BlockSpec(memory_space=pltpu.VMEM)
    rows, key_rows = buckets.shape
    f32, bf = jnp.float32, jnp.bfloat16
    S, V = jax.ShapeDtypeStruct, pltpu.VMEM
    w = V((96, 8, D), bf)
    return pl.pallas_call(
        forward_kernel,
        out_shape=[
            S((16, CHIP, 8, D), bf), S((rows, D), f32), S((rows, D), bf), S((rows, D), bf), S((key_rows, D), bf), S((key_rows, D), bf),
            S((rows, D), bf), S((H, key_rows, rows), bf), S((key_rows, rows), jnp.int32), S((rows, LF), bf),
        ],
        in_specs=[any_, any_, vm, vm, any_, pl.BlockSpec(memory_space=pltpu.SMEM)],
        out_specs=[any_] * 10,
        scratch_shapes=[
            V((ROWS, 128), f32), V((TAIL, 128), f32), V((HEAD, 128), f32), V((WIN, 128), f32), V((SLOTS, 8, D), bf),
            sem, sem((2,)), sem((2,)), sem((2,)),
            sem((5,)), sem((16, 6)), sem((16,)),
            V((2, 8, rows), jnp.int32), V((rows, D), f32), V((rows, D), bf), V((rows, D), bf), V((key_rows, D), bf), V((key_rows, D), bf),
            V((rows, D), bf), V((key_rows, rows), jnp.int32), V((rows, key_rows), jnp.int32), V((rows, D), bf), V((rows, LF), bf),
            V((H, key_rows, rows), bf), V((key_rows, rows), f32), V((16, 128), f32),
            V((16, 8, D), bf), w, w, w, V((3, 8, D), bf), V((3, 8, D), f32),
            sem((3,)), sem((3,)), sem((20,)), sem((3,)), sem((8,)), sem((H // 2,)),
        ],
        compiler_params=pltpu.CompilerParams(collective_id=0, has_side_effects=True, vmem_limit_bytes=60 << 20),
        name="gather_and_attend",
    )(x, tokens, boxes, pad, buckets, page_lengths)


def guarded(cond, f):
    if cond is True:
        f()
    elif cond is not False:
        pl.when(cond)(f)


class Reducer:
    def __init__(self, where, zs, want, spare, g_ref, acc, crecv, a1, b1, a2, b2, asem, cs, cr, a1s, a1r, b1s, b1r, a2s, a2r, b2s, b2r):
        self.k, self.c, self.z, self.y, self.x = where
        self.zs, self.want, self.spare = zs, want, spare
        self.g_ref, self.acc, self.crecv = g_ref, acc, crecv
        self.bufs = (a1, b1, a2, b2)
        self.asem, self.cs, self.cr = asem, cs, cr
        self.sems = ((a1s, a1r), (b1s, b1r), (a2s, a2r), (b2s, b2r))
        z, y, x, c = self.z, self.y, self.x, self.c
        self.xdev, self.ydev, self.cdev = (z * 4 + y * 2 + 1 - x, c), (z * 4 + (1 - y) * 2 + x, c), (self.k, 1 - c)

    def at(self, zo, oy, ox):
        return zo, (1 - self.y if oy else self.y), (1 - self.x if ox else self.x)

    def chip(self, zo, yo, xo):
        return zo * 4 + yo * 2 + xo

    def local(self, zo, yo, xo):
        return self.chip(zo, yo, xo)

    def load(self, item):
        i = self.local(*item)
        return pltpu.make_async_copy(self.g_ref.at[self.chip(*item), pl.ds(37 * self.c, 37)], self.acc.at[i], self.asem.at[i])

    def ccopy(self, item):
        i = self.local(*item)
        return rcopy(self.g_ref.at[self.chip(*item), pl.ds(37 * (1 - self.c), 37)], self.crecv.at[i + self.spare], self.cs.at[i], self.cr.at[i], self.cdev)

    def hop(self, which, item, slot, p, dev):
        s, r = self.sems[which]
        return rcopy(self.acc.at[self.local(*item), pl.ds(*PARTS[p])], self.bufs[which].at[slot], s.at[slot], r.at[slot], dev)

    def a1(self, zo, xo):
        return self.hop(0, (zo, 1 - self.y, xo), self.zs.index(zo) * 2 + xo, 0, self.ydev)

    def b1(self, zo, yo):
        return self.hop(1, (zo, yo, 1 - self.x), self.zs.index(zo) * 2 + yo, 1, self.xdev)

    def a2(self, zo):
        return self.hop(2, (zo, self.y, 1 - self.x), self.zs.index(zo), 0, self.xdev)

    def b2(self, zo):
        return self.hop(3, (zo, 1 - self.y, self.x), self.zs.index(zo), 1, self.ydev)

    def gain(self, item, p, which, slot):
        off, n = PARTS[p]
        i, acc, buf = self.local(*item), self.acc, self.bufs[which]
        acc[i, pl.ds(off, n)] = acc[i, pl.ds(off, n)] + buf[slot]

    def begin(self, zo, oy, ox):
        item = self.at(zo, oy, ox)

        def go():
            self.load(item).start()
            self.ccopy(item).start()
        guarded(self.want(*item), go)

    def first(self, zo, oy, ox):
        item = self.at(zo, oy, ox)

        def go():
            self.load(item).wait()
            self.ccopy(item).wait_recv()
            i = self.local(*item)
            self.acc[i] = self.acc[i] + self.crecv[i + self.spare]
            if oy:
                self.a1(zo, item[2]).start()
            if ox:
                self.b1(zo, item[1]).start()
        guarded(self.want(*item), go)

    def second(self, zo):
        ia, ib = self.at(zo, 0, 1), self.at(zo, 1, 0)
        n = self.zs.index(zo) * 2

        def go_a():
            self.a1(zo, 1 - self.x).wait_recv()
            self.gain(ia, 0, 0, n + 1 - self.x)
            self.a2(zo).start()

        def go_b():
            self.b1(zo, 1 - self.y).wait_recv()
            self.gain(ib, 1, 1, n + 1 - self.y)
            self.b2(zo).start()
        guarded(self.want(*ia), go_a)
        guarded(self.want(*ib), go_b)

    def third(self, zo):
        item = self.at(zo, 0, 0)
        n = self.zs.index(zo)

        def go():
            self.a1(zo, self.x).wait_recv()
            self.b1(zo, self.y).wait_recv()
            self.a2(zo).wait_recv()
            self.b2(zo).wait_recv()
            i = self.local(*item)
            for p, (h, u), at in ((0, (0, 2), self.x), (1, (1, 3), self.y)):
                off, m = PARTS[p]
                self.acc[i, pl.ds(off, m)] = (self.acc[i, pl.ds(off, m)] + self.bufs[h][n * 2 + at]) + self.bufs[u][n]
        guarded(self.want(*item), go)

    def finish(self):
        for zo in self.zs:
            for oy in (0, 1):
                for ox in (0, 1):
                    item = self.at(zo, oy, ox)

                    def sent(item=item, oy=oy, ox=ox, zo=zo):
                        self.ccopy(item).wait_send()
                        if oy:
                            self.a1(zo, item[2]).wait_send()
                        if ox:
                            self.b1(zo, item[1]).wait_send()
                        if ox and not oy:
                            self.a2(zo).wait_send()
                        if oy and not ox:
                            self.b2(zo).wait_send()
                    guarded(self.want(*item), sent)


def reducer_scratch():
    bf, sem = jnp.bfloat16, pltpu.SemaphoreType.DMA
    tile = (8, D)
    return [
        pltpu.VMEM((16, 37) + tile, bf), pltpu.VMEM((11, 37) + tile, bf),
        pltpu.VMEM((8, 19) + tile, bf), pltpu.VMEM((8, 18) + tile, bf), pltpu.VMEM((4, 19) + tile, bf), pltpu.VMEM((4, 18) + tile, bf),
        sem((16,)), sem((16,)), sem((16,)),
        sem((8,)), sem((8,)), sem((8,)), sem((8,)), sem((4,)), sem((4,)), sem((4,)), sem((4,)),
    ]


def early_item(zo, yo, xo):
    return zo >= 2 if zo != 1 else yo + xo > 0


def late_item(zo, yo, xo):
    return zo == 0 if zo != 1 else yo + xo == 0


ZCUTS = ((0, 10), (10, 9), (19, 9), (28, 9))


class Chain:
    def __init__(self, where, acc, up, dn, us, ur, ds_, dr):
        self.k, self.c, self.z, self.y, self.x = where
        self.acc = acc
        self.ways = {1: (up, us, ur, (jnp.minimum(self.k + 4, 15), self.c)), -1: (dn, ds_, dr, (jnp.maximum(self.k - 4, 0), self.c))}

    def chip(self, zo):
        return zo * 4 + self.y * 2 + self.x

    def copy(self, zo, way, p):
        buf, s, r, dev = self.ways[way]
        part = pl.ds(*ZCUTS[p])
        return rcopy(self.acc.at[self.chip(zo), part], buf.at[zo, part], s.at[zo, p], r.at[zo, p], dev)

    def move(self, zs, zo, way, take=True, give=True, also=None):
        cond = self.z == zs if also is None else (self.z == zs) & also

        @pl.when(cond)
        def _():
            i = self.chip(zo)
            for p in range(4):
                if take:
                    self.copy(zo, way, p).wait_recv()
                    part = pl.ds(*ZCUTS[p])
                    self.acc[i, part] = self.acc[i, part] + self.ways[way][0][zo, part]
                if give:
                    self.copy(zo, way, p).start()

    def sent(self, zs, zo, way):
        @pl.when(self.z == zs)
        def _():
            for p in range(4):
                self.copy(zo, way, p).wait_send()


def chain_scratch():
    bf, sem = jnp.bfloat16, pltpu.SemaphoreType.DMA
    return [pltpu.VMEM((4, 37, 8, D), bf)] * 2 + [sem((4, 4))] * 4


def backward_kernel(tiles, q_ref, k_ref, v_ref, do_ref, p_hbm, code_hbm, gfi_in, low_in, feats_in, grads_in, m_ref, one_ref, two_ref,
                    grad_out, grads, step_ref, new1_ref, new2_ref, spread,
                    pbuf, qv, kv, vv, dov, psem, code_ref, csem, dsv, dssem, group, gsem, counts, dks, dvs, out, come, sends, recvs, back, bias,
                    wq, wk, wv, low, gfi, feats, dwl, dwq, dwk, dwv, vgrads, wsem, ssem, isem,
                    total, ebuf, sq, sqr, win, mv, onev, twov, lsem, es, er, qs, qr, *scratch):
    f32, bf = jnp.float32, jnp.bfloat16
    where = place()
    k, c, z, y, x = where
    d = 2 * k + c
    shared = grads.reshape(16, CHIP, 8, D)
    rs = Reducer(where, (0, 1, 2, 3), early_item, -5, shared, *scratch[:17])
    late = Reducer(where, (0, 1, 2, 3), late_item, 6, shared, *scratch[:17])
    acc = rs.acc
    zc = Chain(where, acc, *scratch[17:])
    xdev, ydev, cdev = rs.xdev, rs.ydev, rs.cdev
    column_devs = [((z + s) % 4 * 4 + y * 2 + x, c) for s in (1, 2, 3)]
    prev = (jnp.where(c == 1, k, jnp.maximum(k - 1, 0)), 1 - c)
    nxt = (jnp.where(c == 0, k, jnp.minimum(k + 1, 15)), 1 - c)
    bar = pltpu.get_barrier_semaphore()
    far_next, far_prev = (c == 1) & (k < 15), (c == 0) & (k > 0)
    plane_devs = [(z * 4 + (1 - y if oy else y) * 2 + (1 - x if ox else x), 1 - c if oc else c) for oc in (0, 1) for oy in (0, 1) for ox in (0, 1)][1:]
    for dev in plane_devs + column_devs:
        pl.semaphore_signal(bar, inc=1, device_id=dev, device_id_type=MESH)

    @pl.when(far_next)
    def _():
        pl.semaphore_signal(bar, inc=1, device_id=nxt, device_id_type=MESH)

    @pl.when(far_prev)
    def _():
        pl.semaphore_signal(bar, inc=1, device_id=prev, device_id_type=MESH)

    keys, rows = code_ref.shape

    def fetch_soft(pair, hh):
        return pltpu.make_async_copy(p_hbm.at[2 * pair + hh], pbuf.at[hh], psem.at[0, hh])

    def fetch(p):
        slot = p % 2
        lanes = pl.ds(pl.multiple_of(p * 128, 128), 128)
        return [pltpu.make_async_copy(r.at[:, lanes], v.at[slot], psem.at[1 + i, slot]) for i, (r, v) in enumerate(((q_ref, qv), (k_ref, kv), (v_ref, vv), (do_ref, dov)))]

    for copy in fetch(0) + [fetch_soft(0, 0), fetch_soft(0, 1)]:
        copy.start()
    pl.semaphore_wait(bar, 10 + jnp.where(far_next | far_prev, 1, 0))
    corners = ((1, 1), (1, 0), (0, 1), (0, 0))
    for oy, ox in corners:
        rs.begin(3, oy, ox)
    code_copy = pltpu.make_async_copy(code_hbm, code_ref, csem.at[0])
    inputs = [pltpu.make_async_copy(r, v, isem.at[i]) for i, (r, v) in enumerate(((low_in, low), (gfi_in, gfi), (feats_in, feats)))]
    loads = pieces(tiles, wq, 16, 96, wsem, 8) + pieces(tiles, wv, 208, 96, wsem, 4) + pieces(tiles, wk, 112, 96, wsem, 0)
    shards = [pltpu.make_async_copy(r, v, lsem.at[i]) for i, (r, v) in enumerate(((m_ref, mv), (one_ref, onev), (two_ref, twov)))]
    for copy in [code_copy] + inputs + loads + shards:
        copy.start()
    own, other = pl.ds(c * rows, rows), pl.ds((1 - c) * rows, rows)

    def swap(pair):
        return rcopy(out.at[pair], come.at[pair], sends.at[pair], recvs.at[pair], cdev)

    def settle(pair):
        slot = pair % 2
        swap(pair).wait_recv()
        lanes = pl.ds(pl.multiple_of(pair * 128, 128), 128)
        dk = dks[slot, own, :] + come[pair, 0].astype(f32)
        dv = dvs[slot, own, :] + come[pair, 1].astype(f32)
        back[1, :, lanes] = dk.astype(bf)
        back[2, :, lanes] = dv.astype(bf)
        bias[1, :, lanes] = col_sum(dv)

    def lay(pair, hh):
        return pltpu.make_async_copy(dsv.at[hh], spread.at[:, 2 * pair + hh], dssem.at[hh])

    plan = {
        0: [(rs.first, 3, 1, 0), (rs.begin, 2, 1, 1), (rs.begin, 2, 1, 0), (rs.begin, 2, 0, 1), (rs.begin, 2, 0, 0), (rs.first, 3, 0, 1)],
        1: [(rs.begin, 1, 1, 1), (rs.begin, 1, 1, 0), (rs.begin, 1, 0, 1), (rs.begin, 1, 0, 0), (rs.first, 2, 1, 1), (rs.first, 2, 0, 1), (rs.second, 3)],
        2: [(rs.first, 2, 1, 0)],
        4: [(rs.first, 2, 0, 0), (rs.second, 2), (rs.first, 3, 0, 0), (rs.first, 1, 1, 1)],
    }
    rs.first(3, 1, 1)

    def pair_of_heads(pair, _):
        slot = pair % 2

        @pl.when(pair < H // 2 - 1)
        def _():
            for copy in fetch(pair + 1):
                copy.start()

        for copy in fetch(pair):
            copy.wait()
        lanes = pl.ds(pl.multiple_of(pair * 128, 128), 128)
        dq = []
        for hh in range(2):
            fetch_soft(pair, hh).wait()
            qm = half(qv[slot], hh)
            dom = half(dov[slot], hh)
            g = lax.dot_general(vv[slot], dom, NT, preferred_element_type=f32)
            p = pbuf[hh]
            pf = p.astype(f32)
            inner = jnp.sum(jnp.sum((g * pf).reshape(keys // 8, 8, rows), axis=0), axis=0, keepdims=True)
            ds = (pf * (g - inner)).astype(bf)

            @pl.when(pair > 0)
            def _():
                lay(pair - 1, hh).wait()

            dsv[hh] = ds.reshape(keys // 8, 8, rows)
            lay(pair, hh).start()
            dv = jnp.dot(p, dom, preferred_element_type=f32)

            @pl.when(pair < H // 2 - 1)
            def _():
                fetch_soft(pair + 1, hh).start()

            dk = jnp.dot(ds, qm, preferred_element_type=f32)
            if hh == 0:
                dvs[slot] = dv
                dks[slot] = dk
            else:
                dvs[slot] += dv
                dks[slot] += dk
            dq.append(lax.dot_general(kv[slot], ds, TN, preferred_element_type=f32))
        out[pair, 0] = dks[slot, other, :].astype(bf)
        out[pair, 1] = dvs[slot, other, :].astype(bf)
        swap(pair).start()
        sub = lax.broadcasted_iota(jnp.int32, dq[0].shape, 0)
        dqf = jnp.where(sub < 64, dq[0], dq[1]).T * 0.125
        back[0, :, lanes] = dqf.astype(bf)
        bias[0, :, lanes] = col_sum(dqf)

        @pl.when(pair > 0)
        def _():
            settle(pair - 1)

        for i, steps in plan.items():
            @pl.when(pair == i)
            def _():
                for f, *a in steps:
                    f(*a)
        return 0

    lax.fori_loop(0, H // 2, pair_of_heads, 0)
    for hh in range(2):
        lay(H // 2 - 1, hh).wait()
    for copy in inputs + loads:
        copy.wait()

    def through(i, w, dw):
        dw[...] = lax.dot_general(low[...], back[i], TN, preferred_element_type=f32).astype(bf).reshape(96, 8, D)
        return lax.dot_general(back[i], matrix(w[...]), NT, preferred_element_type=f32)

    stores = []

    def keep(dw, first, count, base):
        made = pieces(grads, dw, first, count, ssem, base, True)
        for copy in made:
            copy.start()
        stores.extend(made)

    gfi[...] += through(0, wq, dwq)
    keep(dwq, 16, 96, 0)
    settle(H // 2 - 1)
    gfi[...] += through(2, wv, dwv)
    keep(dwv, 208, 96, 8)
    whole = gfi[...] + through(1, wk, dwk)
    keep(dwk, 112, 96, 4)
    gfi[...] = whole
    shown = pltpu.make_async_copy(gfi, grad_out, isem.at[6])
    shown.start()
    layout_bias = jnp.sum(col_sum(whole), axis=0, keepdims=True)
    dwl[...] = lax.dot_general(feats[...], whole.astype(bf), TN, preferred_element_type=f32).astype(bf).reshape(16, 8, D)
    keep(dwl, 0, 16, 12)

    def block(lines):
        return jnp.concatenate(lines + [jnp.zeros((8 - len(lines), D), f32)]).astype(bf)

    vgrads[0] = block([layout_bias])
    vgrads[1] = block([jnp.sum(bias[0], axis=0, keepdims=True)])
    vgrads[2] = block([jnp.sum(bias[1], axis=0, keepdims=True)])
    vgrads[3] = jnp.zeros((8, D), bf)
    held = {0: 0, 1: 1, 4: 2}
    for i, ch in enumerate((0, 1, 2, 3, 4)):
        copy = pltpu.make_async_copy(vgrads.at[held.get(ch, 3)], grads.at[vector_at(ch)], ssem.at[16 + i])
        copy.start()
        stores.append(copy)
    for copy in stores:
        copy.wait()
    for oy, ox in corners:
        for zo in (0, 1):
            late.begin(zo, oy, ox)

    GROUPS = 16

    def take_groups(i):
        return pltpu.make_async_copy(spread.at[pl.ds(i * GROUPS, GROUPS)], group.at[i % 2], gsem.at[i % 2])

    bucket = lax.broadcasted_iota(jnp.int32, (BUCKETS, rows), 0)
    steps = keys // 8 // GROUPS
    code_copy.wait()
    take_groups(0).start()
    counts[...] = jnp.zeros_like(counts)

    def count_some(first, n):
        for i in range(first, first + n):
            if i + 1 < steps:
                take_groups(i + 1).start()
            take_groups(i).wait()

            def count(j, run, i=i):
                code = code_ref[pl.ds(pl.multiple_of((i * GROUPS + j) * 8, 8), 8), :]
                hot = jnp.concatenate(
                    [jnp.where(jnp.broadcast_to(code[r : r + 1], bucket.shape) == bucket, 1.0, 0.0) for r in range(8)]
                ).astype(bf)
                return run + lax.dot_general(group[i % 2, j].reshape(8 * H, rows), hot, NT, preferred_element_type=f32)

            counts[...] = lax.fori_loop(0, GROUPS, count, counts[...], unroll=8)

    early_one, late_one = rs.want(1, y, x), late.want(1, y, x)
    rs.third(3)
    zc.move(0, 3, 1, take=False)
    late.first(0, 1, 1)
    late.first(1, 1, 1)
    zc.move(1, 3, 1)
    late.first(0, 1, 0)
    late.first(1, 1, 0)
    count_some(0, 1)
    late.first(0, 0, 1)
    late.first(1, 0, 1)
    rs.third(2)
    count_some(1, 1)
    count_some(2, 1)
    late.first(0, 0, 0)
    late.first(1, 0, 0)
    zc.move(0, 2, 1, take=False)
    zc.move(2, 3, 1)
    zc.move(3, 2, -1, take=False)
    count_some(3, 1)
    late.second(0)
    late.second(1)
    rs.first(1, 0, 1)
    count_some(4, 1)
    rs.first(1, 1, 0)
    count_some(5, 1)
    zc.move(1, 2, 1)
    rs.second(1)
    count_some(6, 1)
    late.third(0)
    zc.move(3, 0, -1, take=False)
    late.third(1)
    zc.move(0, 1, 1, take=False, also=late_one)
    zc.move(3, 1, -1, take=False, also=late_one)
    zc.move(2, 0, -1)
    zc.move(2, 1, -1, also=late_one)
    zc.move(1, 0, -1)
    count_some(7, 1)
    rs.first(1, 0, 0)
    rs.third(1)
    zc.move(2, 1, -1, also=early_one)
    zc.move(3, 1, -1, take=False, also=early_one)
    zc.move(0, 1, 1, take=False, also=early_one)
    table = table_row(counts[...], (8, D))

    total[...] = acc[k].astype(f32)

    def add(way, zo):
        buf = zc.ways[way][0]
        for p in range(4):
            zc.copy(zo, way, p).wait_recv()
        total[...] = total[...] + buf[zo].astype(f32)

    @pl.when(z == 0)
    def _():
        add(-1, 0)

    @pl.when(z == 1)
    def _():
        add(1, 1)
        add(-1, 1)

    @pl.when(z == 2)
    def _():
        add(1, 2)
        add(-1, 2)

    @pl.when(z == 3)
    def _():
        add(1, 3)

    early = early_vectors(k)
    nw0 = jnp.where(early, 36, 37)
    vecs = early == (c == 0)
    mine = jnp.where(vecs, 36, 37)
    to_next = rcopy(total.at[pl.ds(mine - EDGE, EDGE)], ebuf.at[0], es.at[0], er.at[0], nxt)
    to_prev = rcopy(total.at[pl.ds(0, EDGE)], ebuf.at[1], es.at[1], er.at[1], prev)

    @pl.when(d < 31)
    def _():
        to_next.start()

    @pl.when(d > 0)
    def _():
        to_prev.start()

    def square(i, run):
        t = total[i]
        t = t * t
        for j in range(6):
            run = run + t[:, 128 * j:128 * j + 128]
        return run

    squares = lax.fori_loop(0, 37, square, jnp.zeros((8, 128), f32))
    lines = [jnp.sum(squares, axis=0, keepdims=True)] + [table[0:1, 128 * i : 128 * i + 128] for i in range(3)]
    place_in = c * 4 + y * 2 + x
    sq[0] = jnp.concatenate(lines + [jnp.zeros((4, 128), f32)])
    sqr[place_in] = sq[0]
    rounds = [rcopy(sq.at[0], sqr.at[place_in], qs.at[i], qr.at[place_in], dev) for i, dev in enumerate(plane_devs)]
    hops = [rcopy(sq.at[1], sqr.at[8 + z], qs.at[7 + i], qr.at[8 + z], dev) for i, dev in enumerate(column_devs)]
    for h in rounds:
        h.start()

    def arrived(slot):
        return rcopy(sqr.at[slot], sqr.at[slot], qs.at[0], qr.at[slot], cdev)

    rs.finish()
    late.finish()
    for zs in (0, 1, 2):
        zc.sent(zs, 3, 1)
    for zs in (0, 1):
        zc.sent(zs, 2, 1)
    zc.sent(3, 2, -1)
    zc.sent(0, 1, 1)
    zc.sent(3, 1, -1)
    zc.sent(2, 1, -1)
    for zs in (1, 2, 3):
        zc.sent(zs, 0, -1)
    for pair in range(H // 2):
        swap(pair).wait_send()
    q, sh = shard_start(d)
    base = q - FRONT

    def flatten(ref, i, at, wide):
        @pl.when(wide)
        def _():
            t = ref[i]
            for j in range(6):
                win[pl.ds(at + j, 8, stride=24), :] = t[:, 128 * j:128 * j + 128]

        @pl.when(jnp.logical_not(wide))
        def _():
            t = ref[i]
            for j in range(6):
                win[pl.ds(at + j, 8, stride=6), :] = t[:, 128 * j:128 * j + 128]

    own_vectors = vecs & (vector_row(k, -1) >= 0)

    @pl.when(own_vectors)
    def _():
        flatten(total, 36, vector_row(k, q) - base, k < 0)

    w0 = jnp.where(c == 0, 73 * k, 73 * k + nw0)

    @pl.loop(0, mine)
    def _(t):
        at, wide = tile_start(w0 + t)
        flatten(total, t, at - base, wide)

    for i in range(8):
        @pl.when(place_in != i)
        def _():
            arrived(i).wait_recv()
    layer = sqr[0]
    for i in range(1, 8):
        layer = layer + sqr[i]
    sq[1] = layer
    sqr[8 + z] = layer
    for h in hops:
        h.start()
    @pl.when(d > 0)
    def _():
        to_next.wait_recv()

        @pl.loop(0, EDGE)
        def _(t):
            at, wide = tile_start(w0 - EDGE + t)
            flatten(ebuf.at[0], t, at - base, wide)

    @pl.when(d < 31)
    def _():
        to_prev.wait_recv()

        @pl.loop(0, EDGE)
        def _(t):
            at, wide = tile_start(w0 + mine + t)
            flatten(ebuf.at[1], t, at - base, wide)

    for i in range(4):
        @pl.when(z != i)
        def _():
            arrived(8 + i).wait_recv()
    summed = (sqr[8] + sqr[9]) + (sqr[10] + sqr[11])

    @pl.when(d == 0)
    def _():
        for i in range(3):
            win[pl.ds(FRONT + 774 + i, 1), :] = summed[1 + i : 2 + i]

    sub = lax.broadcasted_iota(jnp.int32, (8, 128), 0)
    entries = jnp.where(sub == 0, summed, jnp.where(sub < 4, summed * summed, 0.0))
    square_sum = jnp.sum(jnp.sum(entries, axis=1, keepdims=True), axis=0, keepdims=True)
    factor = jnp.minimum(1.0, lax.rsqrt(square_sum / RAW + 1e-06))
    for s in shards:
        s.wait()
    lanes = lax.broadcasted_iota(jnp.int32, (80, 128), 1)
    rowi = lax.broadcasted_iota(jnp.int32, (80, 128), 0)
    back = (128 - sh) % 128

    @pl.loop(0, ROWS // 80)
    def _(i):
        r = pl.multiple_of(i * 80, 8)
        here = pltpu.roll(win[pl.ds(FRONT + r, 80), :], back, 1)
        there = pltpu.roll(win[pl.ds(FRONT + 1 + r, 80), :], back, 1)
        grad = jnp.where(lanes < 128 - sh, here, there) * factor
        entry = (d == 0) & (rowi + r < ENTRY_ROWS)
        rate = jnp.where(entry, learn_rate * layer_decay, learn_rate)
        one = beta_one * onev[pl.ds(r, 80), :] + (1.0 - beta_one) * grad
        two = beta_two * twov[pl.ds(r, 80), :] + (1.0 - beta_two) * grad * grad
        fixed_one = one / (1.0 - beta_one ** STEP)
        fixed_two = two / (1.0 - beta_two ** STEP)
        step = -rate * (fixed_one / (jnp.sqrt(fixed_two) + adam_eps) + weight_decay * mv[pl.ds(r, 80), :])
        mv[pl.ds(r, 80), :] = step
        onev[pl.ds(r, 80), :] = one
        twov[pl.ds(r, 80), :] = two

    results = [pltpu.make_async_copy(v, r, lsem.at[i]) for i, (v, r) in enumerate(((mv, step_ref), (onev, new1_ref), (twov, new2_ref)))]
    for copy in results:
        copy.start()

    for h in rounds + hops:
        h.wait_send()

    @pl.when(d < 31)
    def _():
        to_next.wait_send()

    @pl.when(d > 0)
    def _():
        to_prev.wait_send()

    shown.wait()
    for copy in results:
        copy.wait()


def backward_and_step(tiles, query, key_all, value_all, grad_context, soft, code, gfi, low, feats, grads, master, first_moment, second_moment):
    def rows_of(v):
        return jnp.pad(v, (0, ROWS * 128 - SHARD)).reshape(ROWS, 128)

    rows, keys = query.shape[0], key_all.shape[0]
    f32, bf = jnp.float32, jnp.bfloat16
    any_ = pl.BlockSpec(memory_space=pl.ANY)
    S, V, sem = jax.ShapeDtypeStruct, pltpu.VMEM, pltpu.SemaphoreType.DMA
    w = V((96, 8, D), bf)
    tile = (8, D)
    line = V((ROWS, 128), f32)
    outs = pl.pallas_call(
        backward_kernel,
        out_shape=[S((rows, D), f32), S(grads.shape, bf)] + [S((ROWS, 128), f32)] * 3 + [S((keys // 8, H, 8, rows), bf)],
        in_specs=[any_] * 14,
        out_specs=[any_] * 6,
        scratch_shapes=[
            V((2, keys, rows), bf), V((2, rows, 128), bf), V((2, keys, 128), bf), V((2, keys, 128), bf), V((2, rows, 128), bf), sem((5, 2)),
            V((keys, rows), jnp.int32), sem((1,)), V((2, keys // 8, 8, rows), bf), sem((2,)), V((2, 16, H, 8, rows), bf), sem((2,)),
            V((8 * H, 8 * BUCKETS), f32),
            V((2, keys, 128), f32), V((2, keys, 128), f32), V((6, 2, rows, 128), bf), V((6, 2, rows, 128), bf), sem((6,)), sem((6,)),
            V((3, rows, D), bf), V((2, 8, D), f32),
            w, w, w, V((rows, D), bf), V((rows, D), f32), V((rows, LF), bf), V((16, 8, D), bf), w, w, w, V((4, 8, D), bf),
            sem((12,)), sem((24,)), sem((7,)),
            V((37,) + tile, f32), V((2, EDGE) + tile, f32), V((2, 8, 128), f32), V((12, 8, 128), f32),
            V((WIN2, 128), f32), line, line, line, sem((3,)), sem((2,)), sem((2,)), sem((10,)), sem((12,)),
        ] + reducer_scratch() + chain_scratch(),
        input_output_aliases={10: 1},
        compiler_params=pltpu.CompilerParams(collective_id=5, has_side_effects=True, vmem_limit_bytes=63 << 20),
        name="backward_and_step",
    )(tiles, query, key_all, value_all, grad_context, soft, code, gfi, low, feats, grads, rows_of(master), rows_of(first_moment), rows_of(second_moment))
    return outs[0], [o.reshape(-1)[:SHARD] for o in outs[2:5]]


def from_tiles(tiles):
    got = {}
    for name, first, count in WEIGHTS:
        block = jnp.concatenate([tiles[s : s + n] for s, _, n in slots_of(first, count)])
        if name == 12:
            block = block.reshape(96, 4, 8, D).transpose(0, 2, 1, 3)
        got[name] = block.reshape(-1, FF if name == 12 else D)
    for name, chip, row in VECTORS:
        block = tiles[vector_at(chip)]
        if name == 13:
            got[name] = block[row : row + 4].reshape(FF)
        elif name == 2:
            got[name] = block[row, : BUCKETS * H].reshape(BUCKETS, H)
        else:
            got[name] = block[row]
    return [got[i] for i in range(18)]


def to_tiles(whole):
    by_name = [p.astype(jnp.bfloat16) for p in whole]
    weights = []
    for name, first, count in WEIGHTS:
        got = by_name[name]
        if name == 12:
            got = got.reshape(96, 8, 4, D).transpose(0, 2, 1, 3)
        weights.append(got.reshape(count, 8, D))
    cuts = []
    for chip in range(16):
        held = [(r, by_name[n]) for n, c, r in VECTORS if c == chip]
        rows = [jnp.pad(v.reshape(-1), (0, -v.size % D)).reshape(-1, D) for _, v in held]
        block = jnp.concatenate(rows + [jnp.zeros((8 - sum(r.shape[0] for r in rows), D), jnp.bfloat16)])
        cuts.append((73 * chip + vector_slot(chip), block[None]))
    parts = []
    for (name, first, count), tiles in zip(WEIGHTS, weights):
        at = first
        for w, block in [c for c in cuts if first <= c[0] < first + count]:
            if w > at:
                parts.append(tiles[at - first : w - first])
            parts.append(block)
            at = w
        parts.append(tiles[at - first :])
    parts.extend(block for w, block in cuts if w == 1168)
    return jnp.concatenate(parts)


def per_device(
    custom, tokens, cotangent, page_boxes, page_lengths, padding, buckets, master, first_moment, second_moment
):
    rows = tokens.shape[1]
    if custom:
        tiles, hidden, low, query, keys, values, ctx, soft, code, feats = gather_and_attend(
            master, tokens[0], page_boxes, padding, buckets[0], page_lengths
        )
        tiles = tiles.reshape(16 * CHIP, 8, D)
    else:
        feats = layout_features(page_boxes.reshape(4, rows)).astype(jnp.bfloat16)
        tiles = to_tiles(unpack(lax.all_gather(master.astype(jnp.bfloat16), ("dp", "seq"), axis=0, tiled=True)))
        hidden, low, query, keys, values, pads = enter(tiles, tokens[0], feats, jnp.broadcast_to(padding, (8, rows)))
        ctx, soft, code = attend(query, keys, values, buckets[0], page_lengths, pads, tiles[vector_at(0)])
    activations, grad_first_in, grad_context, grads = middle(tiles, ctx, hidden, cotangent[0])
    if custom:
        input_grad, stepped = backward_and_step(
            tiles, query, keys, values, grad_context, soft, code, grad_first_in, low, feats, grads, master, first_moment, second_moment
        )
    else:
        dq, dk, dv, table = soft_back(query, keys, values, grad_context, soft, code)
        input_grad, grads = leave(tiles, dq, dk, dv, grad_first_in, low, feats, table, grads)
        flat = jnp.concatenate([p.astype(jnp.float32).reshape(-1) for p in from_tiles(grads)])
        grad = lax.psum_scatter(flat, ("dp", "seq"), scatter_dimension=0, tiled=True)
        square = lax.psum(jnp.sum(grad * grad), ("dp", "seq"))
        factor = jnp.minimum(1.0, lax.rsqrt(square / RAW + 1e-06))
        size = master.shape[0]
        index = lax.axis_index(("dp", "seq")) * size + jnp.arange(size, dtype=jnp.int32)
        stepped = adam_update(master, first_moment, second_moment, grad * factor, index)
    return (activations[None], input_grad[None]) + tuple(stepped)


def solution(mesh):
    in_specs = (
        P("dp", "seq", None),
        P("dp", "seq", None),
        P(None, "dp", "seq"),
        P("dp", None),
        P("dp", "seq"),
        P("dp", "seq", None),
        P(("dp", "seq")),
        P(("dp", "seq")),
        P(("dp", "seq")),
    )
    out_specs = (
        P("dp", "seq", None),
        P("dp", "seq", None),
        P(("dp", "seq")),
        P(("dp", "seq")),
        P(("dp", "seq")),
    )
    custom = dict(mesh.shape) == {"dp": 16, "seq": 2}
    return jax.shard_map(
        functools.partial(per_device, custom), mesh=mesh, in_specs=in_specs, out_specs=out_specs, check_vma=False
    )
```

```python
import functools
import math

import jax
import jax.numpy as jnp
from jax import lax
from jax.experimental import pallas as pl
from jax.experimental.pallas import tpu as pltpu
from jax.sharding import PartitionSpec as P

D = 768
H = 12
HD = 64
FF = 3072
BUCKETS = 32
FREQ = 16
LF = 128
LAYERS = 1
BLOCK = 1024
STEP = 10
ENTRY = 99456
LAYER_PARAMS = 7087104
RAW = 7186560


beta_one = 0.8
beta_two = 0.98
adam_eps = 1e-06
learn_rate = 0.0006
layer_decay = 0.8
weight_decay = 0.1
norm_eps = 1e-05
masked_score = -1000000000.0


SHAPES = (
    (LF, D), (D,), (BUCKETS, H),
    (D, D), (D,), (D, D), (D, D), (D,), (D, D), (D,), (D,), (D,),
    (D, FF), (FF,), (FF, D), (D,), (D,), (D,),
)


def unpack(flat_params):
    pieces, offset = [], 0
    for shape in SHAPES:
        amount = shape[0] * (shape[1] if len(shape) > 1 else 1)
        pieces.append(flat_params[offset : offset + amount].reshape(shape))
        offset = offset + amount
    return pieces


def adam_update(master, first_moment, second_moment, gradient, global_index):
    exponent = jnp.where(
        global_index < ENTRY,
        LAYERS,
        jnp.maximum(LAYERS - 1 - (global_index - ENTRY) // LAYER_PARAMS, 0),
    )
    rate = jnp.where(
        global_index < RAW, learn_rate * jnp.power(layer_decay, exponent.astype(jnp.float32)), 0.0
    )
    moment_one = beta_one * first_moment + (1.0 - beta_one) * gradient
    moment_two = beta_two * second_moment + (1.0 - beta_two) * gradient * gradient
    fixed_one = moment_one / (1.0 - beta_one**STEP)
    fixed_two = moment_two / (1.0 - beta_two**STEP)
    param_step = -rate * (fixed_one / (jnp.sqrt(fixed_two) + adam_eps) + weight_decay * master)
    return (param_step, moment_one, moment_two)


def layout_features(page_boxes):
    rates_sin = jnp.power(10000.0, -jnp.arange(FREQ, dtype=jnp.float32) / FREQ)
    angles = page_boxes.astype(jnp.float32)[:, :, None] * rates_sin
    stacked = jnp.stack([jnp.sin(angles), jnp.cos(angles)], axis=1)
    return jnp.transpose(stacked, (2, 0, 1, 3)).reshape(page_boxes.shape[1], LF)


MESH = pl.DeviceIdType.MESH
SHARD = 224580
ROWS = 1760
TAIL, HEAD = 160, 176
WIN = 2176
SLOTS = 37
CHIP = 74
PARTS = ((0, 19), (19, 18))


def place():
    k = lax.axis_index("dp")
    return k, lax.axis_index("seq"), k // 4, (k // 2) % 2, k % 2


def shard_start(d):
    return d * 1754 + (d * 68) // 128, (d * 68) % 128


def early_vectors(k):
    return (k == 0) | (k == 4) | (k == 5)


def vector_row(k, other):
    at = other
    for chip, row in ((0, 768), (1, 5385), (4, 14607), (5, 19221), (10, 37671), (15, 56127)):
        at = jnp.where(k == chip, row, at)
    return at


def tile_start(w):
    at = w * 48
    for first, shift in ((16, 777 - 16 * 48), (112, 5391 - 112 * 48), (208, 9999 - 208 * 48), (304, 14613 - 304 * 48), (784, 37695 - 784 * 48)):
        at = jnp.where(w >= first, w * 48 + shift, at)
    wide = (w >= 400) & (w < 784)
    v = w - 400
    at = jnp.where(wide, 19239 + (v // 4) * 192 + (v % 4) * 6, at)
    return at, wide


def neighbours(k, c, z, y, x):
    t = k >= 0
    return [
        (t, (k, 1 - c)),
        (t, (z * 4 + y * 2 + 1 - x, c)),
        (t, (z * 4 + (1 - y) * 2 + x, c)),
        (z < 3, (jnp.minimum(k + 4, 15), c)),
        (z > 0, (jnp.maximum(k - 4, 0), c)),
        ((c == 1) & (k < 15), (jnp.minimum(k + 1, 15), 0)),
        ((c == 0) & (k > 0), (jnp.maximum(k - 1, 0), 1)),
    ]


def greet(k, c, z, y, x):
    bar = pltpu.get_barrier_semaphore()
    for cond, dev in neighbours(k, c, z, y, x):
        @pl.when(cond)
        def _():
            pl.semaphore_signal(bar, inc=1, device_id=dev, device_id_type=MESH)
    peers = 3
    for cond, _ in neighbours(k, c, z, y, x)[3:]:
        peers = peers + jnp.where(cond, 1, 0)
    pl.semaphore_wait(bar, peers)


def rcopy(src, dst, ssem, rsem, dev):
    return pltpu.make_async_remote_copy(src_ref=src, dst_ref=dst, send_sem=ssem, recv_sem=rsem, device_id=dev, device_id_type=MESH)


FRONT = 344
WIN2 = 2464
EDGE = 4
ENTRY_ROWS = 777


WEIGHTS = (
    (0, 0, 16),
    (3, 16, 96),
    (5, 112, 96),
    (6, 208, 96),
    (8, 304, 96),
    (12, 400, 384),
    (14, 784, 384),
)
VECTORS = (
    (1, 0, 0),
    (2, 0, 1),
    (4, 1, 0),
    (7, 4, 0),
    (9, 5, 0),
    (10, 5, 1),
    (11, 5, 2),
    (13, 10, 0),
    (15, 15, 0),
    (16, 15, 1),
    (17, 15, 2),
)


def slots_of(first, count):
    runs = []
    for w in range(first, first + count):
        chip, at = divmod(w, 73)
        slot = chip * CHIP + at + (1 if at >= vector_slot(chip) else 0)
        if runs and runs[-1][0] + runs[-1][2] == slot:
            runs[-1][2] += 1
        else:
            runs.append([slot, w - first, 1])
    return runs


def vector_slot(chip):
    return 36 if chip in (0, 4, 5) else 73


def vector_at(chip):
    return chip * CHIP + vector_slot(chip)


def pieces(tiles, held, first, count, sems, base, out=False):
    made = []
    for i, (slot, at, n) in enumerate(slots_of(first, count)):
        a, b = tiles.at[pl.ds(slot, n)], held.at[pl.ds(at, n)]
        a, b = (b, a) if out else (a, b)
        made.append(pltpu.make_async_copy(a, b, sems.at[base + i]))
    return made


def matrix(tile_rows):
    return tile_rows.reshape(-1, D)


def col_sum(v):
    return jnp.sum(v.reshape(-1, 8, v.shape[-1]), axis=0)


def norm_stats(v):
    mean = jnp.mean(v, axis=-1, keepdims=True)
    center = v - mean
    spread = jnp.mean(center * center, axis=-1, keepdims=True)
    inv = lax.rsqrt(spread + norm_eps)
    return center * inv, inv


def norm_back(grad, gain, hat, inv):
    g = grad * gain
    return inv * (g - jnp.mean(g, axis=-1, keepdims=True) - hat * jnp.mean(g * hat, axis=-1, keepdims=True))


ROOT_HALF = 0.7071067811865476
ROOT_TAU = 0.3989422804014327


def middle_kernel(tiles, ctx_in, hidden_in, cot_in, act_hbm, gfi_hbm, gctx_hbm, grads,
                  ctx, hidden, cot, act_out, gfi_out, gctx_out, iosem, wo, wup, wdn, vecs, vf, act, slope, low1, hat1, inv1, hat2, inv2, a, sums, dwo, dwup, dwdn, vgrads, lsem, ssem):
    f32, bf = jnp.float32, jnp.bfloat16
    rows = ctx.shape[0]
    R = 128
    steps = rows // R
    loads_o = pieces(tiles, wo, 304, 96, lsem, 0)
    loads_u = pieces(tiles, wup, 400, 384, lsem, 4)
    loads_d = pieces(tiles, wdn, 784, 384, lsem, 12)
    loads_v = [pltpu.make_async_copy(tiles.at[vector_at(c)], vecs.at[i], lsem.at[20 + i]) for i, c in enumerate((5, 10, 15))]
    ins = [pltpu.make_async_copy(r, v, iosem.at[i]) for i, (r, v) in enumerate(((ctx_in, ctx), (hidden_in, hidden), (cot_in, cot)))]
    outs = [pltpu.make_async_copy(v, r, iosem.at[3 + i]) for i, (v, r) in enumerate(((act_out, act_hbm), (gfi_out, gfi_hbm), (gctx_out, gctx_hbm)))]
    for c in ins[:1] + loads_v + loads_o + ins[1:2] + loads_u + loads_d + ins[2:]:
        c.start()
    up4 = wup.reshape(96, 4, 8, D)
    dup4 = dwup.reshape(96, 4, 8, D)

    def vec(i, r):
        return vf[i, pl.ds(r, 1), :]

    def each(f):
        @pl.loop(0, steps)
        def _(i):
            f(pl.ds(pl.multiple_of(i * R, R), R))

    for c in ins[:2] + loads_v + loads_o:
        c.wait()
    vf[...] = vecs[...].astype(f32)
    a[...] = jnp.dot(ctx[...], matrix(wo[...]), preferred_element_type=f32)

    def first(sl):
        hat, inv = norm_stats(hidden[sl, :] + a[sl, :] + vec(0, 0))
        hat1[sl, :] = hat
        inv1[sl, :] = inv
        out = hat * vec(0, 1) + vec(0, 2)
        a[sl, :] = out
        low1[sl, :] = out.astype(bf)

    each(first)
    for c in loads_u:
        c.wait()

    def up(j, _):
        for half in range(2):
            sl = pl.ds(half * (rows // 2), rows // 2)
            u = jnp.dot(low1[sl, :], matrix(up4[:, j]), preferred_element_type=f32) + vec(1, j)
            share = 0.5 * (1.0 + lax.erf(u * ROOT_HALF))
            act[j, sl, :] = (u * share).astype(bf)
            slope[j, sl, :] = share + u * jnp.exp(-0.5 * u * u) * ROOT_TAU
        return 0

    lax.fori_loop(0, 4, up, 0)
    for c in loads_d:
        c.wait()

    def down(j, _):
        a[...] += jnp.dot(act[j], matrix(wdn[pl.ds(96 * j, 96)]), preferred_element_type=f32)
        return 0

    lax.fori_loop(0, 4, down, 0)
    sums[...] = jnp.zeros_like(sums)

    def second(sl):
        hat, inv = norm_stats(a[sl, :] + vec(2, 0))
        act_out[sl, :] = (hat * vec(2, 1) + vec(2, 2)).astype(bf)
        g = cot[sl, :].astype(f32)
        sums[6] += col_sum(g * hat)
        sums[7] += col_sum(g)
        back = norm_back(g, vec(2, 1), hat, inv)
        sums[5] += col_sum(back)
        a[sl, :] = back
        hat2[sl, :] = back.astype(bf)

    ins[2].wait()
    each(second)
    outs[0].start()
    down_back = hat2

    def back(j, _):
        for half in range(2):
            sl = pl.ds(half * (rows // 2), rows // 2)
            g = lax.dot_general(down_back[sl, :], matrix(wdn[pl.ds(96 * j, 96)]), NT, preferred_element_type=f32) * slope[j, sl, :]
            sums[8 + j] += col_sum(g)
            act_back[sl, :] = g.astype(bf)
        dwdn[pl.ds(96 * j, 96)] = lax.dot_general(act[j], down_back[...], TN, preferred_element_type=f32).astype(bf).reshape(96, 8, D)
        dup4[:, j] = lax.dot_general(low1[...], act_back[...], TN, preferred_element_type=f32).astype(bf).reshape(96, 8, D)
        a[...] += lax.dot_general(act_back[...], matrix(up4[:, j]), NT, preferred_element_type=f32)
        return 0

    act_back = inv2
    lax.fori_loop(0, 4, back, 0)
    stores = pieces(grads, dwup, 400, 384, ssem, 4, True) + pieces(grads, dwdn, 784, 384, ssem, 12, True)
    for c in stores:
        c.start()

    def third(sl):
        g = a[sl, :]
        sums[3] += col_sum(g * hat1[sl, :])
        sums[4] += col_sum(g)
        back = norm_back(g, vec(0, 1), hat1[sl, :], inv1[sl, :])
        sums[2] += col_sum(back)
        gfi_out[sl, :] = back
        hat2[sl, :] = back.astype(bf)

    each(third)
    outs[1].start()
    gctx_out[...] = lax.dot_general(hat2[...], matrix(wo[...]), NT, preferred_element_type=f32).astype(bf)
    outs[2].start()
    dwo[...] = lax.dot_general(ctx[...], hat2[...], TN, preferred_element_type=f32).astype(bf).reshape(96, 8, D)
    for i, held in enumerate(((2, 3, 4), (8, 9, 10, 11), (5, 6, 7))):
        lines = [jnp.sum(sums[s], axis=0, keepdims=True) for s in held]
        lines.append(jnp.zeros((8 - len(held), D), f32))
        vgrads[i] = jnp.concatenate(lines).astype(bf)
    last = pieces(grads, dwo, 304, 96, ssem, 0, True)
    quiet = [ch for ch in range(6, 15) if ch != 10]
    vgrads[3] = jnp.zeros((8, D), bf)
    last += [pltpu.make_async_copy(vgrads.at[min(i, 3)], grads.at[vector_at(ch)], ssem.at[20 + i]) for i, ch in enumerate([5, 10, 15] + quiet)]
    for c in last:
        c.start()
    for c in stores + last + outs:
        c.wait()


def middle(tiles, ctx, hidden, cot):
    rows = ctx.shape[0]
    f32, bf = jnp.float32, jnp.bfloat16
    vm, any_ = pl.BlockSpec(memory_space=pltpu.VMEM), pl.BlockSpec(memory_space=pl.ANY)
    S = jax.ShapeDtypeStruct
    return pl.pallas_call(
        middle_kernel,
        out_shape=[S((rows, D), bf), S((rows, D), f32), S((rows, D), bf), S((16 * CHIP, 8, D), bf)],
        in_specs=[any_] * 4,
        out_specs=[any_] * 4,
        scratch_shapes=[
            pltpu.VMEM((rows, D), bf), pltpu.VMEM((rows, D), f32), pltpu.VMEM((rows, D), bf),
            pltpu.VMEM((rows, D), bf), pltpu.VMEM((rows, D), f32), pltpu.VMEM((rows, D), bf), pltpu.SemaphoreType.DMA((6,)),
            pltpu.VMEM((96, 8, D), bf), pltpu.VMEM((384, 8, D), bf), pltpu.VMEM((384, 8, D), bf), pltpu.VMEM((3, 8, D), bf), pltpu.VMEM((3, 8, D), f32),
            pltpu.VMEM((4, rows, D), bf), pltpu.VMEM((4, rows, D), f32), pltpu.VMEM((rows, D), bf),
            pltpu.VMEM((rows, D), f32), pltpu.VMEM((rows, 1), f32), pltpu.VMEM((rows, D), bf), pltpu.VMEM((rows, D), bf),
            pltpu.VMEM((rows, D), f32), pltpu.VMEM((12, 8, D), f32),
            pltpu.VMEM((96, 8, D), bf), pltpu.VMEM((384, 8, D), bf), pltpu.VMEM((384, 8, D), bf), pltpu.VMEM((4, 8, D), bf),
            pltpu.SemaphoreType.DMA((24,)), pltpu.SemaphoreType.DMA((32,)),
        ],
        compiler_params=pltpu.CompilerParams(vmem_limit_bytes=58 << 20),
        name="middle",
    )(tiles, ctx, hidden, cot)


NT = (((1,), (1,)), ((), ()))
TN = (((0,), (0,)), ((), ()))


def half(ref_value, hh):
    lanes = lax.broadcasted_iota(jnp.int32, ref_value.shape, 1)
    keep = lanes // 64 == hh
    return jnp.where(keep, ref_value, jnp.zeros_like(ref_value))


def page_of(at, lengths):
    end, page = 0, jnp.zeros(at.shape, jnp.int32)
    for i in range(4):
        end = end + lengths[0, i]
        page = page + jnp.where(at >= end, 1, 0)
    return page


def fill_codes(code_ref, buckets, pads, lengths):
    keys, rows = code_ref.shape
    own = lax.axis_index("seq") * rows
    tag = page_of(lax.broadcasted_iota(jnp.int32, (1, keys), 1), lengths) + 1
    tag = jnp.where(jnp.concatenate([pads[0, 0:1], pads[1, 0:1]], axis=1) > 0, tag, 0)
    for i in range(rows // 128):
        at = own + 128 * i + lax.broadcasted_iota(jnp.int32, (128, 1), 0)
        page = page_of(at, lengths) + 1
        for j in range(keys // 128):
            key_at = 128 * j + lax.broadcasted_iota(jnp.int32, (1, 128), 1)
            allowed = (page == tag[:, 128 * j : 128 * j + 128]) | (key_at == at)
            code = jnp.where(allowed, buckets[128 * i : 128 * i + 128, 128 * j : 128 * j + 128], BUCKETS)
            code_ref[128 * j : 128 * j + 128, 128 * i : 128 * i + 128] = code.T


def fill_table(tab_ref, lines):
    f32 = jnp.float32
    head = lax.broadcasted_iota(jnp.int32, (16, 128), 0)
    bucket = lax.broadcasted_iota(jnp.int32, (16, 128), 1)
    place_of = bucket * H + head
    tab = jnp.full((16, 128), masked_score, f32)
    for i in range(BUCKETS * H // 128):
        row = jnp.broadcast_to(lines[1:2, 128 * i : 128 * i + 128].astype(f32), (16, 128))
        inside = jnp.clip(place_of - 128 * i, 0, 127)
        got = jnp.take_along_axis(row, inside, axis=1, mode="promise_in_bounds")
        tab = jnp.where((place_of // 128 == i) & (bucket < BUCKETS) & (head < H), got, tab)
    tab_ref[...] = tab


def soft_head(head, q, k, code_ref, tab_ref, s_scr, p_ref):
    keys, rows = s_scr.shape
    f32, bf = jnp.float32, jnp.bfloat16
    qm = half(q, head % 2)
    line = jnp.broadcast_to(tab_ref[pl.ds(head, 1), :], (keys, 128))
    s = lax.dot_general(k, qm, NT, preferred_element_type=f32)
    cols = []
    for j in range(rows // 128):
        code = code_ref[:, 128 * j : 128 * j + 128]
        bias = jnp.take_along_axis(line, code, axis=1, mode="promise_in_bounds")
        cols.append(jnp.where(bias < 0.5 * masked_score, masked_score, s[:, 128 * j : 128 * j + 128] + bias))
    s = jnp.concatenate(cols, axis=1)
    s_scr[...] = s
    top = jnp.max(jnp.max(s.reshape(keys // 8, 8, rows), axis=0), axis=0, keepdims=True)
    e = jnp.exp(s_scr[...] - top)
    s_scr[...] = e
    inverse = 1.0 / jnp.sum(jnp.sum(e.reshape(keys // 8, 8, rows), axis=0), axis=0, keepdims=True)
    p_ref[...] = (s_scr[...] * inverse).astype(bf)


def context_pair(v, p_ref):
    vt = v.T
    out = [jnp.dot(vt, p_ref[hh], preferred_element_type=jnp.float32) for hh in range(2)]
    sub = lax.broadcasted_iota(jnp.int32, out[0].shape, 0)
    return jnp.where(sub < 64, out[0], out[1]).T.astype(jnp.bfloat16)


def attend_kernel(lengths, q_ref, k_ref, v_ref, buckets, pads, lines, ctx_ref, p_ref, code_ref, s_scr, tab_ref):
    pair = pl.program_id(0)

    @pl.when(pair == 0)
    def _():
        fill_codes(code_ref, buckets, pads, lengths)
        fill_table(tab_ref, lines)

    for hh in range(2):
        soft_head(2 * pair + hh, q_ref[...], k_ref[...], code_ref, tab_ref, s_scr, p_ref.at[hh])
    ctx_ref[...] = context_pair(v_ref[...], p_ref)


def attend(query, key_all, value_all, buckets, page_lengths, pads, lines):
    rows, keys = query.shape[0], key_all.shape[0]
    bf = jnp.bfloat16
    const = lambda p: (0, 0)
    return pl.pallas_call(
        attend_kernel,
        grid=(H // 2,),
        out_shape=[
            jax.ShapeDtypeStruct((rows, D), bf),
            jax.ShapeDtypeStruct((H, keys, rows), bf),
            jax.ShapeDtypeStruct((keys, rows), jnp.int32),
        ],
        in_specs=[
            pl.BlockSpec(memory_space=pltpu.SMEM),
            pl.BlockSpec((rows, 128), lambda p: (0, p)),
            pl.BlockSpec((keys, 128), lambda p: (0, p)),
            pl.BlockSpec((keys, 128), lambda p: (0, p)),
            pl.BlockSpec((rows, keys), const),
            pl.BlockSpec((2, 8, rows), lambda p: (0, 0, 0)),
            pl.BlockSpec((8, D), const),
        ],
        out_specs=[pl.BlockSpec((rows, 128), lambda p: (0, p)), pl.BlockSpec((2, keys, rows), lambda p: (p, 0, 0)), pl.BlockSpec((keys, rows), const)],
        scratch_shapes=[pltpu.VMEM((keys, rows), jnp.float32), pltpu.VMEM((16, 128), jnp.float32)],
        compiler_params=pltpu.CompilerParams(vmem_limit_bytes=56 << 20),
        name="attend",
    )(page_lengths, query, key_all, value_all, buckets, pads, lines)


def table_row(acc, shape):
    f32 = jnp.float32
    a = lax.broadcasted_iota(jnp.int32, acc.shape, 0) % 8
    b = lax.broadcasted_iota(jnp.int32, acc.shape, 1) // BUCKETS
    acc = jnp.where(a == b, acc, 0.0)
    heads = jnp.sum(acc.reshape(H, 8, 8 * BUCKETS), axis=1)
    lane = lax.broadcasted_iota(jnp.int32, (8 * BUCKETS, D), 1) // H
    wide = jnp.where(lane == lax.broadcasted_iota(jnp.int32, lane.shape, 0) % BUCKETS, 1.0, 0.0)
    out = jnp.dot(heads, wide, precision=lax.Precision.HIGHEST, preferred_element_type=f32)
    mine = lax.broadcasted_iota(jnp.int32, out.shape, 1) % H == lax.broadcasted_iota(jnp.int32, out.shape, 0)
    out = jnp.sum(jnp.where(mine, out, 0.0), axis=0, keepdims=True)
    return jnp.broadcast_to(out, shape)


def attend_back_kernel(q_ref, k_ref, v_ref, do_ref, p_ref, code_ref, dq_ref, dk_ref, dv_ref, tab_ref, spread, held):
    pair = pl.program_id(0)
    keys, rows = code_ref.shape
    f32, bf = jnp.float32, jnp.bfloat16
    STEP_ROWS = keys
    kt = k_ref[...].T
    dq = []
    for hh in range(2):
        qm = half(q_ref[...], hh)
        dom = half(do_ref[...], hh)

        def inner(i, total):
            at = pl.multiple_of(i * STEP_ROWS, STEP_ROWS)
            g = lax.dot_general(v_ref[pl.ds(at, STEP_ROWS), :], dom, NT, preferred_element_type=f32)
            w = g * p_ref[hh, pl.ds(at, STEP_ROWS), :].astype(f32)
            return total + jnp.sum(w.reshape(STEP_ROWS // 8, 8, rows), axis=0)

        total = lax.fori_loop(0, keys // STEP_ROWS, inner, jnp.zeros((8, rows), f32))
        total = jnp.sum(total, axis=0, keepdims=True)

        def grads(i, acc):
            at = pl.multiple_of(i * STEP_ROWS, STEP_ROWS)
            sl = pl.ds(at, STEP_ROWS)
            g = lax.dot_general(v_ref[sl, :], dom, NT, preferred_element_type=f32)
            p = p_ref[hh, sl, :]
            ds = p.astype(f32) * (g - total)
            wide = ds.reshape(STEP_ROWS // 8, 8, rows)
            if hh == 0:
                held[...] = wide
            else:
                both = jnp.concatenate([held[...], wide], axis=1).astype(bf)
                spread[:, pl.ds(pl.multiple_of(pair * 16, 16), 16), :] = both
            ds = ds.astype(bf)
            dv = jnp.dot(p, dom, preferred_element_type=f32)
            dk = jnp.dot(ds, qm, preferred_element_type=f32)
            if hh == 0:
                dv_ref[sl, :] = dv
                dk_ref[sl, :] = dk
            else:
                dv_ref[sl, :] += dv
                dk_ref[sl, :] += dk
            return acc + lax.dot_general(k_ref[sl, :], ds, TN, preferred_element_type=f32)

        dq.append(lax.fori_loop(0, keys // STEP_ROWS, grads, jnp.zeros((128, rows), f32)))
    sub = lax.broadcasted_iota(jnp.int32, dq[0].shape, 0)
    dq_ref[...] = jnp.where(sub < 64, dq[0], dq[1]).T * 0.125

    @pl.when(pair == H // 2 - 1)
    def _():
        bucket = lax.broadcasted_iota(jnp.int32, (BUCKETS, rows), 0)

        def count(i, acc):
            code = code_ref[pl.ds(pl.multiple_of(i * 8, 8), 8), :]
            hot = jnp.concatenate(
                [jnp.where(jnp.broadcast_to(code[r : r + 1], bucket.shape) == bucket, 1.0, 0.0) for r in range(8)]
            ).astype(bf)
            return acc + lax.dot_general(spread[i], hot, NT, preferred_element_type=f32)

        acc = lax.fori_loop(0, keys // 8, count, jnp.zeros((8 * H, 8 * BUCKETS), f32), unroll=8)
        tab_ref[...] = table_row(acc, tab_ref.shape)


def soft_back(query, key_all, value_all, grad_context, soft, code):
    rows, keys = query.shape[0], key_all.shape[0]
    f32 = jnp.float32
    row = pl.BlockSpec((rows, 128), lambda p: (0, p))
    key = pl.BlockSpec((keys, 128), lambda p: (0, p))
    dq, dk, dv, tab = pl.pallas_call(
        attend_back_kernel,
        grid=(H // 2,),
        out_shape=[
            jax.ShapeDtypeStruct((rows, D), f32),
            jax.ShapeDtypeStruct((keys, D), f32),
            jax.ShapeDtypeStruct((keys, D), f32),
            jax.ShapeDtypeStruct((8, D), f32),
        ],
        in_specs=[row, key, key, row, pl.BlockSpec((2, keys, rows), lambda p: (p, 0, 0)), pl.BlockSpec((keys, rows), lambda p: (0, 0))],
        out_specs=[row, key, key, pl.BlockSpec((8, D), lambda p: (0, 0))],
        scratch_shapes=[pltpu.VMEM((keys // 8, 8 * H, rows), jnp.bfloat16), pltpu.VMEM((keys // 8, 8, rows), f32)],
        compiler_params=pltpu.CompilerParams(vmem_limit_bytes=58 << 20),
        name="attend_back",
    )(query, key_all, value_all, grad_context, soft, code)
    return dq, dk, dv, tab


def meet_partner():
    dp, c = lax.axis_index("dp"), lax.axis_index("seq")
    partner = (dp, 1 - c)
    bar = pltpu.get_barrier_semaphore()
    pl.semaphore_signal(bar, inc=1, device_id=partner, device_id_type=MESH)
    pl.semaphore_wait(bar, 1)
    return c, partner


def enter_kernel(tiles, tokens, feats, pad, hidden, low, query, keys, values, pads, wl, wq, wk, wv, vecs, vf, lsem, sends, recvs):
    f32, bf = jnp.float32, jnp.bfloat16
    rows = tokens.shape[0]
    loads = [pltpu.make_async_copy(tiles.at[vector_at(ch)], vecs.at[i], lsem.at[i]) for i, ch in enumerate((0, 1, 4))]
    loads += pieces(tiles, wl, 0, 16, lsem, 4) + pieces(tiles, wk, 112, 96, lsem, 8)
    loads += pieces(tiles, wv, 208, 96, lsem, 12) + pieces(tiles, wq, 16, 96, lsem, 16)
    for c in loads:
        c.start()
    c, partner = meet_partner()
    own = pl.ds(c * rows, rows)

    def share(ref, i):
        return rcopy(ref.at[own], ref.at[own], sends.at[i], recvs.at[i], partner)

    pads[pl.ds(c, 1)] = pad[...].reshape(1, 8, rows)
    pair_pads = rcopy(pads.at[pl.ds(c, 1)], pads.at[pl.ds(c, 1)], sends.at[2], recvs.at[2], partner)
    pair_pads.start()
    for copy in loads:
        copy.wait()
    vf[...] = vecs[...].astype(f32)
    h = tokens[...].astype(f32) + jnp.dot(feats[...], matrix(wl[...]), preferred_element_type=f32) + vf[0, 0:1, :]
    hidden[...] = h
    low[...] = h.astype(bf)
    keys[own, :] = jnp.dot(low[...], matrix(wk[...]), preferred_element_type=f32).astype(bf)
    send_keys = share(keys, 0)
    send_keys.start()
    values[own, :] = (jnp.dot(low[...], matrix(wv[...]), preferred_element_type=f32) + vf[2, 0:1, :]).astype(bf)
    send_values = share(values, 1)
    send_values.start()
    query[...] = ((jnp.dot(low[...], matrix(wq[...]), preferred_element_type=f32) + vf[1, 0:1, :]) * 0.125).astype(bf)
    for copy in (pair_pads, send_keys, send_values):
        copy.wait()


def enter(tiles, tokens, feats, pad):
    rows = tokens.shape[0]
    f32, bf = jnp.float32, jnp.bfloat16
    vm, any_ = pl.BlockSpec(memory_space=pltpu.VMEM), pl.BlockSpec(memory_space=pl.ANY)
    S, sem = jax.ShapeDtypeStruct, pltpu.SemaphoreType.DMA
    w = pltpu.VMEM((96, 8, D), bf)
    return pl.pallas_call(
        enter_kernel,
        out_shape=[S((rows, D), f32), S((rows, D), bf), S((rows, D), bf), S((2 * rows, D), bf), S((2 * rows, D), bf), S((2, 8, rows), jnp.int32)],
        in_specs=[any_, vm, vm, vm],
        out_specs=[vm] * 6,
        scratch_shapes=[pltpu.VMEM((16, 8, D), bf), w, w, w, pltpu.VMEM((3, 8, D), bf), pltpu.VMEM((3, 8, D), f32), sem((20,)), sem((3,)), sem((3,))],
        compiler_params=pltpu.CompilerParams(collective_id=2, has_side_effects=True, vmem_limit_bytes=40 << 20),
        name="enter",
    )(tiles, tokens, feats, pad)


def leave_kernel(tiles, dq, dk, dv, gfi, low, feats, table, grads_in, input_grad, grads,
                 wq, wk, wv, out, come, back, dwl, dwq, dwk, dwv, vgrads, lsem, ssem, sends, recvs):
    f32, bf = jnp.float32, jnp.bfloat16
    rows = gfi.shape[0]
    loads = pieces(tiles, wk, 112, 96, lsem, 0) + pieces(tiles, wv, 208, 96, lsem, 4) + pieces(tiles, wq, 16, 96, lsem, 8)
    for c in loads:
        c.start()
    c, partner = meet_partner()
    own, other = pl.ds(c * rows, rows), pl.ds((1 - c) * rows, rows)
    swaps = []
    for i, ref in enumerate((dk, dv)):
        out[i] = ref[other, :].astype(bf)
        swaps.append(rcopy(out.at[i], come.at[i], sends.at[i], recvs.at[i], partner))
        swaps[i].start()
    back[0] = dq[...].astype(bf)
    query_bias = jnp.sum(col_sum(dq[...]), axis=0, keepdims=True)
    for copy in loads:
        copy.wait()

    def through(i, w, dw):
        dw[...] = lax.dot_general(low[...], back[i], TN, preferred_element_type=f32).astype(bf).reshape(96, 8, D)
        return lax.dot_general(back[i], matrix(w[...]), NT, preferred_element_type=f32)

    input_grad[...] = gfi[...] + through(0, wq, dwq)
    stores = pieces(grads, dwq, 16, 96, ssem, 0, True)
    swaps[0].wait_recv()
    back[1] = (dk[own, :] + come[0].astype(f32)).astype(bf)
    input_grad[...] += through(1, wk, dwk)
    stores += pieces(grads, dwk, 112, 96, ssem, 4, True)
    swaps[1].wait_recv()
    grad_value = dv[own, :] + come[1].astype(f32)
    value_bias = jnp.sum(col_sum(grad_value), axis=0, keepdims=True)
    back[2] = grad_value.astype(bf)
    total = input_grad[...] + through(2, wv, dwv)
    stores += pieces(grads, dwv, 208, 96, ssem, 8, True)
    input_grad[...] = total
    layout_bias = jnp.sum(col_sum(total), axis=0, keepdims=True)
    dwl[...] = lax.dot_general(feats[...], total.astype(bf), TN, preferred_element_type=f32).astype(bf).reshape(16, 8, D)
    stores += pieces(grads, dwl, 0, 16, ssem, 12, True)

    def block(lines):
        return jnp.concatenate(lines + [jnp.zeros((8 - len(lines), D), f32)]).astype(bf)

    vgrads[0] = block([layout_bias, table[0:1, :]])
    vgrads[1] = block([query_bias])
    vgrads[2] = block([value_bias])
    vgrads[3] = jnp.zeros((8, D), bf)
    held = {0: 0, 1: 1, 4: 2}
    for i, chip in enumerate(ch for ch in range(5)):
        stores.append(pltpu.make_async_copy(vgrads.at[held.get(chip, 3)], grads.at[vector_at(chip)], ssem.at[16 + i]))
    for copy in stores:
        copy.start()
    for copy in stores:
        copy.wait()
    for swap in swaps:
        swap.wait_send()


def leave(tiles, dq, dk, dv, gfi, low, feats, table, grads):
    rows = gfi.shape[0]
    f32, bf = jnp.float32, jnp.bfloat16
    vm, any_ = pl.BlockSpec(memory_space=pltpu.VMEM), pl.BlockSpec(memory_space=pl.ANY)
    S, sem = jax.ShapeDtypeStruct, pltpu.SemaphoreType.DMA
    w = pltpu.VMEM((96, 8, D), bf)
    return pl.pallas_call(
        leave_kernel,
        out_shape=[S((rows, D), f32), S(grads.shape, bf)],
        in_specs=[any_] + [vm] * 7 + [any_],
        out_specs=[vm, any_],
        scratch_shapes=[w, w, w, pltpu.VMEM((2, rows, D), bf), pltpu.VMEM((2, rows, D), bf), pltpu.VMEM((3, rows, D), bf),
                        pltpu.VMEM((16, 8, D), bf), w, w, w, pltpu.VMEM((4, 8, D), bf), sem((12,)), sem((32,)), sem((2,)), sem((2,))],
        input_output_aliases={8: 1},
        compiler_params=pltpu.CompilerParams(collective_id=3, has_side_effects=True, vmem_limit_bytes=56 << 20),
        name="leave",
    )(tiles, dq, dk, dv, gfi, low, feats, table, grads)


GATHER_PARTS = ((0, 8), (8, 7), (15, 7), (22, 7), (29, 4), (33, 4))
GATHER_STEPS = (
    ((647, 384, 128, 256, 385, 129, 257, 386, 130, 258, 387, 131, 259, 388, 132, 260, 389, 133, 261),
     (17, 145, 8, 264, 19, 147, 12, 396, 20, 404, 10, 266, 9, 11, 13, 655, 397, 16, 18, 21, 663, 32, 33, 34, 35, 36, 37, 679, 405, 149, 268, 160, 288, 161, 289, 29, 413, 24, 25, 26, 27, 28, 671, 412, 162, 290),
     {-1: (163, 291), 0: (49, 177, 40, 296, 64, 65, 66, 67, 68, 69, 711), 1: (42, 298, 51, 179, 192), 2: (320,), 3: (41, 43, 44, 45, 687, 193, 321, 48, 50, 52, 53, 695), 4: (194, 322), 5: (195, 323, 56, 57, 58, 59, 60, 61, 703), 6: (96, 224, 352), 7: (97, 225, 353), 8: (81, 209, 72, 328, 98, 99, 100, 101, 743), 9: (226, 74, 330), 10: (227, 354, -1), 11: (73, 75, 76, 77, 719, 83, 211, 355, 113, 241, 104, 360, 105, 106, 107, 108, 109, 751, 80, 82, 84, 85, 727, 362, 112, 114, 115, 116, 117, 759, 243, 120, 121, 122, 123, 124, 125, 767, 88, 89, 90, 91, 92, 93, 735)}),
    ((679, 544, 416, 160, 288, 545, 417, 161, 289, 546),
     (0, 384, 128, 256, 547, 1, 385, 129, 257, 548, 549, 2, 386, 130, 258, 64, 576, 8, 264, 3, 387, 131, 17, 145, 4, 388, 65, 577, 259, 5, 647, 66, 67, 68, 69, 711, 389, 162, 578, 10, 266, 12, 396, 20, 404, 579, 290, 9, 11, 13, 655, 397, 19, 147, 163, 16, 18, 21, 663, 405, 580, 291, 418, 581, 164, 292, 96, 608, 29, 413, 165, 293, 24, 25, 26, 27, 28, 671, 412, 49, 177, 40, 296, 419),
     {-1: (97, 98, 99, 100, 101, 743, 51, 179, 44, 556, 52, 564, 42, 298, 420, 41, 43, 45, 687, 557, 48, 50, 53, 695, 565, 421, 181), 0: (300, 609, 428, 192, 320, 436), 1: (429, 193, 321, 61, 573), 2: (437, 56, 57, 58, 59, 60, 703, 572, 610, 194, 445, 322), 3: (444, 611, 195, 323), 4: (612, 224, 352), 5: (613, 108, 620, 225, 353), 6: (76, 588, 72, 73, 74, 75, 77, 719, 226, 116, 628, 354), 7: (589, 227, 109, 621, 355), 8: (84, 596, 81, 209, 80, 82, 83, 85, 727, 328, 117, 629), 9: (597, 211, 330), 10: (104, 105, 106, 107, 751, 112, 113, 114, 115, 759, 241, 360, -1), 11: (243, 362, 125, 637, 124, 636, 93, 605, 88, 89, 90, 91, 92, 735, 604, 120, 121, 122, 123, 767)}),
    ((711, 576, 448, 192, 320, 577, 449, 193, 321, 578),
     (32, 416, 160, 288, 579, 33, 417, 161, 289, 580, 581, 0, 384, 128, 256, 96, 608, 1, 385, 129, 257, 97, 609, 98, 99, 100, 101, 743, 2, 386, 130, 258, 610, 8, 264, 3, 387, 131, 611, 17, 145, 4, 388, 259, 5, 647, 389, 612, 49, 177, 10, 266, 12, 396, 613, 20, 404, 40, 296, 9, 11, 13, 655, 397, 19, 147, 16, 18, 21, 663, 405, 34, 162, 290, 418, 194, 322, 29, 413, 195, 24, 25, 26, 27, 28, 671, 412, 42, 298),
     {-1: (35, 419, 163, 291, 36, 420, 196, 37, 679, 421, 323), 0: (197, 44, 428, 324, 52, 436), 1: (108, 620, 325, 41, 43, 45, 687, 429, 51, 179, 224, 76, 588, 72, 328), 2: (48, 50, 53, 695, 437, 116, 628, 73, 74, 75, 77, 719, 589, 61, 445, 81, 209, 109, 621), 3: (84, 596, 352, 60, 444, 56, 57, 58, 59, 703, 117, 629, 80, 82, 83, 85, 727, 450, 225), 4: (597, 353, 451, 226), 5: (354, 452, 227), 6: (453, 355, 460, 211), 7: (330, 461, 213, 468), 8: (332, 113, 241, 104, 105, 106, 107, 751, 469, 360, 112, 114, 115, 759), 9: (125, 637, 243, 124, 636, 362, 93, 477, 605), 10: (88, 89, 90, 91, 92, 735, 476, 604, -1), 11: (120, 121, 122, 123, 767)}),
    ((743, 608, 224, 352, 609, 225, 353, 610, 226, 354, 611, 227, 355, 612, 613),
     (32, 160, 288, 33, 161, 289, 0, 128, 256, 1, 129, 257, 2, 130, 8, 264, 258, 17, 145, 3, 131, 259, 4, 5, 647, 49, 177, 10, 266, 40, 296, 9, 11, 12, 13, 655, 19, 147, 228, 16, 18, 20, 21, 663, 34, 290, 162, 356, 229, 357, 64, 192, 24, 25, 26, 27, 28, 29, 671, 108, 620),
     {-1: (42, 298, 35, 163, 291, 116, 628, 104, 105, 106, 107, 109, 751, 621, 117, 629, 112, 113, 114, 115, 759, 65, 193, 36, 37, 679, 320), 0: (360,), 1: (41, 43, 44, 45, 687, 51, 179, 241), 2: (48, 50, 52, 53, 695, 321, 243), 3: (362, 56, 57, 58, 59, 60, 61, 703, 245), 4: (364, 66, 194, 72, 328), 5: (81, 209, 322, 125, 637), 6: (67, 195, 120, 121, 122, 123, 124, 767, 636, 68, 69, 711, 323), 7: (74, 330), 8: (73, 75, 76, 77, 719), 9: (83, 211, 80, 82, 84, 85, 727), 10: (-1,), 11: (88, 89, 90, 91, 92, 93, 735)}),
)


def fill_features(out, boxes):
    rows = out.shape[0]
    f32 = jnp.float32
    cols = jnp.concatenate([boxes[i].astype(f32) for i in range(4)] + [jnp.zeros((4, rows), f32)]).T
    lane = lax.broadcasted_iota(jnp.int32, (rows, LF), 1)
    rate = jnp.exp((lane % FREQ).astype(f32) * (-math.log(10000.0) / FREQ))
    coordinate = lane // (2 * FREQ)
    at = cols[:, 3:4]
    for i in range(3):
        at = jnp.where(coordinate == i, cols[:, i : i + 1], at)
    angle = at * rate
    out[...] = jnp.where(lane // FREQ % 2 == 0, jnp.sin(angle), jnp.cos(angle)).astype(jnp.bfloat16)


def forward_kernel(x_ref, tokens, boxes, pad, buckets, lengths,
                   g_ref, hidden, low, query, keys, values, ctx, soft, code_out, feats,
                   xv, tail, head, win, chunk, lsem, hsend, hrecv, own,
                   ssem, rsem, cr,
                   pads, hidden_v, low_v, query_v, keys_v, values_v, ctx_v, code, buckets_v, tokens_v, feats_v, p_v, s_scr, tab,
                   wl, wq, wk, wv, vrows, vf, ksend, krecv, wsem, isem, osem, psem):
    f32, bf = jnp.float32, jnp.bfloat16
    rows = tokens.shape[0]
    k, c, z, y, x = place()
    d = 2 * k + c
    inputs = [pltpu.make_async_copy(r, v, isem.at[i]) for i, (r, v) in enumerate(((buckets, buckets_v), (tokens, tokens_v)))]
    for copy in inputs:
        copy.start()
    pads[pl.ds(c, 1)] = jnp.broadcast_to(pad[...], (8, rows)).reshape(1, 8, rows)
    greet(k, c, z, y, x)
    load = pltpu.make_async_copy(x_ref, xv, lsem)
    load.start()
    prev = (jnp.where(c == 1, k, jnp.maximum(k - 1, 0)), 1 - c)
    nxt = (jnp.where(c == 0, k, jnp.minimum(k + 1, 15)), 1 - c)
    to_next = rcopy(x_ref.at[pl.ds(ROWS - TAIL, TAIL)], tail, hsend.at[0], hrecv.at[0], nxt)
    to_prev = rcopy(x_ref.at[pl.ds(0, HEAD)], head, hsend.at[1], hrecv.at[1], prev)

    @pl.when(d < 31)
    def _():
        to_next.start()

    @pl.when(d > 0)
    def _():
        to_prev.start()

    win[...] = jnp.zeros_like(win)
    lanes = lax.broadcasted_iota(jnp.int32, (80, 128), 1)
    q, sh = shard_start(d)
    load.wait()

    @pl.loop(0, ROWS // 80)
    def _(i):
        r = pl.multiple_of(i * 80, 8)
        rolled = pltpu.roll(xv[pl.ds(r, 80), :], sh, 1)
        win[pl.ds(160 + r, 80), :] += jnp.where(lanes >= sh, rolled, 0.0)
        win[pl.ds(161 + r, 80), :] += jnp.where(lanes < sh, rolled, 0.0)

    @pl.when(d > 0)
    def _():
        to_next.wait_recv()
        qp, shp = shard_start(d - 1)
        lanes = lax.broadcasted_iota(jnp.int32, (TAIL, 128), 1)
        rolled = pltpu.roll(tail[...], shp, 1)
        at = 1760 - (q - qp)
        win[pl.ds(at, TAIL), :] += jnp.where(lanes >= shp, rolled, 0.0)
        win[pl.ds(at + 1, TAIL), :] += jnp.where(lanes < shp, rolled, 0.0)

    @pl.when(d < 31)
    def _():
        to_prev.wait_recv()
        qn, shn = shard_start(d + 1)
        lanes = lax.broadcasted_iota(jnp.int32, (HEAD, 128), 1)
        rolled = pltpu.roll(head[...], shn, 1)
        at = 160 + (qn - q)
        win[pl.ds(at, HEAD), :] += jnp.where(lanes >= shn, rolled, 0.0)
        win[pl.ds(at + 1, HEAD), :] += jnp.where(lanes < shn, rolled, 0.0)

    early = early_vectors(k)
    nw0 = jnp.where(early, 36, 37)
    vecs = early == (c == 0)
    first = jnp.where(c == 0, 73 * k, 73 * k + nw0)
    base = q - 160

    @pl.loop(0, SLOTS)
    def _(t):
        at, wide = tile_start(first + t)
        is_vec = vecs & (t == 36)
        at = jnp.where(is_vec, vector_row(k, q), at) - base
        wide = wide & jnp.logical_not(is_vec)

        @pl.when(wide)
        def _():
            parts = [win[pl.ds(at + j, 8, stride=24), :] for j in range(6)]
            chunk[t] = jnp.concatenate(parts, axis=1).astype(jnp.bfloat16)

        @pl.when(jnp.logical_not(wide))
        def _():
            parts = [win[pl.ds(at + j, 8, stride=6), :] for j in range(6)]
            chunk[t] = jnp.concatenate(parts, axis=1).astype(jnp.bfloat16)

    @pl.when(d < 31)
    def _():
        to_next.wait_send()

    @pl.when(d > 0)
    def _():
        to_prev.wait_send()

    xdev, ydev, cdev = (z * 4 + y * 2 + 1 - x, c), (z * 4 + (1 - y) * 2 + x, c), (k, 1 - c)
    targets = {1: xdev, 2: ydev, 3: (jnp.minimum(k + 4, 15), c), 4: (jnp.maximum(k - 4, 0), c), 5: cdev}
    tiles = g_ref.reshape(16 * CHIP, 8, D)

    def step(zz, op):
        if op < 0:
            make_values()
            return
        link, item, p = op // 128, op // 8 % 16, op % 8
        chip = item // 4 * 4 + (1 - y if item // 2 % 2 else y) * 2 + (1 - x if item % 2 else x)
        off, n = (0, 37) if link == 5 else GATHER_PARTS[p]
        there = g_ref.at[chip, pl.ds(37 * c + off, n)]
        if link == 0:
            rcopy(there, there, ssem.at[0], rsem.at[chip, p], xdev).wait_recv()
            return
        here = chunk.at[pl.ds(off, n)] if item == zz * 4 else there
        rcopy(here, there, ssem.at[link - 1], cr.at[chip] if link == 5 else rsem.at[chip, p], targets[link]).start()

    def steps_of(zz, which, head=0):
        for op in GATHER_STEPS[zz][which] if which < 2 else GATHER_STEPS[zz][2].get(head, ()):
            step(zz, op)

    def sent_rows(zz, link):
        ops = [op for w in (0, 1) for op in GATHER_STEPS[zz][w]] + [op for v in GATHER_STEPS[zz][2].values() for op in v]
        return sum(37 if link == 5 else GATHER_PARTS[op % 8][1] for op in ops if op // 128 == link)

    pair_pads = rcopy(pads.at[pl.ds(c, 1)], pads.at[pl.ds(c, 1)], ksend.at[2], krecv.at[2], cdev)
    pair_pads.start()
    mine = pltpu.make_async_copy(chunk, g_ref.at[k, pl.ds(37 * c, 37)], own.at[0])

    for zz in range(4):
        @pl.when(z == zz)
        def _():
            steps_of(zz, 0)
    mine.start()
    for copy in inputs:
        copy.wait()
    pair_pads.wait()
    fill_codes(code, buckets_v, pads, lengths)
    fill_features(feats_v, boxes)
    outs = [pltpu.make_async_copy(code, code_out, osem.at[0]), pltpu.make_async_copy(feats_v, feats, osem.at[7])]
    for copy in outs:
        copy.start()
    for zz in range(4):
        @pl.when(z == zz)
        def _():
            steps_of(zz, 1)
    mine.wait()

    def from_partner(chip):
        theirs = g_ref.at[chip, pl.ds(37 * (1 - c), 37)]
        rcopy(theirs, theirs, ssem.at[4], cr.at[chip], cdev).wait_recv()

    for chip in range(3):
        from_partner(chip)

    loads = [pltpu.make_async_copy(tiles.at[vector_at(ch)], vrows.at[i], wsem.at[i]) for i, ch in enumerate((0, 1))]
    loads += pieces(tiles, wl, 0, 16, wsem, 4) + pieces(tiles, wk, 112, 96, wsem, 8) + pieces(tiles, wq, 16, 96, wsem, 16)
    for copy in loads:
        copy.start()
    for copy in loads:
        copy.wait()
    vf[0] = vrows[0].astype(f32)
    vf[1] = vrows[1].astype(f32)
    fill_table(tab, vrows.at[0])
    h = tokens_v[...].astype(f32) + jnp.dot(feats_v[...], matrix(wl[...]), preferred_element_type=f32) + vf[0, 0:1, :]
    hidden_v[...] = h
    low_v[...] = h.astype(bf)
    half_rows = pl.ds(c * rows, rows)

    def share(ref, i):
        return rcopy(ref.at[half_rows], ref.at[half_rows], ksend.at[i], krecv.at[i], cdev)

    keys_v[half_rows, :] = jnp.dot(low_v[...], matrix(wk[...]), preferred_element_type=f32).astype(bf)
    share(keys_v, 0).start()
    query_v[...] = ((jnp.dot(low_v[...], matrix(wq[...]), preferred_element_type=f32) + vf[1, 0:1, :]) * 0.125).astype(bf)
    share(keys_v, 0).wait()
    outs += [pltpu.make_async_copy(v, r, osem.at[1 + i]) for i, (v, r) in enumerate(((hidden_v, hidden), (low_v, low), (query_v, query), (keys_v, keys)))]
    for copy in outs[2:]:
        copy.start()

    def make_values():
        for chip in (3, 4):
            from_partner(chip)
        copies = [pltpu.make_async_copy(tiles.at[vector_at(4)], vrows.at[2], wsem.at[2])] + pieces(tiles, wv, 208, 96, wsem, 12)
        for copy in copies:
            copy.start()
        for copy in copies:
            copy.wait()
        vf[2] = vrows[2].astype(f32)
        values_v[half_rows, :] = (jnp.dot(low_v[...], matrix(wv[...]), preferred_element_type=f32) + vf[2, 0:1, :]).astype(bf)
        share(values_v, 1).start()

    def keep(pair):
        return pltpu.make_async_copy(p_v.at[pl.ds(2 * pair, 2)], soft.at[pl.ds(2 * pair, 2)], psem.at[pair])

    for zz in range(4):
        if -1 in GATHER_STEPS[zz][2]:
            @pl.when(z == zz)
            def _():
                steps_of(zz, 2, -1)

    def one_head(head, _):
        lanes = pl.ds(pl.multiple_of(head // 2 * 128, 128), 128)
        soft_head(head, query_v[:, lanes], keys_v[:, lanes], code, tab, s_scr, p_v.at[head])

        @pl.when(head % 2 == 1)
        def _():
            keep(head // 2).start()

        for zz in range(4):
            for i in range(H):
                if i in GATHER_STEPS[zz][2]:
                    @pl.when((head == i) & (z == zz))
                    def _():
                        steps_of(zz, 2, i)
        return 0

    lax.fori_loop(0, H, one_head, 0)
    share(values_v, 1).wait()
    outs.append(pltpu.make_async_copy(values_v, values, osem.at[5]))
    outs[-1].start()

    def context(pair, _):
        lanes = pl.ds(pl.multiple_of(pair * 128, 128), 128)
        ctx_v[:, lanes] = context_pair(values_v[:, lanes], p_v.at[pl.ds(2 * pair, 2)])
        return 0

    lax.fori_loop(0, H // 2, context, 0)
    outs.append(pltpu.make_async_copy(ctx_v, ctx, osem.at[6]))
    outs[-1].start()

    for zz in range(4):
        @pl.when(z == zz)
        def _():
            for link in range(1, 6):
                n = sent_rows(zz, link)
                if n:
                    whole = tiles.at[pl.ds(0, n)]
                    rcopy(whole, whole, ssem.at[link - 1], cr.at[0], targets[link]).wait_send()
    for chip in range(5, 16):
        from_partner(chip)
    for pair in range(H // 2):
        keep(pair).wait()
    for copy in outs:
        copy.wait()


def gather_and_attend(master, tokens, boxes, pad, buckets, page_lengths):
    x = jnp.pad(master, (0, ROWS * 128 - SHARD)).reshape(ROWS, 128)
    sem = pltpu.SemaphoreType.DMA
    any_, vm = pl.BlockSpec(memory_space=pl.ANY), pl.BlockSpec(memory_space=pltpu.VMEM)
    rows, key_rows = buckets.shape
    f32, bf = jnp.float32, jnp.bfloat16
    S, V = jax.ShapeDtypeStruct, pltpu.VMEM
    w = V((96, 8, D), bf)
    return pl.pallas_call(
        forward_kernel,
        out_shape=[
            S((16, CHIP, 8, D), bf), S((rows, D), f32), S((rows, D), bf), S((rows, D), bf), S((key_rows, D), bf), S((key_rows, D), bf),
            S((rows, D), bf), S((H, key_rows, rows), bf), S((key_rows, rows), jnp.int32), S((rows, LF), bf),
        ],
        in_specs=[any_, any_, vm, vm, any_, pl.BlockSpec(memory_space=pltpu.SMEM)],
        out_specs=[any_] * 10,
        scratch_shapes=[
            V((ROWS, 128), f32), V((TAIL, 128), f32), V((HEAD, 128), f32), V((WIN, 128), f32), V((SLOTS, 8, D), bf),
            sem, sem((2,)), sem((2,)), sem((2,)),
            sem((5,)), sem((16, 6)), sem((16,)),
            V((2, 8, rows), jnp.int32), V((rows, D), f32), V((rows, D), bf), V((rows, D), bf), V((key_rows, D), bf), V((key_rows, D), bf),
            V((rows, D), bf), V((key_rows, rows), jnp.int32), V((rows, key_rows), jnp.int32), V((rows, D), bf), V((rows, LF), bf),
            V((H, key_rows, rows), bf), V((key_rows, rows), f32), V((16, 128), f32),
            V((16, 8, D), bf), w, w, w, V((3, 8, D), bf), V((3, 8, D), f32),
            sem((3,)), sem((3,)), sem((20,)), sem((3,)), sem((8,)), sem((H // 2,)),
        ],
        compiler_params=pltpu.CompilerParams(collective_id=0, has_side_effects=True, vmem_limit_bytes=60 << 20),
        name="gather_and_attend",
    )(x, tokens, boxes, pad, buckets, page_lengths)


def guarded(cond, f):
    if cond is True:
        f()
    elif cond is not False:
        pl.when(cond)(f)


class Reducer:
    def __init__(self, where, zs, want, spare, g_ref, acc, crecv, a1, b1, a2, b2, asem, cs, cr, a1s, a1r, b1s, b1r, a2s, a2r, b2s, b2r):
        self.k, self.c, self.z, self.y, self.x = where
        self.zs, self.want, self.spare = zs, want, spare
        self.g_ref, self.acc, self.crecv = g_ref, acc, crecv
        self.bufs = (a1, b1, a2, b2)
        self.asem, self.cs, self.cr = asem, cs, cr
        self.sems = ((a1s, a1r), (b1s, b1r), (a2s, a2r), (b2s, b2r))
        z, y, x, c = self.z, self.y, self.x, self.c
        self.xdev, self.ydev, self.cdev = (z * 4 + y * 2 + 1 - x, c), (z * 4 + (1 - y) * 2 + x, c), (self.k, 1 - c)

    def at(self, zo, oy, ox):
        return zo, (1 - self.y if oy else self.y), (1 - self.x if ox else self.x)

    def chip(self, zo, yo, xo):
        return zo * 4 + yo * 2 + xo

    def local(self, zo, yo, xo):
        return self.chip(zo, yo, xo)

    def load(self, item):
        i = self.local(*item)
        return pltpu.make_async_copy(self.g_ref.at[self.chip(*item), pl.ds(37 * self.c, 37)], self.acc.at[i], self.asem.at[i])

    def ccopy(self, item):
        i = self.local(*item)
        return rcopy(self.g_ref.at[self.chip(*item), pl.ds(37 * (1 - self.c), 37)], self.crecv.at[i + self.spare], self.cs.at[i], self.cr.at[i], self.cdev)

    def hop(self, which, item, slot, p, dev):
        s, r = self.sems[which]
        return rcopy(self.acc.at[self.local(*item), pl.ds(*PARTS[p])], self.bufs[which].at[slot], s.at[slot], r.at[slot], dev)

    def a1(self, zo, xo):
        return self.hop(0, (zo, 1 - self.y, xo), self.zs.index(zo) * 2 + xo, 0, self.ydev)

    def b1(self, zo, yo):
        return self.hop(1, (zo, yo, 1 - self.x), self.zs.index(zo) * 2 + yo, 1, self.xdev)

    def a2(self, zo):
        return self.hop(2, (zo, self.y, 1 - self.x), self.zs.index(zo), 0, self.xdev)

    def b2(self, zo):
        return self.hop(3, (zo, 1 - self.y, self.x), self.zs.index(zo), 1, self.ydev)

    def gain(self, item, p, which, slot):
        off, n = PARTS[p]
        i, acc, buf = self.local(*item), self.acc, self.bufs[which]
        acc[i, pl.ds(off, n)] = acc[i, pl.ds(off, n)] + buf[slot]

    def begin(self, zo, oy, ox):
        item = self.at(zo, oy, ox)

        def go():
            self.load(item).start()
            self.ccopy(item).start()
        guarded(self.want(*item), go)

    def first(self, zo, oy, ox):
        item = self.at(zo, oy, ox)

        def go():
            self.load(item).wait()
            self.ccopy(item).wait_recv()
            i = self.local(*item)
            self.acc[i] = self.acc[i] + self.crecv[i + self.spare]
            if oy:
                self.a1(zo, item[2]).start()
            if ox:
                self.b1(zo, item[1]).start()
        guarded(self.want(*item), go)

    def second(self, zo):
        ia, ib = self.at(zo, 0, 1), self.at(zo, 1, 0)
        n = self.zs.index(zo) * 2

        def go_a():
            self.a1(zo, 1 - self.x).wait_recv()
            self.gain(ia, 0, 0, n + 1 - self.x)
            self.a2(zo).start()

        def go_b():
            self.b1(zo, 1 - self.y).wait_recv()
            self.gain(ib, 1, 1, n + 1 - self.y)
            self.b2(zo).start()
        guarded(self.want(*ia), go_a)
        guarded(self.want(*ib), go_b)

    def third(self, zo):
        item = self.at(zo, 0, 0)
        n = self.zs.index(zo)

        def go():
            self.a1(zo, self.x).wait_recv()
            self.b1(zo, self.y).wait_recv()
            self.a2(zo).wait_recv()
            self.b2(zo).wait_recv()
            i = self.local(*item)
            for p, (h, u), at in ((0, (0, 2), self.x), (1, (1, 3), self.y)):
                off, m = PARTS[p]
                self.acc[i, pl.ds(off, m)] = (self.acc[i, pl.ds(off, m)] + self.bufs[h][n * 2 + at]) + self.bufs[u][n]
        guarded(self.want(*item), go)

    def finish(self):
        for zo in self.zs:
            for oy in (0, 1):
                for ox in (0, 1):
                    item = self.at(zo, oy, ox)

                    def sent(item=item, oy=oy, ox=ox, zo=zo):
                        self.ccopy(item).wait_send()
                        if oy:
                            self.a1(zo, item[2]).wait_send()
                        if ox:
                            self.b1(zo, item[1]).wait_send()
                        if ox and not oy:
                            self.a2(zo).wait_send()
                        if oy and not ox:
                            self.b2(zo).wait_send()
                    guarded(self.want(*item), sent)


def reducer_scratch():
    bf, sem = jnp.bfloat16, pltpu.SemaphoreType.DMA
    tile = (8, D)
    return [
        pltpu.VMEM((16, 37) + tile, bf), pltpu.VMEM((11, 37) + tile, bf),
        pltpu.VMEM((8, 19) + tile, bf), pltpu.VMEM((8, 18) + tile, bf), pltpu.VMEM((4, 19) + tile, bf), pltpu.VMEM((4, 18) + tile, bf),
        sem((16,)), sem((16,)), sem((16,)),
        sem((8,)), sem((8,)), sem((8,)), sem((8,)), sem((4,)), sem((4,)), sem((4,)), sem((4,)),
    ]


def early_item(zo, yo, xo):
    return zo >= 2 if zo != 1 else yo + xo > 0


def late_item(zo, yo, xo):
    return zo == 0 if zo != 1 else yo + xo == 0


ZCUTS = ((0, 10), (10, 9), (19, 9), (28, 9))


class Chain:
    def __init__(self, where, acc, up, dn, us, ur, ds_, dr):
        self.k, self.c, self.z, self.y, self.x = where
        self.acc = acc
        self.ways = {1: (up, us, ur, (jnp.minimum(self.k + 4, 15), self.c)), -1: (dn, ds_, dr, (jnp.maximum(self.k - 4, 0), self.c))}

    def chip(self, zo):
        return zo * 4 + self.y * 2 + self.x

    def copy(self, zo, way, p):
        buf, s, r, dev = self.ways[way]
        part = pl.ds(*ZCUTS[p])
        return rcopy(self.acc.at[self.chip(zo), part], buf.at[zo, part], s.at[zo, p], r.at[zo, p], dev)

    def move(self, zs, zo, way, take=True, give=True, also=None):
        cond = self.z == zs if also is None else (self.z == zs) & also

        @pl.when(cond)
        def _():
            i = self.chip(zo)
            for p in range(4):
                if take:
                    self.copy(zo, way, p).wait_recv()
                    part = pl.ds(*ZCUTS[p])
                    self.acc[i, part] = self.acc[i, part] + self.ways[way][0][zo, part]
                if give:
                    self.copy(zo, way, p).start()

    def sent(self, zs, zo, way):
        @pl.when(self.z == zs)
        def _():
            for p in range(4):
                self.copy(zo, way, p).wait_send()


def chain_scratch():
    bf, sem = jnp.bfloat16, pltpu.SemaphoreType.DMA
    return [pltpu.VMEM((4, 37, 8, D), bf)] * 2 + [sem((4, 4))] * 4


def backward_kernel(tiles, q_ref, k_ref, v_ref, do_ref, p_hbm, code_hbm, gfi_in, low_in, feats_in, grads_in, m_ref, one_ref, two_ref,
                    grad_out, grads, step_ref, new1_ref, new2_ref, spread,
                    pbuf, qv, kv, vv, dov, psem, code_ref, csem, dsv, dssem, group, gsem, counts, dks, dvs, out, come, sends, recvs, back, bias,
                    wq, wk, wv, low, gfi, feats, dwl, dwq, dwk, dwv, vgrads, wsem, ssem, isem,
                    total, ebuf, sq, sqr, win, mv, onev, twov, lsem, es, er, qs, qr, *scratch):
    f32, bf = jnp.float32, jnp.bfloat16
    where = place()
    k, c, z, y, x = where
    d = 2 * k + c
    shared = grads.reshape(16, CHIP, 8, D)
    rs = Reducer(where, (0, 1, 2, 3), early_item, -5, shared, *scratch[:17])
    late = Reducer(where, (0, 1, 2, 3), late_item, 6, shared, *scratch[:17])
    acc = rs.acc
    zc = Chain(where, acc, *scratch[17:])
    xdev, ydev, cdev = rs.xdev, rs.ydev, rs.cdev
    column_devs = [((z + s) % 4 * 4 + y * 2 + x, c) for s in (1, 2, 3)]
    prev = (jnp.where(c == 1, k, jnp.maximum(k - 1, 0)), 1 - c)
    nxt = (jnp.where(c == 0, k, jnp.minimum(k + 1, 15)), 1 - c)
    bar = pltpu.get_barrier_semaphore()
    far_next, far_prev = (c == 1) & (k < 15), (c == 0) & (k > 0)
    plane_devs = [(z * 4 + (1 - y if oy else y) * 2 + (1 - x if ox else x), 1 - c if oc else c) for oc in (0, 1) for oy in (0, 1) for ox in (0, 1)][1:]
    for dev in plane_devs + column_devs:
        pl.semaphore_signal(bar, inc=1, device_id=dev, device_id_type=MESH)

    @pl.when(far_next)
    def _():
        pl.semaphore_signal(bar, inc=1, device_id=nxt, device_id_type=MESH)

    @pl.when(far_prev)
    def _():
        pl.semaphore_signal(bar, inc=1, device_id=prev, device_id_type=MESH)

    keys, rows = code_ref.shape

    def fetch_soft(pair, hh):
        return pltpu.make_async_copy(p_hbm.at[2 * pair + hh], pbuf.at[hh], psem.at[0, hh])

    def fetch(p):
        slot = p % 2
        lanes = pl.ds(pl.multiple_of(p * 128, 128), 128)
        return [pltpu.make_async_copy(r.at[:, lanes], v.at[slot], psem.at[1 + i, slot]) for i, (r, v) in enumerate(((q_ref, qv), (k_ref, kv), (v_ref, vv), (do_ref, dov)))]

    for copy in fetch(0) + [fetch_soft(0, 0), fetch_soft(0, 1)]:
        copy.start()
    pl.semaphore_wait(bar, 10 + jnp.where(far_next | far_prev, 1, 0))
    corners = ((1, 1), (1, 0), (0, 1), (0, 0))
    for oy, ox in corners:
        rs.begin(3, oy, ox)
    code_copy = pltpu.make_async_copy(code_hbm, code_ref, csem.at[0])
    inputs = [pltpu.make_async_copy(r, v, isem.at[i]) for i, (r, v) in enumerate(((low_in, low), (gfi_in, gfi), (feats_in, feats)))]
    loads = pieces(tiles, wq, 16, 96, wsem, 8) + pieces(tiles, wv, 208, 96, wsem, 4) + pieces(tiles, wk, 112, 96, wsem, 0)
    shards = [pltpu.make_async_copy(r, v, lsem.at[i]) for i, (r, v) in enumerate(((m_ref, mv), (one_ref, onev), (two_ref, twov)))]
    for copy in [code_copy] + inputs + loads + shards:
        copy.start()
    own, other = pl.ds(c * rows, rows), pl.ds((1 - c) * rows, rows)

    def swap(pair):
        return rcopy(out.at[pair], come.at[pair], sends.at[pair], recvs.at[pair], cdev)

    def settle(pair):
        slot = pair % 2
        swap(pair).wait_recv()
        lanes = pl.ds(pl.multiple_of(pair * 128, 128), 128)
        dk = dks[slot, own, :] + come[pair, 0].astype(f32)
        dv = dvs[slot, own, :] + come[pair, 1].astype(f32)
        back[1, :, lanes] = dk.astype(bf)
        back[2, :, lanes] = dv.astype(bf)
        bias[1, :, lanes] = col_sum(dv)

    def lay(pair, hh):
        return pltpu.make_async_copy(dsv.at[hh], spread.at[:, 2 * pair + hh], dssem.at[hh])

    plan = {
        0: [(rs.first, 3, 1, 0), (rs.begin, 2, 1, 1), (rs.begin, 2, 1, 0), (rs.begin, 2, 0, 1), (rs.begin, 2, 0, 0), (rs.first, 3, 0, 1)],
        1: [(rs.begin, 1, 1, 1), (rs.begin, 1, 1, 0), (rs.begin, 1, 0, 1), (rs.begin, 1, 0, 0), (rs.first, 2, 1, 1), (rs.first, 2, 0, 1), (rs.second, 3)],
        2: [(rs.first, 2, 1, 0)],
        4: [(rs.first, 2, 0, 0), (rs.second, 2), (rs.first, 3, 0, 0), (rs.first, 1, 1, 1)],
    }
    rs.first(3, 1, 1)

    def pair_of_heads(pair, _):
        slot = pair % 2

        @pl.when(pair < H // 2 - 1)
        def _():
            for copy in fetch(pair + 1):
                copy.start()

        for copy in fetch(pair):
            copy.wait()
        lanes = pl.ds(pl.multiple_of(pair * 128, 128), 128)
        dq = []
        for hh in range(2):
            fetch_soft(pair, hh).wait()
            qm = half(qv[slot], hh)
            dom = half(dov[slot], hh)
            g = lax.dot_general(vv[slot], dom, NT, preferred_element_type=f32)
            p = pbuf[hh]
            pf = p.astype(f32)
            inner = jnp.sum(jnp.sum((g * pf).reshape(keys // 8, 8, rows), axis=0), axis=0, keepdims=True)
            ds = (pf * (g - inner)).astype(bf)

            @pl.when(pair > 0)
            def _():
                lay(pair - 1, hh).wait()

            dsv[hh] = ds.reshape(keys // 8, 8, rows)
            lay(pair, hh).start()
            dv = jnp.dot(p, dom, preferred_element_type=f32)

            @pl.when(pair < H // 2 - 1)
            def _():
                fetch_soft(pair + 1, hh).start()

            dk = jnp.dot(ds, qm, preferred_element_type=f32)
            if hh == 0:
                dvs[slot] = dv
                dks[slot] = dk
            else:
                dvs[slot] += dv
                dks[slot] += dk
            dq.append(lax.dot_general(kv[slot], ds, TN, preferred_element_type=f32))
        out[pair, 0] = dks[slot, other, :].astype(bf)
        out[pair, 1] = dvs[slot, other, :].astype(bf)
        swap(pair).start()
        sub = lax.broadcasted_iota(jnp.int32, dq[0].shape, 0)
        dqf = jnp.where(sub < 64, dq[0], dq[1]).T * 0.125
        back[0, :, lanes] = dqf.astype(bf)
        bias[0, :, lanes] = col_sum(dqf)

        @pl.when(pair > 0)
        def _():
            settle(pair - 1)

        for i, steps in plan.items():
            @pl.when(pair == i)
            def _():
                for f, *a in steps:
                    f(*a)
        return 0

    lax.fori_loop(0, H // 2, pair_of_heads, 0)
    for hh in range(2):
        lay(H // 2 - 1, hh).wait()
    for copy in inputs + loads:
        copy.wait()

    def through(i, w, dw):
        dw[...] = lax.dot_general(low[...], back[i], TN, preferred_element_type=f32).astype(bf).reshape(96, 8, D)
        return lax.dot_general(back[i], matrix(w[...]), NT, preferred_element_type=f32)

    stores = []

    def keep(dw, first, count, base):
        made = pieces(grads, dw, first, count, ssem, base, True)
        for copy in made:
            copy.start()
        stores.extend(made)

    gfi[...] += through(0, wq, dwq)
    keep(dwq, 16, 96, 0)
    settle(H // 2 - 1)
    gfi[...] += through(2, wv, dwv)
    keep(dwv, 208, 96, 8)
    whole = gfi[...] + through(1, wk, dwk)
    keep(dwk, 112, 96, 4)
    gfi[...] = whole
    shown = pltpu.make_async_copy(gfi, grad_out, isem.at[6])
    shown.start()
    layout_bias = jnp.sum(col_sum(whole), axis=0, keepdims=True)
    dwl[...] = lax.dot_general(feats[...], whole.astype(bf), TN, preferred_element_type=f32).astype(bf).reshape(16, 8, D)
    keep(dwl, 0, 16, 12)

    def block(lines):
        return jnp.concatenate(lines + [jnp.zeros((8 - len(lines), D), f32)]).astype(bf)

    vgrads[0] = block([layout_bias])
    vgrads[1] = block([jnp.sum(bias[0], axis=0, keepdims=True)])
    vgrads[2] = block([jnp.sum(bias[1], axis=0, keepdims=True)])
    vgrads[3] = jnp.zeros((8, D), bf)
    held = {0: 0, 1: 1, 4: 2}
    for i, ch in enumerate((0, 1, 2, 3, 4)):
        copy = pltpu.make_async_copy(vgrads.at[held.get(ch, 3)], grads.at[vector_at(ch)], ssem.at[16 + i])
        copy.start()
        stores.append(copy)
    for copy in stores:
        copy.wait()
    for oy, ox in corners:
        for zo in (0, 1):
            late.begin(zo, oy, ox)

    GROUPS = 16

    def take_groups(i):
        return pltpu.make_async_copy(spread.at[pl.ds(i * GROUPS, GROUPS)], group.at[i % 2], gsem.at[i % 2])

    bucket = lax.broadcasted_iota(jnp.int32, (BUCKETS, rows), 0)
    steps = keys // 8 // GROUPS
    code_copy.wait()
    take_groups(0).start()
    counts[...] = jnp.zeros_like(counts)

    def count_some(first, n):
        for i in range(first, first + n):
            if i + 1 < steps:
                take_groups(i + 1).start()
            take_groups(i).wait()

            def count(j, run, i=i):
                code = code_ref[pl.ds(pl.multiple_of((i * GROUPS + j) * 8, 8), 8), :]
                hot = jnp.concatenate(
                    [jnp.where(jnp.broadcast_to(code[r : r + 1], bucket.shape) == bucket, 1.0, 0.0) for r in range(8)]
                ).astype(bf)
                return run + lax.dot_general(group[i % 2, j].reshape(8 * H, rows), hot, NT, preferred_element_type=f32)

            counts[...] = lax.fori_loop(0, GROUPS, count, counts[...], unroll=8)

    early_one, late_one = rs.want(1, y, x), late.want(1, y, x)
    rs.third(3)
    zc.move(0, 3, 1, take=False)
    late.first(0, 1, 1)
    late.first(1, 1, 1)
    zc.move(1, 3, 1)
    late.first(0, 1, 0)
    late.first(1, 1, 0)
    count_some(0, 1)
    late.first(0, 0, 1)
    late.first(1, 0, 1)
    rs.third(2)
    count_some(1, 1)
    count_some(2, 1)
    late.first(0, 0, 0)
    late.first(1, 0, 0)
    zc.move(0, 2, 1, take=False)
    zc.move(2, 3, 1)
    zc.move(3, 2, -1, take=False)
    count_some(3, 1)
    late.second(0)
    late.second(1)
    rs.first(1, 0, 1)
    count_some(4, 1)
    rs.first(1, 1, 0)
    count_some(5, 1)
    zc.move(1, 2, 1)
    rs.second(1)
    count_some(6, 1)
    late.third(0)
    zc.move(3, 0, -1, take=False)
    late.third(1)
    zc.move(0, 1, 1, take=False, also=late_one)
    zc.move(3, 1, -1, take=False, also=late_one)
    zc.move(2, 0, -1)
    zc.move(2, 1, -1, also=late_one)
    zc.move(1, 0, -1)
    count_some(7, 1)
    rs.first(1, 0, 0)
    rs.third(1)
    zc.move(2, 1, -1, also=early_one)
    zc.move(3, 1, -1, take=False, also=early_one)
    zc.move(0, 1, 1, take=False, also=early_one)
    table = table_row(counts[...], (8, D))

    total[...] = acc[k].astype(f32)

    def add(way, zo):
        buf = zc.ways[way][0]
        for p in range(4):
            zc.copy(zo, way, p).wait_recv()
        total[...] = total[...] + buf[zo].astype(f32)

    @pl.when(z == 0)
    def _():
        add(-1, 0)

    @pl.when(z == 1)
    def _():
        add(1, 1)
        add(-1, 1)

    @pl.when(z == 2)
    def _():
        add(1, 2)
        add(-1, 2)

    @pl.when(z == 3)
    def _():
        add(1, 3)

    early = early_vectors(k)
    nw0 = jnp.where(early, 36, 37)
    vecs = early == (c == 0)
    mine = jnp.where(vecs, 36, 37)
    to_next = rcopy(total.at[pl.ds(mine - EDGE, EDGE)], ebuf.at[0], es.at[0], er.at[0], nxt)
    to_prev = rcopy(total.at[pl.ds(0, EDGE)], ebuf.at[1], es.at[1], er.at[1], prev)

    @pl.when(d < 31)
    def _():
        to_next.start()

    @pl.when(d > 0)
    def _():
        to_prev.start()

    def square(i, run):
        t = total[i]
        t = t * t
        for j in range(6):
            run = run + t[:, 128 * j:128 * j + 128]
        return run

    squares = lax.fori_loop(0, 37, square, jnp.zeros((8, 128), f32))
    lines = [jnp.sum(squares, axis=0, keepdims=True)] + [table[0:1, 128 * i : 128 * i + 128] for i in range(3)]
    place_in = c * 4 + y * 2 + x
    sq[0] = jnp.concatenate(lines + [jnp.zeros((4, 128), f32)])
    sqr[place_in] = sq[0]
    rounds = [rcopy(sq.at[0], sqr.at[place_in], qs.at[i], qr.at[place_in], dev) for i, dev in enumerate(plane_devs)]
    hops = [rcopy(sq.at[1], sqr.at[8 + z], qs.at[7 + i], qr.at[8 + z], dev) for i, dev in enumerate(column_devs)]
    for h in rounds:
        h.start()

    def arrived(slot):
        return rcopy(sqr.at[slot], sqr.at[slot], qs.at[0], qr.at[slot], cdev)

    rs.finish()
    late.finish()
    for zs in (0, 1, 2):
        zc.sent(zs, 3, 1)
    for zs in (0, 1):
        zc.sent(zs, 2, 1)
    zc.sent(3, 2, -1)
    zc.sent(0, 1, 1)
    zc.sent(3, 1, -1)
    zc.sent(2, 1, -1)
    for zs in (1, 2, 3):
        zc.sent(zs, 0, -1)
    for pair in range(H // 2):
        swap(pair).wait_send()
    q, sh = shard_start(d)
    base = q - FRONT

    def flatten(ref, i, at, wide):
        @pl.when(wide)
        def _():
            t = ref[i]
            for j in range(6):
                win[pl.ds(at + j, 8, stride=24), :] = t[:, 128 * j:128 * j + 128]

        @pl.when(jnp.logical_not(wide))
        def _():
            t = ref[i]
            for j in range(6):
                win[pl.ds(at + j, 8, stride=6), :] = t[:, 128 * j:128 * j + 128]

    own_vectors = vecs & (vector_row(k, -1) >= 0)

    @pl.when(own_vectors)
    def _():
        flatten(total, 36, vector_row(k, q) - base, k < 0)

    w0 = jnp.where(c == 0, 73 * k, 73 * k + nw0)

    @pl.loop(0, mine)
    def _(t):
        at, wide = tile_start(w0 + t)
        flatten(total, t, at - base, wide)

    for i in range(8):
        @pl.when(place_in != i)
        def _():
            arrived(i).wait_recv()
    layer = sqr[0]
    for i in range(1, 8):
        layer = layer + sqr[i]
    sq[1] = layer
    sqr[8 + z] = layer
    for h in hops:
        h.start()
    @pl.when(d > 0)
    def _():
        to_next.wait_recv()

        @pl.loop(0, EDGE)
        def _(t):
            at, wide = tile_start(w0 - EDGE + t)
            flatten(ebuf.at[0], t, at - base, wide)

    @pl.when(d < 31)
    def _():
        to_prev.wait_recv()

        @pl.loop(0, EDGE)
        def _(t):
            at, wide = tile_start(w0 + mine + t)
            flatten(ebuf.at[1], t, at - base, wide)

    for i in range(4):
        @pl.when(z != i)
        def _():
            arrived(8 + i).wait_recv()
    summed = (sqr[8] + sqr[9]) + (sqr[10] + sqr[11])

    @pl.when(d == 0)
    def _():
        for i in range(3):
            win[pl.ds(FRONT + 774 + i, 1), :] = summed[1 + i : 2 + i]

    sub = lax.broadcasted_iota(jnp.int32, (8, 128), 0)
    entries = jnp.where(sub == 0, summed, jnp.where(sub < 4, summed * summed, 0.0))
    square_sum = jnp.sum(jnp.sum(entries, axis=1, keepdims=True), axis=0, keepdims=True)
    factor = jnp.minimum(1.0, lax.rsqrt(square_sum / RAW + 1e-06))
    for s in shards:
        s.wait()
    lanes = lax.broadcasted_iota(jnp.int32, (80, 128), 1)
    rowi = lax.broadcasted_iota(jnp.int32, (80, 128), 0)
    back = (128 - sh) % 128

    @pl.loop(0, ROWS // 80)
    def _(i):
        r = pl.multiple_of(i * 80, 8)
        here = pltpu.roll(win[pl.ds(FRONT + r, 80), :], back, 1)
        there = pltpu.roll(win[pl.ds(FRONT + 1 + r, 80), :], back, 1)
        grad = jnp.where(lanes < 128 - sh, here, there) * factor
        entry = (d == 0) & (rowi + r < ENTRY_ROWS)
        rate = jnp.where(entry, learn_rate * layer_decay, learn_rate)
        one = beta_one * onev[pl.ds(r, 80), :] + (1.0 - beta_one) * grad
        two = beta_two * twov[pl.ds(r, 80), :] + (1.0 - beta_two) * grad * grad
        fixed_one = one / (1.0 - beta_one ** STEP)
        fixed_two = two / (1.0 - beta_two ** STEP)
        step = -rate * (fixed_one / (jnp.sqrt(fixed_two) + adam_eps) + weight_decay * mv[pl.ds(r, 80), :])
        mv[pl.ds(r, 80), :] = step
        onev[pl.ds(r, 80), :] = one
        twov[pl.ds(r, 80), :] = two

    results = [pltpu.make_async_copy(v, r, lsem.at[i]) for i, (v, r) in enumerate(((mv, step_ref), (onev, new1_ref), (twov, new2_ref)))]
    for copy in results:
        copy.start()

    for h in rounds + hops:
        h.wait_send()

    @pl.when(d < 31)
    def _():
        to_next.wait_send()

    @pl.when(d > 0)
    def _():
        to_prev.wait_send()

    shown.wait()
    for copy in results:
        copy.wait()


def backward_and_step(tiles, query, key_all, value_all, grad_context, soft, code, gfi, low, feats, grads, master, first_moment, second_moment):
    def rows_of(v):
        return jnp.pad(v, (0, ROWS * 128 - SHARD)).reshape(ROWS, 128)

    rows, keys = query.shape[0], key_all.shape[0]
    f32, bf = jnp.float32, jnp.bfloat16
    any_ = pl.BlockSpec(memory_space=pl.ANY)
    S, V, sem = jax.ShapeDtypeStruct, pltpu.VMEM, pltpu.SemaphoreType.DMA
    w = V((96, 8, D), bf)
    tile = (8, D)
    line = V((ROWS, 128), f32)
    outs = pl.pallas_call(
        backward_kernel,
        out_shape=[S((rows, D), f32), S(grads.shape, bf)] + [S((ROWS, 128), f32)] * 3 + [S((keys // 8, H, 8, rows), bf)],
        in_specs=[any_] * 14,
        out_specs=[any_] * 6,
        scratch_shapes=[
            V((2, keys, rows), bf), V((2, rows, 128), bf), V((2, keys, 128), bf), V((2, keys, 128), bf), V((2, rows, 128), bf), sem((5, 2)),
            V((keys, rows), jnp.int32), sem((1,)), V((2, keys // 8, 8, rows), bf), sem((2,)), V((2, 16, H, 8, rows), bf), sem((2,)),
            V((8 * H, 8 * BUCKETS), f32),
            V((2, keys, 128), f32), V((2, keys, 128), f32), V((6, 2, rows, 128), bf), V((6, 2, rows, 128), bf), sem((6,)), sem((6,)),
            V((3, rows, D), bf), V((2, 8, D), f32),
            w, w, w, V((rows, D), bf), V((rows, D), f32), V((rows, LF), bf), V((16, 8, D), bf), w, w, w, V((4, 8, D), bf),
            sem((12,)), sem((24,)), sem((7,)),
            V((37,) + tile, f32), V((2, EDGE) + tile, f32), V((2, 8, 128), f32), V((12, 8, 128), f32),
            V((WIN2, 128), f32), line, line, line, sem((3,)), sem((2,)), sem((2,)), sem((10,)), sem((12,)),
        ] + reducer_scratch() + chain_scratch(),
        input_output_aliases={10: 1},
        compiler_params=pltpu.CompilerParams(collective_id=5, has_side_effects=True, vmem_limit_bytes=63 << 20),
        name="backward_and_step",
    )(tiles, query, key_all, value_all, grad_context, soft, code, gfi, low, feats, grads, rows_of(master), rows_of(first_moment), rows_of(second_moment))
    return outs[0], [o.reshape(-1)[:SHARD] for o in outs[2:5]]


def from_tiles(tiles):
    got = {}
    for name, first, count in WEIGHTS:
        block = jnp.concatenate([tiles[s : s + n] for s, _, n in slots_of(first, count)])
        if name == 12:
            block = block.reshape(96, 4, 8, D).transpose(0, 2, 1, 3)
        got[name] = block.reshape(-1, FF if name == 12 else D)
    for name, chip, row in VECTORS:
        block = tiles[vector_at(chip)]
        if name == 13:
            got[name] = block[row : row + 4].reshape(FF)
        elif name == 2:
            got[name] = block[row, : BUCKETS * H].reshape(BUCKETS, H)
        else:
            got[name] = block[row]
    return [got[i] for i in range(18)]


def to_tiles(whole):
    by_name = [p.astype(jnp.bfloat16) for p in whole]
    weights = []
    for name, first, count in WEIGHTS:
        got = by_name[name]
        if name == 12:
            got = got.reshape(96, 8, 4, D).transpose(0, 2, 1, 3)
        weights.append(got.reshape(count, 8, D))
    cuts = []
    for chip in range(16):
        held = [(r, by_name[n]) for n, c, r in VECTORS if c == chip]
        rows = [jnp.pad(v.reshape(-1), (0, -v.size % D)).reshape(-1, D) for _, v in held]
        block = jnp.concatenate(rows + [jnp.zeros((8 - sum(r.shape[0] for r in rows), D), jnp.bfloat16)])
        cuts.append((73 * chip + vector_slot(chip), block[None]))
    parts = []
    for (name, first, count), tiles in zip(WEIGHTS, weights):
        at = first
        for w, block in [c for c in cuts if first <= c[0] < first + count]:
            if w > at:
                parts.append(tiles[at - first : w - first])
            parts.append(block)
            at = w
        parts.append(tiles[at - first :])
    parts.extend(block for w, block in cuts if w == 1168)
    return jnp.concatenate(parts)


def per_device(
    custom, tokens, cotangent, page_boxes, page_lengths, padding, buckets, master, first_moment, second_moment
):
    rows = tokens.shape[1]
    if custom:
        tiles, hidden, low, query, keys, values, ctx, soft, code, feats = gather_and_attend(
            master, tokens[0], page_boxes, padding, buckets[0], page_lengths
        )
        tiles = tiles.reshape(16 * CHIP, 8, D)
    else:
        feats = layout_features(page_boxes.reshape(4, rows)).astype(jnp.bfloat16)
        tiles = to_tiles(unpack(lax.all_gather(master.astype(jnp.bfloat16), ("dp", "seq"), axis=0, tiled=True)))
        hidden, low, query, keys, values, pads = enter(tiles, tokens[0], feats, jnp.broadcast_to(padding, (8, rows)))
        ctx, soft, code = attend(query, keys, values, buckets[0], page_lengths, pads, tiles[vector_at(0)])
    activations, grad_first_in, grad_context, grads = middle(tiles, ctx, hidden, cotangent[0])
    if custom:
        input_grad, stepped = backward_and_step(
            tiles, query, keys, values, grad_context, soft, code, grad_first_in, low, feats, grads, master, first_moment, second_moment
        )
    else:
        dq, dk, dv, table = soft_back(query, keys, values, grad_context, soft, code)
        input_grad, grads = leave(tiles, dq, dk, dv, grad_first_in, low, feats, table, grads)
        flat = jnp.concatenate([p.astype(jnp.float32).reshape(-1) for p in from_tiles(grads)])
        grad = lax.psum_scatter(flat, ("dp", "seq"), scatter_dimension=0, tiled=True)
        square = lax.psum(jnp.sum(grad * grad), ("dp", "seq"))
        factor = jnp.minimum(1.0, lax.rsqrt(square / RAW + 1e-06))
        size = master.shape[0]
        index = lax.axis_index(("dp", "seq")) * size + jnp.arange(size, dtype=jnp.int32)
        stepped = adam_update(master, first_moment, second_moment, grad * factor, index)
    return (activations[None], input_grad[None]) + tuple(stepped)


def solution(mesh):
    in_specs = (
        P("dp", "seq", None),
        P("dp", "seq", None),
        P(None, "dp", "seq"),
        P("dp", None),
        P("dp", "seq"),
        P("dp", "seq", None),
        P(("dp", "seq")),
        P(("dp", "seq")),
        P(("dp", "seq")),
    )
    out_specs = (
        P("dp", "seq", None),
        P("dp", "seq", None),
        P(("dp", "seq")),
        P(("dp", "seq")),
        P(("dp", "seq")),
    )
    custom = dict(mesh.shape) == {"dp": 16, "seq": 2}
    return jax.shard_map(
        functools.partial(per_device, custom), mesh=mesh, in_specs=in_specs, out_specs=out_specs, check_vma=False
    )
```

```python
import functools
import math

import jax
import jax.numpy as jnp
from jax import lax
from jax.experimental import pallas as pl
from jax.experimental.pallas import tpu as pltpu
from jax.sharding import PartitionSpec as P

D = 768
H = 12
HD = 64
FF = 3072
BUCKETS = 32
FREQ = 16
LF = 128
LAYERS = 1
BLOCK = 1024
STEP = 10
ENTRY = 99456
LAYER_PARAMS = 7087104
RAW = 7186560


beta_one = 0.8
beta_two = 0.98
adam_eps = 1e-06
learn_rate = 0.0006
layer_decay = 0.8
weight_decay = 0.1
norm_eps = 1e-05
masked_score = -1000000000.0


SHAPES = (
    (LF, D), (D,), (BUCKETS, H),
    (D, D), (D,), (D, D), (D, D), (D,), (D, D), (D,), (D,), (D,),
    (D, FF), (FF,), (FF, D), (D,), (D,), (D,),
)


def unpack(flat_params):
    pieces, offset = [], 0
    for shape in SHAPES:
        amount = shape[0] * (shape[1] if len(shape) > 1 else 1)
        pieces.append(flat_params[offset : offset + amount].reshape(shape))
        offset = offset + amount
    return pieces


def adam_update(master, first_moment, second_moment, gradient, global_index):
    exponent = jnp.where(
        global_index < ENTRY,
        LAYERS,
        jnp.maximum(LAYERS - 1 - (global_index - ENTRY) // LAYER_PARAMS, 0),
    )
    rate = jnp.where(
        global_index < RAW, learn_rate * jnp.power(layer_decay, exponent.astype(jnp.float32)), 0.0
    )
    moment_one = beta_one * first_moment + (1.0 - beta_one) * gradient
    moment_two = beta_two * second_moment + (1.0 - beta_two) * gradient * gradient
    fixed_one = moment_one / (1.0 - beta_one**STEP)
    fixed_two = moment_two / (1.0 - beta_two**STEP)
    param_step = -rate * (fixed_one / (jnp.sqrt(fixed_two) + adam_eps) + weight_decay * master)
    return (param_step, moment_one, moment_two)


def layout_features(page_boxes):
    rates_sin = jnp.power(10000.0, -jnp.arange(FREQ, dtype=jnp.float32) / FREQ)
    angles = page_boxes.astype(jnp.float32)[:, :, None] * rates_sin
    stacked = jnp.stack([jnp.sin(angles), jnp.cos(angles)], axis=1)
    return jnp.transpose(stacked, (2, 0, 1, 3)).reshape(page_boxes.shape[1], LF)


MESH = pl.DeviceIdType.MESH
SHARD = 224580
ROWS = 1760
TAIL, HEAD = 160, 176
WIN = 2176
SLOTS = 37
CHIP = 74
PARTS = ((0, 19), (19, 18))


def place():
    k = lax.axis_index("dp")
    return k, lax.axis_index("seq"), k // 4, (k // 2) % 2, k % 2


def shard_start(d):
    return d * 1754 + (d * 68) // 128, (d * 68) % 128


def early_vectors(k):
    return (k == 0) | (k == 4) | (k == 5)


def vector_row(k, other):
    at = other
    for chip, row in ((0, 768), (1, 5385), (4, 14607), (5, 19221), (10, 37671), (15, 56127)):
        at = jnp.where(k == chip, row, at)
    return at


def tile_start(w):
    at = w * 48
    for first, shift in ((16, 777 - 16 * 48), (112, 5391 - 112 * 48), (208, 9999 - 208 * 48), (304, 14613 - 304 * 48), (784, 37695 - 784 * 48)):
        at = jnp.where(w >= first, w * 48 + shift, at)
    wide = (w >= 400) & (w < 784)
    v = w - 400
    at = jnp.where(wide, 19239 + (v // 4) * 192 + (v % 4) * 6, at)
    return at, wide


def neighbours(k, c, z, y, x):
    t = k >= 0
    return [
        (t, (k, 1 - c)),
        (t, (z * 4 + y * 2 + 1 - x, c)),
        (t, (z * 4 + (1 - y) * 2 + x, c)),
        (z < 3, (jnp.minimum(k + 4, 15), c)),
        (z > 0, (jnp.maximum(k - 4, 0), c)),
        ((c == 1) & (k < 15), (jnp.minimum(k + 1, 15), 0)),
        ((c == 0) & (k > 0), (jnp.maximum(k - 1, 0), 1)),
    ]


def greet(k, c, z, y, x):
    bar = pltpu.get_barrier_semaphore()
    for cond, dev in neighbours(k, c, z, y, x):
        @pl.when(cond)
        def _():
            pl.semaphore_signal(bar, inc=1, device_id=dev, device_id_type=MESH)
    peers = 3
    for cond, _ in neighbours(k, c, z, y, x)[3:]:
        peers = peers + jnp.where(cond, 1, 0)
    pl.semaphore_wait(bar, peers)


def rcopy(src, dst, ssem, rsem, dev):
    return pltpu.make_async_remote_copy(src_ref=src, dst_ref=dst, send_sem=ssem, recv_sem=rsem, device_id=dev, device_id_type=MESH)


FRONT = 344
WIN2 = 2464
EDGE = 4
ENTRY_ROWS = 777


WEIGHTS = (
    (0, 0, 16),
    (3, 16, 96),
    (5, 112, 96),
    (6, 208, 96),
    (8, 304, 96),
    (12, 400, 384),
    (14, 784, 384),
)
VECTORS = (
    (1, 0, 0),
    (2, 0, 1),
    (4, 1, 0),
    (7, 4, 0),
    (9, 5, 0),
    (10, 5, 1),
    (11, 5, 2),
    (13, 10, 0),
    (15, 15, 0),
    (16, 15, 1),
    (17, 15, 2),
)


def slots_of(first, count):
    runs = []
    for w in range(first, first + count):
        chip, at = divmod(w, 73)
        slot = chip * CHIP + at + (1 if at >= vector_slot(chip) else 0)
        if runs and runs[-1][0] + runs[-1][2] == slot:
            runs[-1][2] += 1
        else:
            runs.append([slot, w - first, 1])
    return runs


def vector_slot(chip):
    return 36 if chip in (0, 4, 5) else 73


def vector_at(chip):
    return chip * CHIP + vector_slot(chip)


def pieces(tiles, held, first, count, sems, base, out=False):
    made = []
    for i, (slot, at, n) in enumerate(slots_of(first, count)):
        a, b = tiles.at[pl.ds(slot, n)], held.at[pl.ds(at, n)]
        a, b = (b, a) if out else (a, b)
        made.append(pltpu.make_async_copy(a, b, sems.at[base + i]))
    return made


def matrix(tile_rows):
    return tile_rows.reshape(-1, D)


def col_sum(v):
    return jnp.sum(v.reshape(-1, 8, v.shape[-1]), axis=0)


def norm_stats(v):
    mean = jnp.mean(v, axis=-1, keepdims=True)
    center = v - mean
    spread = jnp.mean(center * center, axis=-1, keepdims=True)
    inv = lax.rsqrt(spread + norm_eps)
    return center * inv, inv


def norm_back(grad, gain, hat, inv):
    g = grad * gain
    return inv * (g - jnp.mean(g, axis=-1, keepdims=True) - hat * jnp.mean(g * hat, axis=-1, keepdims=True))


ROOT_HALF = 0.7071067811865476
ROOT_TAU = 0.3989422804014327


def middle_kernel(tiles, ctx_in, hidden_in, cot_in, act_hbm, gfi_hbm, gctx_hbm, grads,
                  ctx, hidden, cot, act_out, gfi_out, gctx_out, iosem, wo, wup, wdn, vecs, vf, act, slope, low1, hat1, inv1, hat2, inv2, a, sums, dwo, dwup, dwdn, vgrads, lsem, ssem):
    f32, bf = jnp.float32, jnp.bfloat16
    rows = ctx.shape[0]
    R = 128
    steps = rows // R
    loads_o = pieces(tiles, wo, 304, 96, lsem, 0)
    loads_u = pieces(tiles, wup, 400, 384, lsem, 4)
    loads_d = pieces(tiles, wdn, 784, 384, lsem, 12)
    loads_v = [pltpu.make_async_copy(tiles.at[vector_at(c)], vecs.at[i], lsem.at[20 + i]) for i, c in enumerate((5, 10, 15))]
    ins = [pltpu.make_async_copy(r, v, iosem.at[i]) for i, (r, v) in enumerate(((ctx_in, ctx), (hidden_in, hidden), (cot_in, cot)))]
    outs = [pltpu.make_async_copy(v, r, iosem.at[3 + i]) for i, (v, r) in enumerate(((act_out, act_hbm), (gfi_out, gfi_hbm), (gctx_out, gctx_hbm)))]
    for c in ins[:1] + loads_v + loads_o + ins[1:2] + loads_u + loads_d + ins[2:]:
        c.start()
    up4 = wup.reshape(96, 4, 8, D)
    dup4 = dwup.reshape(96, 4, 8, D)

    def vec(i, r):
        return vf[i, pl.ds(r, 1), :]

    def each(f):
        @pl.loop(0, steps)
        def _(i):
            f(pl.ds(pl.multiple_of(i * R, R), R))

    for c in ins[:2] + loads_v + loads_o:
        c.wait()
    vf[...] = vecs[...].astype(f32)
    a[...] = jnp.dot(ctx[...], matrix(wo[...]), preferred_element_type=f32)

    def first(sl):
        hat, inv = norm_stats(hidden[sl, :] + a[sl, :] + vec(0, 0))
        hat1[sl, :] = hat
        inv1[sl, :] = inv
        out = hat * vec(0, 1) + vec(0, 2)
        a[sl, :] = out
        low1[sl, :] = out.astype(bf)

    each(first)
    for c in loads_u:
        c.wait()

    def up(j, _):
        for half in range(2):
            sl = pl.ds(half * (rows // 2), rows // 2)
            u = jnp.dot(low1[sl, :], matrix(up4[:, j]), preferred_element_type=f32) + vec(1, j)
            share = 0.5 * (1.0 + lax.erf(u * ROOT_HALF))
            act[j, sl, :] = (u * share).astype(bf)
            slope[j, sl, :] = share + u * jnp.exp(-0.5 * u * u) * ROOT_TAU
        return 0

    lax.fori_loop(0, 4, up, 0)
    for c in loads_d:
        c.wait()

    def down(j, _):
        a[...] += jnp.dot(act[j], matrix(wdn[pl.ds(96 * j, 96)]), preferred_element_type=f32)
        return 0

    lax.fori_loop(0, 4, down, 0)
    sums[...] = jnp.zeros_like(sums)

    def second(sl):
        hat, inv = norm_stats(a[sl, :] + vec(2, 0))
        act_out[sl, :] = (hat * vec(2, 1) + vec(2, 2)).astype(bf)
        g = cot[sl, :].astype(f32)
        sums[6] += col_sum(g * hat)
        sums[7] += col_sum(g)
        back = norm_back(g, vec(2, 1), hat, inv)
        sums[5] += col_sum(back)
        a[sl, :] = back
        hat2[sl, :] = back.astype(bf)

    ins[2].wait()
    each(second)
    outs[0].start()
    down_back = hat2

    def back(j, _):
        for half in range(2):
            sl = pl.ds(half * (rows // 2), rows // 2)
            g = lax.dot_general(down_back[sl, :], matrix(wdn[pl.ds(96 * j, 96)]), NT, preferred_element_type=f32) * slope[j, sl, :]
            sums[8 + j] += col_sum(g)
            act_back[sl, :] = g.astype(bf)
        dwdn[pl.ds(96 * j, 96)] = lax.dot_general(act[j], down_back[...], TN, preferred_element_type=f32).astype(bf).reshape(96, 8, D)
        dup4[:, j] = lax.dot_general(low1[...], act_back[...], TN, preferred_element_type=f32).astype(bf).reshape(96, 8, D)
        a[...] += lax.dot_general(act_back[...], matrix(up4[:, j]), NT, preferred_element_type=f32)
        return 0

    act_back = inv2
    lax.fori_loop(0, 4, back, 0)
    stores = pieces(grads, dwup, 400, 384, ssem, 4, True) + pieces(grads, dwdn, 784, 384, ssem, 12, True)
    for c in stores:
        c.start()

    def third(sl):
        g = a[sl, :]
        sums[3] += col_sum(g * hat1[sl, :])
        sums[4] += col_sum(g)
        back = norm_back(g, vec(0, 1), hat1[sl, :], inv1[sl, :])
        sums[2] += col_sum(back)
        gfi_out[sl, :] = back
        hat2[sl, :] = back.astype(bf)

    each(third)
    outs[1].start()
    gctx_out[...] = lax.dot_general(hat2[...], matrix(wo[...]), NT, preferred_element_type=f32).astype(bf)
    outs[2].start()
    dwo[...] = lax.dot_general(ctx[...], hat2[...], TN, preferred_element_type=f32).astype(bf).reshape(96, 8, D)
    for i, held in enumerate(((2, 3, 4), (8, 9, 10, 11), (5, 6, 7))):
        lines = [jnp.sum(sums[s], axis=0, keepdims=True) for s in held]
        lines.append(jnp.zeros((8 - len(held), D), f32))
        vgrads[i] = jnp.concatenate(lines).astype(bf)
    last = pieces(grads, dwo, 304, 96, ssem, 0, True)
    quiet = [ch for ch in range(6, 15) if ch != 10]
    vgrads[3] = jnp.zeros((8, D), bf)
    last += [pltpu.make_async_copy(vgrads.at[min(i, 3)], grads.at[vector_at(ch)], ssem.at[20 + i]) for i, ch in enumerate([5, 10, 15] + quiet)]
    for c in last:
        c.start()
    for c in stores + last + outs:
        c.wait()


def middle(tiles, ctx, hidden, cot):
    rows = ctx.shape[0]
    f32, bf = jnp.float32, jnp.bfloat16
    vm, any_ = pl.BlockSpec(memory_space=pltpu.VMEM), pl.BlockSpec(memory_space=pl.ANY)
    S = jax.ShapeDtypeStruct
    return pl.pallas_call(
        middle_kernel,
        out_shape=[S((rows, D), bf), S((rows, D), f32), S((rows, D), bf), S((16 * CHIP, 8, D), bf)],
        in_specs=[any_] * 4,
        out_specs=[any_] * 4,
        scratch_shapes=[
            pltpu.VMEM((rows, D), bf), pltpu.VMEM((rows, D), f32), pltpu.VMEM((rows, D), bf),
            pltpu.VMEM((rows, D), bf), pltpu.VMEM((rows, D), f32), pltpu.VMEM((rows, D), bf), pltpu.SemaphoreType.DMA((6,)),
            pltpu.VMEM((96, 8, D), bf), pltpu.VMEM((384, 8, D), bf), pltpu.VMEM((384, 8, D), bf), pltpu.VMEM((3, 8, D), bf), pltpu.VMEM((3, 8, D), f32),
            pltpu.VMEM((4, rows, D), bf), pltpu.VMEM((4, rows, D), f32), pltpu.VMEM((rows, D), bf),
            pltpu.VMEM((rows, D), f32), pltpu.VMEM((rows, 1), f32), pltpu.VMEM((rows, D), bf), pltpu.VMEM((rows, D), bf),
            pltpu.VMEM((rows, D), f32), pltpu.VMEM((12, 8, D), f32),
            pltpu.VMEM((96, 8, D), bf), pltpu.VMEM((384, 8, D), bf), pltpu.VMEM((384, 8, D), bf), pltpu.VMEM((4, 8, D), bf),
            pltpu.SemaphoreType.DMA((24,)), pltpu.SemaphoreType.DMA((32,)),
        ],
        compiler_params=pltpu.CompilerParams(vmem_limit_bytes=58 << 20),
        name="middle",
    )(tiles, ctx, hidden, cot)


NT = (((1,), (1,)), ((), ()))
TN = (((0,), (0,)), ((), ()))


def half(ref_value, hh):
    lanes = lax.broadcasted_iota(jnp.int32, ref_value.shape, 1)
    keep = lanes // 64 == hh
    return jnp.where(keep, ref_value, jnp.zeros_like(ref_value))


def page_of(at, lengths):
    end, page = 0, jnp.zeros(at.shape, jnp.int32)
    for i in range(4):
        end = end + lengths[0, i]
        page = page + jnp.where(at >= end, 1, 0)
    return page


def fill_codes(code_ref, buckets, pads, lengths):
    keys, rows = code_ref.shape
    own = lax.axis_index("seq") * rows
    tag = page_of(lax.broadcasted_iota(jnp.int32, (1, keys), 1), lengths) + 1
    tag = jnp.where(jnp.concatenate([pads[0, 0:1], pads[1, 0:1]], axis=1) > 0, tag, 0)
    for i in range(rows // 128):
        at = own + 128 * i + lax.broadcasted_iota(jnp.int32, (128, 1), 0)
        page = page_of(at, lengths) + 1
        for j in range(keys // 128):
            key_at = 128 * j + lax.broadcasted_iota(jnp.int32, (1, 128), 1)
            allowed = (page == tag[:, 128 * j : 128 * j + 128]) | (key_at == at)
            code = jnp.where(allowed, buckets[128 * i : 128 * i + 128, 128 * j : 128 * j + 128], BUCKETS)
            code_ref[128 * j : 128 * j + 128, 128 * i : 128 * i + 128] = code.T


def fill_table(tab_ref, lines):
    f32 = jnp.float32
    head = lax.broadcasted_iota(jnp.int32, (16, 128), 0)
    bucket = lax.broadcasted_iota(jnp.int32, (16, 128), 1)
    place_of = bucket * H + head
    tab = jnp.full((16, 128), masked_score, f32)
    for i in range(BUCKETS * H // 128):
        row = jnp.broadcast_to(lines[1:2, 128 * i : 128 * i + 128].astype(f32), (16, 128))
        inside = jnp.clip(place_of - 128 * i, 0, 127)
        got = jnp.take_along_axis(row, inside, axis=1, mode="promise_in_bounds")
        tab = jnp.where((place_of // 128 == i) & (bucket < BUCKETS) & (head < H), got, tab)
    tab_ref[...] = tab


def soft_head(head, q, k, code_ref, tab_ref, s_scr, p_ref):
    keys, rows = s_scr.shape
    f32, bf = jnp.float32, jnp.bfloat16
    qm = half(q, head % 2)
    line = jnp.broadcast_to(tab_ref[pl.ds(head, 1), :], (keys, 128))
    s = lax.dot_general(k, qm, NT, preferred_element_type=f32)
    cols = []
    for j in range(rows // 128):
        code = code_ref[:, 128 * j : 128 * j + 128]
        bias = jnp.take_along_axis(line, code, axis=1, mode="promise_in_bounds")
        cols.append(jnp.where(bias < 0.5 * masked_score, masked_score, s[:, 128 * j : 128 * j + 128] + bias))
    s = jnp.concatenate(cols, axis=1)
    s_scr[...] = s
    top = jnp.max(jnp.max(s.reshape(keys // 8, 8, rows), axis=0), axis=0, keepdims=True)
    e = jnp.exp(s_scr[...] - top)
    inverse = 1.0 / jnp.sum(jnp.sum(e.reshape(keys // 8, 8, rows), axis=0), axis=0, keepdims=True)
    p_ref[...] = (jnp.exp(s_scr[...] - top) * inverse).astype(bf)


def context_pair(v, p_ref):
    vt = v.T
    out = [jnp.dot(vt, p_ref[hh], preferred_element_type=jnp.float32) for hh in range(2)]
    sub = lax.broadcasted_iota(jnp.int32, out[0].shape, 0)
    return jnp.where(sub < 64, out[0], out[1]).T.astype(jnp.bfloat16)


def attend_kernel(lengths, q_ref, k_ref, v_ref, buckets, pads, lines, ctx_ref, p_ref, code_ref, s_scr, tab_ref):
    pair = pl.program_id(0)

    @pl.when(pair == 0)
    def _():
        fill_codes(code_ref, buckets, pads, lengths)
        fill_table(tab_ref, lines)

    for hh in range(2):
        soft_head(2 * pair + hh, q_ref[...], k_ref[...], code_ref, tab_ref, s_scr, p_ref.at[hh])
    ctx_ref[...] = context_pair(v_ref[...], p_ref)


def attend(query, key_all, value_all, buckets, page_lengths, pads, lines):
    rows, keys = query.shape[0], key_all.shape[0]
    bf = jnp.bfloat16
    const = lambda p: (0, 0)
    return pl.pallas_call(
        attend_kernel,
        grid=(H // 2,),
        out_shape=[
            jax.ShapeDtypeStruct((rows, D), bf),
            jax.ShapeDtypeStruct((H, keys, rows), bf),
            jax.ShapeDtypeStruct((keys, rows), jnp.int32),
        ],
        in_specs=[
            pl.BlockSpec(memory_space=pltpu.SMEM),
            pl.BlockSpec((rows, 128), lambda p: (0, p)),
            pl.BlockSpec((keys, 128), lambda p: (0, p)),
            pl.BlockSpec((keys, 128), lambda p: (0, p)),
            pl.BlockSpec((rows, keys), const),
            pl.BlockSpec((2, 8, rows), lambda p: (0, 0, 0)),
            pl.BlockSpec((8, D), const),
        ],
        out_specs=[pl.BlockSpec((rows, 128), lambda p: (0, p)), pl.BlockSpec((2, keys, rows), lambda p: (p, 0, 0)), pl.BlockSpec((keys, rows), const)],
        scratch_shapes=[pltpu.VMEM((keys, rows), jnp.float32), pltpu.VMEM((16, 128), jnp.float32)],
        compiler_params=pltpu.CompilerParams(vmem_limit_bytes=56 << 20),
        name="attend",
    )(page_lengths, query, key_all, value_all, buckets, pads, lines)


def table_row(acc, shape):
    f32 = jnp.float32
    a = lax.broadcasted_iota(jnp.int32, acc.shape, 0) % 8
    b = lax.broadcasted_iota(jnp.int32, acc.shape, 1) // BUCKETS
    acc = jnp.where(a == b, acc, 0.0)
    heads = jnp.sum(acc.reshape(H, 8, 8 * BUCKETS), axis=1)
    lane = lax.broadcasted_iota(jnp.int32, (8 * BUCKETS, D), 1) // H
    wide = jnp.where(lane == lax.broadcasted_iota(jnp.int32, lane.shape, 0) % BUCKETS, 1.0, 0.0)
    out = jnp.dot(heads, wide, precision=lax.Precision.HIGHEST, preferred_element_type=f32)
    mine = lax.broadcasted_iota(jnp.int32, out.shape, 1) % H == lax.broadcasted_iota(jnp.int32, out.shape, 0)
    out = jnp.sum(jnp.where(mine, out, 0.0), axis=0, keepdims=True)
    return jnp.broadcast_to(out, shape)


def attend_back_kernel(q_ref, k_ref, v_ref, do_ref, p_ref, code_ref, dq_ref, dk_ref, dv_ref, tab_ref, spread, held):
    pair = pl.program_id(0)
    keys, rows = code_ref.shape
    f32, bf = jnp.float32, jnp.bfloat16
    STEP_ROWS = keys
    kt = k_ref[...].T
    dq = []
    for hh in range(2):
        qm = half(q_ref[...], hh)
        dom = half(do_ref[...], hh)

        def inner(i, total):
            at = pl.multiple_of(i * STEP_ROWS, STEP_ROWS)
            g = lax.dot_general(v_ref[pl.ds(at, STEP_ROWS), :], dom, NT, preferred_element_type=f32)
            w = g * p_ref[hh, pl.ds(at, STEP_ROWS), :].astype(f32)
            return total + jnp.sum(w.reshape(STEP_ROWS // 8, 8, rows), axis=0)

        total = lax.fori_loop(0, keys // STEP_ROWS, inner, jnp.zeros((8, rows), f32))
        total = jnp.sum(total, axis=0, keepdims=True)

        def grads(i, acc):
            at = pl.multiple_of(i * STEP_ROWS, STEP_ROWS)
            sl = pl.ds(at, STEP_ROWS)
            g = lax.dot_general(v_ref[sl, :], dom, NT, preferred_element_type=f32)
            p = p_ref[hh, sl, :]
            ds = p.astype(f32) * (g - total)
            wide = ds.reshape(STEP_ROWS // 8, 8, rows)
            if hh == 0:
                held[...] = wide
            else:
                both = jnp.concatenate([held[...], wide], axis=1).astype(bf)
                spread[:, pl.ds(pl.multiple_of(pair * 16, 16), 16), :] = both
            ds = ds.astype(bf)
            dv = jnp.dot(p, dom, preferred_element_type=f32)
            dk = jnp.dot(ds, qm, preferred_element_type=f32)
            if hh == 0:
                dv_ref[sl, :] = dv
                dk_ref[sl, :] = dk
            else:
                dv_ref[sl, :] += dv
                dk_ref[sl, :] += dk
            return acc + lax.dot_general(k_ref[sl, :], ds, TN, preferred_element_type=f32)

        dq.append(lax.fori_loop(0, keys // STEP_ROWS, grads, jnp.zeros((128, rows), f32)))
    sub = lax.broadcasted_iota(jnp.int32, dq[0].shape, 0)
    dq_ref[...] = jnp.where(sub < 64, dq[0], dq[1]).T * 0.125

    @pl.when(pair == H // 2 - 1)
    def _():
        bucket = lax.broadcasted_iota(jnp.int32, (BUCKETS, rows), 0)

        def count(i, acc):
            code = code_ref[pl.ds(pl.multiple_of(i * 8, 8), 8), :]
            hot = jnp.concatenate(
                [jnp.where(jnp.broadcast_to(code[r : r + 1], bucket.shape) == bucket, 1.0, 0.0) for r in range(8)]
            ).astype(bf)
            return acc + lax.dot_general(spread[i], hot, NT, preferred_element_type=f32)

        acc = lax.fori_loop(0, keys // 8, count, jnp.zeros((8 * H, 8 * BUCKETS), f32), unroll=8)
        tab_ref[...] = table_row(acc, tab_ref.shape)


def soft_back(query, key_all, value_all, grad_context, soft, code):
    rows, keys = query.shape[0], key_all.shape[0]
    f32 = jnp.float32
    row = pl.BlockSpec((rows, 128), lambda p: (0, p))
    key = pl.BlockSpec((keys, 128), lambda p: (0, p))
    dq, dk, dv, tab = pl.pallas_call(
        attend_back_kernel,
        grid=(H // 2,),
        out_shape=[
            jax.ShapeDtypeStruct((rows, D), f32),
            jax.ShapeDtypeStruct((keys, D), f32),
            jax.ShapeDtypeStruct((keys, D), f32),
            jax.ShapeDtypeStruct((8, D), f32),
        ],
        in_specs=[row, key, key, row, pl.BlockSpec((2, keys, rows), lambda p: (p, 0, 0)), pl.BlockSpec((keys, rows), lambda p: (0, 0))],
        out_specs=[row, key, key, pl.BlockSpec((8, D), lambda p: (0, 0))],
        scratch_shapes=[pltpu.VMEM((keys // 8, 8 * H, rows), jnp.bfloat16), pltpu.VMEM((keys // 8, 8, rows), f32)],
        compiler_params=pltpu.CompilerParams(vmem_limit_bytes=58 << 20),
        name="attend_back",
    )(query, key_all, value_all, grad_context, soft, code)
    return dq, dk, dv, tab


def meet_partner():
    dp, c = lax.axis_index("dp"), lax.axis_index("seq")
    partner = (dp, 1 - c)
    bar = pltpu.get_barrier_semaphore()
    pl.semaphore_signal(bar, inc=1, device_id=partner, device_id_type=MESH)
    pl.semaphore_wait(bar, 1)
    return c, partner


def enter_kernel(tiles, tokens, feats, pad, hidden, low, query, keys, values, pads, wl, wq, wk, wv, vecs, vf, lsem, sends, recvs):
    f32, bf = jnp.float32, jnp.bfloat16
    rows = tokens.shape[0]
    loads = [pltpu.make_async_copy(tiles.at[vector_at(ch)], vecs.at[i], lsem.at[i]) for i, ch in enumerate((0, 1, 4))]
    loads += pieces(tiles, wl, 0, 16, lsem, 4) + pieces(tiles, wk, 112, 96, lsem, 8)
    loads += pieces(tiles, wv, 208, 96, lsem, 12) + pieces(tiles, wq, 16, 96, lsem, 16)
    for c in loads:
        c.start()
    c, partner = meet_partner()
    own = pl.ds(c * rows, rows)

    def share(ref, i):
        return rcopy(ref.at[own], ref.at[own], sends.at[i], recvs.at[i], partner)

    pads[pl.ds(c, 1)] = pad[...].reshape(1, 8, rows)
    pair_pads = rcopy(pads.at[pl.ds(c, 1)], pads.at[pl.ds(c, 1)], sends.at[2], recvs.at[2], partner)
    pair_pads.start()
    for copy in loads:
        copy.wait()
    vf[...] = vecs[...].astype(f32)
    h = tokens[...].astype(f32) + jnp.dot(feats[...], matrix(wl[...]), preferred_element_type=f32) + vf[0, 0:1, :]
    hidden[...] = h
    low[...] = h.astype(bf)
    keys[own, :] = jnp.dot(low[...], matrix(wk[...]), preferred_element_type=f32).astype(bf)
    send_keys = share(keys, 0)
    send_keys.start()
    values[own, :] = (jnp.dot(low[...], matrix(wv[...]), preferred_element_type=f32) + vf[2, 0:1, :]).astype(bf)
    send_values = share(values, 1)
    send_values.start()
    query[...] = ((jnp.dot(low[...], matrix(wq[...]), preferred_element_type=f32) + vf[1, 0:1, :]) * 0.125).astype(bf)
    for copy in (pair_pads, send_keys, send_values):
        copy.wait()


def enter(tiles, tokens, feats, pad):
    rows = tokens.shape[0]
    f32, bf = jnp.float32, jnp.bfloat16
    vm, any_ = pl.BlockSpec(memory_space=pltpu.VMEM), pl.BlockSpec(memory_space=pl.ANY)
    S, sem = jax.ShapeDtypeStruct, pltpu.SemaphoreType.DMA
    w = pltpu.VMEM((96, 8, D), bf)
    return pl.pallas_call(
        enter_kernel,
        out_shape=[S((rows, D), f32), S((rows, D), bf), S((rows, D), bf), S((2 * rows, D), bf), S((2 * rows, D), bf), S((2, 8, rows), jnp.int32)],
        in_specs=[any_, vm, vm, vm],
        out_specs=[vm] * 6,
        scratch_shapes=[pltpu.VMEM((16, 8, D), bf), w, w, w, pltpu.VMEM((3, 8, D), bf), pltpu.VMEM((3, 8, D), f32), sem((20,)), sem((3,)), sem((3,))],
        compiler_params=pltpu.CompilerParams(collective_id=2, has_side_effects=True, vmem_limit_bytes=40 << 20),
        name="enter",
    )(tiles, tokens, feats, pad)


def leave_kernel(tiles, dq, dk, dv, gfi, low, feats, table, grads_in, input_grad, grads,
                 wq, wk, wv, out, come, back, dwl, dwq, dwk, dwv, vgrads, lsem, ssem, sends, recvs):
    f32, bf = jnp.float32, jnp.bfloat16
    rows = gfi.shape[0]
    loads = pieces(tiles, wk, 112, 96, lsem, 0) + pieces(tiles, wv, 208, 96, lsem, 4) + pieces(tiles, wq, 16, 96, lsem, 8)
    for c in loads:
        c.start()
    c, partner = meet_partner()
    own, other = pl.ds(c * rows, rows), pl.ds((1 - c) * rows, rows)
    swaps = []
    for i, ref in enumerate((dk, dv)):
        out[i] = ref[other, :].astype(bf)
        swaps.append(rcopy(out.at[i], come.at[i], sends.at[i], recvs.at[i], partner))
        swaps[i].start()
    back[0] = dq[...].astype(bf)
    query_bias = jnp.sum(col_sum(dq[...]), axis=0, keepdims=True)
    for copy in loads:
        copy.wait()

    def through(i, w, dw):
        dw[...] = lax.dot_general(low[...], back[i], TN, preferred_element_type=f32).astype(bf).reshape(96, 8, D)
        return lax.dot_general(back[i], matrix(w[...]), NT, preferred_element_type=f32)

    input_grad[...] = gfi[...] + through(0, wq, dwq)
    stores = pieces(grads, dwq, 16, 96, ssem, 0, True)
    swaps[0].wait_recv()
    back[1] = (dk[own, :] + come[0].astype(f32)).astype(bf)
    input_grad[...] += through(1, wk, dwk)
    stores += pieces(grads, dwk, 112, 96, ssem, 4, True)
    swaps[1].wait_recv()
    grad_value = dv[own, :] + come[1].astype(f32)
    value_bias = jnp.sum(col_sum(grad_value), axis=0, keepdims=True)
    back[2] = grad_value.astype(bf)
    total = input_grad[...] + through(2, wv, dwv)
    stores += pieces(grads, dwv, 208, 96, ssem, 8, True)
    input_grad[...] = total
    layout_bias = jnp.sum(col_sum(total), axis=0, keepdims=True)
    dwl[...] = lax.dot_general(feats[...], total.astype(bf), TN, preferred_element_type=f32).astype(bf).reshape(16, 8, D)
    stores += pieces(grads, dwl, 0, 16, ssem, 12, True)

    def block(lines):
        return jnp.concatenate(lines + [jnp.zeros((8 - len(lines), D), f32)]).astype(bf)

    vgrads[0] = block([layout_bias, table[0:1, :]])
    vgrads[1] = block([query_bias])
    vgrads[2] = block([value_bias])
    vgrads[3] = jnp.zeros((8, D), bf)
    held = {0: 0, 1: 1, 4: 2}
    for i, chip in enumerate(ch for ch in range(5)):
        stores.append(pltpu.make_async_copy(vgrads.at[held.get(chip, 3)], grads.at[vector_at(chip)], ssem.at[16 + i]))
    for copy in stores:
        copy.start()
    for copy in stores:
        copy.wait()
    for swap in swaps:
        swap.wait_send()


def leave(tiles, dq, dk, dv, gfi, low, feats, table, grads):
    rows = gfi.shape[0]
    f32, bf = jnp.float32, jnp.bfloat16
    vm, any_ = pl.BlockSpec(memory_space=pltpu.VMEM), pl.BlockSpec(memory_space=pl.ANY)
    S, sem = jax.ShapeDtypeStruct, pltpu.SemaphoreType.DMA
    w = pltpu.VMEM((96, 8, D), bf)
    return pl.pallas_call(
        leave_kernel,
        out_shape=[S((rows, D), f32), S(grads.shape, bf)],
        in_specs=[any_] + [vm] * 7 + [any_],
        out_specs=[vm, any_],
        scratch_shapes=[w, w, w, pltpu.VMEM((2, rows, D), bf), pltpu.VMEM((2, rows, D), bf), pltpu.VMEM((3, rows, D), bf),
                        pltpu.VMEM((16, 8, D), bf), w, w, w, pltpu.VMEM((4, 8, D), bf), sem((12,)), sem((32,)), sem((2,)), sem((2,))],
        input_output_aliases={8: 1},
        compiler_params=pltpu.CompilerParams(collective_id=3, has_side_effects=True, vmem_limit_bytes=56 << 20),
        name="leave",
    )(tiles, dq, dk, dv, gfi, low, feats, table, grads)


GATHER_PARTS = ((0, 8), (8, 7), (15, 7), (22, 7), (29, 4), (33, 4))
GATHER_STEPS = (
    ((647, 384, 128, 256, 385, 129, 257, 386, 130, 258, 387, 131, 259, 388, 132, 260, 389, 133, 261),
     (17, 145, 8, 264, 19, 147, 12, 396, 20, 404, 10, 266, 9, 11, 13, 655, 397, 16, 18, 21, 663, 32, 33, 34, 35, 36, 37, 679, 405, 149, 268, 160, 288, 161, 289, 29, 413, 24, 25, 26, 27, 28, 671, 412, 162, 290),
     {-1: (163, 291), 0: (49, 177, 40, 296, 64, 65, 66, 67, 68, 69, 711), 1: (42, 298, 51, 179, 192), 2: (320,), 3: (41, 43, 44, 45, 687, 193, 321, 48, 50, 52, 53, 695), 4: (194, 322), 5: (195, 323, 56, 57, 58, 59, 60, 61, 703), 6: (96, 224, 352), 7: (97, 225, 353), 8: (81, 209, 72, 328, 98, 99, 100, 101, 743), 9: (226, 74, 330), 10: (227, 354, -1), 11: (73, 75, 76, 77, 719, 83, 211, 355, 113, 241, 104, 360, 105, 106, 107, 108, 109, 751, 80, 82, 84, 85, 727, 362, 112, 114, 115, 116, 117, 759, 243, 120, 121, 122, 123, 124, 125, 767, 88, 89, 90, 91, 92, 93, 735)}),
    ((679, 544, 416, 160, 288, 545, 417, 161, 289, 546),
     (0, 384, 128, 256, 547, 1, 385, 129, 257, 548, 549, 2, 386, 130, 258, 64, 576, 8, 264, 3, 387, 131, 17, 145, 4, 388, 65, 577, 259, 5, 647, 66, 67, 68, 69, 711, 389, 162, 578, 10, 266, 12, 396, 20, 404, 579, 290, 9, 11, 13, 655, 397, 19, 147, 163, 16, 18, 21, 663, 405, 580, 291, 418, 581, 164, 292, 96, 608, 29, 413, 165, 293, 24, 25, 26, 27, 28, 671, 412, 49, 177, 40, 296, 419),
     {-1: (97, 98, 99, 100, 101, 743, 51, 179, 44, 556, 52, 564, 42, 298, 420, 41, 43, 45, 687, 557, 48, 50, 53, 695, 565, 421, 181), 0: (300, 609, 428, 192, 320, 436), 1: (429, 193, 321, 61, 573), 2: (437, 56, 57, 58, 59, 60, 703, 572, 610, 194, 445, 322), 3: (444, 611, 195, 323), 4: (612, 224, 352), 5: (613, 108, 620, 225, 353), 6: (76, 588, 72, 73, 74, 75, 77, 719, 226, 116, 628, 354), 7: (589, 227, 109, 621, 355), 8: (84, 596, 81, 209, 80, 82, 83, 85, 727, 328, 117, 629), 9: (597, 211, 330), 10: (104, 105, 106, 107, 751, 112, 113, 114, 115, 759, 241, 360, -1), 11: (243, 362, 125, 637, 124, 636, 93, 605, 88, 89, 90, 91, 92, 735, 604, 120, 121, 122, 123, 767)}),
    ((711, 576, 448, 192, 320, 577, 449, 193, 321, 578),
     (32, 416, 160, 288, 579, 33, 417, 161, 289, 580, 581, 0, 384, 128, 256, 96, 608, 1, 385, 129, 257, 97, 609, 98, 99, 100, 101, 743, 2, 386, 130, 258, 610, 8, 264, 3, 387, 131, 611, 17, 145, 4, 388, 259, 5, 647, 389, 612, 49, 177, 10, 266, 12, 396, 613, 20, 404, 40, 296, 9, 11, 13, 655, 397, 19, 147, 16, 18, 21, 663, 405, 34, 162, 290, 418, 194, 322, 29, 413, 195, 24, 25, 26, 27, 28, 671, 412, 42, 298),
     {-1: (35, 419, 163, 291, 36, 420, 196, 37, 679, 421, 323), 0: (197, 44, 428, 324, 52, 436), 1: (108, 620, 325, 41, 43, 45, 687, 429, 51, 179, 224, 76, 588, 72, 328), 2: (48, 50, 53, 695, 437, 116, 628, 73, 74, 75, 77, 719, 589, 61, 445, 81, 209, 109, 621), 3: (84, 596, 352, 60, 444, 56, 57, 58, 59, 703, 117, 629, 80, 82, 83, 85, 727, 450, 225), 4: (597, 353, 451, 226), 5: (354, 452, 227), 6: (453, 355, 460, 211), 7: (330, 461, 213, 468), 8: (332, 113, 241, 104, 105, 106, 107, 751, 469, 360, 112, 114, 115, 759), 9: (125, 637, 243, 124, 636, 362, 93, 477, 605), 10: (88, 89, 90, 91, 92, 735, 476, 604, -1), 11: (120, 121, 122, 123, 767)}),
    ((743, 608, 224, 352, 609, 225, 353, 610, 226, 354, 611, 227, 355, 612, 613),
     (32, 160, 288, 33, 161, 289, 0, 128, 256, 1, 129, 257, 2, 130, 8, 264, 258, 17, 145, 3, 131, 259, 4, 5, 647, 49, 177, 10, 266, 40, 296, 9, 11, 12, 13, 655, 19, 147, 228, 16, 18, 20, 21, 663, 34, 290, 162, 356, 229, 357, 64, 192, 24, 25, 26, 27, 28, 29, 671, 108, 620),
     {-1: (42, 298, 35, 163, 291, 116, 628, 104, 105, 106, 107, 109, 751, 621, 117, 629, 112, 113, 114, 115, 759, 65, 193, 36, 37, 679, 320), 0: (360,), 1: (41, 43, 44, 45, 687, 51, 179, 241), 2: (48, 50, 52, 53, 695, 321, 243), 3: (362, 56, 57, 58, 59, 60, 61, 703, 245), 4: (364, 66, 194, 72, 328), 5: (81, 209, 322, 125, 637), 6: (67, 195, 120, 121, 122, 123, 124, 767, 636, 68, 69, 711, 323), 7: (74, 330), 8: (73, 75, 76, 77, 719), 9: (83, 211, 80, 82, 84, 85, 727), 10: (-1,), 11: (88, 89, 90, 91, 92, 93, 735)}),
)


def fill_features(out, boxes):
    rows = out.shape[0]
    f32 = jnp.float32
    cols = jnp.concatenate([boxes[i].astype(f32) for i in range(4)] + [jnp.zeros((4, rows), f32)]).T
    lane = lax.broadcasted_iota(jnp.int32, (rows, LF), 1)
    rate = jnp.exp((lane % FREQ).astype(f32) * (-math.log(10000.0) / FREQ))
    coordinate = lane // (2 * FREQ)
    at = cols[:, 3:4]
    for i in range(3):
        at = jnp.where(coordinate == i, cols[:, i : i + 1], at)
    angle = at * rate
    out[...] = jnp.where(lane // FREQ % 2 == 0, jnp.sin(angle), jnp.cos(angle)).astype(jnp.bfloat16)


def forward_kernel(x_ref, tokens, boxes, pad, buckets, lengths,
                   g_ref, hidden, low, query, keys, values, ctx, soft, code_out, feats,
                   xv, tail, head, win, chunk, lsem, hsend, hrecv, own,
                   ssem, rsem, cr,
                   pads, hidden_v, low_v, query_v, keys_v, values_v, ctx_v, code, buckets_v, tokens_v, feats_v, p_v, s_scr, tab,
                   wl, wq, wk, wv, vrows, vf, ksend, krecv, wsem, isem, osem, psem):
    f32, bf = jnp.float32, jnp.bfloat16
    rows = tokens.shape[0]
    k, c, z, y, x = place()
    d = 2 * k + c
    inputs = [pltpu.make_async_copy(r, v, isem.at[i]) for i, (r, v) in enumerate(((buckets, buckets_v), (tokens, tokens_v)))]
    for copy in inputs:
        copy.start()
    pads[pl.ds(c, 1)] = jnp.broadcast_to(pad[...], (8, rows)).reshape(1, 8, rows)
    greet(k, c, z, y, x)
    load = pltpu.make_async_copy(x_ref, xv, lsem)
    load.start()
    prev = (jnp.where(c == 1, k, jnp.maximum(k - 1, 0)), 1 - c)
    nxt = (jnp.where(c == 0, k, jnp.minimum(k + 1, 15)), 1 - c)
    to_next = rcopy(x_ref.at[pl.ds(ROWS - TAIL, TAIL)], tail, hsend.at[0], hrecv.at[0], nxt)
    to_prev = rcopy(x_ref.at[pl.ds(0, HEAD)], head, hsend.at[1], hrecv.at[1], prev)

    @pl.when(d < 31)
    def _():
        to_next.start()

    @pl.when(d > 0)
    def _():
        to_prev.start()

    win[...] = jnp.zeros_like(win)
    lanes = lax.broadcasted_iota(jnp.int32, (80, 128), 1)
    q, sh = shard_start(d)
    load.wait()

    @pl.loop(0, ROWS // 80)
    def _(i):
        r = pl.multiple_of(i * 80, 8)
        rolled = pltpu.roll(xv[pl.ds(r, 80), :], sh, 1)
        win[pl.ds(160 + r, 80), :] += jnp.where(lanes >= sh, rolled, 0.0)
        win[pl.ds(161 + r, 80), :] += jnp.where(lanes < sh, rolled, 0.0)

    @pl.when(d > 0)
    def _():
        to_next.wait_recv()
        qp, shp = shard_start(d - 1)
        lanes = lax.broadcasted_iota(jnp.int32, (TAIL, 128), 1)
        rolled = pltpu.roll(tail[...], shp, 1)
        at = 1760 - (q - qp)
        win[pl.ds(at, TAIL), :] += jnp.where(lanes >= shp, rolled, 0.0)
        win[pl.ds(at + 1, TAIL), :] += jnp.where(lanes < shp, rolled, 0.0)

    @pl.when(d < 31)
    def _():
        to_prev.wait_recv()
        qn, shn = shard_start(d + 1)
        lanes = lax.broadcasted_iota(jnp.int32, (HEAD, 128), 1)
        rolled = pltpu.roll(head[...], shn, 1)
        at = 160 + (qn - q)
        win[pl.ds(at, HEAD), :] += jnp.where(lanes >= shn, rolled, 0.0)
        win[pl.ds(at + 1, HEAD), :] += jnp.where(lanes < shn, rolled, 0.0)

    early = early_vectors(k)
    nw0 = jnp.where(early, 36, 37)
    vecs = early == (c == 0)
    first = jnp.where(c == 0, 73 * k, 73 * k + nw0)
    base = q - 160

    @pl.loop(0, SLOTS)
    def _(t):
        at, wide = tile_start(first + t)
        is_vec = vecs & (t == 36)
        at = jnp.where(is_vec, vector_row(k, q), at) - base
        wide = wide & jnp.logical_not(is_vec)

        @pl.when(wide)
        def _():
            parts = [win[pl.ds(at + j, 8, stride=24), :] for j in range(6)]
            chunk[t] = jnp.concatenate(parts, axis=1).astype(jnp.bfloat16)

        @pl.when(jnp.logical_not(wide))
        def _():
            parts = [win[pl.ds(at + j, 8, stride=6), :] for j in range(6)]
            chunk[t] = jnp.concatenate(parts, axis=1).astype(jnp.bfloat16)

    @pl.when(d < 31)
    def _():
        to_next.wait_send()

    @pl.when(d > 0)
    def _():
        to_prev.wait_send()

    xdev, ydev, cdev = (z * 4 + y * 2 + 1 - x, c), (z * 4 + (1 - y) * 2 + x, c), (k, 1 - c)
    targets = {1: xdev, 2: ydev, 3: (jnp.minimum(k + 4, 15), c), 4: (jnp.maximum(k - 4, 0), c), 5: cdev}
    tiles = g_ref.reshape(16 * CHIP, 8, D)

    def step(zz, op):
        if op < 0:
            make_values()
            return
        link, item, p = op // 128, op // 8 % 16, op % 8
        chip = item // 4 * 4 + (1 - y if item // 2 % 2 else y) * 2 + (1 - x if item % 2 else x)
        off, n = (0, 37) if link == 5 else GATHER_PARTS[p]
        there = g_ref.at[chip, pl.ds(37 * c + off, n)]
        if link == 0:
            rcopy(there, there, ssem.at[0], rsem.at[chip, p], xdev).wait_recv()
            return
        here = chunk.at[pl.ds(off, n)] if item == zz * 4 else there
        rcopy(here, there, ssem.at[link - 1], cr.at[chip] if link == 5 else rsem.at[chip, p], targets[link]).start()

    def steps_of(zz, which, head=0):
        for op in GATHER_STEPS[zz][which] if which < 2 else GATHER_STEPS[zz][2].get(head, ()):
            step(zz, op)

    def sent_rows(zz, link):
        ops = [op for w in (0, 1) for op in GATHER_STEPS[zz][w]] + [op for v in GATHER_STEPS[zz][2].values() for op in v]
        return sum(37 if link == 5 else GATHER_PARTS[op % 8][1] for op in ops if op // 128 == link)

    pair_pads = rcopy(pads.at[pl.ds(c, 1)], pads.at[pl.ds(c, 1)], ksend.at[2], krecv.at[2], cdev)
    pair_pads.start()
    mine = pltpu.make_async_copy(chunk, g_ref.at[k, pl.ds(37 * c, 37)], own.at[0])

    for zz in range(4):
        @pl.when(z == zz)
        def _():
            steps_of(zz, 0)
    mine.start()
    for copy in inputs:
        copy.wait()
    pair_pads.wait()
    fill_codes(code, buckets_v, pads, lengths)
    fill_features(feats_v, boxes)
    outs = [pltpu.make_async_copy(code, code_out, osem.at[0]), pltpu.make_async_copy(feats_v, feats, osem.at[7])]
    for copy in outs:
        copy.start()
    for zz in range(4):
        @pl.when(z == zz)
        def _():
            steps_of(zz, 1)
    mine.wait()

    def from_partner(chip):
        theirs = g_ref.at[chip, pl.ds(37 * (1 - c), 37)]
        rcopy(theirs, theirs, ssem.at[4], cr.at[chip], cdev).wait_recv()

    for chip in range(3):
        from_partner(chip)

    loads = [pltpu.make_async_copy(tiles.at[vector_at(ch)], vrows.at[i], wsem.at[i]) for i, ch in enumerate((0, 1))]
    loads += pieces(tiles, wl, 0, 16, wsem, 4) + pieces(tiles, wk, 112, 96, wsem, 8) + pieces(tiles, wq, 16, 96, wsem, 16)
    for copy in loads:
        copy.start()
    for copy in loads:
        copy.wait()
    vf[0] = vrows[0].astype(f32)
    vf[1] = vrows[1].astype(f32)
    fill_table(tab, vrows.at[0])
    h = tokens_v[...].astype(f32) + jnp.dot(feats_v[...], matrix(wl[...]), preferred_element_type=f32) + vf[0, 0:1, :]
    hidden_v[...] = h
    low_v[...] = h.astype(bf)
    half_rows = pl.ds(c * rows, rows)

    def share(ref, i):
        return rcopy(ref.at[half_rows], ref.at[half_rows], ksend.at[i], krecv.at[i], cdev)

    keys_v[half_rows, :] = jnp.dot(low_v[...], matrix(wk[...]), preferred_element_type=f32).astype(bf)
    share(keys_v, 0).start()
    query_v[...] = ((jnp.dot(low_v[...], matrix(wq[...]), preferred_element_type=f32) + vf[1, 0:1, :]) * 0.125).astype(bf)
    share(keys_v, 0).wait()
    outs += [pltpu.make_async_copy(v, r, osem.at[1 + i]) for i, (v, r) in enumerate(((hidden_v, hidden), (low_v, low), (query_v, query), (keys_v, keys)))]
    for copy in outs[2:]:
        copy.start()

    def make_values():
        for chip in (3, 4):
            from_partner(chip)
        copies = [pltpu.make_async_copy(tiles.at[vector_at(4)], vrows.at[2], wsem.at[2])] + pieces(tiles, wv, 208, 96, wsem, 12)
        for copy in copies:
            copy.start()
        for copy in copies:
            copy.wait()
        vf[2] = vrows[2].astype(f32)
        values_v[half_rows, :] = (jnp.dot(low_v[...], matrix(wv[...]), preferred_element_type=f32) + vf[2, 0:1, :]).astype(bf)
        share(values_v, 1).start()

    def keep(pair):
        return pltpu.make_async_copy(p_v.at[pl.ds(2 * pair, 2)], soft.at[pl.ds(2 * pair, 2)], psem.at[pair])

    for zz in range(4):
        if -1 in GATHER_STEPS[zz][2]:
            @pl.when(z == zz)
            def _():
                steps_of(zz, 2, -1)

    def one_head(head, _):
        lanes = pl.ds(pl.multiple_of(head // 2 * 128, 128), 128)
        soft_head(head, query_v[:, lanes], keys_v[:, lanes], code, tab, s_scr, p_v.at[head])

        @pl.when(head % 2 == 1)
        def _():
            keep(head // 2).start()

        for zz in range(4):
            for i in range(H):
                if i in GATHER_STEPS[zz][2]:
                    @pl.when((head == i) & (z == zz))
                    def _():
                        steps_of(zz, 2, i)
        return 0

    lax.fori_loop(0, H, one_head, 0)
    share(values_v, 1).wait()
    outs.append(pltpu.make_async_copy(values_v, values, osem.at[5]))
    outs[-1].start()

    def context(pair, _):
        lanes = pl.ds(pl.multiple_of(pair * 128, 128), 128)
        ctx_v[:, lanes] = context_pair(values_v[:, lanes], p_v.at[pl.ds(2 * pair, 2)])
        return 0

    lax.fori_loop(0, H // 2, context, 0)
    outs.append(pltpu.make_async_copy(ctx_v, ctx, osem.at[6]))
    outs[-1].start()

    for zz in range(4):
        @pl.when(z == zz)
        def _():
            for link in range(1, 6):
                n = sent_rows(zz, link)
                if n:
                    whole = tiles.at[pl.ds(0, n)]
                    rcopy(whole, whole, ssem.at[link - 1], cr.at[0], targets[link]).wait_send()
    for chip in range(5, 16):
        from_partner(chip)
    for pair in range(H // 2):
        keep(pair).wait()
    for copy in outs:
        copy.wait()


def gather_and_attend(master, tokens, boxes, pad, buckets, page_lengths):
    x = jnp.pad(master, (0, ROWS * 128 - SHARD)).reshape(ROWS, 128)
    sem = pltpu.SemaphoreType.DMA
    any_, vm = pl.BlockSpec(memory_space=pl.ANY), pl.BlockSpec(memory_space=pltpu.VMEM)
    rows, key_rows = buckets.shape
    f32, bf = jnp.float32, jnp.bfloat16
    S, V = jax.ShapeDtypeStruct, pltpu.VMEM
    w = V((96, 8, D), bf)
    return pl.pallas_call(
        forward_kernel,
        out_shape=[
            S((16, CHIP, 8, D), bf), S((rows, D), f32), S((rows, D), bf), S((rows, D), bf), S((key_rows, D), bf), S((key_rows, D), bf),
            S((rows, D), bf), S((H, key_rows, rows), bf), S((key_rows, rows), jnp.int32), S((rows, LF), bf),
        ],
        in_specs=[any_, any_, vm, vm, any_, pl.BlockSpec(memory_space=pltpu.SMEM)],
        out_specs=[any_] * 10,
        scratch_shapes=[
            V((ROWS, 128), f32), V((TAIL, 128), f32), V((HEAD, 128), f32), V((WIN, 128), f32), V((SLOTS, 8, D), bf),
            sem, sem((2,)), sem((2,)), sem((2,)),
            sem((5,)), sem((16, 6)), sem((16,)),
            V((2, 8, rows), jnp.int32), V((rows, D), f32), V((rows, D), bf), V((rows, D), bf), V((key_rows, D), bf), V((key_rows, D), bf),
            V((rows, D), bf), V((key_rows, rows), jnp.int32), V((rows, key_rows), jnp.int32), V((rows, D), bf), V((rows, LF), bf),
            V((H, key_rows, rows), bf), V((key_rows, rows), f32), V((16, 128), f32),
            V((16, 8, D), bf), w, w, w, V((3, 8, D), bf), V((3, 8, D), f32),
            sem((3,)), sem((3,)), sem((20,)), sem((3,)), sem((8,)), sem((H // 2,)),
        ],
        compiler_params=pltpu.CompilerParams(collective_id=0, has_side_effects=True, vmem_limit_bytes=60 << 20),
        name="gather_and_attend",
    )(x, tokens, boxes, pad, buckets, page_lengths)


def guarded(cond, f):
    if cond is True:
        f()
    elif cond is not False:
        pl.when(cond)(f)


class Reducer:
    def __init__(self, where, zs, want, spare, g_ref, acc, crecv, a1, b1, a2, b2, asem, cs, cr, a1s, a1r, b1s, b1r, a2s, a2r, b2s, b2r):
        self.k, self.c, self.z, self.y, self.x = where
        self.zs, self.want, self.spare = zs, want, spare
        self.g_ref, self.acc, self.crecv = g_ref, acc, crecv
        self.bufs = (a1, b1, a2, b2)
        self.asem, self.cs, self.cr = asem, cs, cr
        self.sems = ((a1s, a1r), (b1s, b1r), (a2s, a2r), (b2s, b2r))
        z, y, x, c = self.z, self.y, self.x, self.c
        self.xdev, self.ydev, self.cdev = (z * 4 + y * 2 + 1 - x, c), (z * 4 + (1 - y) * 2 + x, c), (self.k, 1 - c)

    def at(self, zo, oy, ox):
        return zo, (1 - self.y if oy else self.y), (1 - self.x if ox else self.x)

    def chip(self, zo, yo, xo):
        return zo * 4 + yo * 2 + xo

    def local(self, zo, yo, xo):
        return self.chip(zo, yo, xo)

    def load(self, item):
        i = self.local(*item)
        return pltpu.make_async_copy(self.g_ref.at[self.chip(*item), pl.ds(37 * self.c, 37)], self.acc.at[i], self.asem.at[i])

    def ccopy(self, item):
        i = self.local(*item)
        return rcopy(self.g_ref.at[self.chip(*item), pl.ds(37 * (1 - self.c), 37)], self.crecv.at[i + self.spare], self.cs.at[i], self.cr.at[i], self.cdev)

    def hop(self, which, item, slot, p, dev):
        s, r = self.sems[which]
        return rcopy(self.acc.at[self.local(*item), pl.ds(*PARTS[p])], self.bufs[which].at[slot], s.at[slot], r.at[slot], dev)

    def a1(self, zo, xo):
        return self.hop(0, (zo, 1 - self.y, xo), self.zs.index(zo) * 2 + xo, 0, self.ydev)

    def b1(self, zo, yo):
        return self.hop(1, (zo, yo, 1 - self.x), self.zs.index(zo) * 2 + yo, 1, self.xdev)

    def a2(self, zo):
        return self.hop(2, (zo, self.y, 1 - self.x), self.zs.index(zo), 0, self.xdev)

    def b2(self, zo):
        return self.hop(3, (zo, 1 - self.y, self.x), self.zs.index(zo), 1, self.ydev)

    def gain(self, item, p, which, slot):
        off, n = PARTS[p]
        i, acc, buf = self.local(*item), self.acc, self.bufs[which]
        acc[i, pl.ds(off, n)] = acc[i, pl.ds(off, n)] + buf[slot]

    def begin(self, zo, oy, ox):
        item = self.at(zo, oy, ox)

        def go():
            self.load(item).start()
            self.ccopy(item).start()
        guarded(self.want(*item), go)

    def first(self, zo, oy, ox):
        item = self.at(zo, oy, ox)

        def go():
            self.load(item).wait()
            self.ccopy(item).wait_recv()
            i = self.local(*item)
            self.acc[i] = self.acc[i] + self.crecv[i + self.spare]
            if oy:
                self.a1(zo, item[2]).start()
            if ox:
                self.b1(zo, item[1]).start()
        guarded(self.want(*item), go)

    def second(self, zo):
        ia, ib = self.at(zo, 0, 1), self.at(zo, 1, 0)
        n = self.zs.index(zo) * 2

        def go_a():
            self.a1(zo, 1 - self.x).wait_recv()
            self.gain(ia, 0, 0, n + 1 - self.x)
            self.a2(zo).start()

        def go_b():
            self.b1(zo, 1 - self.y).wait_recv()
            self.gain(ib, 1, 1, n + 1 - self.y)
            self.b2(zo).start()
        guarded(self.want(*ia), go_a)
        guarded(self.want(*ib), go_b)

    def third(self, zo):
        item = self.at(zo, 0, 0)
        n = self.zs.index(zo)

        def go():
            self.a1(zo, self.x).wait_recv()
            self.b1(zo, self.y).wait_recv()
            self.a2(zo).wait_recv()
            self.b2(zo).wait_recv()
            i = self.local(*item)
            for p, (h, u), at in ((0, (0, 2), self.x), (1, (1, 3), self.y)):
                off, m = PARTS[p]
                self.acc[i, pl.ds(off, m)] = (self.acc[i, pl.ds(off, m)] + self.bufs[h][n * 2 + at]) + self.bufs[u][n]
        guarded(self.want(*item), go)

    def finish(self):
        for zo in self.zs:
            for oy in (0, 1):
                for ox in (0, 1):
                    item = self.at(zo, oy, ox)

                    def sent(item=item, oy=oy, ox=ox, zo=zo):
                        self.ccopy(item).wait_send()
                        if oy:
                            self.a1(zo, item[2]).wait_send()
                        if ox:
                            self.b1(zo, item[1]).wait_send()
                        if ox and not oy:
                            self.a2(zo).wait_send()
                        if oy and not ox:
                            self.b2(zo).wait_send()
                    guarded(self.want(*item), sent)


def reducer_scratch():
    bf, sem = jnp.bfloat16, pltpu.SemaphoreType.DMA
    tile = (8, D)
    return [
        pltpu.VMEM((16, 37) + tile, bf), pltpu.VMEM((11, 37) + tile, bf),
        pltpu.VMEM((8, 19) + tile, bf), pltpu.VMEM((8, 18) + tile, bf), pltpu.VMEM((4, 19) + tile, bf), pltpu.VMEM((4, 18) + tile, bf),
        sem((16,)), sem((16,)), sem((16,)),
        sem((8,)), sem((8,)), sem((8,)), sem((8,)), sem((4,)), sem((4,)), sem((4,)), sem((4,)),
    ]


def early_item(zo, yo, xo):
    return zo >= 2 if zo != 1 else yo + xo > 0


def late_item(zo, yo, xo):
    return zo == 0 if zo != 1 else yo + xo == 0


ZCUTS = ((0, 10), (10, 9), (19, 9), (28, 9))


class Chain:
    def __init__(self, where, acc, up, dn, us, ur, ds_, dr):
        self.k, self.c, self.z, self.y, self.x = where
        self.acc = acc
        self.ways = {1: (up, us, ur, (jnp.minimum(self.k + 4, 15), self.c)), -1: (dn, ds_, dr, (jnp.maximum(self.k - 4, 0), self.c))}

    def chip(self, zo):
        return zo * 4 + self.y * 2 + self.x

    def copy(self, zo, way, p):
        buf, s, r, dev = self.ways[way]
        part = pl.ds(*ZCUTS[p])
        return rcopy(self.acc.at[self.chip(zo), part], buf.at[zo, part], s.at[zo, p], r.at[zo, p], dev)

    def move(self, zs, zo, way, take=True, give=True, also=None):
        cond = self.z == zs if also is None else (self.z == zs) & also

        @pl.when(cond)
        def _():
            i = self.chip(zo)
            for p in range(4):
                if take:
                    self.copy(zo, way, p).wait_recv()
                    part = pl.ds(*ZCUTS[p])
                    self.acc[i, part] = self.acc[i, part] + self.ways[way][0][zo, part]
                if give:
                    self.copy(zo, way, p).start()

    def sent(self, zs, zo, way):
        @pl.when(self.z == zs)
        def _():
            for p in range(4):
                self.copy(zo, way, p).wait_send()


def chain_scratch():
    bf, sem = jnp.bfloat16, pltpu.SemaphoreType.DMA
    return [pltpu.VMEM((4, 37, 8, D), bf)] * 2 + [sem((4, 4))] * 4


def backward_kernel(tiles, q_ref, k_ref, v_ref, do_ref, p_hbm, code_hbm, gfi_in, low_in, feats_in, grads_in, m_ref, one_ref, two_ref,
                    grad_out, grads, step_ref, new1_ref, new2_ref, spread,
                    pbuf, qv, kv, vv, dov, psem, code_ref, csem, dsv, dssem, group, gsem, counts, dks, dvs, out, come, sends, recvs, back, bias,
                    wq, wk, wv, low, gfi, feats, dwl, dwq, dwk, dwv, vgrads, wsem, ssem, isem,
                    total, ebuf, sq, sqr, win, mv, onev, twov, lsem, es, er, qs, qr, *scratch):
    f32, bf = jnp.float32, jnp.bfloat16
    where = place()
    k, c, z, y, x = where
    d = 2 * k + c
    shared = grads.reshape(16, CHIP, 8, D)
    rs = Reducer(where, (0, 1, 2, 3), early_item, -5, shared, *scratch[:17])
    late = Reducer(where, (0, 1, 2, 3), late_item, 6, shared, *scratch[:17])
    acc = rs.acc
    zc = Chain(where, acc, *scratch[17:])
    xdev, ydev, cdev = rs.xdev, rs.ydev, rs.cdev
    column_devs = [((z + s) % 4 * 4 + y * 2 + x, c) for s in (1, 2, 3)]
    prev = (jnp.where(c == 1, k, jnp.maximum(k - 1, 0)), 1 - c)
    nxt = (jnp.where(c == 0, k, jnp.minimum(k + 1, 15)), 1 - c)
    bar = pltpu.get_barrier_semaphore()
    far_next, far_prev = (c == 1) & (k < 15), (c == 0) & (k > 0)
    plane_devs = [(z * 4 + (1 - y if oy else y) * 2 + (1 - x if ox else x), 1 - c if oc else c) for oc in (0, 1) for oy in (0, 1) for ox in (0, 1)][1:]
    for dev in plane_devs + column_devs:
        pl.semaphore_signal(bar, inc=1, device_id=dev, device_id_type=MESH)

    @pl.when(far_next)
    def _():
        pl.semaphore_signal(bar, inc=1, device_id=nxt, device_id_type=MESH)

    @pl.when(far_prev)
    def _():
        pl.semaphore_signal(bar, inc=1, device_id=prev, device_id_type=MESH)

    keys, rows = code_ref.shape

    def fetch_soft(pair, hh):
        return pltpu.make_async_copy(p_hbm.at[2 * pair + hh], pbuf.at[hh], psem.at[0, hh])

    def fetch(p):
        slot = p % 2
        lanes = pl.ds(pl.multiple_of(p * 128, 128), 128)
        return [pltpu.make_async_copy(r.at[:, lanes], v.at[slot], psem.at[1 + i, slot]) for i, (r, v) in enumerate(((q_ref, qv), (k_ref, kv), (v_ref, vv), (do_ref, dov)))]

    for copy in fetch(0) + [fetch_soft(0, 0), fetch_soft(0, 1)]:
        copy.start()
    pl.semaphore_wait(bar, 10 + jnp.where(far_next | far_prev, 1, 0))
    corners = ((1, 1), (1, 0), (0, 1), (0, 0))
    for oy, ox in corners:
        rs.begin(3, oy, ox)
    code_copy = pltpu.make_async_copy(code_hbm, code_ref, csem.at[0])
    inputs = [pltpu.make_async_copy(r, v, isem.at[i]) for i, (r, v) in enumerate(((low_in, low), (gfi_in, gfi), (feats_in, feats)))]
    loads = pieces(tiles, wq, 16, 96, wsem, 8) + pieces(tiles, wv, 208, 96, wsem, 4) + pieces(tiles, wk, 112, 96, wsem, 0)
    shards = [pltpu.make_async_copy(r, v, lsem.at[i]) for i, (r, v) in enumerate(((m_ref, mv), (one_ref, onev), (two_ref, twov)))]
    for copy in [code_copy] + inputs + loads + shards:
        copy.start()
    own, other = pl.ds(c * rows, rows), pl.ds((1 - c) * rows, rows)

    def swap(pair):
        return rcopy(out.at[pair], come.at[pair], sends.at[pair], recvs.at[pair], cdev)

    def settle(pair):
        slot = pair % 2
        swap(pair).wait_recv()
        lanes = pl.ds(pl.multiple_of(pair * 128, 128), 128)
        dk = dks[slot, own, :] + come[pair, 0].astype(f32)
        dv = dvs[slot, own, :] + come[pair, 1].astype(f32)
        back[1, :, lanes] = dk.astype(bf)
        back[2, :, lanes] = dv.astype(bf)
        bias[1, :, lanes] = col_sum(dv)

    def lay(pair, hh):
        return pltpu.make_async_copy(dsv.at[hh], spread.at[:, 2 * pair + hh], dssem.at[hh])

    plan = {
        0: [(rs.first, 3, 1, 0), (rs.begin, 2, 1, 1), (rs.begin, 2, 1, 0), (rs.begin, 2, 0, 1), (rs.begin, 2, 0, 0), (rs.first, 3, 0, 1)],
        1: [(rs.begin, 1, 1, 1), (rs.begin, 1, 1, 0), (rs.begin, 1, 0, 1), (rs.begin, 1, 0, 0), (rs.first, 2, 1, 1), (rs.first, 2, 0, 1), (rs.second, 3)],
        2: [(rs.first, 2, 1, 0)],
        4: [(rs.first, 2, 0, 0), (rs.second, 2), (rs.first, 3, 0, 0), (rs.first, 1, 1, 1)],
    }
    rs.first(3, 1, 1)

    def pair_of_heads(pair, _):
        slot = pair % 2

        @pl.when(pair < H // 2 - 1)
        def _():
            for copy in fetch(pair + 1):
                copy.start()

        for copy in fetch(pair):
            copy.wait()
        lanes = pl.ds(pl.multiple_of(pair * 128, 128), 128)
        dq = []
        for hh in range(2):
            fetch_soft(pair, hh).wait()
            qm = half(qv[slot], hh)
            dom = half(dov[slot], hh)
            g = lax.dot_general(vv[slot], dom, NT, preferred_element_type=f32)
            p = pbuf[hh]
            pf = p.astype(f32)
            inner = jnp.sum(jnp.sum((g * pf).reshape(keys // 8, 8, rows), axis=0), axis=0, keepdims=True)
            ds = (pf * (g - inner)).astype(bf)

            @pl.when(pair > 0)
            def _():
                lay(pair - 1, hh).wait()

            dsv[hh] = ds.reshape(keys // 8, 8, rows)
            lay(pair, hh).start()
            dv = jnp.dot(p, dom, preferred_element_type=f32)

            @pl.when(pair < H // 2 - 1)
            def _():
                fetch_soft(pair + 1, hh).start()

            dk = jnp.dot(ds, qm, preferred_element_type=f32)
            if hh == 0:
                dvs[slot] = dv
                dks[slot] = dk
            else:
                dvs[slot] += dv
                dks[slot] += dk
            dq.append(lax.dot_general(kv[slot], ds, TN, preferred_element_type=f32))
        out[pair, 0] = dks[slot, other, :].astype(bf)
        out[pair, 1] = dvs[slot, other, :].astype(bf)
        swap(pair).start()
        sub = lax.broadcasted_iota(jnp.int32, dq[0].shape, 0)
        dqf = jnp.where(sub < 64, dq[0], dq[1]).T * 0.125
        back[0, :, lanes] = dqf.astype(bf)
        bias[0, :, lanes] = col_sum(dqf)

        @pl.when(pair > 0)
        def _():
            settle(pair - 1)

        for i, steps in plan.items():
            @pl.when(pair == i)
            def _():
                for f, *a in steps:
                    f(*a)
        return 0

    lax.fori_loop(0, H // 2, pair_of_heads, 0)
    for hh in range(2):
        lay(H // 2 - 1, hh).wait()
    for copy in inputs + loads:
        copy.wait()

    def through(i, w, dw):
        dw[...] = lax.dot_general(low[...], back[i], TN, preferred_element_type=f32).astype(bf).reshape(96, 8, D)
        return lax.dot_general(back[i], matrix(w[...]), NT, preferred_element_type=f32)

    stores = []

    def keep(dw, first, count, base):
        made = pieces(grads, dw, first, count, ssem, base, True)
        for copy in made:
            copy.start()
        stores.extend(made)

    gfi[...] += through(0, wq, dwq)
    keep(dwq, 16, 96, 0)
    settle(H // 2 - 1)
    gfi[...] += through(2, wv, dwv)
    keep(dwv, 208, 96, 8)
    whole = gfi[...] + through(1, wk, dwk)
    keep(dwk, 112, 96, 4)
    gfi[...] = whole
    shown = pltpu.make_async_copy(gfi, grad_out, isem.at[6])
    shown.start()
    layout_bias = jnp.sum(col_sum(whole), axis=0, keepdims=True)
    dwl[...] = lax.dot_general(feats[...], whole.astype(bf), TN, preferred_element_type=f32).astype(bf).reshape(16, 8, D)
    keep(dwl, 0, 16, 12)

    def block(lines):
        return jnp.concatenate(lines + [jnp.zeros((8 - len(lines), D), f32)]).astype(bf)

    vgrads[0] = block([layout_bias])
    vgrads[1] = block([jnp.sum(bias[0], axis=0, keepdims=True)])
    vgrads[2] = block([jnp.sum(bias[1], axis=0, keepdims=True)])
    vgrads[3] = jnp.zeros((8, D), bf)
    held = {0: 0, 1: 1, 4: 2}
    for i, ch in enumerate((0, 1, 2, 3, 4)):
        copy = pltpu.make_async_copy(vgrads.at[held.get(ch, 3)], grads.at[vector_at(ch)], ssem.at[16 + i])
        copy.start()
        stores.append(copy)
    for copy in stores:
        copy.wait()
    for oy, ox in corners:
        for zo in (0, 1):
            late.begin(zo, oy, ox)

    GROUPS = 16

    def take_groups(i):
        return pltpu.make_async_copy(spread.at[pl.ds(i * GROUPS, GROUPS)], group.at[i % 2], gsem.at[i % 2])

    bucket = lax.broadcasted_iota(jnp.int32, (BUCKETS, rows), 0)
    steps = keys // 8 // GROUPS
    code_copy.wait()
    take_groups(0).start()
    counts[...] = jnp.zeros_like(counts)

    def count_some(first, n):
        for i in range(first, first + n):
            if i + 1 < steps:
                take_groups(i + 1).start()
            take_groups(i).wait()

            def count(j, run, i=i):
                code = code_ref[pl.ds(pl.multiple_of((i * GROUPS + j) * 8, 8), 8), :]
                hot = jnp.concatenate(
                    [jnp.where(jnp.broadcast_to(code[r : r + 1], bucket.shape) == bucket, 1.0, 0.0) for r in range(8)]
                ).astype(bf)
                return run + lax.dot_general(group[i % 2, j].reshape(8 * H, rows), hot, NT, preferred_element_type=f32)

            counts[...] = lax.fori_loop(0, GROUPS, count, counts[...], unroll=8)

    early_one, late_one = rs.want(1, y, x), late.want(1, y, x)
    rs.third(3)
    zc.move(0, 3, 1, take=False)
    late.first(0, 1, 1)
    late.first(1, 1, 1)
    zc.move(1, 3, 1)
    late.first(0, 1, 0)
    late.first(1, 1, 0)
    count_some(0, 1)
    late.first(0, 0, 1)
    late.first(1, 0, 1)
    rs.third(2)
    count_some(1, 1)
    count_some(2, 1)
    late.first(0, 0, 0)
    late.first(1, 0, 0)
    zc.move(0, 2, 1, take=False)
    zc.move(2, 3, 1)
    zc.move(3, 2, -1, take=False)
    count_some(3, 1)
    late.second(0)
    late.second(1)
    rs.first(1, 0, 1)
    count_some(4, 1)
    rs.first(1, 1, 0)
    count_some(5, 1)
    zc.move(1, 2, 1)
    rs.second(1)
    count_some(6, 1)
    late.third(0)
    zc.move(3, 0, -1, take=False)
    late.third(1)
    zc.move(0, 1, 1, take=False, also=late_one)
    zc.move(3, 1, -1, take=False, also=late_one)
    zc.move(2, 0, -1)
    zc.move(2, 1, -1, also=late_one)
    zc.move(1, 0, -1)
    count_some(7, 1)
    rs.first(1, 0, 0)
    rs.third(1)
    zc.move(2, 1, -1, also=early_one)
    zc.move(3, 1, -1, take=False, also=early_one)
    zc.move(0, 1, 1, take=False, also=early_one)
    table = table_row(counts[...], (8, D))

    total[...] = acc[k].astype(f32)

    def add(way, zo):
        buf = zc.ways[way][0]
        for p in range(4):
            zc.copy(zo, way, p).wait_recv()
        total[...] = total[...] + buf[zo].astype(f32)

    @pl.when(z == 0)
    def _():
        add(-1, 0)

    @pl.when(z == 1)
    def _():
        add(1, 1)
        add(-1, 1)

    @pl.when(z == 2)
    def _():
        add(1, 2)
        add(-1, 2)

    @pl.when(z == 3)
    def _():
        add(1, 3)

    early = early_vectors(k)
    nw0 = jnp.where(early, 36, 37)
    vecs = early == (c == 0)
    mine = jnp.where(vecs, 36, 37)
    to_next = rcopy(total.at[pl.ds(mine - EDGE, EDGE)], ebuf.at[0], es.at[0], er.at[0], nxt)
    to_prev = rcopy(total.at[pl.ds(0, EDGE)], ebuf.at[1], es.at[1], er.at[1], prev)

    @pl.when(d < 31)
    def _():
        to_next.start()

    @pl.when(d > 0)
    def _():
        to_prev.start()

    def square(i, run):
        t = total[i]
        t = t * t
        for j in range(6):
            run = run + t[:, 128 * j:128 * j + 128]
        return run

    squares = lax.fori_loop(0, 37, square, jnp.zeros((8, 128), f32))
    lines = [jnp.sum(squares, axis=0, keepdims=True)] + [table[0:1, 128 * i : 128 * i + 128] for i in range(3)]
    place_in = c * 4 + y * 2 + x
    sq[0] = jnp.concatenate(lines + [jnp.zeros((4, 128), f32)])
    sqr[place_in] = sq[0]
    rounds = [rcopy(sq.at[0], sqr.at[place_in], qs.at[i], qr.at[place_in], dev) for i, dev in enumerate(plane_devs)]
    hops = [rcopy(sq.at[1], sqr.at[8 + z], qs.at[7 + i], qr.at[8 + z], dev) for i, dev in enumerate(column_devs)]
    for h in rounds:
        h.start()

    def arrived(slot):
        return rcopy(sqr.at[slot], sqr.at[slot], qs.at[0], qr.at[slot], cdev)

    rs.finish()
    late.finish()
    for zs in (0, 1, 2):
        zc.sent(zs, 3, 1)
    for zs in (0, 1):
        zc.sent(zs, 2, 1)
    zc.sent(3, 2, -1)
    zc.sent(0, 1, 1)
    zc.sent(3, 1, -1)
    zc.sent(2, 1, -1)
    for zs in (1, 2, 3):
        zc.sent(zs, 0, -1)
    for pair in range(H // 2):
        swap(pair).wait_send()
    q, sh = shard_start(d)
    base = q - FRONT

    def flatten(ref, i, at, wide):
        @pl.when(wide)
        def _():
            t = ref[i]
            for j in range(6):
                win[pl.ds(at + j, 8, stride=24), :] = t[:, 128 * j:128 * j + 128]

        @pl.when(jnp.logical_not(wide))
        def _():
            t = ref[i]
            for j in range(6):
                win[pl.ds(at + j, 8, stride=6), :] = t[:, 128 * j:128 * j + 128]

    own_vectors = vecs & (vector_row(k, -1) >= 0)

    @pl.when(own_vectors)
    def _():
        flatten(total, 36, vector_row(k, q) - base, k < 0)

    w0 = jnp.where(c == 0, 73 * k, 73 * k + nw0)

    @pl.loop(0, mine)
    def _(t):
        at, wide = tile_start(w0 + t)
        flatten(total, t, at - base, wide)

    for i in range(8):
        @pl.when(place_in != i)
        def _():
            arrived(i).wait_recv()
    layer = sqr[0]
    for i in range(1, 8):
        layer = layer + sqr[i]
    sq[1] = layer
    sqr[8 + z] = layer
    for h in hops:
        h.start()
    @pl.when(d > 0)
    def _():
        to_next.wait_recv()

        @pl.loop(0, EDGE)
        def _(t):
            at, wide = tile_start(w0 - EDGE + t)
            flatten(ebuf.at[0], t, at - base, wide)

    @pl.when(d < 31)
    def _():
        to_prev.wait_recv()

        @pl.loop(0, EDGE)
        def _(t):
            at, wide = tile_start(w0 + mine + t)
            flatten(ebuf.at[1], t, at - base, wide)

    for i in range(4):
        @pl.when(z != i)
        def _():
            arrived(8 + i).wait_recv()
    summed = (sqr[8] + sqr[9]) + (sqr[10] + sqr[11])

    @pl.when(d == 0)
    def _():
        for i in range(3):
            win[pl.ds(FRONT + 774 + i, 1), :] = summed[1 + i : 2 + i]

    sub = lax.broadcasted_iota(jnp.int32, (8, 128), 0)
    entries = jnp.where(sub == 0, summed, jnp.where(sub < 4, summed * summed, 0.0))
    square_sum = jnp.sum(jnp.sum(entries, axis=1, keepdims=True), axis=0, keepdims=True)
    factor = jnp.minimum(1.0, lax.rsqrt(square_sum / RAW + 1e-06))
    for s in shards:
        s.wait()
    lanes = lax.broadcasted_iota(jnp.int32, (80, 128), 1)
    rowi = lax.broadcasted_iota(jnp.int32, (80, 128), 0)
    back = (128 - sh) % 128

    @pl.loop(0, ROWS // 80)
    def _(i):
        r = pl.multiple_of(i * 80, 8)
        here = pltpu.roll(win[pl.ds(FRONT + r, 80), :], back, 1)
        there = pltpu.roll(win[pl.ds(FRONT + 1 + r, 80), :], back, 1)
        grad = jnp.where(lanes < 128 - sh, here, there) * factor
        entry = (d == 0) & (rowi + r < ENTRY_ROWS)
        rate = jnp.where(entry, learn_rate * layer_decay, learn_rate)
        one = beta_one * onev[pl.ds(r, 80), :] + (1.0 - beta_one) * grad
        two = beta_two * twov[pl.ds(r, 80), :] + (1.0 - beta_two) * grad * grad
        fixed_one = one / (1.0 - beta_one ** STEP)
        fixed_two = two / (1.0 - beta_two ** STEP)
        step = -rate * (fixed_one / (jnp.sqrt(fixed_two) + adam_eps) + weight_decay * mv[pl.ds(r, 80), :])
        mv[pl.ds(r, 80), :] = step
        onev[pl.ds(r, 80), :] = one
        twov[pl.ds(r, 80), :] = two

    results = [pltpu.make_async_copy(v, r, lsem.at[i]) for i, (v, r) in enumerate(((mv, step_ref), (onev, new1_ref), (twov, new2_ref)))]
    for copy in results:
        copy.start()

    for h in rounds + hops:
        h.wait_send()

    @pl.when(d < 31)
    def _():
        to_next.wait_send()

    @pl.when(d > 0)
    def _():
        to_prev.wait_send()

    shown.wait()
    for copy in results:
        copy.wait()


def backward_and_step(tiles, query, key_all, value_all, grad_context, soft, code, gfi, low, feats, grads, master, first_moment, second_moment):
    def rows_of(v):
        return jnp.pad(v, (0, ROWS * 128 - SHARD)).reshape(ROWS, 128)

    rows, keys = query.shape[0], key_all.shape[0]
    f32, bf = jnp.float32, jnp.bfloat16
    any_ = pl.BlockSpec(memory_space=pl.ANY)
    S, V, sem = jax.ShapeDtypeStruct, pltpu.VMEM, pltpu.SemaphoreType.DMA
    w = V((96, 8, D), bf)
    tile = (8, D)
    line = V((ROWS, 128), f32)
    outs = pl.pallas_call(
        backward_kernel,
        out_shape=[S((rows, D), f32), S(grads.shape, bf)] + [S((ROWS, 128), f32)] * 3 + [S((keys // 8, H, 8, rows), bf)],
        in_specs=[any_] * 14,
        out_specs=[any_] * 6,
        scratch_shapes=[
            V((2, keys, rows), bf), V((2, rows, 128), bf), V((2, keys, 128), bf), V((2, keys, 128), bf), V((2, rows, 128), bf), sem((5, 2)),
            V((keys, rows), jnp.int32), sem((1,)), V((2, keys // 8, 8, rows), bf), sem((2,)), V((2, 16, H, 8, rows), bf), sem((2,)),
            V((8 * H, 8 * BUCKETS), f32),
            V((2, keys, 128), f32), V((2, keys, 128), f32), V((6, 2, rows, 128), bf), V((6, 2, rows, 128), bf), sem((6,)), sem((6,)),
            V((3, rows, D), bf), V((2, 8, D), f32),
            w, w, w, V((rows, D), bf), V((rows, D), f32), V((rows, LF), bf), V((16, 8, D), bf), w, w, w, V((4, 8, D), bf),
            sem((12,)), sem((24,)), sem((7,)),
            V((37,) + tile, f32), V((2, EDGE) + tile, f32), V((2, 8, 128), f32), V((12, 8, 128), f32),
            V((WIN2, 128), f32), line, line, line, sem((3,)), sem((2,)), sem((2,)), sem((10,)), sem((12,)),
        ] + reducer_scratch() + chain_scratch(),
        input_output_aliases={10: 1},
        compiler_params=pltpu.CompilerParams(collective_id=5, has_side_effects=True, vmem_limit_bytes=63 << 20),
        name="backward_and_step",
    )(tiles, query, key_all, value_all, grad_context, soft, code, gfi, low, feats, grads, rows_of(master), rows_of(first_moment), rows_of(second_moment))
    return outs[0], [o.reshape(-1)[:SHARD] for o in outs[2:5]]


def from_tiles(tiles):
    got = {}
    for name, first, count in WEIGHTS:
        block = jnp.concatenate([tiles[s : s + n] for s, _, n in slots_of(first, count)])
        if name == 12:
            block = block.reshape(96, 4, 8, D).transpose(0, 2, 1, 3)
        got[name] = block.reshape(-1, FF if name == 12 else D)
    for name, chip, row in VECTORS:
        block = tiles[vector_at(chip)]
        if name == 13:
            got[name] = block[row : row + 4].reshape(FF)
        elif name == 2:
            got[name] = block[row, : BUCKETS * H].reshape(BUCKETS, H)
        else:
            got[name] = block[row]
    return [got[i] for i in range(18)]


def to_tiles(whole):
    by_name = [p.astype(jnp.bfloat16) for p in whole]
    weights = []
    for name, first, count in WEIGHTS:
        got = by_name[name]
        if name == 12:
            got = got.reshape(96, 8, 4, D).transpose(0, 2, 1, 3)
        weights.append(got.reshape(count, 8, D))
    cuts = []
    for chip in range(16):
        held = [(r, by_name[n]) for n, c, r in VECTORS if c == chip]
        rows = [jnp.pad(v.reshape(-1), (0, -v.size % D)).reshape(-1, D) for _, v in held]
        block = jnp.concatenate(rows + [jnp.zeros((8 - sum(r.shape[0] for r in rows), D), jnp.bfloat16)])
        cuts.append((73 * chip + vector_slot(chip), block[None]))
    parts = []
    for (name, first, count), tiles in zip(WEIGHTS, weights):
        at = first
        for w, block in [c for c in cuts if first <= c[0] < first + count]:
            if w > at:
                parts.append(tiles[at - first : w - first])
            parts.append(block)
            at = w
        parts.append(tiles[at - first :])
    parts.extend(block for w, block in cuts if w == 1168)
    return jnp.concatenate(parts)


def per_device(
    custom, tokens, cotangent, page_boxes, page_lengths, padding, buckets, master, first_moment, second_moment
):
    rows = tokens.shape[1]
    if custom:
        tiles, hidden, low, query, keys, values, ctx, soft, code, feats = gather_and_attend(
            master, tokens[0], page_boxes, padding, buckets[0], page_lengths
        )
        tiles = tiles.reshape(16 * CHIP, 8, D)
    else:
        feats = layout_features(page_boxes.reshape(4, rows)).astype(jnp.bfloat16)
        tiles = to_tiles(unpack(lax.all_gather(master.astype(jnp.bfloat16), ("dp", "seq"), axis=0, tiled=True)))
        hidden, low, query, keys, values, pads = enter(tiles, tokens[0], feats, jnp.broadcast_to(padding, (8, rows)))
        ctx, soft, code = attend(query, keys, values, buckets[0], page_lengths, pads, tiles[vector_at(0)])
    activations, grad_first_in, grad_context, grads = middle(tiles, ctx, hidden, cotangent[0])
    if custom:
        input_grad, stepped = backward_and_step(
            tiles, query, keys, values, grad_context, soft, code, grad_first_in, low, feats, grads, master, first_moment, second_moment
        )
    else:
        dq, dk, dv, table = soft_back(query, keys, values, grad_context, soft, code)
        input_grad, grads = leave(tiles, dq, dk, dv, grad_first_in, low, feats, table, grads)
        flat = jnp.concatenate([p.astype(jnp.float32).reshape(-1) for p in from_tiles(grads)])
        grad = lax.psum_scatter(flat, ("dp", "seq"), scatter_dimension=0, tiled=True)
        square = lax.psum(jnp.sum(grad * grad), ("dp", "seq"))
        factor = jnp.minimum(1.0, lax.rsqrt(square / RAW + 1e-06))
        size = master.shape[0]
        index = lax.axis_index(("dp", "seq")) * size + jnp.arange(size, dtype=jnp.int32)
        stepped = adam_update(master, first_moment, second_moment, grad * factor, index)
    return (activations[None], input_grad[None]) + tuple(stepped)


def solution(mesh):
    in_specs = (
        P("dp", "seq", None),
        P("dp", "seq", None),
        P(None, "dp", "seq"),
        P("dp", None),
        P("dp", "seq"),
        P("dp", "seq", None),
        P(("dp", "seq")),
        P(("dp", "seq")),
        P(("dp", "seq")),
    )
    out_specs = (
        P("dp", "seq", None),
        P("dp", "seq", None),
        P(("dp", "seq")),
        P(("dp", "seq")),
        P(("dp", "seq")),
    )
    custom = dict(mesh.shape) == {"dp": 16, "seq": 2}
    return jax.shard_map(
        functools.partial(per_device, custom), mesh=mesh, in_specs=in_specs, out_specs=out_specs, check_vma=False
    )
```
